32 devices in a mesh: rows: 4 (over y, x), seq: 8 (over z, core).
Axes of the slice: x: 2, y: 2, z: 4, core: 2. Of those that a mesh axis runs over, the one named last changes fastest.
Arguments:
- residual_in: float32 [32, 1024, 512], P('rows', 'seq'), may hold values from -6 to 6
- cotangent: float32 [32, 1024, 512], P('rows', 'seq'), may hold values from -6 to 6
- segments: int32 [32, 1024], P('rows'), may hold values from 0 to 7, never falling along the last dimension, each value on 1 to 512 neighbouring positions
- owners: int32 [96], replicated, may hold values from 0 to 7, as said below
- master_tiles: float32 [128, 512, 128], P('seq'), may hold values from -0.53033009 to 0.53033009, as said below
- first_tiles: float32 [128, 512, 128], P('seq'), may hold values from -0.0024414062 to 0.0024414062
- second_tiles: float32 [128, 512, 128], P('seq'), may hold values from 1.5873903e-07 to 6.349561e-07
- norm_params: float32 [8, 512], replicated, may hold values from -2 to 2
- norm_first: float32 [8, 512], replicated, may hold values from -0.009765625 to 0.009765625
- norm_second: float32 [8, 512], replicated, may hold values from 2.5398244e-06 to 1.0159298e-05
Outputs:
- residual_out: float32 [32, 1024, 512], P('rows', 'seq')
- input_grad: float32 [32, 1024, 512], P('rows', 'seq')
- tile_grads: float32 [128, 512, 128], P('seq')
- grad_norm: float32 [1], replicated
- new_first: float32 [128, 512, 128], P('seq')
- new_second: float32 [128, 512, 128], P('seq')
- new_master: float32 [128, 512, 128], P('seq')
- new_copies: bfloat16 [128, 512, 128], P('seq')
- norm_grads: float32 [8, 512], replicated
- new_norm_first: float32 [8, 512], replicated
- new_norm_second: float32 [8, 512], replicated
- new_norm_params: float32 [8, 512], replicated
The draws below stay inside these ranges and needn't reach their ends.
Inputs may be any that keep to these rules, and one draw needn't show every extreme that they name: `owners`: no device owns more than 16 tiles, and one device owns exactly 16. `segments`: along a row the document numbers never fall; a document has 1 to 512 positions and some document exactly 512. `master_tiles`: slot 16 d + n holds the tile with the n-th smallest number among those owned by device d; slots that hold no tile are ignored.
All inputs are finite; a program needn't handle non-finite values.
Results may differ from the reference program's by a relative error of at most 0.013.
Values may be sent and summed in bfloat16 or wider, within the bound.
A program may use at most 256 MiB of HBM per device.

```python
import math
from functools import partial
import jax
import jax.numpy as jnp
import numpy as np
from jax import lax

D = 512
HEADS = 8
HD = 64
LAYERS = 2
STEP = 5
LEN = 1024
ROWS = 32
DOCS = 8
DOC_MAX = 512
TW = 128
NT = 96
CAP = 16
SLOTS = 128


def owner_draw(key):
    first_key, second_key, third_key = jax.random.split(jax.random.fold_in(key, 31), 3)
    heavy = jax.random.randint(first_key, (), 0, SLOTS // CAP, dtype=jnp.int32)
    others = jax.random.permutation(second_key, SLOTS - CAP)[:NT - CAP].astype(jnp.int32)
    others = others + CAP * (others >= heavy * CAP).astype(jnp.int32)
    chosen = jnp.concatenate([heavy * CAP + jnp.arange(CAP, dtype=jnp.int32), others])
    order = jax.random.permutation(third_key, NT)
    slot_ids = jnp.zeros((NT,), jnp.int32).at[order].set(chosen)
    return (slot_ids // CAP).astype(jnp.int32)


def slot_of(owners):
    places = jnp.arange(NT, dtype=jnp.int32)
    before = (owners[None, :] == owners[:, None]) & (places[None, :] < places[:, None])
    return (owners * CAP + jnp.sum(before.astype(jnp.int32), axis=1)).astype(jnp.int32)


def draw_owners(key, part):
    return owner_draw(key)


def draw_master_tiles(key, part):
    slot_ids = slot_of(owner_draw(key))
    kinds = jnp.arange(NT) % 48
    spread = jnp.where(kinds < 12, 1.0, jnp.where(kinds < 16, 3.0, jnp.where(kinds < 32, 1.0, 0.5))) * D ** (-0.5)
    scales = jnp.zeros((SLOTS,), jnp.float32).at[slot_ids].set(spread.astype(jnp.float32))
    noise_key = jax.random.fold_in(key, 57)
    noise = jnp.clip(jax.random.normal(noise_key, (SLOTS, D, TW), jnp.float32), -4.0, 4.0)
    return noise * scales[:, None, None]


def draw_norm_params(key, part):
    noise_key = jax.random.fold_in(key, 73)
    noise = jnp.clip(jax.random.normal(noise_key, (4 * LAYERS, D), jnp.float32), -4.0, 4.0)
    parity = (jnp.arange(4 * LAYERS) % 2)[:, None]
    return jnp.where(parity == 0, 1.0 + 0.15 * noise, 0.3 * noise)


def steps_of(key, extent, cuts, smallest, top_value):
    loudness, own = 1.0, jax.random.fold_in(key, 6)
    for position, blocks in cuts:
        steps = jnp.exp(jax.random.uniform(jax.random.fold_in(own, position), (blocks,), jnp.float32, smallest / len(cuts), top_value / len(cuts)))
        loudness = loudness * jnp.repeat(steps, extent[position] // blocks).reshape([-1 if axis == position else 1 for axis in range(len(extent))])
    return loudness


def length_profile(count, total, limit, slope):
    portions = [(1 << 20) // math.isqrt(grade ** slope) + 1 for grade in range(2, count + 1)]
    rest, given = total - limit - (count - 1), [1] * (count - 1)
    while rest > 0:
        movable = [i for i in range(count - 1) if given[i] < limit]
        mass, left = sum([portions[i] for i in movable]), rest
        for i in movable:
            more = min(limit - given[i], max(1, left * portions[i] // mass), rest)
            given[i] = given[i] + more
            rest = rest - more
    return np.array([limit] + given)


def ragged_sizes(stream_key, amount, total, most, slope):
    if amount == 2:
        one = jax.random.randint(stream_key, (), max(1, total - most), min(most, total - 1) + 1)
        return jnp.stack([one, total - one])
    lengths = jnp.asarray(length_profile(amount, total, most, slope), jnp.int32)
    pairs = (amount - 1) // 2
    giver, taker = lengths[1:1 + 2 * pairs:2], lengths[2:2 + 2 * pairs:2]
    slack = jnp.minimum(giver - 1, most - taker)
    moved = jax.random.randint(jax.random.fold_in(stream_key, 1), (pairs,), 0, 1 << 20) % (slack + 1)
    lengths = lengths.at[1:1 + 2 * pairs:2].set(giver - moved).at[2:2 + 2 * pairs:2].set(taker + moved)
    return lengths[jax.random.permutation(jax.random.fold_in(stream_key, 2), amount)]


def bell_draw(own_key, shape, deviation, reach, shards=(), kind=jnp.bfloat16):
    factor_of = steps_of(own_key, shape, shards, -0.22, 0.18) if shards else 1.0
    drawn = jax.random.normal(own_key, shape, jnp.float32) * deviation * factor_of
    return jnp.minimum(jnp.maximum(drawn, -reach), reach).astype(kind)


def setup_inputs(seed: int = 0) -> dict:
    splits = jax.random.split(jax.random.key(seed), 11)
    residual_in = bell_draw(splits[0], (ROWS, LEN, D), 1.0, 6.0, ((0, 4), (1, 8)), jnp.float32)
    cotangent = bell_draw(splits[1], (ROWS, LEN, D), 1.0, 6.0, ((0, 4), (1, 8)), jnp.float32)
    segments = jax.vmap(lambda own: jnp.searchsorted(jnp.cumsum(ragged_sizes(own, DOCS, LEN, DOC_MAX, 2)), jnp.arange(LEN), side="right"))(jax.random.split(splits[2], ROWS)).reshape((ROWS, LEN)).astype(jnp.int32)
    owners = draw_owners(jax.random.fold_in(splits[10], 71), 0)
    master_tiles = draw_master_tiles(jax.random.fold_in(splits[10], 71), 0)
    first_tiles = bell_draw(splits[5], (SLOTS, D, TW), (24 * D * D + 16 * D) ** -0.5, 0.0024414062, ((0, 8),), jnp.float32)
    second_tiles = jnp.clip(jnp.exp(math.log(6.349561090246425e-07) - 1.3862944 * jax.random.uniform(splits[6], (SLOTS, D, TW), jnp.float32) ** steps_of(splits[6], (SLOTS, D, TW), ((0, 8),), -0.2, 0.2)), 1.5873902725616063e-07, 6.349561090246425e-07)
    norm_params = draw_norm_params(jax.random.fold_in(splits[10], 71), 0)
    norm_first = bell_draw(splits[8], (4 * LAYERS, D), ((24 * D * D + 16 * D) // 16) ** -0.5, 0.009765625, (), jnp.float32)
    norm_second = jnp.clip(jnp.exp(jax.random.uniform(splits[9], (4 * LAYERS, D), jnp.float32, math.log(2.53982443609857e-06), math.log(1.015929774439428e-05))), 2.53982443609857e-06, 1.015929774439428e-05)
    return dict(residual_in=residual_in, cotangent=cotangent, segments=segments, owners=owners, master_tiles=master_tiles, first_tiles=first_tiles, second_tiles=second_tiles, norm_params=norm_params, norm_first=norm_first, norm_second=norm_second)


@jax.custom_vjp
def low(v):
    return lax.optimization_barrier(v.astype(jnp.bfloat16)).astype(jnp.float32)

@jax.custom_vjp
def low_back(v):
    return v

def low_keep(v):
    return (low(v), None)

def low_pass(kept, grad):
    return (grad,)

def back_keep(v):
    return (v, None)

def back_low(kept, grad):
    return (low(grad),)
low.defvjp(low_keep, low_pass)
low_back.defvjp(back_keep, back_low)
highest = lax.Precision.HIGHEST

def slot_table(owners):
    places = jnp.arange(NT, dtype=jnp.int32)
    before = (owners[None, :] == owners[:, None]) & (places[None, :] < places[:, None])
    return (owners * CAP + lax.optimization_barrier(jnp.sum(before.astype(jnp.int32), axis=1))).astype(jnp.int32)

def assemble(weight_tiles, layer_number):
    first_tile = 48 * layer_number
    model_width = weight_tiles.shape[1]
    qkv_weight = weight_tiles[first_tile:first_tile + 12].transpose(1, 0, 2).reshape(model_width, -1)
    out_weight = weight_tiles[first_tile + 12:first_tile + 16].transpose(1, 0, 2).reshape(model_width, -1)
    up_weight = weight_tiles[first_tile + 16:first_tile + 32].transpose(1, 0, 2).reshape(model_width, -1)
    down_block = weight_tiles[first_tile + 32:first_tile + 48].reshape(4, 4, model_width, -1)
    down_weight = down_block.transpose(0, 2, 1, 3).reshape(4 * model_width, model_width)
    return (qkv_weight, out_weight, up_weight, down_weight)

def norm_layer(values, gain, offset):
    center = values - lax.optimization_barrier(jnp.mean(values, axis=-1, keepdims=True))
    spread = lax.optimization_barrier(jnp.mean(center * center, axis=-1, keepdims=True))
    return center * lax.rsqrt(spread + 1e-05) * gain + offset

def head_attention(doc_ids, items):
    queries, key_rows, value_rows = items
    scores = low_back(jnp.dot(queries, key_rows.T, precision=highest) * HD ** (-0.5))
    same_doc = doc_ids[:, None] == doc_ids[None, :]
    weights = low(jax.nn.softmax(jnp.where(same_doc, scores, -1e+30), axis=-1))
    return low(low_back(jnp.dot(weights, value_rows, precision=highest)))

def forward_row(master_rows, params, row_values, doc_ids):
    copies = low(master_rows)
    attend = jax.checkpoint(partial(head_attention, doc_ids))
    hidden = row_values
    for layer_number in range(LAYERS):
        qkv_weight, out_weight, up_weight, down_weight = assemble(copies, layer_number)
        normed = low(norm_layer(hidden, params[4 * layer_number], params[4 * layer_number + 1]))
        packed = low(low_back(jnp.dot(normed, qkv_weight, precision=highest)))
        split_heads = packed.reshape(LEN, 3, HEADS, HD).transpose(1, 2, 0, 3)
        attended = lax.map(attend, (split_heads[0], split_heads[1], split_heads[2]))
        mixed = attended.transpose(1, 0, 2).reshape(LEN, D)
        middle = hidden + low_back(jnp.dot(mixed, out_weight, precision=highest))
        normed_two = low(norm_layer(middle, params[4 * layer_number + 2], params[4 * layer_number + 3]))
        inner = low_back(jnp.dot(normed_two, up_weight, precision=highest))
        active = low(jax.nn.gelu(inner))
        hidden = middle + low_back(jnp.dot(active, down_weight, precision=highest))
    return hidden

def adamw(weight, grad, first, second, learn_rate, correction):
    first = 0.5 * first + 0.5 * grad
    second = 0.5 * second + 0.5 * grad * grad
    update = first / correction / (jnp.sqrt(second / correction) + 1e-08)
    return (weight - learn_rate * (update + 0.01 * weight), first, second)

def reference(residual_in, cotangent, segments, owners, master_tiles, first_tiles, second_tiles, norm_params, norm_first, norm_second):
    slots = slot_table(owners)
    master_rows = jnp.take(master_tiles, slots, axis=0)

    def one_row(carry, inputs):
        row_values, doc_ids, row_grad = inputs

        def row_forward(weights, params, values):
            return forward_row(weights, params, values, doc_ids)
        output, pull = jax.vjp(row_forward, master_rows, norm_params, row_values)
        tile_part, norm_part, input_part = pull(row_grad)
        return ((carry[0] + tile_part, carry[1] + norm_part), (output, input_part))
    start = (jnp.zeros(master_rows.shape, jnp.float32), jnp.zeros(norm_params.shape, jnp.float32))
    (tile_sum, norm_sum), (residual_out, input_grad) = lax.scan(one_row, start, (residual_in, segments, cotangent))
    total = jnp.sqrt(jnp.sum(tile_sum * tile_sum) + jnp.sum(norm_sum * norm_sum))
    factor = 1.0 / jnp.maximum(total, 1.0)
    clipped = tile_sum * factor
    norm_clip = norm_sum * factor
    correction = 1.0 - 0.5 ** STEP
    new_weight, new_first_rows, new_second_rows = adamw(master_rows, clipped, jnp.take(first_tiles, slots, axis=0), jnp.take(second_tiles, slots, axis=0), 0.05, correction)
    new_norm, new_norm_f, new_norm_s = adamw(norm_params, norm_clip, norm_first, norm_second, 0.25, correction)

    def place(values):
        return jnp.zeros(master_tiles.shape, jnp.float32).at[slots].set(values)
    placed_weight = place(new_weight)
    return (residual_out, input_grad, place(clipped), total[None], place(new_first_rows), place(new_second_rows), placed_weight, placed_weight.astype(jnp.bfloat16), norm_clip, new_norm_f, new_norm_s, new_norm)
```

```python
import jax
import jax.numpy as jnp
from jax import lax
from jax.experimental import pallas as pl
from jax.experimental.pallas import tpu as pltpu

from jax.sharding import PartitionSpec as P

HEADS = 8
LAYERS = 2
STEP = 5


def norm_layer(values, gain, offset):
    center = values - jnp.mean(values, axis=-1, keepdims=True)
    spread = jnp.mean(center * center, axis=-1, keepdims=True)
    return center * lax.rsqrt(spread + 1e-05) * gain + offset


def matmul(left, right):
    return jnp.dot(left, right, preferred_element_type=jnp.float32)


def left_product(left, right):
    return lax.dot_general(
        left, right, (((0,), (0,)), ((), ())), preferred_element_type=jnp.float32
    )


def right_product(left, right):
    return lax.dot_general(
        left, right, (((1,), (1,)), ((), ())), preferred_element_type=jnp.float32
    )


def assemble(weight_tiles, layer_number):
    first_tile = 48 * layer_number
    model_width = weight_tiles.shape[1]
    qkv_weight = (
        weight_tiles[first_tile : first_tile + 12].transpose(1, 0, 2).reshape(model_width, -1)
    )
    out_weight = (
        weight_tiles[first_tile + 12 : first_tile + 16].transpose(1, 0, 2).reshape(model_width, -1)
    )
    up_weight = (
        weight_tiles[first_tile + 16 : first_tile + 32].transpose(1, 0, 2).reshape(model_width, -1)
    )
    down_block = weight_tiles[first_tile + 32 : first_tile + 48].reshape(4, 4, model_width, -1)
    down_weight = down_block.transpose(0, 2, 1, 3).reshape(4 * model_width, model_width)
    return (qkv_weight, out_weight, up_weight, down_weight)


def split_tiles(qkv_grad, out_grad, up_grad, down_grad, tile_width):
    model_width = qkv_grad.shape[0]
    pieces = [
        qkv_grad.reshape(model_width, -1, tile_width).transpose(1, 0, 2),
        out_grad.reshape(model_width, -1, tile_width).transpose(1, 0, 2),
        up_grad.reshape(model_width, -1, tile_width).transpose(1, 0, 2),
        down_grad.reshape(4, model_width, 4, tile_width)
        .transpose(0, 2, 1, 3)
        .reshape(16, model_width, tile_width),
    ]
    return jnp.concatenate(pieces, axis=0)


def attend_forward(queries, key_rows, value_rows, doc_ids, block_rows, scale):
    length = queries.shape[0]

    def one_block(number):
        first_row = number * block_rows
        query_block = lax.dynamic_slice_in_dim(queries, first_row, block_rows, 0)
        doc_block = lax.dynamic_slice_in_dim(doc_ids, first_row, block_rows, 0)
        same_doc = doc_block[:, None] == doc_ids[None, :]
        scores = jnp.where(same_doc, right_product(query_block, key_rows) * scale, -1e30)
        largest = jnp.max(scores, axis=-1, keepdims=True)
        row_total = jnp.sum(jnp.exp(scores - largest), axis=-1, keepdims=True)
        logsum = largest + jnp.log(row_total)
        weights = jnp.where(same_doc, jnp.exp(scores - logsum), 0.0).astype(jnp.bfloat16)
        return (matmul(weights, value_rows).astype(jnp.bfloat16), logsum[:, 0])

    outputs, logsums = lax.map(one_block, jnp.arange(length // block_rows))
    return (outputs.reshape(length, -1), logsums.reshape(length))


def attend_backward(queries, key_rows, value_rows, doc_ids, logsums, out_grads, block_rows, scale):
    length, head_dim = queries.shape

    def one_block(carry, number):
        key_grad, value_grad = carry
        first_row = number * block_rows
        query_block = lax.dynamic_slice_in_dim(queries, first_row, block_rows, 0)
        doc_block = lax.dynamic_slice_in_dim(doc_ids, first_row, block_rows, 0)
        logsum_block = lax.dynamic_slice_in_dim(logsums, first_row, block_rows, 0)
        grad_block = lax.dynamic_slice_in_dim(out_grads, first_row, block_rows, 0)
        same_doc = doc_block[:, None] == doc_ids[None, :]
        scores = jnp.where(same_doc, right_product(query_block, key_rows) * scale, -1e30)
        probs = jnp.where(same_doc, jnp.exp(scores - logsum_block[:, None]), 0.0)
        prob_grad = right_product(grad_block, value_rows)
        inner_sum = jnp.sum(probs * prob_grad, axis=-1, keepdims=True)
        score_grad = (probs * (prob_grad - inner_sum)).astype(jnp.bfloat16)
        query_grad = matmul(score_grad, key_rows) * scale
        key_grad = key_grad + left_product(score_grad, query_block) * scale
        value_grad = value_grad + left_product(probs.astype(jnp.bfloat16), grad_block)
        return ((key_grad, value_grad), query_grad)

    zeros_block = jnp.zeros((length, head_dim), jnp.float32)
    (key_grad, value_grad), query_grads = lax.scan(
        one_block, (zeros_block, zeros_block), jnp.arange(length // block_rows)
    )
    stacked = jnp.stack([query_grads.reshape(length, head_dim), key_grad, value_grad], axis=1)
    return stacked.astype(jnp.bfloat16)


def adamw(weight, grad, first, second, learn_rate, correction):
    first = 0.5 * first + 0.5 * grad
    second = 0.5 * second + 0.5 * grad * grad
    update = first / correction / (jnp.sqrt(second / correction) + 1e-08)
    return (weight - learn_rate * (update + 0.01 * weight), first, second)


def local_by_heads(
    residual_in,
    cotangent,
    segments,
    owners,
    master_tiles,
    first_tiles,
    second_tiles,
    norm_params,
    norm_first,
    norm_second,
):
    local_rows, positions, model_width = residual_in.shape
    seq_devices = lax.axis_size("seq")
    seq_index = lax.axis_index("seq")
    head_dim = model_width // HEADS
    group_count = seq_devices // HEADS
    group_rows = local_rows // group_count
    length = positions * seq_devices
    block_rows = min(512, length)
    scale = head_dim ** (-0.5)
    tile_total = owners.shape[0]
    capacity = master_tiles.shape[0]
    tile_width = master_tiles.shape[2]
    places = jnp.arange(tile_total, dtype=jnp.int32)
    before = (owners[None, :] == owners[:, None]) & (places[None, :] < places[:, None])
    ranks = jnp.sum(before.astype(jnp.int32), axis=1)
    slot_ids = owners * capacity + ranks
    local_slots = jnp.arange(capacity, dtype=jnp.int32)
    matches = (owners[:, None] == seq_index) & (ranks[:, None] == local_slots[None, :])
    chosen = jnp.sum(jnp.where(matches, places[:, None], 0), axis=0)
    present = jnp.any(matches, axis=0)
    copies = lax.all_gather(master_tiles.astype(jnp.bfloat16), "seq", axis=0, tiled=True)
    weight_tiles = jnp.take(copies, slot_ids, axis=0)
    my_group = seq_index // HEADS
    doc_rows = lax.dynamic_slice_in_dim(segments, my_group * group_rows, group_rows, 0)
    hidden = residual_in.reshape(-1, model_width)
    saved = []
    for layer_number in range(LAYERS):
        qkv_weight, out_weight, up_weight, down_weight = assemble(weight_tiles, layer_number)
        params = norm_params[4 * layer_number : 4 * layer_number + 4]
        normed, first_pull = jax.vjp(norm_layer, hidden, params[0], params[1])
        normed_low = normed.astype(jnp.bfloat16)
        packed = matmul(normed_low, qkv_weight).astype(jnp.bfloat16)
        outgoing = packed.reshape(group_count, group_rows, positions, 3, HEADS, head_dim)
        outgoing = outgoing.transpose(0, 4, 1, 2, 3, 5).reshape(
            seq_devices, group_rows, positions * 3 * head_dim
        )
        arrived = lax.all_to_all(outgoing, "seq", split_axis=0, concat_axis=2, tiled=True).reshape(
            group_rows, length, 3, head_dim
        )

        def forward_item(items):
            return attend_forward(
                items[0][:, 0], items[0][:, 1], items[0][:, 2], items[1], block_rows, scale
            )

        attended, logsums = lax.map(forward_item, (arrived, doc_rows))
        returning = attended.reshape(1, group_rows, seq_devices, positions * head_dim)
        mixed = lax.all_to_all(returning, "seq", split_axis=2, concat_axis=0, tiled=True)
        mixed = (
            mixed.reshape(group_count, HEADS, group_rows, positions, head_dim)
            .transpose(0, 2, 3, 1, 4)
            .reshape(-1, model_width)
        )
        middle = hidden + matmul(mixed, out_weight)
        normed_two, second_pull = jax.vjp(norm_layer, middle, params[2], params[3])
        normed_two_low = normed_two.astype(jnp.bfloat16)
        inner = matmul(normed_two_low, up_weight)
        active = jax.nn.gelu(inner).astype(jnp.bfloat16)
        hidden = middle + matmul(active, down_weight)
        saved.append(
            (
                first_pull,
                normed_low,
                arrived,
                logsums,
                mixed,
                second_pull,
                normed_two_low,
                inner,
                active,
            )
        )
    grad = cotangent.reshape(-1, model_width)
    tile_parts = [None] * LAYERS
    norm_parts = [None] * LAYERS
    for layer_number in reversed(range(LAYERS)):
        (
            first_pull,
            normed_low,
            arrived,
            logsums,
            mixed,
            second_pull,
            normed_two_low,
            inner,
            active,
        ) = saved[layer_number]
        qkv_weight, out_weight, up_weight, down_weight = assemble(weight_tiles, layer_number)
        grad_low = grad.astype(jnp.bfloat16)
        down_grad = left_product(active, grad_low)
        active_grad = right_product(grad_low, down_weight)
        inner_grad = jax.vjp(jax.nn.gelu, inner)[1](active_grad)[0].astype(jnp.bfloat16)
        up_grad = left_product(normed_two_low, inner_grad)
        middle_part, gain_two, offset_two = second_pull(right_product(inner_grad, up_weight))
        middle_grad = grad + middle_part
        middle_low = middle_grad.astype(jnp.bfloat16)
        out_grad = left_product(mixed, middle_low)
        mixed_grad = right_product(middle_low, out_weight).astype(jnp.bfloat16)
        sending = mixed_grad.reshape(group_count, group_rows, positions, HEADS, head_dim)
        sending = sending.transpose(0, 3, 1, 2, 4).reshape(
            seq_devices, group_rows, positions * head_dim
        )
        head_grads = lax.all_to_all(
            sending, "seq", split_axis=0, concat_axis=2, tiled=True
        ).reshape(group_rows, length, head_dim)

        def backward_item(items):
            arrived_row, doc_row, logsum_row, grad_row = items
            return attend_backward(
                arrived_row[:, 0],
                arrived_row[:, 1],
                arrived_row[:, 2],
                doc_row,
                logsum_row,
                grad_row,
                block_rows,
                scale,
            )

        packed_grads = lax.map(backward_item, (arrived, doc_rows, logsums, head_grads))
        coming = lax.all_to_all(
            packed_grads.reshape(1, group_rows, seq_devices, positions * 3 * head_dim),
            "seq",
            split_axis=2,
            concat_axis=0,
            tiled=True,
        )
        qkv_grad = coming.reshape(group_count, HEADS, group_rows, positions, 3, head_dim)
        qkv_grad = qkv_grad.transpose(0, 2, 3, 4, 1, 5).reshape(-1, 3 * model_width)
        qkv_weight_grad = left_product(normed_low, qkv_grad)
        input_part, gain_one, offset_one = first_pull(right_product(qkv_grad, qkv_weight))
        grad = middle_grad + input_part
        tile_parts[layer_number] = split_tiles(
            qkv_weight_grad, out_grad, up_grad, down_grad, tile_width
        )
        norm_parts[layer_number] = jnp.stack([gain_one, offset_one, gain_two, offset_two])
    dense = jnp.concatenate(tile_parts, axis=0)
    norm_part = jnp.concatenate(norm_parts, axis=0)
    piece = lax.psum_scatter(
        dense.reshape(-1, tile_width), ("rows", "seq"), scatter_dimension=0, tiled=True
    )
    squares, norm_sum = lax.psum((jnp.sum(piece * piece), norm_part), ("rows", "seq"))
    summed = (
        lax.all_gather(piece.astype(jnp.bfloat16), ("rows", "seq"), axis=0, tiled=True)
        .astype(piece.dtype)
        .reshape(dense.shape)
    )
    owned = jnp.take(summed, chosen, axis=0)
    keep = present[:, None, None]
    owned = jnp.where(keep, owned, 0.0)
    total = jnp.sqrt(squares + jnp.sum(norm_sum * norm_sum))
    factor = 1.0 / jnp.maximum(total, 1.0)
    clipped = owned * factor
    norm_clip = norm_sum * factor
    correction = 1.0 - 0.5**STEP
    new_weight, new_first_rows, new_second_rows = adamw(
        master_tiles, clipped, first_tiles, second_tiles, 0.05, correction
    )
    new_weight = jnp.where(keep, new_weight, 0.0)
    new_first_rows = jnp.where(keep, new_first_rows, 0.0)
    new_second_rows = jnp.where(keep, new_second_rows, 0.0)
    new_norm, new_norm_f, new_norm_s = adamw(
        norm_params, norm_clip, norm_first, norm_second, 0.25, correction
    )
    return (
        hidden.reshape(local_rows, positions, model_width),
        grad.reshape(local_rows, positions, model_width),
        clipped,
        total[None],
        new_first_rows,
        new_second_rows,
        new_weight,
        new_weight.astype(jnp.bfloat16),
        norm_clip,
        new_norm_f,
        new_norm_s,
        new_norm,
    )


F32 = jnp.float32
BF16 = jnp.bfloat16
BLOCK = 256
VMEM_BYTES = 60 * 1024 * 1024


def dot_nn(left, right):
    return jnp.dot(left, right, preferred_element_type=F32)


def dot_nt(left, right, precision=None):
    return lax.dot_general(
        left, right, (((1,), (1,)), ((), ())), preferred_element_type=F32, precision=precision
    )


def dot_tn(left, right):
    return lax.dot_general(left, right, (((0,), (0,)), ((), ())), preferred_element_type=F32)


def rows_of(number, size=BLOCK):
    return pl.ds(pl.multiple_of(number * size, size), size)


def normalized(values):
    center = values - jnp.mean(values, axis=-1, keepdims=True)
    spread = jnp.mean(center * center, axis=-1, keepdims=True)
    scale = lax.rsqrt(spread + 1e-05)
    return center * scale, scale


GELU_A = 0.7978845608028654
GELU_B = 0.044715


def gelu_value(inner):
    return 0.5 * inner * (1.0 + jnp.tanh(GELU_A * (inner + GELU_B * inner * inner * inner)))


def gelu_both(inner):
    square = inner * inner
    bent = jnp.tanh(inner * (GELU_A + GELU_A * GELU_B * square))
    half = 0.5 + 0.5 * bent
    slope = half + 0.5 * inner * (1.0 - bent * bent) * (GELU_A + 3.0 * GELU_A * GELU_B * square)
    return inner * half, slope


def weight_copy(tiles, table, number, target, column, row, sem):
    depth, width = tiles.shape[1], tiles.shape[2]
    rows = pl.ds(pl.multiple_of(row * depth, depth), depth)
    columns = pl.ds(pl.multiple_of(column * width, width), width)
    return pltpu.make_async_copy(
        tiles.at[table[number]], target.at[rows, columns], sem.at[number]
    )


def weight_group(tiles, table, first, count, per_row, target, sem, act):
    @pl.loop(0, count)
    def _(j):
        copy = weight_copy(
            tiles, table, first + j, target, lax.rem(j, per_row), lax.div(j, per_row), sem
        )
        getattr(copy, act)()


def lane_is_first(shape):
    return lax.broadcasted_iota(jnp.int32, shape, 1) < shape[1] // 2


def pair_of(values, lanes_first):
    zero = jnp.zeros_like(values)
    return (
        jnp.where(lanes_first, values, zero).astype(BF16),
        jnp.where(lanes_first, zero, values).astype(BF16),
    )


def forward_kernel(
    table, spans, norms, doc_row, doc_col, hidden, tiles,
    normed_out, packed_out, mixed_out, logsum_out, middle_out, normed_two_out, hidden_out,
    w_qkv, w_out, w_up, w_down, normed, packed, mixed, logcol, logsum, middle, normed_two, after,
    w_sem, o_sem,
):
    length, width = hidden.shape
    blocks = length // BLOCK
    pairs = mixed.shape[0]
    lanes = mixed.shape[2]
    groups = (
        (0, 12, 12, w_qkv), (12, 4, 4, w_out), (16, 16, 16, w_up), (32, 16, 4, w_down),
    )
    for first, count, per_row, target in groups:
        weight_group(tiles, table, first, count, per_row, target, w_sem, "start")

    def ready(group):
        first, count, per_row, target = groups[group]
        weight_group(tiles, table, first, count, per_row, target, w_sem, "wait")

    outs = (
        (normed, normed_out), (packed, packed_out), (mixed, mixed_out), (logsum, logsum_out),
        (middle, middle_out), (normed_two, normed_two_out), (after, hidden_out),
    )

    def flush(number):
        return pltpu.make_async_copy(outs[number][0], outs[number][1], o_sem.at[number])

    ready(0)

    @pl.loop(0, blocks)
    def _(number):
        here = rows_of(number)
        unit, _ = normalized(hidden[here, :])
        low = (unit * norms[0:1, :] + norms[1:2, :]).astype(BF16)
        normed[here, :] = low
        product = dot_nn(low, w_qkv[...])
        for j in range(3 * pairs):
            packed[j, here, :] = product[:, j * lanes : (j + 1) * lanes].astype(BF16)

    flush(0).start()
    flush(1).start()
    lane_ids = lax.broadcasted_iota(jnp.int32, (BLOCK, lanes), 1)
    first_half = lane_is_first((BLOCK, lanes))

    @pl.loop(0, blocks)
    def _(number):
        here = rows_of(number)
        low_key = spans[0, number]
        key_count = spans[1, number]
        doc_here = doc_col[here, 0:1]

        def with_keys(many):
            keys_here = pl.ds(pl.multiple_of(low_key * BLOCK, BLOCK), many * BLOCK)
            same = doc_here == doc_row[0:1, keys_here]

            def one_pair(pair, carry):
                heads = pair_of(packed[pair, here, :].astype(F32) * 0.125, first_half)
                keys = packed[pairs + pair, keys_here, :]
                values = packed[2 * pairs + pair, keys_here, :]
                results = []
                logs = logcol[here, :]
                for side in range(2):
                    scores = jnp.where(same, dot_nt(heads[side], keys), -1e30)
                    top = jnp.max(scores, axis=-1, keepdims=True)
                    weights = jnp.exp(scores - top)
                    total = jnp.sum(weights, axis=-1, keepdims=True)
                    results.append(dot_nn(weights.astype(BF16), values) / total)
                    logs = jnp.where(lane_ids == 8 * pair + side, top + jnp.log(total), logs)
                mixed[pair, here, :] = jnp.where(first_half, results[0], results[1]).astype(BF16)
                logcol[here, :] = logs
                return carry

            lax.fori_loop(0, pairs, one_pair, 0)

        for many in range(1, blocks + 1):
            pl.when(key_count == many)(lambda many=many: with_keys(many))

    flush(2).start()
    turned = logcol[...].T
    for pair in range(pairs):
        logsum[pair, :, :] = turned[8 * pair : 8 * pair + 8, :]
    flush(3).start()
    ready(1)
    ready(2)
    ready(3)
    chunk = width

    @pl.loop(0, blocks)
    def _(number):
        here = rows_of(number)
        side_by_side = jnp.concatenate([mixed[pair, here, :] for pair in range(pairs)], axis=1)
        mid = hidden[here, :] + dot_nn(side_by_side, w_out[...])
        middle[here, :] = mid
        unit, _ = normalized(mid)
        low = (unit * norms[2:3, :] + norms[3:4, :]).astype(BF16)
        normed_two[here, :] = low
        total = mid
        for c in range(w_up.shape[1] // chunk):
            part = slice(c * chunk, (c + 1) * chunk)
            active = gelu_value(dot_nn(low, w_up[:, part])).astype(BF16)
            total = total + dot_nn(active, w_down[part, :])
        after[here, :] = total

    flush(4).start()
    flush(5).start()
    flush(6).start()
    for number in range(len(outs)):
        flush(number).wait()


def vmem_spec():
    return pl.BlockSpec(memory_space=pltpu.VMEM)


def any_spec():
    return pl.BlockSpec(memory_space=pl.ANY)


def smem_spec():
    return pl.BlockSpec(memory_space=pltpu.SMEM)


def forward_layer(table, spans, norms, doc_row, doc_col, hidden, tiles, pairs):
    length, width = hidden.shape
    lanes = tiles.shape[2]
    shapes = (
        ((length, width), BF16),
        ((3 * pairs, length, lanes), BF16),
        ((pairs, length, lanes), BF16),
        ((pairs, 8, length), F32),
        ((length, width), F32),
        ((length, width), BF16),
        ((length, width), F32),
    )
    return pl.pallas_call(
        forward_kernel,
        name="forward_layer",
        out_shape=[jax.ShapeDtypeStruct(s, d) for s, d in shapes],
        in_specs=[smem_spec(), smem_spec()] + [vmem_spec()] * 4 + [any_spec()],
        out_specs=[any_spec()] * len(shapes),
        scratch_shapes=[
            pltpu.VMEM((width, 3 * width), BF16),
            pltpu.VMEM((width, width), BF16),
            pltpu.VMEM((width, 4 * width), BF16),
            pltpu.VMEM((4 * width, width), BF16),
            pltpu.VMEM(shapes[0][0], BF16),
            pltpu.VMEM(shapes[1][0], BF16),
            pltpu.VMEM(shapes[2][0], BF16),
            pltpu.VMEM((length, lanes), F32),
            pltpu.VMEM(shapes[3][0], F32),
            pltpu.VMEM(shapes[4][0], F32),
            pltpu.VMEM(shapes[5][0], BF16),
            pltpu.VMEM(shapes[6][0], F32),
            pltpu.SemaphoreType.DMA((48,)),
            pltpu.SemaphoreType.DMA((7,)),
        ],
        compiler_params=pltpu.CompilerParams(vmem_limit_bytes=VMEM_BYTES),
        cost_estimate=pl.CostEstimate(
            flops=length * width * width * 26, bytes_accessed=18 * 2**20,
            transcendentals=length * length * 4,
        ),
    )(table, spans, norms, doc_row, doc_col, hidden, tiles)


def backward_kernel(
    fill, table, spans, counts, norms, doc_row, doc_col, selector,
    grad_in, normed_in, packed_in, mixed_in, logsum_in, middle_in, normed_two_in, hidden_in, tiles,
    *rest,
):
    rest = list(rest)
    if not fill:
        rest.pop(0)
    (
        grad_out, tile_grads, norm_grads,
        w_qkv, w_out, w_up, w_down,
        grad, normed, packed, mixed, logsum, middle, normed_two, hidden,
        active, inner_grad, grad_low, mid_grad, mid_low, mixed_grad, delta, packed_grad,
        key_sum, value_sum, below, staged, blank,
        w_sem, i_sem, t_sem, z_sem, o_sem,
    ) = rest
    length, width = grad.shape
    blocks = length // BLOCK
    pairs, lanes = mixed.shape[0], mixed.shape[2]
    groups = (
        (0, 12, 12, w_qkv), (12, 4, 4, w_out), (16, 16, 16, w_up), (32, 16, 4, w_down),
    )
    ins = (
        (grad_in, grad), (normed_two_in, normed_two), (middle_in, middle), (mixed_in, mixed),
        (packed_in, packed), (logsum_in, logsum), (hidden_in, hidden), (normed_in, normed),
    )

    def load(number):
        return pltpu.make_async_copy(ins[number][0], ins[number][1], i_sem.at[number])

    def fetch(group, act):
        first, count, per_row, target = groups[group]
        weight_group(tiles, table, first, count, per_row, target, w_sem, act)

    load(0).start()
    load(1).start()
    fetch(2, "start")
    fetch(3, "start")
    load(2).start()
    fetch(1, "start")
    load(3).start()
    load(4).start()
    load(5).start()
    fetch(0, "start")
    load(6).start()
    load(7).start()

    def blank_copies(act):
        capacity = tile_grads.shape[0] // counts.shape[0]
        quarter = capacity // 4

        @pl.loop(0, counts.shape[0])
        def _(owner):
            @pl.loop(counts[owner], capacity)
            def _(place):
                index = (lax.div(place, quarter) * counts.shape[0] + owner) * quarter + lax.rem(
                    place, quarter
                )
                getattr(
                    pltpu.make_async_copy(blank, tile_grads.at[index], z_sem.at[index]), act
                )()

    if fill:
        blank[...] = jnp.zeros_like(blank)
        blank_copies("start")

    norm_grads[...] = jnp.zeros_like(norm_grads)
    load(0).wait()
    load(1).wait()
    load(2).wait()
    fetch(2, "wait")
    fetch(3, "wait")
    fetch(1, "wait")
    load(3).wait()
    chunk = width
    chunks = w_up.shape[1] // chunk

    def norm_back(values, out_grad, gain, gain_row):
        unit, scale = normalized(values)
        norm_grads[gain_row : gain_row + 1, :] += jnp.sum(out_grad * unit, axis=0, keepdims=True)
        norm_grads[gain_row + 1 : gain_row + 2, :] += jnp.sum(out_grad, axis=0, keepdims=True)
        turned = out_grad * gain
        average = jnp.mean(turned, axis=-1, keepdims=True)
        along = jnp.mean(turned * unit, axis=-1, keepdims=True)
        return scale * (turned - average - unit * along)

    @pl.loop(0, blocks)
    def _(number):
        here = rows_of(number)
        upper = grad[here, :]
        low = upper.astype(BF16)
        grad_low[here, :] = low
        normed_here = normed_two[here, :]
        total = jnp.zeros((BLOCK, width), F32)
        for c in range(chunks):
            part = slice(c * chunk, (c + 1) * chunk)
            value, slope = gelu_both(dot_nn(normed_here, w_up[:, part]))
            active[here, part] = value.astype(BF16)
            inner = (slope * dot_nt(low, w_down[part, :])).astype(BF16)
            inner_grad[here, part] = inner
            total = total + dot_nt(inner, w_up[:, part])
        mid = upper + norm_back(middle[here, :], total, norms[2:3, :], 2)
        mid_grad[here, :] = mid
        mid_here = mid.astype(BF16)
        mid_low[here, :] = mid_here
        back = dot_nt(mid_here, w_out[...]).astype(BF16)
        for pair in range(pairs):
            mixed_grad[pair, here, :] = back[:, pair * lanes : (pair + 1) * lanes]
        side_by_side = jnp.concatenate([mixed[pair, here, :] for pair in range(pairs)], axis=1)
        both = side_by_side.astype(F32) * back.astype(F32)
        sums = dot_nt(selector[...], both, precision=lax.Precision.HIGHEST)
        for pair in range(pairs):
            delta[pair, :, here] = sums[8 * pair : 8 * pair + 8, :]

    def send_tile(place):
        return pltpu.make_async_copy(
            staged.at[place], tile_grads.at[table[place]], t_sem.at[place]
        )

    def emit(block, first):
        for c in range(block.shape[1] // lanes):
            staged[first + c] = block[:, c * lanes : (c + 1) * lanes].astype(BF16)
            send_tile(first + c).start()

    @pl.loop(0, chunks)
    def _(c):
        part = rows_of(c, chunk)
        emit(dot_tn(active[:, part], grad_low[...]), 32 + 4 * c)
        emit(dot_tn(normed_two[...], inner_grad[:, part]), 16 + 4 * c)

    side_by_side = jnp.concatenate([mixed[pair] for pair in range(pairs)], axis=1)
    emit(dot_tn(side_by_side, mid_low[...]), 12)
    load(4).wait()
    load(5).wait()
    first_half = lane_is_first((BLOCK, lanes))

    @pl.loop(0, pairs)
    def _(pair):
        key_sum[...] = jnp.zeros_like(key_sum)
        value_sum[...] = jnp.zeros_like(value_sum)

        @pl.loop(0, blocks)
        def _(number):
            here = rows_of(number)
            low_key = spans[0, number]
            key_count = spans[1, number]
            doc_here = doc_row[0:1, here]

            def with_keys(many):
                keys_here = pl.ds(pl.multiple_of(low_key * BLOCK, BLOCK), many * BLOCK)
                same = doc_col[keys_here, 0:1] == doc_here
                heads = pair_of(packed[pair, here, :].astype(F32) * 0.125, first_half)
                outs = pair_of(mixed_grad[pair, here, :].astype(F32), first_half)
                keys = packed[pairs + pair, keys_here, :]
                values = packed[2 * pairs + pair, keys_here, :]
                query_parts = []
                key_part = key_sum[keys_here, :]
                value_part = value_sum[keys_here, :]
                for side in range(2):
                    scores = dot_nt(keys, heads[side])
                    weights = jnp.exp(
                        jnp.where(same, scores - logsum[pair, side : side + 1, here], -1e30)
                    )
                    from_values = dot_nt(values, outs[side])
                    score_grad = (
                        weights * (from_values - delta[pair, side : side + 1, here])
                    ).astype(BF16)
                    value_part = value_part + dot_nn(weights.astype(BF16), outs[side])
                    key_part = key_part + dot_nn(score_grad, heads[side])
                    query_parts.append(dot_tn(score_grad, keys))
                key_sum[keys_here, :] = key_part
                value_sum[keys_here, :] = value_part
                packed_grad[pair, here, :] = (
                    jnp.where(first_half, query_parts[0], query_parts[1]) * 0.125
                ).astype(BF16)

            for many in range(1, blocks + 1):
                pl.when(key_count == many)(lambda many=many: with_keys(many))

        packed_grad[pairs + pair] = key_sum[...].astype(BF16)
        packed_grad[2 * pairs + pair] = value_sum[...].astype(BF16)

    fetch(0, "wait")
    load(6).wait()
    load(7).wait()

    @pl.loop(0, blocks)
    def _(number):
        here = rows_of(number)
        wide = jnp.concatenate([packed_grad[j, here, :] for j in range(3 * pairs)], axis=1)
        total = dot_nt(wide, w_qkv[...])
        below[here, :] = mid_grad[here, :] + norm_back(
            hidden[here, :], total, norms[0:1, :], 0
        )

    flush = pltpu.make_async_copy(below, grad_out, o_sem.at[0])
    flush.start()

    @pl.loop(0, 3)
    def _(c):
        wide = jnp.concatenate([packed_grad[pairs * c + j] for j in range(pairs)], axis=1)
        emit(dot_tn(normed[...], wide), 4 * c)

    flush.wait()

    @pl.loop(0, 48)
    def _(place):
        send_tile(place).wait()

    if fill:
        blank_copies("wait")


def backward_layer(
    table, spans, counts, norms, doc_row, doc_col, selector, grad, saved, hidden, tiles, held
):
    normed, packed, mixed, logsum, middle, normed_two = saved
    length, width = grad.shape
    lanes = tiles.shape[2]
    pairs = mixed.shape[0]
    fill = held is None

    def kernel(*refs):
        backward_kernel(fill, *refs)

    operands = [
        table, spans, counts, norms, doc_row, doc_col, selector,
        grad, normed, packed, mixed, logsum, middle, normed_two, hidden, tiles,
    ]
    specs = [smem_spec()] * 3 + [vmem_spec()] * 4 + [any_spec()] * 9
    aliases = {}
    if not fill:
        operands.append(held)
        specs.append(any_spec())
        aliases = {len(operands) - 1: 1}
    return pl.pallas_call(
        kernel,
        name="backward_layer",
        out_shape=[
            jax.ShapeDtypeStruct((length, width), F32),
            jax.ShapeDtypeStruct(tiles.shape, BF16),
            jax.ShapeDtypeStruct((4, width), F32),
        ],
        in_specs=specs,
        out_specs=[any_spec(), any_spec(), vmem_spec()],
        input_output_aliases=aliases,
        scratch_shapes=[
            pltpu.VMEM((width, 3 * width), BF16),
            pltpu.VMEM((width, width), BF16),
            pltpu.VMEM((width, 4 * width), BF16),
            pltpu.VMEM((4 * width, width), BF16),
            pltpu.VMEM((length, width), F32),
            pltpu.VMEM((length, width), BF16),
            pltpu.VMEM((3 * pairs, length, lanes), BF16),
            pltpu.VMEM((pairs, length, lanes), BF16),
            pltpu.VMEM((pairs, 8, length), F32),
            pltpu.VMEM((length, width), F32),
            pltpu.VMEM((length, width), BF16),
            pltpu.VMEM((length, width), F32),
            pltpu.VMEM((length, 4 * width), BF16),
            pltpu.VMEM((length, 4 * width), BF16),
            pltpu.VMEM((length, width), BF16),
            pltpu.VMEM((length, width), F32),
            pltpu.VMEM((length, width), BF16),
            pltpu.VMEM((pairs, length, lanes), BF16),
            pltpu.VMEM((pairs, 8, length), F32),
            pltpu.VMEM((3 * pairs, length, lanes), BF16),
            pltpu.VMEM((length, lanes), F32),
            pltpu.VMEM((length, lanes), F32),
            pltpu.VMEM((length, width), F32),
            pltpu.VMEM((48, width, lanes), BF16),
            pltpu.VMEM((width, lanes), BF16),
            pltpu.SemaphoreType.DMA((48,)),
            pltpu.SemaphoreType.DMA((8,)),
            pltpu.SemaphoreType.DMA((48,)),
            pltpu.SemaphoreType.DMA((tiles.shape[0],)),
            pltpu.SemaphoreType.DMA((1,)),
        ],
        compiler_params=pltpu.CompilerParams(vmem_limit_bytes=VMEM_BYTES),
        cost_estimate=pl.CostEstimate(
            flops=length * width * width * 60, bytes_accessed=26 * 2**20,
            transcendentals=length * length * 4,
        ),
    )(*operands)


def local_by_rows(
    residual_in,
    cotangent,
    segments,
    owners,
    master_tiles,
    first_tiles,
    second_tiles,
    norm_params,
    norm_first,
    norm_second,
):
    local_rows, positions, model_width = residual_in.shape
    seq_devices = lax.axis_size("seq")
    row_devices = lax.axis_size("rows")
    seq_index = lax.axis_index("seq")
    row_index = lax.axis_index("rows")
    length = positions * seq_devices
    tile_total = owners.shape[0]
    capacity, _, tile_width = master_tiles.shape
    quarter = capacity // row_devices
    pairs = model_width // tile_width
    places = jnp.arange(tile_total, dtype=jnp.int32)
    before = (owners[None, :] == owners[:, None]) & (places[None, :] < places[:, None])
    ranks = jnp.sum(before.astype(jnp.int32), axis=1)
    table = ((ranks // quarter) * seq_devices + owners) * quarter + ranks % quarter
    seats = jnp.arange(seq_devices, dtype=jnp.int32)
    counts = jnp.sum((owners[None, :] == seats[:, None]).astype(jnp.int32), axis=1)
    mine = lax.dynamic_slice_in_dim(master_tiles, row_index * quarter, quarter, 0)
    tiles = lax.all_gather(mine.astype(BF16), ("rows", "seq"), axis=0, tiled=True)
    hidden = lax.all_to_all(residual_in, "seq", split_axis=0, concat_axis=1, tiled=True)[0]
    upper = lax.all_to_all(cotangent, "seq", split_axis=0, concat_axis=1, tiled=True)[0]
    doc_ids = lax.dynamic_slice_in_dim(segments, seq_index, 1, 0)
    doc_row = doc_ids
    doc_col = jnp.broadcast_to(doc_ids[0][:, None], (length, tile_width))
    blocks = length // BLOCK
    firsts = doc_ids[0, ::BLOCK]
    lasts = doc_ids[0, BLOCK - 1 :: BLOCK]
    begin = jnp.sum((doc_ids < firsts[:, None]).astype(jnp.int32), axis=1) // BLOCK
    end = (jnp.sum((doc_ids <= lasts[:, None]).astype(jnp.int32), axis=1) + BLOCK - 1) // BLOCK
    spans = jnp.stack([begin, end - begin])
    lane = jnp.arange(model_width)[None, :] // (model_width // HEADS)
    which = jnp.arange(8 * pairs)[:, None]
    selector = ((which % 8 < 2) & (lane == 2 * (which // 8) + which % 8)).astype(F32)
    saved = []
    for layer_number in range(LAYERS):
        norms = norm_params[4 * layer_number : 4 * layer_number + 4]
        part = table[48 * layer_number : 48 * layer_number + 48]
        *kept, after = forward_layer(part, spans, norms, doc_row, doc_col, hidden, tiles, pairs)
        saved.append((kept, hidden))
        hidden = after
    residual_out = lax.all_to_all(hidden[None], "seq", split_axis=1, concat_axis=0, tiled=True)
    norm_parts = [None] * LAYERS
    held = None
    for layer_number in reversed(range(LAYERS)):
        norms = norm_params[4 * layer_number : 4 * layer_number + 4]
        part = table[48 * layer_number : 48 * layer_number + 48]
        kept, below = saved[layer_number]
        upper, held, norm_parts[layer_number] = backward_layer(
            part, spans, counts, norms, doc_row, doc_col, selector, upper, kept, below, tiles, held
        )
    input_grad = lax.all_to_all(upper[None], "seq", split_axis=1, concat_axis=0, tiled=True)
    norm_part = jnp.concatenate(norm_parts, axis=0)
    piece = lax.psum_scatter(
        held.reshape(-1, tile_width), ("rows", "seq"), scatter_dimension=0, tiled=True
    )
    exact = piece.astype(F32)
    squares, norm_sum = lax.psum((jnp.sum(exact * exact), norm_part), ("rows", "seq"))
    owned = lax.all_gather(piece, "rows", axis=0, tiled=True).reshape(master_tiles.shape)
    keep = (jnp.arange(capacity) < counts[seq_index])[:, None, None]
    owned = jnp.where(keep, owned.astype(F32), 0.0)
    total = jnp.sqrt(squares + jnp.sum(norm_sum * norm_sum))
    factor = 1.0 / jnp.maximum(total, 1.0)
    clipped = owned * factor
    norm_clip = norm_sum * factor
    correction = 1.0 - 0.5**STEP
    new_weight, new_first_rows, new_second_rows = adamw(
        master_tiles, clipped, first_tiles, second_tiles, 0.05, correction
    )
    new_weight = jnp.where(keep, new_weight, 0.0)
    new_first_rows = jnp.where(keep, new_first_rows, 0.0)
    new_second_rows = jnp.where(keep, new_second_rows, 0.0)
    new_norm, new_norm_f, new_norm_s = adamw(
        norm_params, norm_clip, norm_first, norm_second, 0.25, correction
    )
    return (
        residual_out,
        input_grad,
        clipped,
        total[None],
        new_first_rows,
        new_second_rows,
        new_weight,
        new_weight.astype(BF16),
        norm_clip,
        new_norm_f,
        new_norm_s,
        new_norm,
    )


def local(residual_in, *others):
    whole_rows = residual_in.shape[0] == lax.axis_size("seq")
    step = local_by_rows if whole_rows else local_by_heads
    return step(residual_in, *others)


def solution(mesh):
    by_rows = P("rows", "seq", None)
    by_slots = P("seq", None, None)
    return jax.shard_map(
        local,
        mesh=mesh,
        in_specs=(
            by_rows, by_rows, P("rows", None), P(), by_slots, by_slots, by_slots, P(), P(), P(),
        ),
        out_specs=(
            by_rows, by_rows, by_slots, P(), by_slots, by_slots, by_slots, by_slots,
            P(), P(), P(), P(),
        ),
        check_vma=False,
    )
```

```python
import jax
import jax.numpy as jnp
from jax import lax
from jax.experimental import pallas as pl
from jax.experimental.pallas import tpu as pltpu

from jax.sharding import PartitionSpec as P

HEADS = 8
LAYERS = 2
STEP = 5


def norm_layer(values, gain, offset):
    center = values - jnp.mean(values, axis=-1, keepdims=True)
    spread = jnp.mean(center * center, axis=-1, keepdims=True)
    return center * lax.rsqrt(spread + 1e-05) * gain + offset


def matmul(left, right):
    return jnp.dot(left, right, preferred_element_type=jnp.float32)


def left_product(left, right):
    return lax.dot_general(
        left, right, (((0,), (0,)), ((), ())), preferred_element_type=jnp.float32
    )


def right_product(left, right):
    return lax.dot_general(
        left, right, (((1,), (1,)), ((), ())), preferred_element_type=jnp.float32
    )


def assemble(weight_tiles, layer_number):
    first_tile = 48 * layer_number
    model_width = weight_tiles.shape[1]
    qkv_weight = (
        weight_tiles[first_tile : first_tile + 12].transpose(1, 0, 2).reshape(model_width, -1)
    )
    out_weight = (
        weight_tiles[first_tile + 12 : first_tile + 16].transpose(1, 0, 2).reshape(model_width, -1)
    )
    up_weight = (
        weight_tiles[first_tile + 16 : first_tile + 32].transpose(1, 0, 2).reshape(model_width, -1)
    )
    down_block = weight_tiles[first_tile + 32 : first_tile + 48].reshape(4, 4, model_width, -1)
    down_weight = down_block.transpose(0, 2, 1, 3).reshape(4 * model_width, model_width)
    return (qkv_weight, out_weight, up_weight, down_weight)


def split_tiles(qkv_grad, out_grad, up_grad, down_grad, tile_width):
    model_width = qkv_grad.shape[0]
    pieces = [
        qkv_grad.reshape(model_width, -1, tile_width).transpose(1, 0, 2),
        out_grad.reshape(model_width, -1, tile_width).transpose(1, 0, 2),
        up_grad.reshape(model_width, -1, tile_width).transpose(1, 0, 2),
        down_grad.reshape(4, model_width, 4, tile_width)
        .transpose(0, 2, 1, 3)
        .reshape(16, model_width, tile_width),
    ]
    return jnp.concatenate(pieces, axis=0)


def attend_forward(queries, key_rows, value_rows, doc_ids, block_rows, scale):
    length = queries.shape[0]

    def one_block(number):
        first_row = number * block_rows
        query_block = lax.dynamic_slice_in_dim(queries, first_row, block_rows, 0)
        doc_block = lax.dynamic_slice_in_dim(doc_ids, first_row, block_rows, 0)
        same_doc = doc_block[:, None] == doc_ids[None, :]
        scores = jnp.where(same_doc, right_product(query_block, key_rows) * scale, -1e30)
        largest = jnp.max(scores, axis=-1, keepdims=True)
        row_total = jnp.sum(jnp.exp(scores - largest), axis=-1, keepdims=True)
        logsum = largest + jnp.log(row_total)
        weights = jnp.where(same_doc, jnp.exp(scores - logsum), 0.0).astype(jnp.bfloat16)
        return (matmul(weights, value_rows).astype(jnp.bfloat16), logsum[:, 0])

    outputs, logsums = lax.map(one_block, jnp.arange(length // block_rows))
    return (outputs.reshape(length, -1), logsums.reshape(length))


def attend_backward(queries, key_rows, value_rows, doc_ids, logsums, out_grads, block_rows, scale):
    length, head_dim = queries.shape

    def one_block(carry, number):
        key_grad, value_grad = carry
        first_row = number * block_rows
        query_block = lax.dynamic_slice_in_dim(queries, first_row, block_rows, 0)
        doc_block = lax.dynamic_slice_in_dim(doc_ids, first_row, block_rows, 0)
        logsum_block = lax.dynamic_slice_in_dim(logsums, first_row, block_rows, 0)
        grad_block = lax.dynamic_slice_in_dim(out_grads, first_row, block_rows, 0)
        same_doc = doc_block[:, None] == doc_ids[None, :]
        scores = jnp.where(same_doc, right_product(query_block, key_rows) * scale, -1e30)
        probs = jnp.where(same_doc, jnp.exp(scores - logsum_block[:, None]), 0.0)
        prob_grad = right_product(grad_block, value_rows)
        inner_sum = jnp.sum(probs * prob_grad, axis=-1, keepdims=True)
        score_grad = (probs * (prob_grad - inner_sum)).astype(jnp.bfloat16)
        query_grad = matmul(score_grad, key_rows) * scale
        key_grad = key_grad + left_product(score_grad, query_block) * scale
        value_grad = value_grad + left_product(probs.astype(jnp.bfloat16), grad_block)
        return ((key_grad, value_grad), query_grad)

    zeros_block = jnp.zeros((length, head_dim), jnp.float32)
    (key_grad, value_grad), query_grads = lax.scan(
        one_block, (zeros_block, zeros_block), jnp.arange(length // block_rows)
    )
    stacked = jnp.stack([query_grads.reshape(length, head_dim), key_grad, value_grad], axis=1)
    return stacked.astype(jnp.bfloat16)


def adamw(weight, grad, first, second, learn_rate, correction):
    first = 0.5 * first + 0.5 * grad
    second = 0.5 * second + 0.5 * grad * grad
    update = first / correction / (jnp.sqrt(second / correction) + 1e-08)
    return (weight - learn_rate * (update + 0.01 * weight), first, second)


def local_by_heads(
    residual_in,
    cotangent,
    segments,
    owners,
    master_tiles,
    first_tiles,
    second_tiles,
    norm_params,
    norm_first,
    norm_second,
):
    local_rows, positions, model_width = residual_in.shape
    seq_devices = lax.axis_size("seq")
    seq_index = lax.axis_index("seq")
    head_dim = model_width // HEADS
    group_count = seq_devices // HEADS
    group_rows = local_rows // group_count
    length = positions * seq_devices
    block_rows = min(512, length)
    scale = head_dim ** (-0.5)
    tile_total = owners.shape[0]
    capacity = master_tiles.shape[0]
    tile_width = master_tiles.shape[2]
    places = jnp.arange(tile_total, dtype=jnp.int32)
    before = (owners[None, :] == owners[:, None]) & (places[None, :] < places[:, None])
    ranks = jnp.sum(before.astype(jnp.int32), axis=1)
    slot_ids = owners * capacity + ranks
    local_slots = jnp.arange(capacity, dtype=jnp.int32)
    matches = (owners[:, None] == seq_index) & (ranks[:, None] == local_slots[None, :])
    chosen = jnp.sum(jnp.where(matches, places[:, None], 0), axis=0)
    present = jnp.any(matches, axis=0)
    copies = lax.all_gather(master_tiles.astype(jnp.bfloat16), "seq", axis=0, tiled=True)
    weight_tiles = jnp.take(copies, slot_ids, axis=0)
    my_group = seq_index // HEADS
    doc_rows = lax.dynamic_slice_in_dim(segments, my_group * group_rows, group_rows, 0)
    hidden = residual_in.reshape(-1, model_width)
    saved = []
    for layer_number in range(LAYERS):
        qkv_weight, out_weight, up_weight, down_weight = assemble(weight_tiles, layer_number)
        params = norm_params[4 * layer_number : 4 * layer_number + 4]
        normed, first_pull = jax.vjp(norm_layer, hidden, params[0], params[1])
        normed_low = normed.astype(jnp.bfloat16)
        packed = matmul(normed_low, qkv_weight).astype(jnp.bfloat16)
        outgoing = packed.reshape(group_count, group_rows, positions, 3, HEADS, head_dim)
        outgoing = outgoing.transpose(0, 4, 1, 2, 3, 5).reshape(
            seq_devices, group_rows, positions * 3 * head_dim
        )
        arrived = lax.all_to_all(outgoing, "seq", split_axis=0, concat_axis=2, tiled=True).reshape(
            group_rows, length, 3, head_dim
        )

        def forward_item(items):
            return attend_forward(
                items[0][:, 0], items[0][:, 1], items[0][:, 2], items[1], block_rows, scale
            )

        attended, logsums = lax.map(forward_item, (arrived, doc_rows))
        returning = attended.reshape(1, group_rows, seq_devices, positions * head_dim)
        mixed = lax.all_to_all(returning, "seq", split_axis=2, concat_axis=0, tiled=True)
        mixed = (
            mixed.reshape(group_count, HEADS, group_rows, positions, head_dim)
            .transpose(0, 2, 3, 1, 4)
            .reshape(-1, model_width)
        )
        middle = hidden + matmul(mixed, out_weight)
        normed_two, second_pull = jax.vjp(norm_layer, middle, params[2], params[3])
        normed_two_low = normed_two.astype(jnp.bfloat16)
        inner = matmul(normed_two_low, up_weight)
        active = jax.nn.gelu(inner).astype(jnp.bfloat16)
        hidden = middle + matmul(active, down_weight)
        saved.append(
            (
                first_pull,
                normed_low,
                arrived,
                logsums,
                mixed,
                second_pull,
                normed_two_low,
                inner,
                active,
            )
        )
    grad = cotangent.reshape(-1, model_width)
    tile_parts = [None] * LAYERS
    norm_parts = [None] * LAYERS
    for layer_number in reversed(range(LAYERS)):
        (
            first_pull,
            normed_low,
            arrived,
            logsums,
            mixed,
            second_pull,
            normed_two_low,
            inner,
            active,
        ) = saved[layer_number]
        qkv_weight, out_weight, up_weight, down_weight = assemble(weight_tiles, layer_number)
        grad_low = grad.astype(jnp.bfloat16)
        down_grad = left_product(active, grad_low)
        active_grad = right_product(grad_low, down_weight)
        inner_grad = jax.vjp(jax.nn.gelu, inner)[1](active_grad)[0].astype(jnp.bfloat16)
        up_grad = left_product(normed_two_low, inner_grad)
        middle_part, gain_two, offset_two = second_pull(right_product(inner_grad, up_weight))
        middle_grad = grad + middle_part
        middle_low = middle_grad.astype(jnp.bfloat16)
        out_grad = left_product(mixed, middle_low)
        mixed_grad = right_product(middle_low, out_weight).astype(jnp.bfloat16)
        sending = mixed_grad.reshape(group_count, group_rows, positions, HEADS, head_dim)
        sending = sending.transpose(0, 3, 1, 2, 4).reshape(
            seq_devices, group_rows, positions * head_dim
        )
        head_grads = lax.all_to_all(
            sending, "seq", split_axis=0, concat_axis=2, tiled=True
        ).reshape(group_rows, length, head_dim)

        def backward_item(items):
            arrived_row, doc_row, logsum_row, grad_row = items
            return attend_backward(
                arrived_row[:, 0],
                arrived_row[:, 1],
                arrived_row[:, 2],
                doc_row,
                logsum_row,
                grad_row,
                block_rows,
                scale,
            )

        packed_grads = lax.map(backward_item, (arrived, doc_rows, logsums, head_grads))
        coming = lax.all_to_all(
            packed_grads.reshape(1, group_rows, seq_devices, positions * 3 * head_dim),
            "seq",
            split_axis=2,
            concat_axis=0,
            tiled=True,
        )
        qkv_grad = coming.reshape(group_count, HEADS, group_rows, positions, 3, head_dim)
        qkv_grad = qkv_grad.transpose(0, 2, 3, 4, 1, 5).reshape(-1, 3 * model_width)
        qkv_weight_grad = left_product(normed_low, qkv_grad)
        input_part, gain_one, offset_one = first_pull(right_product(qkv_grad, qkv_weight))
        grad = middle_grad + input_part
        tile_parts[layer_number] = split_tiles(
            qkv_weight_grad, out_grad, up_grad, down_grad, tile_width
        )
        norm_parts[layer_number] = jnp.stack([gain_one, offset_one, gain_two, offset_two])
    dense = jnp.concatenate(tile_parts, axis=0)
    norm_part = jnp.concatenate(norm_parts, axis=0)
    piece = lax.psum_scatter(
        dense.reshape(-1, tile_width), ("rows", "seq"), scatter_dimension=0, tiled=True
    )
    squares, norm_sum = lax.psum((jnp.sum(piece * piece), norm_part), ("rows", "seq"))
    summed = (
        lax.all_gather(piece.astype(jnp.bfloat16), ("rows", "seq"), axis=0, tiled=True)
        .astype(piece.dtype)
        .reshape(dense.shape)
    )
    owned = jnp.take(summed, chosen, axis=0)
    keep = present[:, None, None]
    owned = jnp.where(keep, owned, 0.0)
    total = jnp.sqrt(squares + jnp.sum(norm_sum * norm_sum))
    factor = 1.0 / jnp.maximum(total, 1.0)
    clipped = owned * factor
    norm_clip = norm_sum * factor
    correction = 1.0 - 0.5**STEP
    new_weight, new_first_rows, new_second_rows = adamw(
        master_tiles, clipped, first_tiles, second_tiles, 0.05, correction
    )
    new_weight = jnp.where(keep, new_weight, 0.0)
    new_first_rows = jnp.where(keep, new_first_rows, 0.0)
    new_second_rows = jnp.where(keep, new_second_rows, 0.0)
    new_norm, new_norm_f, new_norm_s = adamw(
        norm_params, norm_clip, norm_first, norm_second, 0.25, correction
    )
    return (
        hidden.reshape(local_rows, positions, model_width),
        grad.reshape(local_rows, positions, model_width),
        clipped,
        total[None],
        new_first_rows,
        new_second_rows,
        new_weight,
        new_weight.astype(jnp.bfloat16),
        norm_clip,
        new_norm_f,
        new_norm_s,
        new_norm,
    )


F32 = jnp.float32
BF16 = jnp.bfloat16
BLOCK = 256
VMEM_BYTES = 60 * 1024 * 1024


def dot_nn(left, right):
    return jnp.dot(left, right, preferred_element_type=F32)


def dot_nt(left, right, precision=None):
    return lax.dot_general(
        left, right, (((1,), (1,)), ((), ())), preferred_element_type=F32, precision=precision
    )


def dot_tn(left, right):
    return lax.dot_general(left, right, (((0,), (0,)), ((), ())), preferred_element_type=F32)


def rows_of(number, size=BLOCK):
    return pl.ds(pl.multiple_of(number * size, size), size)


def normalized(values):
    center = values - jnp.mean(values, axis=-1, keepdims=True)
    spread = jnp.mean(center * center, axis=-1, keepdims=True)
    scale = lax.rsqrt(spread + 1e-05)
    return center * scale, scale


GELU_A = 0.7978845608028654
GELU_B = 0.044715


def gelu_value(inner):
    return 0.5 * inner * (1.0 + jnp.tanh(GELU_A * (inner + GELU_B * inner * inner * inner)))


def gelu_both(inner):
    square = inner * inner
    bent = jnp.tanh(inner * (GELU_A + GELU_A * GELU_B * square))
    half = 0.5 + 0.5 * bent
    slope = half + 0.5 * inner * (1.0 - bent * bent) * (GELU_A + 3.0 * GELU_A * GELU_B * square)
    return inner * half, slope


def weight_copy(tiles, table, number, target, column, row, sem):
    depth, width = tiles.shape[1], tiles.shape[2]
    rows = pl.ds(pl.multiple_of(row * depth, depth), depth)
    columns = pl.ds(pl.multiple_of(column * width, width), width)
    return pltpu.make_async_copy(
        tiles.at[table[number]], target.at[rows, columns], sem.at[number]
    )


def weight_group(tiles, table, first, count, per_row, target, sem, act):
    @pl.loop(0, count)
    def _(j):
        copy = weight_copy(
            tiles, table, first + j, target, lax.rem(j, per_row), lax.div(j, per_row), sem
        )
        getattr(copy, act)()


def lane_is_first(shape):
    return lax.broadcasted_iota(jnp.int32, shape, 1) < shape[1] // 2


def pair_of(values, lanes_first):
    zero = jnp.zeros_like(values)
    return (
        jnp.where(lanes_first, values, zero).astype(BF16),
        jnp.where(lanes_first, zero, values).astype(BF16),
    )


def forward_kernel(
    table, spans, norms, doc_row, doc_col, hidden, tiles,
    normed_out, packed_out, mixed_out, logsum_out, middle_out, normed_two_out, hidden_out,
    w_qkv, w_out, w_up, w_down, normed, packed, mixed, logcol, logsum, middle, normed_two, after,
    w_sem, o_sem,
):
    length, width = hidden.shape
    blocks = length // BLOCK
    pairs = mixed.shape[0]
    lanes = mixed.shape[2]
    groups = (
        (0, 12, 12, w_qkv), (12, 4, 4, w_out), (16, 16, 16, w_up), (32, 16, 4, w_down),
    )
    for first, count, per_row, target in groups:
        weight_group(tiles, table, first, count, per_row, target, w_sem, "start")

    def ready(group):
        first, count, per_row, target = groups[group]
        weight_group(tiles, table, first, count, per_row, target, w_sem, "wait")

    outs = (
        (normed, normed_out), (packed, packed_out), (mixed, mixed_out), (logsum, logsum_out),
        (middle, middle_out), (normed_two, normed_two_out), (after, hidden_out),
    )

    def flush(number):
        return pltpu.make_async_copy(outs[number][0], outs[number][1], o_sem.at[number])

    ready(0)

    @pl.loop(0, blocks)
    def _(number):
        here = rows_of(number)
        unit, _ = normalized(hidden[here, :].astype(F32))
        low = (unit * norms[0:1, :] + norms[1:2, :]).astype(BF16)
        normed[here, :] = low
        product = dot_nn(low, w_qkv[...])
        for j in range(3 * pairs):
            packed[j, here, :] = product[:, j * lanes : (j + 1) * lanes].astype(BF16)

    flush(0).start()
    flush(1).start()
    lane_ids = lax.broadcasted_iota(jnp.int32, (BLOCK, lanes), 1)
    first_half = lane_is_first((BLOCK, lanes))

    @pl.loop(0, blocks)
    def _(number):
        here = rows_of(number)
        low_key = spans[0, number]
        key_count = spans[1, number]
        doc_here = doc_col[here, 0:1]

        def with_keys(many):
            keys_here = pl.ds(pl.multiple_of(low_key * BLOCK, BLOCK), many * BLOCK)
            same = doc_here == doc_row[0:1, keys_here]

            def one_pair(pair, carry):
                heads = pair_of(packed[pair, here, :].astype(F32) * 0.125, first_half)
                keys = packed[pairs + pair, keys_here, :]
                values = packed[2 * pairs + pair, keys_here, :]
                results = []
                logs = logcol[here, :]
                for side in range(2):
                    scores = jnp.where(same, dot_nt(heads[side], keys), -1e30)
                    top = jnp.max(scores, axis=-1, keepdims=True)
                    weights = jnp.exp(scores - top)
                    total = jnp.sum(weights, axis=-1, keepdims=True)
                    results.append(dot_nn(weights.astype(BF16), values) / total)
                    logs = jnp.where(lane_ids == 8 * pair + side, top + jnp.log(total), logs)
                mixed[pair, here, :] = jnp.where(first_half, results[0], results[1]).astype(BF16)
                logcol[here, :] = logs
                return carry

            lax.fori_loop(0, pairs, one_pair, 0)

        for many in range(1, blocks + 1):
            pl.when(key_count == many)(lambda many=many: with_keys(many))

    flush(2).start()
    turned = logcol[...].T
    for pair in range(pairs):
        logsum[pair, :, :] = turned[8 * pair : 8 * pair + 8, :]
    flush(3).start()
    ready(1)
    ready(2)
    ready(3)
    chunk = width

    @pl.loop(0, blocks)
    def _(number):
        here = rows_of(number)
        side_by_side = jnp.concatenate([mixed[pair, here, :] for pair in range(pairs)], axis=1)
        mid = hidden[here, :].astype(F32) + dot_nn(side_by_side, w_out[...])
        middle[here, :] = mid
        unit, _ = normalized(mid)
        low = (unit * norms[2:3, :] + norms[3:4, :]).astype(BF16)
        normed_two[here, :] = low
        total = mid
        for c in range(w_up.shape[1] // chunk):
            part = slice(c * chunk, (c + 1) * chunk)
            active = gelu_value(dot_nn(low, w_up[:, part])).astype(BF16)
            total = total + dot_nn(active, w_down[part, :])
        after[here, :] = total

    flush(4).start()
    flush(5).start()
    flush(6).start()
    for number in range(len(outs)):
        flush(number).wait()


def vmem_spec():
    return pl.BlockSpec(memory_space=pltpu.VMEM)


def any_spec():
    return pl.BlockSpec(memory_space=pl.ANY)


def smem_spec():
    return pl.BlockSpec(memory_space=pltpu.SMEM)


def forward_layer(table, spans, norms, doc_row, doc_col, hidden, tiles, pairs):
    length, width = hidden.shape
    lanes = tiles.shape[2]
    shapes = (
        ((length, width), BF16),
        ((3 * pairs, length, lanes), BF16),
        ((pairs, length, lanes), BF16),
        ((pairs, 8, length), F32),
        ((length, width), F32),
        ((length, width), BF16),
        ((length, width), F32),
    )
    return pl.pallas_call(
        forward_kernel,
        name="forward_layer",
        out_shape=[jax.ShapeDtypeStruct(s, d) for s, d in shapes],
        in_specs=[smem_spec(), smem_spec()] + [vmem_spec()] * 4 + [any_spec()],
        out_specs=[any_spec()] * len(shapes),
        scratch_shapes=[
            pltpu.VMEM((width, 3 * width), BF16),
            pltpu.VMEM((width, width), BF16),
            pltpu.VMEM((width, 4 * width), BF16),
            pltpu.VMEM((4 * width, width), BF16),
            pltpu.VMEM(shapes[0][0], BF16),
            pltpu.VMEM(shapes[1][0], BF16),
            pltpu.VMEM(shapes[2][0], BF16),
            pltpu.VMEM((length, lanes), F32),
            pltpu.VMEM(shapes[3][0], F32),
            pltpu.VMEM(shapes[4][0], F32),
            pltpu.VMEM(shapes[5][0], BF16),
            pltpu.VMEM(shapes[6][0], F32),
            pltpu.SemaphoreType.DMA((48,)),
            pltpu.SemaphoreType.DMA((7,)),
        ],
        compiler_params=pltpu.CompilerParams(vmem_limit_bytes=VMEM_BYTES),
        cost_estimate=pl.CostEstimate(
            flops=length * width * width * 26, bytes_accessed=18 * 2**20,
            transcendentals=length * length * 4,
        ),
    )(table, spans, norms, doc_row, doc_col, hidden, tiles)


def backward_kernel(
    fill, table, aims, spans, counts, norms, doc_row, doc_col, selector,
    grad_in, normed_in, packed_in, mixed_in, logsum_in, middle_in, normed_two_in, hidden_in, tiles,
    *rest,
):
    rest = list(rest)
    if not fill:
        rest.pop(0)
    (
        grad_out, tile_grads, norm_grads,
        w_qkv, w_out, w_up, w_down,
        grad, normed, packed, mixed, logsum, middle, normed_two, hidden,
        active, inner_grad, grad_low, mid_grad, mid_low, mixed_grad, delta, packed_grad,
        key_sum, value_sum, below, staged, blank,
        w_sem, i_sem, t_sem, z_sem, o_sem,
    ) = rest
    length, width = grad.shape
    blocks = length // BLOCK
    pairs, lanes = mixed.shape[0], mixed.shape[2]
    groups = (
        (0, 12, 12, w_qkv), (12, 4, 4, w_out), (16, 16, 16, w_up), (32, 16, 4, w_down),
    )
    ins = (
        (grad_in, grad), (normed_two_in, normed_two), (middle_in, middle), (mixed_in, mixed),
        (packed_in, packed), (logsum_in, logsum), (hidden_in, hidden), (normed_in, normed),
    )

    def load(number):
        return pltpu.make_async_copy(ins[number][0], ins[number][1], i_sem.at[number])

    def fetch(group, act):
        first, count, per_row, target = groups[group]
        weight_group(tiles, table, first, count, per_row, target, w_sem, act)

    load(0).start()
    load(1).start()
    fetch(2, "start")
    fetch(3, "start")
    load(2).start()
    fetch(1, "start")
    load(3).start()
    load(4).start()
    load(5).start()
    fetch(0, "start")
    load(6).start()
    load(7).start()

    def blank_copies(act):
        capacity = tile_grads.shape[0] // counts.shape[0]
        quarter = capacity // 4

        @pl.loop(0, counts.shape[0])
        def _(owner):
            @pl.loop(counts[owner], capacity)
            def _(place):
                core, depth_z, part = lax.rem(owner, 2), lax.div(owner, 2), lax.div(place, quarter)
                low_bit, high_bit = lax.rem(part, 2), lax.div(part, 2)
                major = low_bit + core * (high_bit - low_bit)
                minor = high_bit + core * (low_bit - high_bit)
                index = lax.rem(place, quarter) * 32 + core * 16 + major * 8 + minor * 4 + depth_z
                getattr(
                    pltpu.make_async_copy(blank, tile_grads.at[index], z_sem.at[index]), act
                )()

    if fill:
        blank[...] = jnp.zeros_like(blank)
        blank_copies("start")

    norm_grads[...] = jnp.zeros_like(norm_grads)
    load(0).wait()
    load(1).wait()
    load(2).wait()
    fetch(2, "wait")
    fetch(3, "wait")
    fetch(1, "wait")
    load(3).wait()
    chunk = width
    chunks = w_up.shape[1] // chunk

    def norm_back(values, out_grad, gain, gain_row):
        unit, scale = normalized(values)
        norm_grads[gain_row : gain_row + 1, :] += jnp.sum(out_grad * unit, axis=0, keepdims=True)
        norm_grads[gain_row + 1 : gain_row + 2, :] += jnp.sum(out_grad, axis=0, keepdims=True)
        turned = out_grad * gain
        average = jnp.mean(turned, axis=-1, keepdims=True)
        along = jnp.mean(turned * unit, axis=-1, keepdims=True)
        return scale * (turned - average - unit * along)

    @pl.loop(0, blocks)
    def _(number):
        here = rows_of(number)
        upper = grad[here, :].astype(F32)
        low = upper.astype(BF16)
        grad_low[here, :] = low
        normed_here = normed_two[here, :]
        total = jnp.zeros((BLOCK, width), F32)
        for c in range(chunks):
            part = slice(c * chunk, (c + 1) * chunk)
            value, slope = gelu_both(dot_nn(normed_here, w_up[:, part]))
            active[here, part] = value.astype(BF16)
            inner = (slope * dot_nt(low, w_down[part, :])).astype(BF16)
            inner_grad[here, part] = inner
            total = total + dot_nt(inner, w_up[:, part])
        mid = upper + norm_back(middle[here, :], total, norms[2:3, :], 2)
        mid_grad[here, :] = mid
        mid_here = mid.astype(BF16)
        mid_low[here, :] = mid_here
        back = dot_nt(mid_here, w_out[...]).astype(BF16)
        for pair in range(pairs):
            mixed_grad[pair, here, :] = back[:, pair * lanes : (pair + 1) * lanes]
        side_by_side = jnp.concatenate([mixed[pair, here, :] for pair in range(pairs)], axis=1)
        both = side_by_side.astype(F32) * back.astype(F32)
        sums = dot_nt(selector[...], both, precision=lax.Precision.HIGHEST)
        for pair in range(pairs):
            delta[pair, :, here] = sums[8 * pair : 8 * pair + 8, :]

    def send_tile(place):
        return pltpu.make_async_copy(
            staged.at[place], tile_grads.at[aims[place]], t_sem.at[place]
        )

    def emit(block, first):
        for c in range(block.shape[1] // lanes):
            staged[first + c] = block[:, c * lanes : (c + 1) * lanes].astype(BF16)
            send_tile(first + c).start()

    @pl.loop(0, chunks)
    def _(c):
        part = rows_of(c, chunk)
        emit(dot_tn(active[:, part], grad_low[...]), 32 + 4 * c)
        emit(dot_tn(normed_two[...], inner_grad[:, part]), 16 + 4 * c)

    side_by_side = jnp.concatenate([mixed[pair] for pair in range(pairs)], axis=1)
    emit(dot_tn(side_by_side, mid_low[...]), 12)
    load(4).wait()
    load(5).wait()
    first_half = lane_is_first((BLOCK, lanes))

    @pl.loop(0, pairs)
    def _(pair):
        key_sum[...] = jnp.zeros_like(key_sum)
        value_sum[...] = jnp.zeros_like(value_sum)

        @pl.loop(0, blocks)
        def _(number):
            here = rows_of(number)
            low_key = spans[0, number]
            key_count = spans[1, number]
            doc_here = doc_row[0:1, here]

            def with_keys(many):
                keys_here = pl.ds(pl.multiple_of(low_key * BLOCK, BLOCK), many * BLOCK)
                same = doc_col[keys_here, 0:1] == doc_here
                heads = pair_of(packed[pair, here, :].astype(F32) * 0.125, first_half)
                outs = pair_of(mixed_grad[pair, here, :].astype(F32), first_half)
                keys = packed[pairs + pair, keys_here, :]
                values = packed[2 * pairs + pair, keys_here, :]
                query_parts = []
                key_part = key_sum[keys_here, :]
                value_part = value_sum[keys_here, :]
                for side in range(2):
                    scores = dot_nt(keys, heads[side])
                    weights = jnp.exp(
                        jnp.where(same, scores - logsum[pair, side : side + 1, here], -1e30)
                    )
                    from_values = dot_nt(values, outs[side])
                    score_grad = (
                        weights * (from_values - delta[pair, side : side + 1, here])
                    ).astype(BF16)
                    value_part = value_part + dot_nn(weights.astype(BF16), outs[side])
                    key_part = key_part + dot_nn(score_grad, heads[side])
                    query_parts.append(dot_tn(score_grad, keys))
                key_sum[keys_here, :] = key_part
                value_sum[keys_here, :] = value_part
                packed_grad[pair, here, :] = (
                    jnp.where(first_half, query_parts[0], query_parts[1]) * 0.125
                ).astype(BF16)

            for many in range(1, blocks + 1):
                pl.when(key_count == many)(lambda many=many: with_keys(many))

        packed_grad[pairs + pair] = key_sum[...].astype(BF16)
        packed_grad[2 * pairs + pair] = value_sum[...].astype(BF16)

    fetch(0, "wait")
    load(6).wait()
    load(7).wait()

    @pl.loop(0, blocks)
    def _(number):
        here = rows_of(number)
        wide = jnp.concatenate([packed_grad[j, here, :] for j in range(3 * pairs)], axis=1)
        total = dot_nt(wide, w_qkv[...])
        below[here, :] = mid_grad[here, :] + norm_back(
            hidden[here, :].astype(F32), total, norms[0:1, :], 0
        )

    flush = pltpu.make_async_copy(below, grad_out, o_sem.at[0])
    flush.start()

    @pl.loop(0, 3)
    def _(c):
        wide = jnp.concatenate([packed_grad[pairs * c + j] for j in range(pairs)], axis=1)
        emit(dot_tn(normed[...], wide), 4 * c)

    flush.wait()

    @pl.loop(0, 48)
    def _(place):
        send_tile(place).wait()

    if fill:
        blank_copies("wait")


def backward_layer(
    table, aims, spans, counts, norms, doc_row, doc_col, selector, grad, saved, hidden, tiles, held
):
    normed, packed, mixed, logsum, middle, normed_two = saved
    length, width = grad.shape
    lanes = tiles.shape[2]
    pairs = mixed.shape[0]
    fill = held is None

    def kernel(*refs):
        backward_kernel(fill, *refs)

    operands = [
        table, aims, spans, counts, norms, doc_row, doc_col, selector,
        grad, normed, packed, mixed, logsum, middle, normed_two, hidden, tiles,
    ]
    specs = [smem_spec()] * 4 + [vmem_spec()] * 4 + [any_spec()] * 9
    aliases = {}
    if not fill:
        operands.append(held)
        specs.append(any_spec())
        aliases = {len(operands) - 1: 1}
    return pl.pallas_call(
        kernel,
        name="backward_layer",
        out_shape=[
            jax.ShapeDtypeStruct((length, width), F32),
            jax.ShapeDtypeStruct(tiles.shape, BF16),
            jax.ShapeDtypeStruct((4, width), F32),
        ],
        in_specs=specs,
        out_specs=[any_spec(), any_spec(), vmem_spec()],
        input_output_aliases=aliases,
        scratch_shapes=[
            pltpu.VMEM((width, 3 * width), BF16),
            pltpu.VMEM((width, width), BF16),
            pltpu.VMEM((width, 4 * width), BF16),
            pltpu.VMEM((4 * width, width), BF16),
            pltpu.VMEM((length, width), grad.dtype),
            pltpu.VMEM((length, width), BF16),
            pltpu.VMEM((3 * pairs, length, lanes), BF16),
            pltpu.VMEM((pairs, length, lanes), BF16),
            pltpu.VMEM((pairs, 8, length), F32),
            pltpu.VMEM((length, width), F32),
            pltpu.VMEM((length, width), BF16),
            pltpu.VMEM((length, width), hidden.dtype),
            pltpu.VMEM((length, 4 * width), BF16),
            pltpu.VMEM((length, 4 * width), BF16),
            pltpu.VMEM((length, width), BF16),
            pltpu.VMEM((length, width), F32),
            pltpu.VMEM((length, width), BF16),
            pltpu.VMEM((pairs, length, lanes), BF16),
            pltpu.VMEM((pairs, 8, length), F32),
            pltpu.VMEM((3 * pairs, length, lanes), BF16),
            pltpu.VMEM((length, lanes), F32),
            pltpu.VMEM((length, lanes), F32),
            pltpu.VMEM((length, width), F32),
            pltpu.VMEM((48, width, lanes), BF16),
            pltpu.VMEM((width, lanes), BF16),
            pltpu.SemaphoreType.DMA((48,)),
            pltpu.SemaphoreType.DMA((8,)),
            pltpu.SemaphoreType.DMA((48,)),
            pltpu.SemaphoreType.DMA((tiles.shape[0],)),
            pltpu.SemaphoreType.DMA((1,)),
        ],
        compiler_params=pltpu.CompilerParams(vmem_limit_bytes=VMEM_BYTES),
        cost_estimate=pl.CostEstimate(
            flops=length * width * width * 60, bytes_accessed=26 * 2**20,
            transcendentals=length * length * 4,
        ),
    )(*operands)


MESH_IDS = pl.DeviceIdType.MESH


def place_of_device():
    row = lax.axis_index("rows")
    seat = lax.axis_index("seq")
    return row % 2, row // 2, seat // 2, seat % 2


def device_at(x, y, z, core):
    return (2 * y + x, 2 * z + core)


def greet(partners):
    barrier = pltpu.get_barrier_semaphore()
    for partner in partners:
        pl.semaphore_signal(barrier, inc=1, device_id=partner, device_id_type=MESH_IDS)
    pl.semaphore_wait(barrier, len(partners))


def seat_partners(x, y, z, core):
    others = []
    for k in range(1, 8):
        seat = (2 * z + core + k) % 8
        others.append((2 * y + x, seat))
    return others


def post(source, target, send_sem, recv_sem, number, partner):
    copy = pltpu.make_async_remote_copy(
        src_ref=source,
        dst_ref=target,
        send_sem=send_sem.at[number],
        recv_sem=recv_sem.at[number],
        device_id=partner,
        device_id_type=MESH_IDS,
    )
    copy.start()
    return copy


def gather_kernel(master, residual, tiles, rows, wide, low, flat, flat_low, send_sem, recv_sem, l_sem):
    x, y, z, core = place_of_device()
    quarter_id = 2 * y + x
    across = device_at(x, y, z, 1 - core)
    by_x = device_at(1 - x, y, z, core)
    by_y = device_at(x, 1 - y, z, core)
    seats = seat_partners(x, y, z, core)
    load_near = pltpu.make_async_copy(
        master.at[pl.ds(4 * quarter_id, 4)], wide.at[pl.ds(4 * quarter_id, 4)], l_sem.at[0]
    )
    load_near.start()
    load_flat = pltpu.make_async_copy(residual, flat, l_sem.at[1])
    load_flat.start()
    far = []
    for k in range(1, 4):
        part = pl.ds(4 * ((quarter_id + k) % 4), 4)
        copy = pltpu.make_async_copy(master.at[part], wide.at[part], l_sem.at[1 + k])
        copy.start()
        far.append(copy)
    greet(seats + [by_x, by_y])

    def spot(z_from, quarter):
        return core * 64 + z_from * 16 + 4 * quarter

    def convert(first, count):
        @pl.loop(0, count)
        def _(j):
            low[first + j] = wide[first + j].astype(BF16)

    sent = []
    load_near.wait()
    convert(4 * quarter_id, 4)
    arrivals = []
    for k in range(1, 4):
        z_to = (z + k) % 4
        here = pl.ds(spot(z, quarter_id), 4)
        arrivals.append(
            post(
                low.at[pl.ds(4 * quarter_id, 4)], tiles.at[here], send_sem, recv_sem, k - 1,
                device_at(x, y, z_to, core),
            )
        )
    sent += arrivals
    load_flat.wait()

    @pl.loop(0, flat.shape[0])
    def _(j):
        flat_low[j] = flat[j].astype(BF16)

    seat = 2 * z + core
    row_moves = []
    for k in range(1, 8):
        row_moves.append(
            post(
                flat_low.at[(seat + k) % 8], rows.at[seat], send_sem, recv_sem, 2 + k,
                seats[k - 1],
            )
        )
    keep_row = pltpu.make_async_copy(flat_low.at[seat], rows.at[seat], l_sem.at[5])
    keep_row.start()
    for k in range(1, 4):
        far[k - 1].wait()
        convert(4 * ((quarter_id + k) % 4), 4)
    mine = pl.ds(core * 64 + z * 16, 16)
    keep_tiles = pltpu.make_async_copy(low, tiles.at[mine], l_sem.at[6])
    keep_tiles.start()
    core_moves = [post(low, tiles.at[mine], send_sem, recv_sem, 10, across)]
    number = 11

    def relay(part, partner):
        nonlocal number
        copy = post(tiles.at[part], tiles.at[part], send_sem, recv_sem, number, partner)
        number += 1
        return copy

    x_moves, y_moves, corner_moves = [], [], []
    quarter_x = 2 * y + (1 - x)
    quarter_y = 2 * (1 - y) + x
    for k in range(1, 4):
        arrivals[k - 1].wait_recv()
        part = pl.ds(spot((z + 4 - k) % 4, quarter_id), 4)
        x_moves.append(relay(part, by_x))
        y_moves.append(relay(part, by_y))
        core_moves.append(relay(part, across))
    for k in range(1, 4):
        z_from = (z + 4 - k) % 4
        x_moves[k - 1].wait_recv()
        corner_moves.append(relay(pl.ds(spot(z_from, quarter_x), 2), by_y))
        core_moves.append(relay(pl.ds(spot(z_from, quarter_x), 4), across))
        y_moves[k - 1].wait_recv()
        corner_moves.append(relay(pl.ds(spot(z_from, quarter_y) + 2, 2), by_x))
        core_moves.append(relay(pl.ds(spot(z_from, quarter_y), 4), across))
    quarter_c = 3 - quarter_id
    for k in range(1, 4):
        z_from = (z + 4 - k) % 4
        for half in range(2):
            corner_moves[2 * (k - 1) + half].wait_recv()
            core_moves.append(relay(pl.ds(spot(z_from, quarter_c) + 2 * half, 2), across))
    for copy in row_moves + core_moves:
        copy.wait_recv()
    for copy in sent + row_moves + core_moves + x_moves + y_moves + corner_moves:
        copy.wait_send()
    keep_row.wait()
    keep_tiles.wait()


def gather_start(master_tiles, residual):
    capacity, depth, lanes = master_tiles.shape
    count = 3 + 7 + 1 + 9 + 12 + 6
    return pl.pallas_call(
        gather_kernel,
        name="gather_start",
        out_shape=[
            jax.ShapeDtypeStruct((8 * capacity, depth, lanes), BF16),
            jax.ShapeDtypeStruct(residual.shape, BF16),
        ],
        in_specs=[any_spec()] * 2,
        out_specs=[any_spec()] * 2,
        scratch_shapes=[
            pltpu.VMEM(master_tiles.shape, F32),
            pltpu.VMEM(master_tiles.shape, BF16),
            pltpu.VMEM(residual.shape, F32),
            pltpu.VMEM(residual.shape, BF16),
            pltpu.SemaphoreType.DMA((count,)),
            pltpu.SemaphoreType.DMA((count,)),
            pltpu.SemaphoreType.DMA((7,)),
        ],
        compiler_params=pltpu.CompilerParams(
            collective_id=0, has_side_effects=True, vmem_limit_bytes=32 * 2**20
        ),
        cost_estimate=pl.CostEstimate(
            flops=0, bytes_accessed=200 * 2**20, transcendentals=0
        ),
    )(master_tiles, residual)


def reduce_kernel(
    held, upper, norm_part, owned, rows, norm_sum, squares,
    core_in, own, one_in, two_in, z_in, piece, flat, flat_low, norm_in, norm_now, square_in,
    square_now, send_sem, recv_sem, l_sem,
):
    x, y, z, core = place_of_device()
    quarter_id = 2 * y + x
    across = device_at(x, y, z, 1 - core)
    by_x = device_at(1 - x, y, z, core)
    by_y = device_at(x, 1 - y, z, core)
    by_both = device_at(1 - x, 1 - y, z, core)
    plus, minus = core, 1 - core
    first_bit = x * minus + y * plus
    second_bit = y * minus + x * plus
    one = device_at(x + minus * (1 - 2 * x), y + plus * (1 - 2 * y), z, core)
    two = device_at(x + plus * (1 - 2 * x), y + minus * (1 - 2 * y), z, core)
    along_z = [device_at(x, y, (z + k) % 4, core) for k in range(1, 4)]
    seats = seat_partners(x, y, z, core)
    seat = 2 * z + core
    chunks = own.shape[0]
    number = 0
    copies = []

    def move(source, target, partner):
        nonlocal number
        copy = post(source, target, send_sem, recv_sem, number, partner)
        number += 1
        copies.append(copy)
        return copy

    loads = []
    for i in range(chunks):
        copy = pltpu.make_async_copy(
            held.at[pl.ds(32 * i + 16 * core, 16)], own.at[i], l_sem.at[i]
        )
        copy.start()
        loads.append(copy)
    load_flat = pltpu.make_async_copy(upper, flat, l_sem.at[chunks])
    load_flat.start()
    greet(seats + [by_x, by_y, by_both])
    core_moves = [
        move(held.at[pl.ds(32 * i + 16 * (1 - core), 16)], core_in.at[i], across)
        for i in range(chunks)
    ]
    norm_now[0] = norm_part[...]
    norm_moves = [move(norm_now.at[0], norm_in.at[0], across)]
    load_flat.wait()

    @pl.loop(0, flat.shape[0])
    def _(j):
        flat_low[j] = flat[j].astype(BF16)

    for k in range(1, 8):
        move(flat_low.at[(seat + k) % 8], rows.at[seat], seats[k - 1])
    row_moves = copies[-7:]
    keep_row = pltpu.make_async_copy(flat_low.at[seat], rows.at[seat], l_sem.at[chunks + 1])
    keep_row.start()

    def add_in(target, first, incoming, count):
        @pl.loop(0, count)
        def _(j):
            target[first + j] = (
                target[first + j].astype(F32) + incoming[j].astype(F32)
            ).astype(BF16)

    one_moves, two_moves, z_moves, plane_moves, keeps = [], [], [], [], []

    def stage_core(i):
        loads[i].wait()
        core_moves[i].wait_recv()
        add_in(own.at[i], 0, core_in.at[i], 16)
        one_moves.append(
            move(own.at[i, pl.ds(8 * (1 - first_bit), 8)], one_in.at[i], one)
        )

    def stage_one(i):
        one_moves[i].wait_recv()
        add_in(own.at[i], 8 * first_bit, one_in.at[i], 8)
        two_moves.append(
            move(
                own.at[i, pl.ds(8 * first_bit + 4 * (1 - second_bit), 4)], two_in.at[i], two
            )
        )

    def stage_two(i):
        two_moves[i].wait_recv()
        base = 8 * first_bit + 4 * second_bit
        add_in(own.at[i], base, two_in.at[i], 4)
        z_moves.append(
            [
                move(own.at[i, base + (z + k) % 4], z_in.at[i, k - 1], along_z[k - 1])
                for k in range(1, 4)
            ]
        )

    def stage_z(i):
        for copy in z_moves[i]:
            copy.wait_recv()
        total = own[i, 8 * first_bit + 4 * second_bit + z].astype(F32)
        for k in range(3):
            total = total + z_in[i, k].astype(F32)
        piece[i] = total.astype(BF16)
        square_now[0] += jnp.sum((total * total).reshape(-1, 8, total.shape[1]), axis=0)
        here = 4 * quarter_id + i
        for partner in (by_x, by_y, by_both):
            plane_moves.append(move(piece.at[i], owned.at[here], partner))
        keep = pltpu.make_async_copy(piece.at[i], owned.at[here], l_sem.at[chunks + 2 + i])
        keep.start()
        keeps.append(keep)

    def norm_stage(step, partner):
        norm_moves[step].wait_recv()
        norm_now[step + 1] = norm_now[step] + norm_in[step]
        if partner is not None:
            norm_moves.append(move(norm_now.at[step + 1], norm_in.at[step + 1], partner))

    square_now[...] = jnp.zeros_like(square_now)
    stage_core(0)
    stage_core(1)
    norm_stage(0, by_x)
    stage_core(2)
    stage_core(3)
    norm_stage(1, by_y)
    stage_one(0)
    stage_one(1)
    norm_stage(2, None)
    norm_z = [move(norm_now.at[3], norm_in.at[2 + k], along_z[k - 1]) for k in range(1, 4)]
    stage_two(0)
    stage_one(2)
    stage_two(1)
    stage_z(0)
    stage_one(3)
    stage_two(2)
    stage_z(1)
    stage_two(3)
    stage_z(2)
    stage_z(3)

    def in_order(own_value, incoming):
        values = [own_value] + [incoming(k) for k in range(1, 4)]
        total = None
        for place in range(4):
            picked = values[0]
            for k in range(1, 4):
                picked = jnp.where((z + 4 - k) % 4 == place, values[k], picked)
            total = picked if total is None else total + picked
        return total

    square_moves = []

    def square_stage(step, partner):
        square_moves.append(move(square_now.at[step], square_in.at[step], partner))
        square_moves[step].wait_recv()
        square_now[step + 1] = square_now[step] + square_in[step]

    square_stage(0, by_x)
    square_stage(1, by_y)
    square_stage(2, across)
    square_z = [
        move(square_now.at[3], square_in.at[2 + k], along_z[k - 1]) for k in range(1, 4)
    ]
    for copy in norm_z:
        copy.wait_recv()
    norm_sum[...] = in_order(norm_now[3], lambda k: norm_in[2 + k])
    for copy in square_z:
        copy.wait_recv()
    squares[...] = in_order(square_now[3], lambda k: square_in[2 + k])
    for copy in row_moves + plane_moves:
        copy.wait_recv()
    for copy in copies:
        copy.wait_send()
    keep_row.wait()
    for keep in keeps:
        keep.wait()


def reduce_end(held, upper, norm_part):
    slots, depth, lanes = held.shape
    chunks = 4
    count = 4 + 1 + 7 + 4 + 4 + 12 + 12 + 2 + 3 + 3 + 3
    return pl.pallas_call(
        reduce_kernel,
        name="reduce_end",
        out_shape=[
            jax.ShapeDtypeStruct((slots // 8, depth, lanes), BF16),
            jax.ShapeDtypeStruct(upper.shape, BF16),
            jax.ShapeDtypeStruct(norm_part.shape, F32),
            jax.ShapeDtypeStruct((8, lanes), F32),
        ],
        in_specs=[any_spec(), any_spec(), vmem_spec()],
        out_specs=[any_spec(), any_spec(), vmem_spec(), vmem_spec()],
        scratch_shapes=[
            pltpu.VMEM((chunks, 16, depth, lanes), BF16),
            pltpu.VMEM((chunks, 16, depth, lanes), BF16),
            pltpu.VMEM((chunks, 8, depth, lanes), BF16),
            pltpu.VMEM((chunks, 4, depth, lanes), BF16),
            pltpu.VMEM((chunks, 3, depth, lanes), BF16),
            pltpu.VMEM((chunks, depth, lanes), BF16),
            pltpu.VMEM(upper.shape, F32),
            pltpu.VMEM(upper.shape, BF16),
            pltpu.VMEM((6, *norm_part.shape), F32),
            pltpu.VMEM((4, *norm_part.shape), F32),
            pltpu.VMEM((6, 8, lanes), F32),
            pltpu.VMEM((4, 8, lanes), F32),
            pltpu.SemaphoreType.DMA((count,)),
            pltpu.SemaphoreType.DMA((count,)),
            pltpu.SemaphoreType.DMA((2 * chunks + 2,)),
        ],
        compiler_params=pltpu.CompilerParams(
            collective_id=1, has_side_effects=True, vmem_limit_bytes=VMEM_BYTES
        ),
        cost_estimate=pl.CostEstimate(
            flops=0, bytes_accessed=300 * 2**20, transcendentals=0
        ),
    )(held, upper, norm_part)


def local_by_rows(
    residual_in,
    cotangent,
    segments,
    owners,
    master_tiles,
    first_tiles,
    second_tiles,
    norm_params,
    norm_first,
    norm_second,
):
    local_rows, positions, model_width = residual_in.shape
    seq_devices = lax.axis_size("seq")
    seq_index = lax.axis_index("seq")
    length = positions * seq_devices
    tile_total = owners.shape[0]
    capacity, _, tile_width = master_tiles.shape
    quarter = capacity // 4
    pairs = model_width // tile_width
    places = jnp.arange(tile_total, dtype=jnp.int32)
    before = (owners[None, :] == owners[:, None]) & (places[None, :] < places[:, None])
    ranks = jnp.sum(before.astype(jnp.int32), axis=1)
    core, depth_z, part_id = owners % 2, owners // 2, ranks // quarter
    major = jnp.where(core == 0, part_id % 2, part_id // 2)
    minor = jnp.where(core == 0, part_id // 2, part_id % 2)
    weight_table = core * 64 + depth_z * 16 + ranks
    grad_table = (ranks % quarter) * 32 + core * 16 + major * 8 + minor * 4 + depth_z
    seats = jnp.arange(seq_devices, dtype=jnp.int32)
    counts = jnp.sum((owners[None, :] == seats[:, None]).astype(jnp.int32), axis=1)
    tiles, hidden = gather_start(master_tiles, residual_in)
    hidden = hidden.reshape(length, model_width)
    later, tiles = lax.optimization_barrier((cotangent, tiles))
    upper = lax.all_to_all(later.astype(BF16), "seq", split_axis=0, concat_axis=0, tiled=True)
    upper = upper.reshape(length, model_width)
    doc_ids = lax.dynamic_slice_in_dim(segments, seq_index, 1, 0)
    doc_row = doc_ids
    doc_col = jnp.broadcast_to(doc_ids[0][:, None], (length, tile_width))
    blocks = length // BLOCK
    firsts = doc_ids[0, ::BLOCK]
    lasts = doc_ids[0, BLOCK - 1 :: BLOCK]
    begin = jnp.sum((doc_ids < firsts[:, None]).astype(jnp.int32), axis=1) // BLOCK
    end = (jnp.sum((doc_ids <= lasts[:, None]).astype(jnp.int32), axis=1) + BLOCK - 1) // BLOCK
    spans = jnp.stack([begin, end - begin])
    lane = jnp.arange(model_width)[None, :] // (model_width // HEADS)
    which = jnp.arange(8 * pairs)[:, None]
    selector = ((which % 8 < 2) & (lane == 2 * (which // 8) + which % 8)).astype(F32)
    saved = []
    for layer_number in range(LAYERS):
        norms = norm_params[4 * layer_number : 4 * layer_number + 4]
        part = weight_table[48 * layer_number : 48 * layer_number + 48]
        *kept, after = forward_layer(part, spans, norms, doc_row, doc_col, hidden, tiles, pairs)
        saved.append((kept, hidden))
        hidden = after
    residual_out = lax.all_to_all(
        hidden.astype(BF16).reshape(residual_in.shape), "seq", split_axis=0, concat_axis=0, tiled=True
    ).astype(F32)
    norm_parts = [None] * LAYERS
    held = None
    for layer_number in reversed(range(LAYERS)):
        norms = norm_params[4 * layer_number : 4 * layer_number + 4]
        part = weight_table[48 * layer_number : 48 * layer_number + 48]
        aims = grad_table[48 * layer_number : 48 * layer_number + 48]
        kept, below = saved[layer_number]
        upper, held, norm_parts[layer_number] = backward_layer(
            part, aims, spans, counts, norms, doc_row, doc_col, selector, upper, kept, below, tiles, held
        )
    norm_part = jnp.concatenate(norm_parts, axis=0)
    owned, input_grad, norm_sum, squares = reduce_end(
        held, upper.reshape(residual_in.shape), norm_part
    )
    input_grad = input_grad.astype(F32)
    keep = (jnp.arange(capacity) < counts[seq_index])[:, None, None]
    owned = jnp.where(keep, owned.astype(F32), 0.0)
    total = jnp.sqrt(jnp.sum(squares) + jnp.sum(norm_sum * norm_sum))
    factor = 1.0 / jnp.maximum(total, 1.0)
    clipped = owned * factor
    norm_clip = norm_sum * factor
    correction = 1.0 - 0.5**STEP
    new_weight, new_first_rows, new_second_rows = adamw(
        master_tiles, clipped, first_tiles, second_tiles, 0.05, correction
    )
    new_weight = jnp.where(keep, new_weight, 0.0)
    new_first_rows = jnp.where(keep, new_first_rows, 0.0)
    new_second_rows = jnp.where(keep, new_second_rows, 0.0)
    new_norm, new_norm_f, new_norm_s = adamw(
        norm_params, norm_clip, norm_first, norm_second, 0.25, correction
    )
    return (
        residual_out,
        input_grad,
        clipped,
        total[None],
        new_first_rows,
        new_second_rows,
        new_weight,
        new_weight.astype(BF16),
        norm_clip,
        new_norm_f,
        new_norm_s,
        new_norm,
    )


def local(residual_in, *others):
    whole_rows = residual_in.shape[0] == lax.axis_size("seq")
    step = local_by_rows if whole_rows else local_by_heads
    return step(residual_in, *others)


def solution(mesh):
    by_rows = P("rows", "seq", None)
    by_slots = P("seq", None, None)
    return jax.shard_map(
        local,
        mesh=mesh,
        in_specs=(
            by_rows, by_rows, P("rows", None), P(), by_slots, by_slots, by_slots, P(), P(), P(),
        ),
        out_specs=(
            by_rows, by_rows, by_slots, P(), by_slots, by_slots, by_slots, by_slots,
            P(), P(), P(), P(),
        ),
        check_vma=False,
    )
```

```python
import jax
import jax.numpy as jnp
from jax import lax
from jax.experimental import pallas as pl
from jax.experimental.pallas import tpu as pltpu

from jax.sharding import PartitionSpec as P

HEADS = 8
LAYERS = 2
STEP = 5


def norm_layer(values, gain, offset):
    center = values - jnp.mean(values, axis=-1, keepdims=True)
    spread = jnp.mean(center * center, axis=-1, keepdims=True)
    return center * lax.rsqrt(spread + 1e-05) * gain + offset


def matmul(left, right):
    return jnp.dot(left, right, preferred_element_type=jnp.float32)


def left_product(left, right):
    return lax.dot_general(
        left, right, (((0,), (0,)), ((), ())), preferred_element_type=jnp.float32
    )


def right_product(left, right):
    return lax.dot_general(
        left, right, (((1,), (1,)), ((), ())), preferred_element_type=jnp.float32
    )


def assemble(weight_tiles, layer_number):
    first_tile = 48 * layer_number
    model_width = weight_tiles.shape[1]
    qkv_weight = (
        weight_tiles[first_tile : first_tile + 12].transpose(1, 0, 2).reshape(model_width, -1)
    )
    out_weight = (
        weight_tiles[first_tile + 12 : first_tile + 16].transpose(1, 0, 2).reshape(model_width, -1)
    )
    up_weight = (
        weight_tiles[first_tile + 16 : first_tile + 32].transpose(1, 0, 2).reshape(model_width, -1)
    )
    down_block = weight_tiles[first_tile + 32 : first_tile + 48].reshape(4, 4, model_width, -1)
    down_weight = down_block.transpose(0, 2, 1, 3).reshape(4 * model_width, model_width)
    return (qkv_weight, out_weight, up_weight, down_weight)


def split_tiles(qkv_grad, out_grad, up_grad, down_grad, tile_width):
    model_width = qkv_grad.shape[0]
    pieces = [
        qkv_grad.reshape(model_width, -1, tile_width).transpose(1, 0, 2),
        out_grad.reshape(model_width, -1, tile_width).transpose(1, 0, 2),
        up_grad.reshape(model_width, -1, tile_width).transpose(1, 0, 2),
        down_grad.reshape(4, model_width, 4, tile_width)
        .transpose(0, 2, 1, 3)
        .reshape(16, model_width, tile_width),
    ]
    return jnp.concatenate(pieces, axis=0)


def attend_forward(queries, key_rows, value_rows, doc_ids, block_rows, scale):
    length = queries.shape[0]

    def one_block(number):
        first_row = number * block_rows
        query_block = lax.dynamic_slice_in_dim(queries, first_row, block_rows, 0)
        doc_block = lax.dynamic_slice_in_dim(doc_ids, first_row, block_rows, 0)
        same_doc = doc_block[:, None] == doc_ids[None, :]
        scores = jnp.where(same_doc, right_product(query_block, key_rows) * scale, -1e30)
        largest = jnp.max(scores, axis=-1, keepdims=True)
        row_total = jnp.sum(jnp.exp(scores - largest), axis=-1, keepdims=True)
        logsum = largest + jnp.log(row_total)
        weights = jnp.where(same_doc, jnp.exp(scores - logsum), 0.0).astype(jnp.bfloat16)
        return (matmul(weights, value_rows).astype(jnp.bfloat16), logsum[:, 0])

    outputs, logsums = lax.map(one_block, jnp.arange(length // block_rows))
    return (outputs.reshape(length, -1), logsums.reshape(length))


def attend_backward(queries, key_rows, value_rows, doc_ids, logsums, out_grads, block_rows, scale):
    length, head_dim = queries.shape

    def one_block(carry, number):
        key_grad, value_grad = carry
        first_row = number * block_rows
        query_block = lax.dynamic_slice_in_dim(queries, first_row, block_rows, 0)
        doc_block = lax.dynamic_slice_in_dim(doc_ids, first_row, block_rows, 0)
        logsum_block = lax.dynamic_slice_in_dim(logsums, first_row, block_rows, 0)
        grad_block = lax.dynamic_slice_in_dim(out_grads, first_row, block_rows, 0)
        same_doc = doc_block[:, None] == doc_ids[None, :]
        scores = jnp.where(same_doc, right_product(query_block, key_rows) * scale, -1e30)
        probs = jnp.where(same_doc, jnp.exp(scores - logsum_block[:, None]), 0.0)
        prob_grad = right_product(grad_block, value_rows)
        inner_sum = jnp.sum(probs * prob_grad, axis=-1, keepdims=True)
        score_grad = (probs * (prob_grad - inner_sum)).astype(jnp.bfloat16)
        query_grad = matmul(score_grad, key_rows) * scale
        key_grad = key_grad + left_product(score_grad, query_block) * scale
        value_grad = value_grad + left_product(probs.astype(jnp.bfloat16), grad_block)
        return ((key_grad, value_grad), query_grad)

    zeros_block = jnp.zeros((length, head_dim), jnp.float32)
    (key_grad, value_grad), query_grads = lax.scan(
        one_block, (zeros_block, zeros_block), jnp.arange(length // block_rows)
    )
    stacked = jnp.stack([query_grads.reshape(length, head_dim), key_grad, value_grad], axis=1)
    return stacked.astype(jnp.bfloat16)


def adamw(weight, grad, first, second, learn_rate, correction):
    first = 0.5 * first + 0.5 * grad
    second = 0.5 * second + 0.5 * grad * grad
    update = first / correction / (jnp.sqrt(second / correction) + 1e-08)
    return (weight - learn_rate * (update + 0.01 * weight), first, second)


def local_by_heads(
    residual_in,
    cotangent,
    segments,
    owners,
    master_tiles,
    first_tiles,
    second_tiles,
    norm_params,
    norm_first,
    norm_second,
):
    local_rows, positions, model_width = residual_in.shape
    seq_devices = lax.axis_size("seq")
    seq_index = lax.axis_index("seq")
    head_dim = model_width // HEADS
    group_count = seq_devices // HEADS
    group_rows = local_rows // group_count
    length = positions * seq_devices
    block_rows = min(512, length)
    scale = head_dim ** (-0.5)
    tile_total = owners.shape[0]
    capacity = master_tiles.shape[0]
    tile_width = master_tiles.shape[2]
    places = jnp.arange(tile_total, dtype=jnp.int32)
    before = (owners[None, :] == owners[:, None]) & (places[None, :] < places[:, None])
    ranks = jnp.sum(before.astype(jnp.int32), axis=1)
    slot_ids = owners * capacity + ranks
    local_slots = jnp.arange(capacity, dtype=jnp.int32)
    matches = (owners[:, None] == seq_index) & (ranks[:, None] == local_slots[None, :])
    chosen = jnp.sum(jnp.where(matches, places[:, None], 0), axis=0)
    present = jnp.any(matches, axis=0)
    copies = lax.all_gather(master_tiles.astype(jnp.bfloat16), "seq", axis=0, tiled=True)
    weight_tiles = jnp.take(copies, slot_ids, axis=0)
    my_group = seq_index // HEADS
    doc_rows = lax.dynamic_slice_in_dim(segments, my_group * group_rows, group_rows, 0)
    hidden = residual_in.reshape(-1, model_width)
    saved = []
    for layer_number in range(LAYERS):
        qkv_weight, out_weight, up_weight, down_weight = assemble(weight_tiles, layer_number)
        params = norm_params[4 * layer_number : 4 * layer_number + 4]
        normed, first_pull = jax.vjp(norm_layer, hidden, params[0], params[1])
        normed_low = normed.astype(jnp.bfloat16)
        packed = matmul(normed_low, qkv_weight).astype(jnp.bfloat16)
        outgoing = packed.reshape(group_count, group_rows, positions, 3, HEADS, head_dim)
        outgoing = outgoing.transpose(0, 4, 1, 2, 3, 5).reshape(
            seq_devices, group_rows, positions * 3 * head_dim
        )
        arrived = lax.all_to_all(outgoing, "seq", split_axis=0, concat_axis=2, tiled=True).reshape(
            group_rows, length, 3, head_dim
        )

        def forward_item(items):
            return attend_forward(
                items[0][:, 0], items[0][:, 1], items[0][:, 2], items[1], block_rows, scale
            )

        attended, logsums = lax.map(forward_item, (arrived, doc_rows))
        returning = attended.reshape(1, group_rows, seq_devices, positions * head_dim)
        mixed = lax.all_to_all(returning, "seq", split_axis=2, concat_axis=0, tiled=True)
        mixed = (
            mixed.reshape(group_count, HEADS, group_rows, positions, head_dim)
            .transpose(0, 2, 3, 1, 4)
            .reshape(-1, model_width)
        )
        middle = hidden + matmul(mixed, out_weight)
        normed_two, second_pull = jax.vjp(norm_layer, middle, params[2], params[3])
        normed_two_low = normed_two.astype(jnp.bfloat16)
        inner = matmul(normed_two_low, up_weight)
        active = jax.nn.gelu(inner).astype(jnp.bfloat16)
        hidden = middle + matmul(active, down_weight)
        saved.append(
            (
                first_pull,
                normed_low,
                arrived,
                logsums,
                mixed,
                second_pull,
                normed_two_low,
                inner,
                active,
            )
        )
    grad = cotangent.reshape(-1, model_width)
    tile_parts = [None] * LAYERS
    norm_parts = [None] * LAYERS
    for layer_number in reversed(range(LAYERS)):
        (
            first_pull,
            normed_low,
            arrived,
            logsums,
            mixed,
            second_pull,
            normed_two_low,
            inner,
            active,
        ) = saved[layer_number]
        qkv_weight, out_weight, up_weight, down_weight = assemble(weight_tiles, layer_number)
        grad_low = grad.astype(jnp.bfloat16)
        down_grad = left_product(active, grad_low)
        active_grad = right_product(grad_low, down_weight)
        inner_grad = jax.vjp(jax.nn.gelu, inner)[1](active_grad)[0].astype(jnp.bfloat16)
        up_grad = left_product(normed_two_low, inner_grad)
        middle_part, gain_two, offset_two = second_pull(right_product(inner_grad, up_weight))
        middle_grad = grad + middle_part
        middle_low = middle_grad.astype(jnp.bfloat16)
        out_grad = left_product(mixed, middle_low)
        mixed_grad = right_product(middle_low, out_weight).astype(jnp.bfloat16)
        sending = mixed_grad.reshape(group_count, group_rows, positions, HEADS, head_dim)
        sending = sending.transpose(0, 3, 1, 2, 4).reshape(
            seq_devices, group_rows, positions * head_dim
        )
        head_grads = lax.all_to_all(
            sending, "seq", split_axis=0, concat_axis=2, tiled=True
        ).reshape(group_rows, length, head_dim)

        def backward_item(items):
            arrived_row, doc_row, logsum_row, grad_row = items
            return attend_backward(
                arrived_row[:, 0],
                arrived_row[:, 1],
                arrived_row[:, 2],
                doc_row,
                logsum_row,
                grad_row,
                block_rows,
                scale,
            )

        packed_grads = lax.map(backward_item, (arrived, doc_rows, logsums, head_grads))
        coming = lax.all_to_all(
            packed_grads.reshape(1, group_rows, seq_devices, positions * 3 * head_dim),
            "seq",
            split_axis=2,
            concat_axis=0,
            tiled=True,
        )
        qkv_grad = coming.reshape(group_count, HEADS, group_rows, positions, 3, head_dim)
        qkv_grad = qkv_grad.transpose(0, 2, 3, 4, 1, 5).reshape(-1, 3 * model_width)
        qkv_weight_grad = left_product(normed_low, qkv_grad)
        input_part, gain_one, offset_one = first_pull(right_product(qkv_grad, qkv_weight))
        grad = middle_grad + input_part
        tile_parts[layer_number] = split_tiles(
            qkv_weight_grad, out_grad, up_grad, down_grad, tile_width
        )
        norm_parts[layer_number] = jnp.stack([gain_one, offset_one, gain_two, offset_two])
    dense = jnp.concatenate(tile_parts, axis=0)
    norm_part = jnp.concatenate(norm_parts, axis=0)
    piece = lax.psum_scatter(
        dense.reshape(-1, tile_width), ("rows", "seq"), scatter_dimension=0, tiled=True
    )
    squares, norm_sum = lax.psum((jnp.sum(piece * piece), norm_part), ("rows", "seq"))
    summed = (
        lax.all_gather(piece.astype(jnp.bfloat16), ("rows", "seq"), axis=0, tiled=True)
        .astype(piece.dtype)
        .reshape(dense.shape)
    )
    owned = jnp.take(summed, chosen, axis=0)
    keep = present[:, None, None]
    owned = jnp.where(keep, owned, 0.0)
    total = jnp.sqrt(squares + jnp.sum(norm_sum * norm_sum))
    factor = 1.0 / jnp.maximum(total, 1.0)
    clipped = owned * factor
    norm_clip = norm_sum * factor
    correction = 1.0 - 0.5**STEP
    new_weight, new_first_rows, new_second_rows = adamw(
        master_tiles, clipped, first_tiles, second_tiles, 0.05, correction
    )
    new_weight = jnp.where(keep, new_weight, 0.0)
    new_first_rows = jnp.where(keep, new_first_rows, 0.0)
    new_second_rows = jnp.where(keep, new_second_rows, 0.0)
    new_norm, new_norm_f, new_norm_s = adamw(
        norm_params, norm_clip, norm_first, norm_second, 0.25, correction
    )
    return (
        hidden.reshape(local_rows, positions, model_width),
        grad.reshape(local_rows, positions, model_width),
        clipped,
        total[None],
        new_first_rows,
        new_second_rows,
        new_weight,
        new_weight.astype(jnp.bfloat16),
        norm_clip,
        new_norm_f,
        new_norm_s,
        new_norm,
    )


F32 = jnp.float32
BF16 = jnp.bfloat16
BLOCK = 256
DENSE = 1024
QUERY = 128
UNROLL = 4
UNROLL_BACK = 4
VMEM_BYTES = 60 * 1024 * 1024


def dot_nn(left, right):
    return jnp.dot(left, right, preferred_element_type=F32)


def dot_nt(left, right, precision=None):
    return lax.dot_general(
        left, right, (((1,), (1,)), ((), ())), preferred_element_type=F32, precision=precision
    )


def dot_tn(left, right):
    return lax.dot_general(left, right, (((0,), (0,)), ((), ())), preferred_element_type=F32)


def rows_of(number, size=BLOCK):
    return pl.ds(pl.multiple_of(number * size, size), size)


def normalized(values):
    center = values - jnp.mean(values, axis=-1, keepdims=True)
    spread = jnp.mean(center * center, axis=-1, keepdims=True)
    scale = lax.rsqrt(spread + 1e-05)
    return center * scale, scale


GELU_A = 0.7978845608028654
GELU_B = 0.044715


def gelu_value(inner):
    return 0.5 * inner * (1.0 + jnp.tanh(GELU_A * (inner + GELU_B * inner * inner * inner)))


def gelu_both(inner):
    square = inner * inner
    bent = jnp.tanh(inner * (GELU_A + GELU_A * GELU_B * square))
    half = 0.5 + 0.5 * bent
    slope = half + 0.5 * inner * (1.0 - bent * bent) * (GELU_A + 3.0 * GELU_A * GELU_B * square)
    return inner * half, slope


def weight_copy(tiles, table, number, target, column, row, sem):
    depth, width = tiles.shape[1], tiles.shape[2]
    rows = pl.ds(pl.multiple_of(row * depth, depth), depth)
    columns = pl.ds(pl.multiple_of(column * width, width), width)
    return pltpu.make_async_copy(
        tiles.at[table[number]], target.at[rows, columns], sem.at[number]
    )


def weight_group(tiles, table, first, count, per_row, target, sem, act):
    @pl.loop(0, count)
    def _(j):
        copy = weight_copy(
            tiles, table, first + j, target, lax.rem(j, per_row), lax.div(j, per_row), sem
        )
        getattr(copy, act)()


def lane_is_first(shape):
    return lax.broadcasted_iota(jnp.int32, shape, 1) < shape[1] // 2


def stacked(values, lanes_first):
    zero = jnp.zeros_like(values)
    return jnp.concatenate(
        [
            jnp.where(lanes_first, values, zero).astype(BF16),
            jnp.where(lanes_first, zero, values).astype(BF16),
        ],
        axis=0,
    )


def forward_kernel(
    table, spans, norms, doc_row, doc_col, hidden, tiles,
    normed_out, packed_out, mixed_out, logsum_out, middle_out, normed_two_out, hidden_out,
    w_qkv, w_out, w_up, w_down, normed, packed, mixed, logcol, logsum, middle, normed_two, after,
    w_sem, o_sem,
):
    length, width = hidden.shape
    blocks = length // DENSE
    pairs = mixed.shape[0]
    lanes = mixed.shape[2]
    groups = (
        (0, 12, 12, w_qkv), (12, 4, 4, w_out), (16, 16, 16, w_up), (32, 16, 4, w_down),
    )
    for first, count, per_row, target in groups:
        weight_group(tiles, table, first, count, per_row, target, w_sem, "start")

    def ready(group):
        first, count, per_row, target = groups[group]
        weight_group(tiles, table, first, count, per_row, target, w_sem, "wait")

    outs = (
        (normed, normed_out), (packed, packed_out), (mixed, mixed_out), (logsum, logsum_out),
        (middle, middle_out), (normed_two, normed_two_out), (after, hidden_out),
    )

    def flush(number):
        return pltpu.make_async_copy(outs[number][0], outs[number][1], o_sem.at[number])

    ready(0)

    @pl.loop(0, blocks)
    def _(number):
        here = rows_of(number, DENSE)
        unit, _ = normalized(hidden[here, :].astype(F32))
        low = (unit * norms[0:1, :] + norms[1:2, :]).astype(BF16)
        normed[here, :] = low
        product = dot_nn(low, w_qkv[...])
        for j in range(3 * pairs):
            packed[j, here, :] = product[:, j * lanes : (j + 1) * lanes].astype(BF16)

    flush(0).start()
    flush(1).start()
    lane_ids = lax.broadcasted_iota(jnp.int32, (QUERY, lanes), 1)
    first_half = lane_is_first((QUERY, lanes))

    @pl.loop(0, length // QUERY)
    def _(number):
        here = rows_of(number, QUERY)
        low_key = spans[0, number]
        key_count = spans[1, number]
        doc_here = doc_col[here, 0:1]

        def with_keys(many):
            keys_here = pl.ds(pl.multiple_of(low_key * QUERY, QUERY), many * BLOCK)
            same = doc_here == doc_row[0:1, keys_here]
            same = jnp.concatenate([same, same], axis=0)

            def score(pair):
                heads = stacked(packed[pair, here, :].astype(F32) * 0.125, first_half)
                return dot_nt(heads, packed[pairs + pair, keys_here, :])

            def settle(scores):
                scores = jnp.where(same, scores, -1e30)
                top = jnp.max(scores, axis=-1, keepdims=True)
                weights = jnp.exp(scores - top)
                total = jnp.sum(weights, axis=-1, keepdims=True)
                return weights.astype(BF16), total, top + jnp.log(total)

            def finish(pair, weights, total, logs):
                result = dot_nn(weights, packed[2 * pairs + pair, keys_here, :]) / total
                mixed[pair, here, :] = jnp.where(
                    first_half, result[:QUERY], result[QUERY:]
                ).astype(BF16)
                old = logcol[here, :]
                old = jnp.where(lane_ids == 8 * pair, logs[:QUERY], old)
                logcol[here, :] = jnp.where(lane_ids == 8 * pair + 1, logs[QUERY:], old)

            waiting = None
            ahead = score(0)
            for pair in range(pairs):
                now = ahead
                if pair + 1 < pairs:
                    ahead = score(pair + 1)
                done = settle(now)
                if waiting is not None:
                    finish(pair - 1, *waiting)
                waiting = done
            finish(pairs - 1, *waiting)


        for many in range(1, length // BLOCK + 1):
            pl.when(key_count == many)(lambda many=many: with_keys(many))

    flush(2).start()
    turned = logcol[...].T
    for pair in range(pairs):
        logsum[pair, :, :] = turned[8 * pair : 8 * pair + 8, :]
    flush(3).start()
    ready(1)
    ready(2)
    ready(3)
    chunk = width

    @pl.loop(0, blocks)
    def _(number):
        here = rows_of(number, DENSE)
        side_by_side = jnp.concatenate([mixed[pair, here, :] for pair in range(pairs)], axis=1)
        mid = hidden[here, :].astype(F32) + dot_nn(side_by_side, w_out[...])
        middle[here, :] = mid
        unit, _ = normalized(mid)
        low = (unit * norms[2:3, :] + norms[3:4, :]).astype(BF16)
        normed_two[here, :] = low
        total = mid
        for c in range(w_up.shape[1] // chunk):
            part = slice(c * chunk, (c + 1) * chunk)
            active = gelu_value(dot_nn(low, w_up[:, part])).astype(BF16)
            total = total + dot_nn(active, w_down[part, :])
        after[here, :] = total

    flush(4).start()
    flush(5).start()
    flush(6).start()
    for number in range(len(outs)):
        flush(number).wait()


def vmem_spec():
    return pl.BlockSpec(memory_space=pltpu.VMEM)


def any_spec():
    return pl.BlockSpec(memory_space=pl.ANY)


def smem_spec():
    return pl.BlockSpec(memory_space=pltpu.SMEM)


def forward_layer(table, spans, norms, doc_row, doc_col, hidden, tiles, pairs):
    length, width = hidden.shape
    lanes = tiles.shape[2]
    shapes = (
        ((length, width), BF16),
        ((3 * pairs, length, lanes), BF16),
        ((pairs, length, lanes), BF16),
        ((pairs, 8, length), F32),
        ((length, width), F32),
        ((length, width), BF16),
        ((length, width), F32),
    )
    return pl.pallas_call(
        forward_kernel,
        name="forward_layer",
        out_shape=[jax.ShapeDtypeStruct(s, d) for s, d in shapes],
        in_specs=[smem_spec(), smem_spec()] + [vmem_spec()] * 4 + [any_spec()],
        out_specs=[any_spec()] * len(shapes),
        scratch_shapes=[
            pltpu.VMEM((width, 3 * width), BF16),
            pltpu.VMEM((width, width), BF16),
            pltpu.VMEM((width, 4 * width), BF16),
            pltpu.VMEM((4 * width, width), BF16),
            pltpu.VMEM(shapes[0][0], BF16),
            pltpu.VMEM(shapes[1][0], BF16),
            pltpu.VMEM(shapes[2][0], BF16),
            pltpu.VMEM((length, lanes), F32),
            pltpu.VMEM(shapes[3][0], F32),
            pltpu.VMEM(shapes[4][0], F32),
            pltpu.VMEM(shapes[5][0], BF16),
            pltpu.VMEM(shapes[6][0], F32),
            pltpu.SemaphoreType.DMA((48,)),
            pltpu.SemaphoreType.DMA((7,)),
        ],
        compiler_params=pltpu.CompilerParams(vmem_limit_bytes=VMEM_BYTES),
        cost_estimate=pl.CostEstimate(
            flops=length * width * width * 26, bytes_accessed=18 * 2**20,
            transcendentals=length * length * 4,
        ),
    )(table, spans, norms, doc_row, doc_col, hidden, tiles)


def backward_kernel(
    fill, table, aims, spans, counts, norms, doc_row, doc_col, selector,
    grad_in, normed_in, packed_in, mixed_in, logsum_in, middle_in, normed_two_in, hidden_in, tiles,
    *rest,
):
    rest = list(rest)
    if not fill:
        rest.pop(0)
    (
        grad_out, tile_grads, norm_grads,
        w_qkv, w_out, w_up, w_down,
        grad, normed, packed, mixed, logsum, middle, normed_two, hidden,
        active, inner_grad, grad_low, mid_grad, mid_low, mixed_grad, delta, packed_grad,
        key_sum, value_sum, below, staged, blank,
        w_sem, i_sem, t_sem, z_sem, o_sem,
    ) = rest
    length, width = grad.shape
    blocks = length // DENSE
    pairs, lanes = mixed.shape[0], mixed.shape[2]
    groups = (
        (0, 12, 12, w_qkv), (12, 4, 4, w_out), (16, 16, 16, w_up), (32, 16, 4, w_down),
    )
    ins = (
        (grad_in, grad), (normed_two_in, normed_two), (middle_in, middle), (mixed_in, mixed),
        (packed_in, packed), (logsum_in, logsum), (hidden_in, hidden), (normed_in, normed),
    )

    def load(number):
        return pltpu.make_async_copy(ins[number][0], ins[number][1], i_sem.at[number])

    def fetch(group, act):
        first, count, per_row, target = groups[group]
        weight_group(tiles, table, first, count, per_row, target, w_sem, act)

    load(0).start()
    load(1).start()
    fetch(2, "start")
    fetch(3, "start")
    load(2).start()
    fetch(1, "start")
    load(3).start()
    load(4).start()
    load(5).start()
    fetch(0, "start")
    load(6).start()
    load(7).start()

    def blank_copies(act):
        capacity = tile_grads.shape[0] // counts.shape[0]
        quarter = capacity // 4

        @pl.loop(0, counts.shape[0])
        def _(owner):
            @pl.loop(counts[owner], capacity)
            def _(place):
                core, depth_z, part = lax.rem(owner, 2), lax.div(owner, 2), lax.div(place, quarter)
                low_bit, high_bit = lax.rem(part, 2), lax.div(part, 2)
                major = low_bit + core * (high_bit - low_bit)
                minor = high_bit + core * (low_bit - high_bit)
                index = lax.rem(place, quarter) * 32 + core * 16 + major * 8 + minor * 4 + depth_z
                getattr(
                    pltpu.make_async_copy(blank, tile_grads.at[index], z_sem.at[index]), act
                )()

    if fill:
        blank[...] = jnp.zeros_like(blank)
        blank_copies("start")

    norm_grads[...] = jnp.zeros_like(norm_grads)
    load(0).wait()
    load(1).wait()
    load(2).wait()
    fetch(2, "wait")
    fetch(3, "wait")
    fetch(1, "wait")
    load(3).wait()
    chunk = width
    chunks = w_up.shape[1] // chunk

    def norm_back(values, out_grad, gain, gain_row):
        unit, scale = normalized(values)
        norm_grads[gain_row : gain_row + 1, :] += jnp.sum(out_grad * unit, axis=0, keepdims=True)
        norm_grads[gain_row + 1 : gain_row + 2, :] += jnp.sum(out_grad, axis=0, keepdims=True)
        turned = out_grad * gain
        average = jnp.mean(turned, axis=-1, keepdims=True)
        along = jnp.mean(turned * unit, axis=-1, keepdims=True)
        return scale * (turned - average - unit * along)

    @pl.loop(0, blocks)
    def _(number):
        here = rows_of(number, DENSE)
        upper = grad[here, :].astype(F32)
        low = upper.astype(BF16)
        grad_low[here, :] = low
        normed_here = normed_two[here, :]
        total = jnp.zeros((DENSE, width), F32)
        for c in range(chunks):
            part = slice(c * chunk, (c + 1) * chunk)
            value, slope = gelu_both(dot_nn(normed_here, w_up[:, part]))
            active[here, part] = value.astype(BF16)
            inner = (slope * dot_nt(low, w_down[part, :])).astype(BF16)
            inner_grad[here, part] = inner
            total = total + dot_nt(inner, w_up[:, part])
        mid = upper + norm_back(middle[here, :], total, norms[2:3, :], 2)
        mid_grad[here, :] = mid
        mid_here = mid.astype(BF16)
        mid_low[here, :] = mid_here
        back = dot_nt(mid_here, w_out[...]).astype(BF16)
        for pair in range(pairs):
            mixed_grad[pair, here, :] = back[:, pair * lanes : (pair + 1) * lanes]
        side_by_side = jnp.concatenate([mixed[pair, here, :] for pair in range(pairs)], axis=1)
        both = side_by_side.astype(F32) * back.astype(F32)
        sums = dot_nt(selector[...], both, precision=lax.Precision.HIGHEST)
        for pair in range(pairs):
            delta[pair, :, here] = sums[8 * pair : 8 * pair + 8, :]

    def send_tile(place):
        return pltpu.make_async_copy(
            staged.at[place], tile_grads.at[aims[place]], t_sem.at[place]
        )

    def emit(block, first):
        for c in range(block.shape[1] // lanes):
            staged[first + c] = block[:, c * lanes : (c + 1) * lanes].astype(BF16)
            send_tile(first + c).start()

    @pl.loop(0, chunks)
    def _(c):
        part = rows_of(c, chunk)
        emit(dot_tn(active[:, part], grad_low[...]), 32 + 4 * c)
        emit(dot_tn(normed_two[...], inner_grad[:, part]), 16 + 4 * c)

    side_by_side = jnp.concatenate([mixed[pair] for pair in range(pairs)], axis=1)
    emit(dot_tn(side_by_side, mid_low[...]), 12)
    load(4).wait()
    load(5).wait()
    first_half = lane_is_first((QUERY, lanes))

    key_sum[...] = jnp.zeros_like(key_sum)
    value_sum[...] = jnp.zeros_like(value_sum)

    @pl.loop(0, length // QUERY)
    def _(number):
        here = rows_of(number, QUERY)
        low_key = spans[0, number]
        key_count = spans[1, number]
        doc_here = doc_row[0:1, here]
        doc_here = jnp.concatenate([doc_here, doc_here], axis=1)

        def with_keys(many):
            keys_here = pl.ds(pl.multiple_of(low_key * QUERY, QUERY), many * BLOCK)
            same = doc_col[keys_here, 0:1] == doc_here

            def score(pair):
                heads = stacked(packed[pair, here, :].astype(F32) * 0.125, first_half)
                outs = stacked(mixed_grad[pair, here, :].astype(F32), first_half)
                return (
                    heads,
                    outs,
                    dot_nt(packed[pairs + pair, keys_here, :], heads),
                    dot_nt(packed[2 * pairs + pair, keys_here, :], outs),
                )

            def settle(pair, heads, outs, scores, from_values):
                logs = jnp.concatenate([logsum[pair, 0:1, here], logsum[pair, 1:2, here]], axis=1)
                means = jnp.concatenate([delta[pair, 0:1, here], delta[pair, 1:2, here]], axis=1)
                weights = jnp.exp(jnp.where(same, scores - logs, -1e30))
                score_grad = (weights * (from_values - means)).astype(BF16)
                return heads, outs, weights.astype(BF16), score_grad

            def finish(pair, heads, outs, weights, score_grad):
                value_sum[pair, keys_here, :] += dot_nn(weights, outs)
                key_sum[pair, keys_here, :] += dot_nn(score_grad, heads)
                query_part = dot_tn(score_grad, packed[pairs + pair, keys_here, :]) * 0.125
                packed_grad[pair, here, :] = jnp.where(
                    first_half, query_part[:QUERY], query_part[QUERY:]
                ).astype(BF16)

            waiting = None
            ahead = score(0)
            for pair in range(pairs):
                now = ahead
                if pair + 1 < pairs:
                    ahead = score(pair + 1)
                done = settle(pair, *now)
                if waiting is not None:
                    finish(pair - 1, *waiting)
                waiting = done
            finish(pairs - 1, *waiting)

        for many in range(1, length // BLOCK + 1):
            pl.when(key_count == many)(lambda many=many: with_keys(many))

    for pair in range(pairs):
        packed_grad[pairs + pair] = key_sum[pair].astype(BF16)
        packed_grad[2 * pairs + pair] = value_sum[pair].astype(BF16)

    fetch(0, "wait")
    load(6).wait()
    load(7).wait()

    @pl.loop(0, blocks)
    def _(number):
        here = rows_of(number, DENSE)
        wide = jnp.concatenate([packed_grad[j, here, :] for j in range(3 * pairs)], axis=1)
        total = dot_nt(wide, w_qkv[...])
        below[here, :] = mid_grad[here, :] + norm_back(
            hidden[here, :].astype(F32), total, norms[0:1, :], 0
        )

    flush = pltpu.make_async_copy(below, grad_out, o_sem.at[0])
    flush.start()

    @pl.loop(0, 3)
    def _(c):
        wide = jnp.concatenate([packed_grad[pairs * c + j] for j in range(pairs)], axis=1)
        emit(dot_tn(normed[...], wide), 4 * c)

    flush.wait()

    @pl.loop(0, 48)
    def _(place):
        send_tile(place).wait()

    if fill:
        blank_copies("wait")


def backward_layer(
    table, aims, spans, counts, norms, doc_row, doc_col, selector, grad, saved, hidden, tiles, held
):
    normed, packed, mixed, logsum, middle, normed_two = saved
    length, width = grad.shape
    lanes = tiles.shape[2]
    pairs = mixed.shape[0]
    fill = held is None

    def kernel(*refs):
        backward_kernel(fill, *refs)

    operands = [
        table, aims, spans, counts, norms, doc_row, doc_col, selector,
        grad, normed, packed, mixed, logsum, middle, normed_two, hidden, tiles,
    ]
    specs = [smem_spec()] * 4 + [vmem_spec()] * 4 + [any_spec()] * 9
    aliases = {}
    if not fill:
        operands.append(held)
        specs.append(any_spec())
        aliases = {len(operands) - 1: 1}
    return pl.pallas_call(
        kernel,
        name="backward_layer",
        out_shape=[
            jax.ShapeDtypeStruct((length, width), F32),
            jax.ShapeDtypeStruct(tiles.shape, BF16),
            jax.ShapeDtypeStruct((4, width), F32),
        ],
        in_specs=specs,
        out_specs=[any_spec(), any_spec(), vmem_spec()],
        input_output_aliases=aliases,
        scratch_shapes=[
            pltpu.VMEM((width, 3 * width), BF16),
            pltpu.VMEM((width, width), BF16),
            pltpu.VMEM((width, 4 * width), BF16),
            pltpu.VMEM((4 * width, width), BF16),
            pltpu.VMEM((length, width), grad.dtype),
            pltpu.VMEM((length, width), BF16),
            pltpu.VMEM((3 * pairs, length, lanes), BF16),
            pltpu.VMEM((pairs, length, lanes), BF16),
            pltpu.VMEM((pairs, 8, length), F32),
            pltpu.VMEM((length, width), F32),
            pltpu.VMEM((length, width), BF16),
            pltpu.VMEM((length, width), hidden.dtype),
            pltpu.VMEM((length, 4 * width), BF16),
            pltpu.VMEM((length, 4 * width), BF16),
            pltpu.VMEM((length, width), BF16),
            pltpu.VMEM((length, width), F32),
            pltpu.VMEM((length, width), BF16),
            pltpu.VMEM((pairs, length, lanes), BF16),
            pltpu.VMEM((pairs, 8, length), F32),
            pltpu.VMEM((3 * pairs, length, lanes), BF16),
            pltpu.VMEM((pairs, length, lanes), F32),
            pltpu.VMEM((pairs, length, lanes), F32),
            pltpu.VMEM((length, width), F32),
            pltpu.VMEM((48, width, lanes), BF16),
            pltpu.VMEM((width, lanes), BF16),
            pltpu.SemaphoreType.DMA((48,)),
            pltpu.SemaphoreType.DMA((8,)),
            pltpu.SemaphoreType.DMA((48,)),
            pltpu.SemaphoreType.DMA((tiles.shape[0],)),
            pltpu.SemaphoreType.DMA((1,)),
        ],
        compiler_params=pltpu.CompilerParams(vmem_limit_bytes=VMEM_BYTES),
        cost_estimate=pl.CostEstimate(
            flops=length * width * width * 60, bytes_accessed=26 * 2**20,
            transcendentals=length * length * 4,
        ),
    )(*operands)


MESH_IDS = pl.DeviceIdType.MESH


def place_of_device():
    row = lax.axis_index("rows")
    seat = lax.axis_index("seq")
    return row % 2, row // 2, seat // 2, seat % 2


def device_at(x, y, z, core):
    return (2 * y + x, 2 * z + core)


def greet(partners):
    barrier = pltpu.get_barrier_semaphore()
    for partner in partners:
        pl.semaphore_signal(barrier, inc=1, device_id=partner, device_id_type=MESH_IDS)
    pl.semaphore_wait(barrier, len(partners))


def seat_partners(x, y, z, core):
    others = []
    for k in range(1, 8):
        seat = (2 * z + core + k) % 8
        others.append((2 * y + x, seat))
    return others


def post(source, target, send_sem, recv_sem, number, partner):
    copy = pltpu.make_async_remote_copy(
        src_ref=source,
        dst_ref=target,
        send_sem=send_sem.at[number],
        recv_sem=recv_sem.at[number],
        device_id=partner,
        device_id_type=MESH_IDS,
    )
    copy.start()
    return copy


def gather_kernel(master, residual, tiles, rows, wide, low, flat, flat_low, send_sem, recv_sem, l_sem):
    x, y, z, core = place_of_device()
    quarter_id = 2 * y + x
    across = device_at(x, y, z, 1 - core)
    by_x = device_at(1 - x, y, z, core)
    by_y = device_at(x, 1 - y, z, core)
    quarters = (quarter_id, 2 * y + (1 - x), 2 * (1 - y) + x, 3 - quarter_id)
    seats = seat_partners(x, y, z, core)
    seat = 2 * z + core
    load_near = pltpu.make_async_copy(
        master.at[pl.ds(4 * quarter_id, 4)], wide.at[pl.ds(4 * quarter_id, 4)], l_sem.at[0]
    )
    load_near.start()
    far = []
    for k in range(1, 4):
        part = pl.ds(4 * ((quarter_id + k) % 4), 4)
        copy = pltpu.make_async_copy(master.at[part], wide.at[part], l_sem.at[1 + k])
        copy.start()
        far.append(copy)
    load_flat = pltpu.make_async_copy(residual, flat, l_sem.at[1])
    load_flat.start()
    greet(seats + [by_x, by_y])

    def spot(z_from, quarter):
        return core * 64 + z_from * 16 + 4 * quarter

    def convert(first, count):
        @pl.loop(0, count)
        def _(j):
            low[first + j] = wide[first + j].astype(BF16)

    def make(source, target, number, partner):
        return pltpu.make_async_remote_copy(
            src_ref=source, dst_ref=target, send_sem=send_sem.at[number],
            recv_sem=recv_sem.at[number], device_id=partner, device_id_type=MESH_IDS,
        )

    def relay(number, first, count, partner):
        part = pl.ds(first, count)
        return make(tiles.at[part], tiles.at[part], number, partner)

    mine = pl.ds(core * 64 + z * 16, 16)
    own_here = pl.ds(spot(z, quarter_id), 4)

    def hop(way, step):
        toward = device_at(x, y, lax.rem(z + (1 if way == 0 else 3), 4), core)
        number = 3 * way + step - 1
        if step == 1:
            return make(low.at[pl.ds(4 * quarter_id, 4)], tiles.at[own_here], number, toward)
        z_from = lax.rem(z + (5 - step if way == 0 else step - 1), 4)
        return relay(number, spot(z_from, quarter_id), 4, toward)

    def can_send(way, step):
        if way == 0:
            return (z < 3) & (z >= step - 1)
        return (z > 0) & (z <= 4 - step)

    def arrives(way, step):
        return z >= step if way == 0 else z <= 3 - step

    def source(way, step):
        return lax.rem(z + (4 - step if way == 0 else step), 4)

    steps = [(way, step) for step in range(1, 4) for way in range(2)]

    def fan(way, step):
        base = 6 + 9 * (3 * way + step - 1)
        z_from = source(way, step)
        return [
            relay(base, spot(z_from, quarters[0]), 4, by_x),
            relay(base + 1, spot(z_from, quarters[0]), 4, by_y),
            relay(base + 2, spot(z_from, quarters[0]), 4, across),
            relay(base + 3, spot(z_from, quarters[1]), 2, by_y),
            relay(base + 4, spot(z_from, quarters[1]), 4, across),
            relay(base + 5, spot(z_from, quarters[2]) + 2, 2, by_x),
            relay(base + 6, spot(z_from, quarters[2]), 4, across),
            relay(base + 7, spot(z_from, quarters[3]), 2, across),
            relay(base + 8, spot(z_from, quarters[3]) + 2, 2, across),
        ]

    load_near.wait()
    convert(4 * quarter_id, 4)
    for way in range(2):
        pl.when(can_send(way, 1))(lambda way=way: hop(way, 1).start())
    for k in range(1, 4):
        far[k - 1].wait()
        convert(4 * ((quarter_id + k) % 4), 4)
    keep_tiles = pltpu.make_async_copy(low, tiles.at[mine], l_sem.at[6])
    keep_tiles.start()
    own_across = make(low, tiles.at[mine], 60, across)
    own_across.start()
    load_flat.wait()

    @pl.loop(0, flat.shape[0])
    def _(j):
        flat_low[j] = flat[j].astype(BF16)

    keep_row = pltpu.make_async_copy(flat_low.at[seat], rows.at[seat], l_sem.at[5])
    keep_row.start()
    row_moves = [
        make(flat_low.at[(seat + k) % 8], rows.at[seat], 60 + k, seats[k - 1])
        for k in range(1, 8)
    ]

    def take(way, step):
        hop(way, step).wait_recv()
        if step < 3:
            pl.when(can_send(way, step + 1))(lambda: hop(way, step + 1).start())
        for copy in fan(way, step)[:3]:
            copy.start()

    def turn(way, step):
        moves = fan(way, step)
        moves[0].wait_recv()
        moves[3].start()
        moves[4].start()
        moves[1].wait_recv()
        moves[5].start()
        moves[6].start()

    def finish(way, step):
        moves = fan(way, step)
        moves[3].wait_recv()
        moves[7].start()
        moves[5].wait_recv()
        moves[8].start()

    def drain(way, step):
        moves = fan(way, step)
        for number in (2, 4, 6, 7, 8):
            moves[number].wait_recv()
        for copy in moves:
            copy.wait_send()

    def each(act, chosen):
        for way, step in chosen:
            pl.when(arrives(way, step))(lambda way=way, step=step: act(way, step))

    each(take, steps[:2])
    each(take, steps[2:4])
    each(turn, steps[:2])
    each(take, steps[4:])
    for copy in row_moves:
        copy.start()
    each(turn, steps[2:4])
    each(finish, steps[:2])
    each(turn, steps[4:])
    each(finish, steps[2:])
    own_across.wait_recv()
    each(drain, steps)
    for way, step in steps:
        pl.when(can_send(way, step))(lambda way=way, step=step: hop(way, step).wait_send())
    for copy in row_moves:
        copy.wait_recv()
        copy.wait_send()
    own_across.wait_send()
    keep_row.wait()
    keep_tiles.wait()


def gather_start(master_tiles, residual):
    capacity, depth, lanes = master_tiles.shape
    count = 68
    return pl.pallas_call(
        gather_kernel,
        name="gather_start",
        out_shape=[
            jax.ShapeDtypeStruct((8 * capacity, depth, lanes), BF16),
            jax.ShapeDtypeStruct(residual.shape, BF16),
        ],
        in_specs=[any_spec()] * 2,
        out_specs=[any_spec()] * 2,
        scratch_shapes=[
            pltpu.VMEM(master_tiles.shape, F32),
            pltpu.VMEM(master_tiles.shape, BF16),
            pltpu.VMEM(residual.shape, F32),
            pltpu.VMEM(residual.shape, BF16),
            pltpu.SemaphoreType.DMA((count,)),
            pltpu.SemaphoreType.DMA((count,)),
            pltpu.SemaphoreType.DMA((7,)),
        ],
        compiler_params=pltpu.CompilerParams(
            collective_id=0, has_side_effects=True, vmem_limit_bytes=VMEM_BYTES
        ),
        cost_estimate=pl.CostEstimate(
            flops=0, bytes_accessed=200 * 2**20, transcendentals=0
        ),
    )(master_tiles, residual)


def reduce_kernel(
    held, upper, norm_part, owned, rows, norm_sum, squares,
    core_in, own, one_in, two_in, z_in, piece, flat, flat_low, norm_in, norm_now, square_in,
    square_now, send_sem, recv_sem, l_sem,
):
    x, y, z, core = place_of_device()
    quarter_id = 2 * y + x
    across = device_at(x, y, z, 1 - core)
    by_x = device_at(1 - x, y, z, core)
    by_y = device_at(x, 1 - y, z, core)
    by_both = device_at(1 - x, 1 - y, z, core)
    plus, minus = core, 1 - core
    first_bit = x * minus + y * plus
    second_bit = y * minus + x * plus
    one = device_at(x + minus * (1 - 2 * x), y + plus * (1 - 2 * y), z, core)
    two = device_at(x + plus * (1 - 2 * x), y + minus * (1 - 2 * y), z, core)
    along_z = [device_at(x, y, (z + k) % 4, core) for k in range(1, 4)]
    seats = seat_partners(x, y, z, core)
    seat = 2 * z + core
    chunks = own.shape[0]
    number = 0
    copies = []

    def move(source, target, partner):
        nonlocal number
        copy = post(source, target, send_sem, recv_sem, number, partner)
        number += 1
        copies.append(copy)
        return copy

    loads = []
    for i in range(chunks):
        copy = pltpu.make_async_copy(
            held.at[pl.ds(32 * i + 16 * core, 16)], own.at[i], l_sem.at[i]
        )
        copy.start()
        loads.append(copy)
    load_flat = pltpu.make_async_copy(upper, flat, l_sem.at[chunks])
    load_flat.start()
    greet(seats + [by_x, by_y, by_both])
    core_moves = [
        move(held.at[pl.ds(32 * i + 16 * (1 - core), 16)], core_in.at[i], across)
        for i in range(chunks)
    ]
    norm_now[0] = norm_part[...]
    norm_moves = [move(norm_now.at[0], norm_in.at[0], across)]
    load_flat.wait()

    @pl.loop(0, flat.shape[0])
    def _(j):
        flat_low[j] = flat[j].astype(BF16)

    for k in range(1, 8):
        move(flat_low.at[(seat + k) % 8], rows.at[seat], seats[k - 1])
    row_moves = copies[-7:]
    keep_row = pltpu.make_async_copy(flat_low.at[seat], rows.at[seat], l_sem.at[chunks + 1])
    keep_row.start()

    def add_in(target, first, incoming, count):
        @pl.loop(0, count)
        def _(j):
            target[first + j] = (
                target[first + j].astype(F32) + incoming[j].astype(F32)
            ).astype(BF16)

    one_moves, two_moves, z_moves, plane_moves, keeps = [], [], [], [], []

    def stage_core(i):
        loads[i].wait()
        core_moves[i].wait_recv()
        add_in(own.at[i], 0, core_in.at[i], 16)
        one_moves.append(
            move(own.at[i, pl.ds(8 * (1 - first_bit), 8)], one_in.at[i], one)
        )

    def stage_one(i):
        one_moves[i].wait_recv()
        add_in(own.at[i], 8 * first_bit, one_in.at[i], 8)
        two_moves.append(
            move(
                own.at[i, pl.ds(8 * first_bit + 4 * (1 - second_bit), 4)], two_in.at[i], two
            )
        )

    def stage_two(i):
        two_moves[i].wait_recv()
        base = 8 * first_bit + 4 * second_bit
        add_in(own.at[i], base, two_in.at[i], 4)
        z_moves.append(
            [
                move(own.at[i, base + (z + k) % 4], z_in.at[i, k - 1], along_z[k - 1])
                for k in range(1, 4)
            ]
        )

    def stage_z(i):
        for copy in z_moves[i]:
            copy.wait_recv()
        total = own[i, 8 * first_bit + 4 * second_bit + z].astype(F32)
        for k in range(3):
            total = total + z_in[i, k].astype(F32)
        piece[i] = total.astype(BF16)
        square_now[0] += jnp.sum((total * total).reshape(-1, 8, total.shape[1]), axis=0)
        here = 4 * quarter_id + i
        for partner in (by_x, by_y, by_both):
            plane_moves.append(move(piece.at[i], owned.at[here], partner))
        keep = pltpu.make_async_copy(piece.at[i], owned.at[here], l_sem.at[chunks + 2 + i])
        keep.start()
        keeps.append(keep)

    def norm_stage(step, partner):
        norm_moves[step].wait_recv()
        norm_now[step + 1] = norm_now[step] + norm_in[step]
        if partner is not None:
            norm_moves.append(move(norm_now.at[step + 1], norm_in.at[step + 1], partner))

    square_now[...] = jnp.zeros_like(square_now)
    stage_core(0)
    stage_core(1)
    norm_stage(0, by_x)
    stage_core(2)
    stage_core(3)
    norm_stage(1, by_y)
    stage_one(0)
    stage_one(1)
    norm_stage(2, None)
    norm_z = [move(norm_now.at[3], norm_in.at[2 + k], along_z[k - 1]) for k in range(1, 4)]
    stage_two(0)
    stage_one(2)
    stage_two(1)
    stage_z(0)
    stage_one(3)
    stage_two(2)
    stage_z(1)
    stage_two(3)
    stage_z(2)
    stage_z(3)

    def in_order(own_value, incoming):
        values = [own_value] + [incoming(k) for k in range(1, 4)]
        total = None
        for place in range(4):
            picked = values[0]
            for k in range(1, 4):
                picked = jnp.where((z + 4 - k) % 4 == place, values[k], picked)
            total = picked if total is None else total + picked
        return total

    square_moves = []

    def square_stage(step, partner):
        square_moves.append(move(square_now.at[step], square_in.at[step], partner))
        square_moves[step].wait_recv()
        square_now[step + 1] = square_now[step] + square_in[step]

    square_stage(0, by_x)
    square_stage(1, by_y)
    square_stage(2, across)
    square_z = [
        move(square_now.at[3], square_in.at[2 + k], along_z[k - 1]) for k in range(1, 4)
    ]
    for copy in norm_z:
        copy.wait_recv()
    norm_sum[...] = in_order(norm_now[3], lambda k: norm_in[2 + k])
    for copy in square_z:
        copy.wait_recv()
    squares[...] = in_order(square_now[3], lambda k: square_in[2 + k])
    for copy in row_moves + plane_moves:
        copy.wait_recv()
    for copy in copies:
        copy.wait_send()
    keep_row.wait()
    for keep in keeps:
        keep.wait()


def reduce_end(held, upper, norm_part):
    slots, depth, lanes = held.shape
    chunks = 4
    count = 4 + 1 + 7 + 4 + 4 + 12 + 12 + 2 + 3 + 3 + 3
    return pl.pallas_call(
        reduce_kernel,
        name="reduce_end",
        out_shape=[
            jax.ShapeDtypeStruct((slots // 8, depth, lanes), BF16),
            jax.ShapeDtypeStruct(upper.shape, BF16),
            jax.ShapeDtypeStruct(norm_part.shape, F32),
            jax.ShapeDtypeStruct((8, lanes), F32),
        ],
        in_specs=[any_spec(), any_spec(), vmem_spec()],
        out_specs=[any_spec(), any_spec(), vmem_spec(), vmem_spec()],
        scratch_shapes=[
            pltpu.VMEM((chunks, 16, depth, lanes), BF16),
            pltpu.VMEM((chunks, 16, depth, lanes), BF16),
            pltpu.VMEM((chunks, 8, depth, lanes), BF16),
            pltpu.VMEM((chunks, 4, depth, lanes), BF16),
            pltpu.VMEM((chunks, 3, depth, lanes), BF16),
            pltpu.VMEM((chunks, depth, lanes), BF16),
            pltpu.VMEM(upper.shape, F32),
            pltpu.VMEM(upper.shape, BF16),
            pltpu.VMEM((6, *norm_part.shape), F32),
            pltpu.VMEM((4, *norm_part.shape), F32),
            pltpu.VMEM((6, 8, lanes), F32),
            pltpu.VMEM((4, 8, lanes), F32),
            pltpu.SemaphoreType.DMA((count,)),
            pltpu.SemaphoreType.DMA((count,)),
            pltpu.SemaphoreType.DMA((2 * chunks + 2,)),
        ],
        compiler_params=pltpu.CompilerParams(
            collective_id=1, has_side_effects=True, vmem_limit_bytes=VMEM_BYTES
        ),
        cost_estimate=pl.CostEstimate(
            flops=0, bytes_accessed=300 * 2**20, transcendentals=0
        ),
    )(held, upper, norm_part)


def local_by_rows(
    residual_in,
    cotangent,
    segments,
    owners,
    master_tiles,
    first_tiles,
    second_tiles,
    norm_params,
    norm_first,
    norm_second,
):
    local_rows, positions, model_width = residual_in.shape
    seq_devices = lax.axis_size("seq")
    seq_index = lax.axis_index("seq")
    length = positions * seq_devices
    tile_total = owners.shape[0]
    capacity, _, tile_width = master_tiles.shape
    quarter = capacity // 4
    pairs = model_width // tile_width
    places = jnp.arange(tile_total, dtype=jnp.int32)
    before = (owners[None, :] == owners[:, None]) & (places[None, :] < places[:, None])
    ranks = jnp.sum(before.astype(jnp.int32), axis=1)
    core, depth_z, part_id = owners % 2, owners // 2, ranks // quarter
    major = jnp.where(core == 0, part_id % 2, part_id // 2)
    minor = jnp.where(core == 0, part_id // 2, part_id % 2)
    weight_table = core * 64 + depth_z * 16 + ranks
    grad_table = (ranks % quarter) * 32 + core * 16 + major * 8 + minor * 4 + depth_z
    seats = jnp.arange(seq_devices, dtype=jnp.int32)
    counts = jnp.sum((owners[None, :] == seats[:, None]).astype(jnp.int32), axis=1)
    tiles, hidden = gather_start(master_tiles, residual_in)
    hidden = hidden.reshape(length, model_width)
    later, tiles = lax.optimization_barrier((cotangent, tiles))
    upper = lax.all_to_all(later.astype(BF16), "seq", split_axis=0, concat_axis=0, tiled=True)
    upper = upper.reshape(length, model_width)
    doc_ids = lax.dynamic_slice_in_dim(segments, seq_index, 1, 0)
    doc_row = doc_ids
    doc_col = jnp.broadcast_to(doc_ids[0][:, None], (length, tile_width))
    begin = jnp.sum((doc_ids < doc_ids[0, ::QUERY, None]).astype(jnp.int32), axis=1) // QUERY
    end = jnp.sum((doc_ids <= doc_ids[0, QUERY - 1 :: QUERY, None]).astype(jnp.int32), axis=1)
    many = (end - begin * QUERY + BLOCK - 1) // BLOCK
    spans = jnp.stack([jnp.minimum(begin, (length - many * BLOCK) // QUERY), many])
    lane = jnp.arange(model_width)[None, :] // (model_width // HEADS)
    which = jnp.arange(8 * pairs)[:, None]
    selector = ((which % 8 < 2) & (lane == 2 * (which // 8) + which % 8)).astype(F32)
    saved = []
    for layer_number in range(LAYERS):
        norms = norm_params[4 * layer_number : 4 * layer_number + 4]
        part = weight_table[48 * layer_number : 48 * layer_number + 48]
        *kept, after = forward_layer(part, spans, norms, doc_row, doc_col, hidden, tiles, pairs)
        saved.append((kept, hidden))
        hidden = after
    residual_out = lax.all_to_all(
        hidden.astype(BF16).reshape(residual_in.shape), "seq", split_axis=0, concat_axis=0, tiled=True
    ).astype(F32)
    norm_parts = [None] * LAYERS
    held = None
    for layer_number in reversed(range(LAYERS)):
        norms = norm_params[4 * layer_number : 4 * layer_number + 4]
        part = weight_table[48 * layer_number : 48 * layer_number + 48]
        aims = grad_table[48 * layer_number : 48 * layer_number + 48]
        kept, below = saved[layer_number]
        upper, held, norm_parts[layer_number] = backward_layer(
            part, aims, spans, counts, norms, doc_row, doc_col, selector, upper, kept, below, tiles, held
        )
    norm_part = jnp.concatenate(norm_parts, axis=0)
    owned, input_grad, norm_sum, squares = reduce_end(
        held, upper.reshape(residual_in.shape), norm_part
    )
    input_grad = input_grad.astype(F32)
    keep = (jnp.arange(capacity) < counts[seq_index])[:, None, None]
    owned = jnp.where(keep, owned.astype(F32), 0.0)
    total = jnp.sqrt(jnp.sum(squares) + jnp.sum(norm_sum * norm_sum))
    factor = 1.0 / jnp.maximum(total, 1.0)
    clipped = owned * factor
    norm_clip = norm_sum * factor
    correction = 1.0 - 0.5**STEP
    new_weight, new_first_rows, new_second_rows = adamw(
        master_tiles, clipped, first_tiles, second_tiles, 0.05, correction
    )
    new_weight = jnp.where(keep, new_weight, 0.0)
    new_first_rows = jnp.where(keep, new_first_rows, 0.0)
    new_second_rows = jnp.where(keep, new_second_rows, 0.0)
    new_norm, new_norm_f, new_norm_s = adamw(
        norm_params, norm_clip, norm_first, norm_second, 0.25, correction
    )
    return (
        residual_out,
        input_grad,
        clipped,
        total[None],
        new_first_rows,
        new_second_rows,
        new_weight,
        new_weight.astype(BF16),
        norm_clip,
        new_norm_f,
        new_norm_s,
        new_norm,
    )


def local(residual_in, *others):
    whole_rows = residual_in.shape[0] == lax.axis_size("seq")
    step = local_by_rows if whole_rows else local_by_heads
    return step(residual_in, *others)


def solution(mesh):
    by_rows = P("rows", "seq", None)
    by_slots = P("seq", None, None)
    return jax.shard_map(
        local,
        mesh=mesh,
        in_specs=(
            by_rows, by_rows, P("rows", None), P(), by_slots, by_slots, by_slots, P(), P(), P(),
        ),
        out_specs=(
            by_rows, by_rows, by_slots, P(), by_slots, by_slots, by_slots, by_slots,
            P(), P(), P(), P(),
        ),
        check_vma=False,
    )
```

```python
import jax
import jax.numpy as jnp
from jax import lax
from jax.experimental import pallas as pl
from jax.experimental.pallas import tpu as pltpu

from jax.sharding import PartitionSpec as P

HEADS = 8
LAYERS = 2
STEP = 5


def norm_layer(values, gain, offset):
    center = values - jnp.mean(values, axis=-1, keepdims=True)
    spread = jnp.mean(center * center, axis=-1, keepdims=True)
    return center * lax.rsqrt(spread + 1e-05) * gain + offset


def matmul(left, right):
    return jnp.dot(left, right, preferred_element_type=jnp.float32)


def left_product(left, right):
    return lax.dot_general(
        left, right, (((0,), (0,)), ((), ())), preferred_element_type=jnp.float32
    )


def right_product(left, right):
    return lax.dot_general(
        left, right, (((1,), (1,)), ((), ())), preferred_element_type=jnp.float32
    )


def assemble(weight_tiles, layer_number):
    first_tile = 48 * layer_number
    model_width = weight_tiles.shape[1]
    qkv_weight = (
        weight_tiles[first_tile : first_tile + 12].transpose(1, 0, 2).reshape(model_width, -1)
    )
    out_weight = (
        weight_tiles[first_tile + 12 : first_tile + 16].transpose(1, 0, 2).reshape(model_width, -1)
    )
    up_weight = (
        weight_tiles[first_tile + 16 : first_tile + 32].transpose(1, 0, 2).reshape(model_width, -1)
    )
    down_block = weight_tiles[first_tile + 32 : first_tile + 48].reshape(4, 4, model_width, -1)
    down_weight = down_block.transpose(0, 2, 1, 3).reshape(4 * model_width, model_width)
    return (qkv_weight, out_weight, up_weight, down_weight)


def split_tiles(qkv_grad, out_grad, up_grad, down_grad, tile_width):
    model_width = qkv_grad.shape[0]
    pieces = [
        qkv_grad.reshape(model_width, -1, tile_width).transpose(1, 0, 2),
        out_grad.reshape(model_width, -1, tile_width).transpose(1, 0, 2),
        up_grad.reshape(model_width, -1, tile_width).transpose(1, 0, 2),
        down_grad.reshape(4, model_width, 4, tile_width)
        .transpose(0, 2, 1, 3)
        .reshape(16, model_width, tile_width),
    ]
    return jnp.concatenate(pieces, axis=0)


def attend_forward(queries, key_rows, value_rows, doc_ids, block_rows, scale):
    length = queries.shape[0]

    def one_block(number):
        first_row = number * block_rows
        query_block = lax.dynamic_slice_in_dim(queries, first_row, block_rows, 0)
        doc_block = lax.dynamic_slice_in_dim(doc_ids, first_row, block_rows, 0)
        same_doc = doc_block[:, None] == doc_ids[None, :]
        scores = jnp.where(same_doc, right_product(query_block, key_rows) * scale, -1e30)
        largest = jnp.max(scores, axis=-1, keepdims=True)
        row_total = jnp.sum(jnp.exp(scores - largest), axis=-1, keepdims=True)
        logsum = largest + jnp.log(row_total)
        weights = jnp.where(same_doc, jnp.exp(scores - logsum), 0.0).astype(jnp.bfloat16)
        return (matmul(weights, value_rows).astype(jnp.bfloat16), logsum[:, 0])

    outputs, logsums = lax.map(one_block, jnp.arange(length // block_rows))
    return (outputs.reshape(length, -1), logsums.reshape(length))


def attend_backward(queries, key_rows, value_rows, doc_ids, logsums, out_grads, block_rows, scale):
    length, head_dim = queries.shape

    def one_block(carry, number):
        key_grad, value_grad = carry
        first_row = number * block_rows
        query_block = lax.dynamic_slice_in_dim(queries, first_row, block_rows, 0)
        doc_block = lax.dynamic_slice_in_dim(doc_ids, first_row, block_rows, 0)
        logsum_block = lax.dynamic_slice_in_dim(logsums, first_row, block_rows, 0)
        grad_block = lax.dynamic_slice_in_dim(out_grads, first_row, block_rows, 0)
        same_doc = doc_block[:, None] == doc_ids[None, :]
        scores = jnp.where(same_doc, right_product(query_block, key_rows) * scale, -1e30)
        probs = jnp.where(same_doc, jnp.exp(scores - logsum_block[:, None]), 0.0)
        prob_grad = right_product(grad_block, value_rows)
        inner_sum = jnp.sum(probs * prob_grad, axis=-1, keepdims=True)
        score_grad = (probs * (prob_grad - inner_sum)).astype(jnp.bfloat16)
        query_grad = matmul(score_grad, key_rows) * scale
        key_grad = key_grad + left_product(score_grad, query_block) * scale
        value_grad = value_grad + left_product(probs.astype(jnp.bfloat16), grad_block)
        return ((key_grad, value_grad), query_grad)

    zeros_block = jnp.zeros((length, head_dim), jnp.float32)
    (key_grad, value_grad), query_grads = lax.scan(
        one_block, (zeros_block, zeros_block), jnp.arange(length // block_rows)
    )
    stacked = jnp.stack([query_grads.reshape(length, head_dim), key_grad, value_grad], axis=1)
    return stacked.astype(jnp.bfloat16)


def adamw(weight, grad, first, second, learn_rate, correction):
    first = 0.5 * first + 0.5 * grad
    second = 0.5 * second + 0.5 * grad * grad
    update = first / correction / (jnp.sqrt(second / correction) + 1e-08)
    return (weight - learn_rate * (update + 0.01 * weight), first, second)


def local_by_heads(
    residual_in,
    cotangent,
    segments,
    owners,
    master_tiles,
    first_tiles,
    second_tiles,
    norm_params,
    norm_first,
    norm_second,
):
    local_rows, positions, model_width = residual_in.shape
    seq_devices = lax.axis_size("seq")
    seq_index = lax.axis_index("seq")
    head_dim = model_width // HEADS
    group_count = seq_devices // HEADS
    group_rows = local_rows // group_count
    length = positions * seq_devices
    block_rows = min(512, length)
    scale = head_dim ** (-0.5)
    tile_total = owners.shape[0]
    capacity = master_tiles.shape[0]
    tile_width = master_tiles.shape[2]
    places = jnp.arange(tile_total, dtype=jnp.int32)
    before = (owners[None, :] == owners[:, None]) & (places[None, :] < places[:, None])
    ranks = jnp.sum(before.astype(jnp.int32), axis=1)
    slot_ids = owners * capacity + ranks
    local_slots = jnp.arange(capacity, dtype=jnp.int32)
    matches = (owners[:, None] == seq_index) & (ranks[:, None] == local_slots[None, :])
    chosen = jnp.sum(jnp.where(matches, places[:, None], 0), axis=0)
    present = jnp.any(matches, axis=0)
    copies = lax.all_gather(master_tiles.astype(jnp.bfloat16), "seq", axis=0, tiled=True)
    weight_tiles = jnp.take(copies, slot_ids, axis=0)
    my_group = seq_index // HEADS
    doc_rows = lax.dynamic_slice_in_dim(segments, my_group * group_rows, group_rows, 0)
    hidden = residual_in.reshape(-1, model_width)
    saved = []
    for layer_number in range(LAYERS):
        qkv_weight, out_weight, up_weight, down_weight = assemble(weight_tiles, layer_number)
        params = norm_params[4 * layer_number : 4 * layer_number + 4]
        normed, first_pull = jax.vjp(norm_layer, hidden, params[0], params[1])
        normed_low = normed.astype(jnp.bfloat16)
        packed = matmul(normed_low, qkv_weight).astype(jnp.bfloat16)
        outgoing = packed.reshape(group_count, group_rows, positions, 3, HEADS, head_dim)
        outgoing = outgoing.transpose(0, 4, 1, 2, 3, 5).reshape(
            seq_devices, group_rows, positions * 3 * head_dim
        )
        arrived = lax.all_to_all(outgoing, "seq", split_axis=0, concat_axis=2, tiled=True).reshape(
            group_rows, length, 3, head_dim
        )

        def forward_item(items):
            return attend_forward(
                items[0][:, 0], items[0][:, 1], items[0][:, 2], items[1], block_rows, scale
            )

        attended, logsums = lax.map(forward_item, (arrived, doc_rows))
        returning = attended.reshape(1, group_rows, seq_devices, positions * head_dim)
        mixed = lax.all_to_all(returning, "seq", split_axis=2, concat_axis=0, tiled=True)
        mixed = (
            mixed.reshape(group_count, HEADS, group_rows, positions, head_dim)
            .transpose(0, 2, 3, 1, 4)
            .reshape(-1, model_width)
        )
        middle = hidden + matmul(mixed, out_weight)
        normed_two, second_pull = jax.vjp(norm_layer, middle, params[2], params[3])
        normed_two_low = normed_two.astype(jnp.bfloat16)
        inner = matmul(normed_two_low, up_weight)
        active = jax.nn.gelu(inner).astype(jnp.bfloat16)
        hidden = middle + matmul(active, down_weight)
        saved.append(
            (
                first_pull,
                normed_low,
                arrived,
                logsums,
                mixed,
                second_pull,
                normed_two_low,
                inner,
                active,
            )
        )
    grad = cotangent.reshape(-1, model_width)
    tile_parts = [None] * LAYERS
    norm_parts = [None] * LAYERS
    for layer_number in reversed(range(LAYERS)):
        (
            first_pull,
            normed_low,
            arrived,
            logsums,
            mixed,
            second_pull,
            normed_two_low,
            inner,
            active,
        ) = saved[layer_number]
        qkv_weight, out_weight, up_weight, down_weight = assemble(weight_tiles, layer_number)
        grad_low = grad.astype(jnp.bfloat16)
        down_grad = left_product(active, grad_low)
        active_grad = right_product(grad_low, down_weight)
        inner_grad = jax.vjp(jax.nn.gelu, inner)[1](active_grad)[0].astype(jnp.bfloat16)
        up_grad = left_product(normed_two_low, inner_grad)
        middle_part, gain_two, offset_two = second_pull(right_product(inner_grad, up_weight))
        middle_grad = grad + middle_part
        middle_low = middle_grad.astype(jnp.bfloat16)
        out_grad = left_product(mixed, middle_low)
        mixed_grad = right_product(middle_low, out_weight).astype(jnp.bfloat16)
        sending = mixed_grad.reshape(group_count, group_rows, positions, HEADS, head_dim)
        sending = sending.transpose(0, 3, 1, 2, 4).reshape(
            seq_devices, group_rows, positions * head_dim
        )
        head_grads = lax.all_to_all(
            sending, "seq", split_axis=0, concat_axis=2, tiled=True
        ).reshape(group_rows, length, head_dim)

        def backward_item(items):
            arrived_row, doc_row, logsum_row, grad_row = items
            return attend_backward(
                arrived_row[:, 0],
                arrived_row[:, 1],
                arrived_row[:, 2],
                doc_row,
                logsum_row,
                grad_row,
                block_rows,
                scale,
            )

        packed_grads = lax.map(backward_item, (arrived, doc_rows, logsums, head_grads))
        coming = lax.all_to_all(
            packed_grads.reshape(1, group_rows, seq_devices, positions * 3 * head_dim),
            "seq",
            split_axis=2,
            concat_axis=0,
            tiled=True,
        )
        qkv_grad = coming.reshape(group_count, HEADS, group_rows, positions, 3, head_dim)
        qkv_grad = qkv_grad.transpose(0, 2, 3, 4, 1, 5).reshape(-1, 3 * model_width)
        qkv_weight_grad = left_product(normed_low, qkv_grad)
        input_part, gain_one, offset_one = first_pull(right_product(qkv_grad, qkv_weight))
        grad = middle_grad + input_part
        tile_parts[layer_number] = split_tiles(
            qkv_weight_grad, out_grad, up_grad, down_grad, tile_width
        )
        norm_parts[layer_number] = jnp.stack([gain_one, offset_one, gain_two, offset_two])
    dense = jnp.concatenate(tile_parts, axis=0)
    norm_part = jnp.concatenate(norm_parts, axis=0)
    piece = lax.psum_scatter(
        dense.reshape(-1, tile_width), ("rows", "seq"), scatter_dimension=0, tiled=True
    )
    squares, norm_sum = lax.psum((jnp.sum(piece * piece), norm_part), ("rows", "seq"))
    summed = (
        lax.all_gather(piece.astype(jnp.bfloat16), ("rows", "seq"), axis=0, tiled=True)
        .astype(piece.dtype)
        .reshape(dense.shape)
    )
    owned = jnp.take(summed, chosen, axis=0)
    keep = present[:, None, None]
    owned = jnp.where(keep, owned, 0.0)
    total = jnp.sqrt(squares + jnp.sum(norm_sum * norm_sum))
    factor = 1.0 / jnp.maximum(total, 1.0)
    clipped = owned * factor
    norm_clip = norm_sum * factor
    correction = 1.0 - 0.5**STEP
    new_weight, new_first_rows, new_second_rows = adamw(
        master_tiles, clipped, first_tiles, second_tiles, 0.05, correction
    )
    new_weight = jnp.where(keep, new_weight, 0.0)
    new_first_rows = jnp.where(keep, new_first_rows, 0.0)
    new_second_rows = jnp.where(keep, new_second_rows, 0.0)
    new_norm, new_norm_f, new_norm_s = adamw(
        norm_params, norm_clip, norm_first, norm_second, 0.25, correction
    )
    return (
        hidden.reshape(local_rows, positions, model_width),
        grad.reshape(local_rows, positions, model_width),
        clipped,
        total[None],
        new_first_rows,
        new_second_rows,
        new_weight,
        new_weight.astype(jnp.bfloat16),
        norm_clip,
        new_norm_f,
        new_norm_s,
        new_norm,
    )


F32 = jnp.float32
BF16 = jnp.bfloat16
BLOCK = 256
DENSE = 1024
QUERY = 128
UNROLL = 4
UNROLL_BACK = 4
VMEM_BYTES = 60 * 1024 * 1024


def dot_nn(left, right):
    return jnp.dot(left, right, preferred_element_type=F32)


def dot_nt(left, right, precision=None):
    return lax.dot_general(
        left, right, (((1,), (1,)), ((), ())), preferred_element_type=F32, precision=precision
    )


def dot_tn(left, right):
    return lax.dot_general(left, right, (((0,), (0,)), ((), ())), preferred_element_type=F32)


def rows_of(number, size=BLOCK):
    return pl.ds(pl.multiple_of(number * size, size), size)


def normalized(values):
    center = values - jnp.mean(values, axis=-1, keepdims=True)
    spread = jnp.mean(center * center, axis=-1, keepdims=True)
    scale = lax.rsqrt(spread + 1e-05)
    return center * scale, scale


GELU_A = 0.7978845608028654
GELU_B = 0.044715


def gelu_value(inner):
    return 0.5 * inner * (1.0 + jnp.tanh(GELU_A * (inner + GELU_B * inner * inner * inner)))


def gelu_both(inner):
    square = inner * inner
    bent = jnp.tanh(inner * (GELU_A + GELU_A * GELU_B * square))
    half = 0.5 + 0.5 * bent
    slope = half + 0.5 * inner * (1.0 - bent * bent) * (GELU_A + 3.0 * GELU_A * GELU_B * square)
    return inner * half, slope


def weight_copy(tiles, table, number, target, column, row, sem):
    depth, width = tiles.shape[1], tiles.shape[2]
    rows = pl.ds(pl.multiple_of(row * depth, depth), depth)
    columns = pl.ds(pl.multiple_of(column * width, width), width)
    return pltpu.make_async_copy(
        tiles.at[table[number]], target.at[rows, columns], sem.at[number]
    )


def weight_group(tiles, table, first, count, per_row, target, sem, act):
    @pl.loop(0, count)
    def _(j):
        copy = weight_copy(
            tiles, table, first + j, target, lax.rem(j, per_row), lax.div(j, per_row), sem
        )
        getattr(copy, act)()


def lane_is_first(shape):
    return lax.broadcasted_iota(jnp.int32, shape, 1) < shape[1] // 2


def stacked(values, lanes_first):
    zero = jnp.zeros_like(values)
    return jnp.concatenate(
        [
            jnp.where(lanes_first, values, zero).astype(BF16),
            jnp.where(lanes_first, zero, values).astype(BF16),
        ],
        axis=0,
    )


def forward_kernel(
    table, spans, norms, doc_row, hidden, tiles,
    below_out, normed_out, packed_out, mixed_out, logsum_out, middle_out, normed_two_out,
    hidden_out,
    w_qkv, w_out, w_up, w_down, flow, normed, packed, mixed, logcol, logsum, middle, normed_two,
    doc_col, w_sem, o_sem,
):
    length, width = hidden.shape
    blocks = length // DENSE
    pairs = mixed.shape[0]
    lanes = mixed.shape[2]
    groups = (
        (0, 12, 12, w_qkv), (12, 4, 4, w_out), (16, 16, 16, w_up), (32, 16, 4, w_down),
    )

    def fetch(layer, group, act):
        first, count, per_row, target = groups[group]
        weight_group(
            tiles, table, 48 * layer + first, count, per_row, target.at[layer], w_sem, act
        )

    for layer in range(LAYERS):
        for group in range(4):
            fetch(layer, group, "start")
    outs = (
        (normed, normed_out), (packed, packed_out), (mixed, mixed_out), (logsum, logsum_out),
        (middle, middle_out), (normed_two, normed_two_out), (flow, below_out),
    )

    def flush(number, layer):
        return pltpu.make_async_copy(outs[number][0], outs[number][1].at[layer], o_sem.at[number])

    def forward_one(layer):
        def again(number):
            pl.when(layer > 0)(lambda: flush(number, layer).wait())

        flush(6, layer).start()
        again(0)
        again(1)
        fetch(layer, 0, "wait")

        @pl.loop(0, blocks)
        def _(number):
            here = rows_of(number, DENSE)
            unit, _ = normalized(flow[here, :])
            low = (unit * norms[pl.ds(4 * layer + 0, 1), :] + norms[pl.ds(4 * layer + 1, 1), :]).astype(BF16)
            normed[here, :] = low
            product = dot_nn(low, w_qkv[layer])
            for j in range(3 * pairs):
                packed[j, here, :] = product[:, j * lanes : (j + 1) * lanes].astype(BF16)

        flush(0, layer).start()
        flush(1, layer).start()
        again(2)
        lane_ids = lax.broadcasted_iota(jnp.int32, (QUERY, lanes), 1)
        first_half = lane_is_first((QUERY, lanes))

        @pl.loop(0, length // QUERY)
        def _(number):
            here = rows_of(number, QUERY)
            low_key = spans[0, number]
            key_count = spans[1, number]
            doc_here = doc_col[here, 0:1]

            def with_keys(many):
                keys_here = pl.ds(pl.multiple_of(low_key * QUERY, QUERY), many * BLOCK)
                same = doc_here == doc_row[0:1, keys_here]
                same = jnp.concatenate([same, same], axis=0)

                def score(pair):
                    heads = stacked(packed[pair, here, :].astype(F32) * 0.125, first_half)
                    return dot_nt(heads, packed[pairs + pair, keys_here, :])

                def settle(scores):
                    scores = jnp.where(same, scores, -1e30)
                    top = jnp.max(scores, axis=-1, keepdims=True)
                    weights = jnp.exp(scores - top)
                    total = jnp.sum(weights, axis=-1, keepdims=True)
                    return weights.astype(BF16), total, top + jnp.log(total)

                def finish(pair, weights, total, logs):
                    result = dot_nn(weights, packed[2 * pairs + pair, keys_here, :]) / total
                    mixed[pair, here, :] = jnp.where(
                        first_half, result[:QUERY], result[QUERY:]
                    ).astype(BF16)
                    old = logcol[here, :]
                    old = jnp.where(lane_ids == 8 * pair, logs[:QUERY], old)
                    logcol[here, :] = jnp.where(lane_ids == 8 * pair + 1, logs[QUERY:], old)

                waiting = None
                ahead = score(0)
                for pair in range(pairs):
                    now = ahead
                    if pair + 1 < pairs:
                        ahead = score(pair + 1)
                    done = settle(now)
                    if waiting is not None:
                        finish(pair - 1, *waiting)
                    waiting = done
                finish(pairs - 1, *waiting)


            for many in range(1, length // BLOCK + 1):
                pl.when(key_count == many)(lambda many=many: with_keys(many))

        flush(2, layer).start()
        turned = logcol[...].T
        again(3)
        for pair in range(pairs):
            logsum[pair, :, :] = turned[8 * pair : 8 * pair + 8, :]
        flush(3, layer).start()
        fetch(layer, 1, "wait")
        fetch(layer, 2, "wait")
        fetch(layer, 3, "wait")
        again(4)
        again(5)
        flush(6, layer).wait()
        chunk = width

        @pl.loop(0, blocks)
        def _(number):
            here = rows_of(number, DENSE)
            side_by_side = jnp.concatenate([mixed[pair, here, :] for pair in range(pairs)], axis=1)
            mid = flow[here, :] + dot_nn(side_by_side, w_out[layer])
            middle[here, :] = mid
            unit, _ = normalized(mid)
            low = (unit * norms[pl.ds(4 * layer + 2, 1), :] + norms[pl.ds(4 * layer + 3, 1), :]).astype(BF16)
            normed_two[here, :] = low
            total = mid
            for c in range(w_up.shape[2] // chunk):
                part = slice(c * chunk, (c + 1) * chunk)
                active = gelu_value(dot_nn(low, w_up[layer, :, part])).astype(BF16)
                total = total + dot_nn(active, w_down[layer, part, :])
            flow[here, :] = total

        flush(4, layer).start()
        flush(5, layer).start()

    flow[...] = hidden[...].astype(F32)
    fill_columns(doc_row, doc_col)

    @pl.loop(0, LAYERS)
    def _(layer):
        forward_one(layer)

    last = pltpu.make_async_copy(normed, hidden_out, o_sem.at[7])
    flush(0, LAYERS - 1).wait()
    normed[...] = flow[...].astype(BF16)
    last.start()
    for number in range(1, 6):
        flush(number, LAYERS - 1).wait()
    last.wait()


def fill_columns(doc_row, doc_col):
    lanes = doc_col.shape[1]

    @pl.loop(0, doc_col.shape[0] // lanes)
    def _(number):
        here = rows_of(number, lanes)
        spread = jnp.broadcast_to(doc_row[0:1, here].astype(F32), (lanes, lanes))
        doc_col[here, :] = spread.T.astype(jnp.int32)


def vmem_spec():
    return pl.BlockSpec(memory_space=pltpu.VMEM)


def any_spec():
    return pl.BlockSpec(memory_space=pl.ANY)


def smem_spec():
    return pl.BlockSpec(memory_space=pltpu.SMEM)


def forward_layers(table, spans, norms, doc_row, hidden, tiles, pairs):
    length, width = hidden.shape
    lanes = tiles.shape[2]
    one = (
        ((length, width), F32),
        ((length, width), BF16),
        ((3 * pairs, length, lanes), BF16),
        ((pairs, length, lanes), BF16),
        ((pairs, 8, length), F32),
        ((length, width), F32),
        ((length, width), BF16),
    )
    shapes = [((LAYERS, *s), d) for s, d in one] + [((length, width), BF16)]
    keep = [pltpu.VMEM(s, d) for s, d in one]
    return pl.pallas_call(
        forward_kernel,
        name="forward_layers",
        out_shape=[jax.ShapeDtypeStruct(s, d) for s, d in shapes],
        in_specs=[smem_spec(), smem_spec()] + [vmem_spec()] * 3 + [any_spec()],
        out_specs=[any_spec()] * len(shapes),
        scratch_shapes=[
            pltpu.VMEM((LAYERS, width, 3 * width), BF16),
            pltpu.VMEM((LAYERS, width, width), BF16),
            pltpu.VMEM((LAYERS, width, 4 * width), BF16),
            pltpu.VMEM((LAYERS, 4 * width, width), BF16),
            *keep[:4],
            pltpu.VMEM((length, lanes), F32),
            *keep[4:],
            pltpu.VMEM((length, lanes), jnp.int32),
            pltpu.SemaphoreType.DMA((48 * LAYERS,)),
            pltpu.SemaphoreType.DMA((8,)),
        ],
        compiler_params=pltpu.CompilerParams(vmem_limit_bytes=VMEM_BYTES),
        cost_estimate=pl.CostEstimate(
            flops=length * width * width * 52, bytes_accessed=40 * 2**20,
            transcendentals=length * length * 8,
        ),
    )(table, spans, norms, doc_row, hidden, tiles)


def backward_kernel(
    table, aims, spans, counts, norms, doc_row, upper_in,
    below_in, normed_in, packed_in, mixed_in, logsum_in, middle_in, normed_two_in, tiles,
    grad_out, tile_grads, norm_grads,
    w_qkv, w_out, w_up, w_down,
    flow, normed, packed, mixed, logsum, middle, normed_two, hidden,
    active, inner_grad, grad_low, mid_grad, mid_low, mixed_grad, delta, packed_grad,
    key_sum, value_sum, staged, blank, doc_col, selector,
    w_sem, i_sem, t_sem, z_sem, o_sem,
):
    length, width = flow.shape
    blocks = length // DENSE
    pairs, lanes = mixed.shape[0], mixed.shape[2]
    groups = (
        (0, 12, 12, w_qkv), (12, 4, 4, w_out), (16, 16, 16, w_up), (32, 16, 4, w_down),
    )
    ins = (
        (normed_two_in, normed_two), (middle_in, middle), (mixed_in, mixed),
        (packed_in, packed), (logsum_in, logsum), (below_in, hidden), (normed_in, normed),
    )

    def load(number, layer):
        return pltpu.make_async_copy(ins[number][0].at[layer], ins[number][1], i_sem.at[number])

    def fetch(group, layer, act):
        first, count, per_row, target = groups[group]
        weight_group(tiles, table, 48 * layer + first, count, per_row, target, w_sem, act)

    def early(layer):
        load(0, layer).start()
        fetch(2, layer, "start")
        fetch(3, layer, "start")
        load(1, layer).start()
        fetch(1, layer, "start")
        load(2, layer).start()

    def late(layer):
        load(3, layer).start()
        load(4, layer).start()

    take = pltpu.make_async_copy(upper_in, grad_low, o_sem.at[0])
    take.start()
    early(LAYERS - 1)
    late(LAYERS - 1)
    fetch(0, LAYERS - 1, "start")
    load(5, LAYERS - 1).start()
    load(6, LAYERS - 1).start()

    def blank_copies(act):
        capacity = tile_grads.shape[0] // counts.shape[0]
        quarter = capacity // 4

        @pl.loop(0, counts.shape[0])
        def _(owner):
            @pl.loop(counts[owner], capacity)
            def _(place):
                core, depth_z, part = lax.rem(owner, 2), lax.div(owner, 2), lax.div(place, quarter)
                low_bit, high_bit = lax.rem(part, 2), lax.div(part, 2)
                major = low_bit + core * (high_bit - low_bit)
                minor = high_bit + core * (low_bit - high_bit)
                index = lax.rem(place, quarter) * 32 + core * 16 + major * 8 + minor * 4 + depth_z
                getattr(
                    pltpu.make_async_copy(blank, tile_grads.at[index], z_sem.at[index]), act
                )()

    blank[...] = jnp.zeros_like(blank)
    blank_copies("start")
    fill_columns(doc_row, doc_col)
    which = lax.broadcasted_iota(jnp.int32, selector.shape, 0)
    lane = lax.broadcasted_iota(jnp.int32, selector.shape, 1)
    head_dim = width // HEADS
    own_head = 2 * lax.div(which, 8) + lax.rem(which, 8)
    fits = (lax.rem(which, 8) < 2) & (lax.div(lane, head_dim) == own_head)
    selector[...] = jnp.where(fits, 1.0, 0.0)
    take.wait()
    flow[...] = grad_low[...].astype(F32)
    chunk = width
    chunks = w_up.shape[1] // chunk

    def send_tile(place, layer):
        return pltpu.make_async_copy(
            staged.at[place], tile_grads.at[aims[48 * layer + place]], t_sem.at[place]
        )

    def settle_tiles(layer):
        @pl.loop(0, 48)
        def _(place):
            send_tile(place, layer).wait()

    def backward_one(layer):
        def norm_back(values, out_grad, gain, gain_row):
            unit, scale = normalized(values)
            sums = (
                jnp.sum(out_grad * unit, axis=0, keepdims=True),
                jnp.sum(out_grad, axis=0, keepdims=True),
            )
            for which in range(LAYERS):

                @pl.when(layer == which)
                def _(which=which):
                    for side in range(2):
                        row = 4 * which + gain_row + side
                        norm_grads[row : row + 1, :] = sums[side]

            turned = out_grad * gain
            average = jnp.mean(turned, axis=-1, keepdims=True)
            along = jnp.mean(turned * unit, axis=-1, keepdims=True)
            return scale * (turned - average - unit * along)

        load(0, layer).wait()
        fetch(2, layer, "wait")
        fetch(3, layer, "wait")
        load(1, layer).wait()
        fetch(1, layer, "wait")
        load(2, layer).wait()

        @pl.loop(0, blocks)
        def _(number):
            here = rows_of(number, DENSE)
            upper = flow[here, :]
            low = upper.astype(BF16)
            grad_low[here, :] = low
            normed_here = normed_two[here, :]
            total = jnp.zeros((DENSE, width), F32)
            for c in range(chunks):
                part = slice(c * chunk, (c + 1) * chunk)
                value, slope = gelu_both(dot_nn(normed_here, w_up[:, part]))
                active[here, part] = value.astype(BF16)
                inner = (slope * dot_nt(low, w_down[part, :])).astype(BF16)
                inner_grad[here, part] = inner
                total = total + dot_nt(inner, w_up[:, part])
            mid = upper + norm_back(middle[here, :], total, norms[pl.ds(4 * layer + 2, 1), :], 2)
            mid_grad[here, :] = mid
            mid_here = mid.astype(BF16)
            mid_low[here, :] = mid_here
            back = dot_nt(mid_here, w_out[...]).astype(BF16)
            for pair in range(pairs):
                mixed_grad[pair, here, :] = back[:, pair * lanes : (pair + 1) * lanes]
            side_by_side = jnp.concatenate([mixed[pair, here, :] for pair in range(pairs)], axis=1)
            both = side_by_side.astype(F32) * back.astype(F32)
            sums = dot_nt(selector[...], both, precision=lax.Precision.HIGHEST)
            for pair in range(pairs):
                delta[pair, :, here] = sums[8 * pair : 8 * pair + 8, :]

        pl.when(layer < LAYERS - 1)(lambda: settle_tiles(layer + 1))

        def emit(block, first):
            for c in range(block.shape[1] // lanes):
                staged[first + c] = block[:, c * lanes : (c + 1) * lanes].astype(BF16)
                send_tile(first + c, layer).start()

        @pl.loop(0, chunks)
        def _(c):
            part = rows_of(c, chunk)
            emit(dot_tn(active[:, part], grad_low[...]), 32 + 4 * c)
            emit(dot_tn(normed_two[...], inner_grad[:, part]), 16 + 4 * c)

        side_by_side = jnp.concatenate([mixed[pair] for pair in range(pairs)], axis=1)
        emit(dot_tn(side_by_side, mid_low[...]), 12)
        pl.when(layer > 0)(lambda: early(layer - 1))
        load(3, layer).wait()
        load(4, layer).wait()
        first_half = lane_is_first((QUERY, lanes))

        key_sum[...] = jnp.zeros_like(key_sum)
        value_sum[...] = jnp.zeros_like(value_sum)

        @pl.loop(0, length // QUERY)
        def _(number):
            here = rows_of(number, QUERY)
            low_key = spans[0, number]
            key_count = spans[1, number]
            doc_here = doc_row[0:1, here]
            doc_here = jnp.concatenate([doc_here, doc_here], axis=1)

            def with_keys(many):
                keys_here = pl.ds(pl.multiple_of(low_key * QUERY, QUERY), many * BLOCK)
                same = doc_col[keys_here, 0:1] == doc_here

                def score(pair):
                    heads = stacked(packed[pair, here, :].astype(F32) * 0.125, first_half)
                    outs = stacked(mixed_grad[pair, here, :].astype(F32), first_half)
                    return (
                        heads,
                        outs,
                        dot_nt(packed[pairs + pair, keys_here, :], heads),
                        dot_nt(packed[2 * pairs + pair, keys_here, :], outs),
                    )

                def settle(pair, heads, outs, scores, from_values):
                    logs = jnp.concatenate([logsum[pair, 0:1, here], logsum[pair, 1:2, here]], axis=1)
                    means = jnp.concatenate([delta[pair, 0:1, here], delta[pair, 1:2, here]], axis=1)
                    weights = jnp.exp(jnp.where(same, scores - logs, -1e30))
                    score_grad = (weights * (from_values - means)).astype(BF16)
                    return heads, outs, weights.astype(BF16), score_grad

                def finish(pair, heads, outs, weights, score_grad):
                    value_sum[pair, keys_here, :] += dot_nn(weights, outs)
                    key_sum[pair, keys_here, :] += dot_nn(score_grad, heads)
                    query_part = dot_tn(score_grad, packed[pairs + pair, keys_here, :]) * 0.125
                    packed_grad[pair, here, :] = jnp.where(
                        first_half, query_part[:QUERY], query_part[QUERY:]
                    ).astype(BF16)

                waiting = None
                ahead = score(0)
                for pair in range(pairs):
                    now = ahead
                    if pair + 1 < pairs:
                        ahead = score(pair + 1)
                    done = settle(pair, *now)
                    if waiting is not None:
                        finish(pair - 1, *waiting)
                    waiting = done
                finish(pairs - 1, *waiting)

            for many in range(1, length // BLOCK + 1):
                pl.when(key_count == many)(lambda many=many: with_keys(many))

        for pair in range(pairs):
            packed_grad[pairs + pair] = key_sum[pair].astype(BF16)
            packed_grad[2 * pairs + pair] = value_sum[pair].astype(BF16)

        pl.when(layer > 0)(lambda: late(layer - 1))
        fetch(0, layer, "wait")
        load(5, layer).wait()
        load(6, layer).wait()

        @pl.loop(0, blocks)
        def _(number):
            here = rows_of(number, DENSE)
            wide = jnp.concatenate([packed_grad[j, here, :] for j in range(3 * pairs)], axis=1)
            total = dot_nt(wide, w_qkv[...])
            flow[here, :] = mid_grad[here, :] + norm_back(
                hidden[here, :], total, norms[pl.ds(4 * layer + 0, 1), :], 0
            )

        @pl.loop(0, 3)
        def _(c):
            wide = jnp.concatenate([packed_grad[pairs * c + j] for j in range(pairs)], axis=1)
            emit(dot_tn(normed[...], wide), 4 * c)

        @pl.when(layer > 0)
        def _():
            fetch(0, layer - 1, "start")
            load(5, layer - 1).start()
            load(6, layer - 1).start()

    @pl.loop(0, LAYERS)
    def _(step):
        backward_one(LAYERS - 1 - step)

    flush = pltpu.make_async_copy(grad_low, grad_out, o_sem.at[0])
    grad_low[...] = flow[...].astype(BF16)
    flush.start()
    settle_tiles(0)
    flush.wait()
    blank_copies("wait")


def backward_layers(
    table, aims, spans, counts, norms, doc_row, upper, saved, tiles
):
    length, width = upper.shape
    lanes = tiles.shape[2]
    pairs = width // lanes
    slots = tiles.shape[0]
    return pl.pallas_call(
        backward_kernel,
        name="backward_layers",
        out_shape=[
            jax.ShapeDtypeStruct((length, width), BF16),
            jax.ShapeDtypeStruct(tiles.shape, BF16),
            jax.ShapeDtypeStruct(norms.shape, F32),
        ],
        in_specs=[smem_spec()] * 4 + [vmem_spec()] * 2 + [any_spec()] * 9,
        out_specs=[any_spec(), any_spec(), vmem_spec()],
        scratch_shapes=[
            pltpu.VMEM((width, 3 * width), BF16),
            pltpu.VMEM((width, width), BF16),
            pltpu.VMEM((width, 4 * width), BF16),
            pltpu.VMEM((4 * width, width), BF16),
            pltpu.VMEM((length, width), F32),
            pltpu.VMEM((length, width), BF16),
            pltpu.VMEM((3 * pairs, length, lanes), BF16),
            pltpu.VMEM((pairs, length, lanes), BF16),
            pltpu.VMEM((pairs, 8, length), F32),
            pltpu.VMEM((length, width), F32),
            pltpu.VMEM((length, width), BF16),
            pltpu.VMEM((length, width), F32),
            pltpu.VMEM((length, 4 * width), BF16),
            pltpu.VMEM((length, 4 * width), BF16),
            pltpu.VMEM((length, width), BF16),
            pltpu.VMEM((length, width), F32),
            pltpu.VMEM((length, width), BF16),
            pltpu.VMEM((pairs, length, lanes), BF16),
            pltpu.VMEM((pairs, 8, length), F32),
            pltpu.VMEM((3 * pairs, length, lanes), BF16),
            pltpu.VMEM((pairs, length, lanes), F32),
            pltpu.VMEM((pairs, length, lanes), F32),
            pltpu.VMEM((48, width, lanes), BF16),
            pltpu.VMEM((width, lanes), BF16),
            pltpu.VMEM((length, lanes), jnp.int32),
            pltpu.VMEM((8 * pairs, width), F32),
            pltpu.SemaphoreType.DMA((48 * LAYERS,)),
            pltpu.SemaphoreType.DMA((7,)),
            pltpu.SemaphoreType.DMA((48,)),
            pltpu.SemaphoreType.DMA((slots,)),
            pltpu.SemaphoreType.DMA((1,)),
        ],
        compiler_params=pltpu.CompilerParams(vmem_limit_bytes=VMEM_BYTES),
        cost_estimate=pl.CostEstimate(
            flops=length * width * width * 120, bytes_accessed=60 * 2**20,
            transcendentals=length * length * 8,
        ),
    )(
        table, aims, spans, counts, norms, doc_row, upper, *saved, tiles
    )


MESH_IDS = pl.DeviceIdType.MESH


def place_of_device():
    row = lax.axis_index("rows")
    seat = lax.axis_index("seq")
    return row % 2, row // 2, seat // 2, seat % 2


def device_at(x, y, z, core):
    return (2 * y + x, 2 * z + core)


def greet(partners):
    barrier = pltpu.get_barrier_semaphore()
    for partner in partners:
        pl.semaphore_signal(barrier, inc=1, device_id=partner, device_id_type=MESH_IDS)
    pl.semaphore_wait(barrier, len(partners))


def seat_partners(x, y, z, core):
    others = []
    for k in range(1, 8):
        seat = (2 * z + core + k) % 8
        others.append((2 * y + x, seat))
    return others


def post(source, target, send_sem, recv_sem, number, partner):
    copy = pltpu.make_async_remote_copy(
        src_ref=source,
        dst_ref=target,
        send_sem=send_sem.at[number],
        recv_sem=recv_sem.at[number],
        device_id=partner,
        device_id_type=MESH_IDS,
    )
    copy.start()
    return copy


def gather_kernel(master, residual, tiles, rows, wide, low, flat, flat_low, send_sem, recv_sem, l_sem):
    x, y, z, core = place_of_device()
    quarter_id = 2 * y + x
    across = device_at(x, y, z, 1 - core)
    by_x = device_at(1 - x, y, z, core)
    by_y = device_at(x, 1 - y, z, core)
    quarters = (quarter_id, 2 * y + (1 - x), 2 * (1 - y) + x, 3 - quarter_id)
    seats = seat_partners(x, y, z, core)
    seat = 2 * z + core
    load_near = pltpu.make_async_copy(
        master.at[pl.ds(4 * quarter_id, 4)], wide.at[pl.ds(4 * quarter_id, 4)], l_sem.at[0]
    )
    load_near.start()
    far = []
    for k in range(1, 4):
        part = pl.ds(4 * ((quarter_id + k) % 4), 4)
        copy = pltpu.make_async_copy(master.at[part], wide.at[part], l_sem.at[1 + k])
        copy.start()
        far.append(copy)
    load_flat = pltpu.make_async_copy(residual, flat, l_sem.at[1])
    load_flat.start()
    greet(seats + [by_x, by_y])

    def spot(z_from, quarter):
        return core * 64 + z_from * 16 + 4 * quarter

    def convert(first, count):
        @pl.loop(0, count)
        def _(j):
            low[first + j] = wide[first + j].astype(BF16)

    def make(source, target, number, partner):
        return pltpu.make_async_remote_copy(
            src_ref=source, dst_ref=target, send_sem=send_sem.at[number],
            recv_sem=recv_sem.at[number], device_id=partner, device_id_type=MESH_IDS,
        )

    def relay(number, first, count, partner):
        part = pl.ds(first, count)
        return make(tiles.at[part], tiles.at[part], number, partner)

    mine = pl.ds(core * 64 + z * 16, 16)
    own_here = pl.ds(spot(z, quarter_id), 4)

    def hop(way, step):
        toward = device_at(x, y, lax.rem(z + (1 if way == 0 else 3), 4), core)
        number = 3 * way + step - 1
        if step == 1:
            return make(low.at[pl.ds(4 * quarter_id, 4)], tiles.at[own_here], number, toward)
        z_from = lax.rem(z + (5 - step if way == 0 else step - 1), 4)
        return relay(number, spot(z_from, quarter_id), 4, toward)

    def can_send(way, step):
        if way == 0:
            return (z < 3) & (z >= step - 1)
        return (z > 0) & (z <= 4 - step)

    def arrives(way, step):
        return z >= step if way == 0 else z <= 3 - step

    def source(way, step):
        return lax.rem(z + (4 - step if way == 0 else step), 4)

    steps = [(way, step) for step in range(1, 4) for way in range(2)]

    def fan(way, step):
        base = 6 + 9 * (3 * way + step - 1)
        z_from = source(way, step)
        return [
            relay(base, spot(z_from, quarters[0]), 4, by_x),
            relay(base + 1, spot(z_from, quarters[0]), 4, by_y),
            relay(base + 2, spot(z_from, quarters[0]), 4, across),
            relay(base + 3, spot(z_from, quarters[1]), 2, by_y),
            relay(base + 4, spot(z_from, quarters[1]), 4, across),
            relay(base + 5, spot(z_from, quarters[2]) + 2, 2, by_x),
            relay(base + 6, spot(z_from, quarters[2]), 4, across),
            relay(base + 7, spot(z_from, quarters[3]), 2, across),
            relay(base + 8, spot(z_from, quarters[3]) + 2, 2, across),
        ]

    load_near.wait()
    convert(4 * quarter_id, 4)
    for way in range(2):
        pl.when(can_send(way, 1))(lambda way=way: hop(way, 1).start())
    for k in range(1, 4):
        far[k - 1].wait()
        convert(4 * ((quarter_id + k) % 4), 4)
    keep_tiles = pltpu.make_async_copy(low, tiles.at[mine], l_sem.at[6])
    keep_tiles.start()
    own_across = make(low, tiles.at[mine], 60, across)
    own_across.start()
    load_flat.wait()

    @pl.loop(0, flat.shape[0])
    def _(j):
        flat_low[j] = flat[j].astype(BF16)

    keep_row = pltpu.make_async_copy(flat_low.at[seat], rows.at[seat], l_sem.at[5])
    keep_row.start()
    row_moves = [
        make(flat_low.at[(seat + k) % 8], rows.at[seat], 60 + k, seats[k - 1])
        for k in range(1, 8)
    ]

    def take(way, step):
        hop(way, step).wait_recv()
        if step < 3:
            pl.when(can_send(way, step + 1))(lambda: hop(way, step + 1).start())
        for copy in fan(way, step)[:3]:
            copy.start()

    def turn(way, step):
        moves = fan(way, step)
        moves[0].wait_recv()
        moves[3].start()
        moves[4].start()
        moves[1].wait_recv()
        moves[5].start()
        moves[6].start()

    def finish(way, step):
        moves = fan(way, step)
        moves[3].wait_recv()
        moves[7].start()
        moves[5].wait_recv()
        moves[8].start()

    def drain(way, step):
        moves = fan(way, step)
        for number in (2, 4, 6, 7, 8):
            moves[number].wait_recv()
        for copy in moves:
            copy.wait_send()

    def each(act, chosen):
        for way, step in chosen:
            pl.when(arrives(way, step))(lambda way=way, step=step: act(way, step))

    each(take, steps[:2])
    each(take, steps[2:4])
    each(turn, steps[:2])
    each(take, steps[4:])
    for copy in row_moves:
        copy.start()
    each(turn, steps[2:4])
    each(finish, steps[:2])
    each(turn, steps[4:])
    each(finish, steps[2:])
    own_across.wait_recv()
    each(drain, steps)
    for way, step in steps:
        pl.when(can_send(way, step))(lambda way=way, step=step: hop(way, step).wait_send())
    for copy in row_moves:
        copy.wait_recv()
        copy.wait_send()
    own_across.wait_send()
    keep_row.wait()
    keep_tiles.wait()


def gather_start(master_tiles, residual):
    capacity, depth, lanes = master_tiles.shape
    count = 68
    return pl.pallas_call(
        gather_kernel,
        name="gather_start",
        out_shape=[
            jax.ShapeDtypeStruct((8 * capacity, depth, lanes), BF16),
            jax.ShapeDtypeStruct(residual.shape, BF16),
        ],
        in_specs=[any_spec()] * 2,
        out_specs=[any_spec()] * 2,
        scratch_shapes=[
            pltpu.VMEM(master_tiles.shape, F32),
            pltpu.VMEM(master_tiles.shape, BF16),
            pltpu.VMEM(residual.shape, F32),
            pltpu.VMEM(residual.shape, BF16),
            pltpu.SemaphoreType.DMA((count,)),
            pltpu.SemaphoreType.DMA((count,)),
            pltpu.SemaphoreType.DMA((7,)),
        ],
        compiler_params=pltpu.CompilerParams(
            collective_id=0, has_side_effects=True, vmem_limit_bytes=VMEM_BYTES
        ),
        cost_estimate=pl.CostEstimate(
            flops=0, bytes_accessed=200 * 2**20, transcendentals=0
        ),
    )(master_tiles, residual)


def reduce_kernel(
    held, upper, norm_part, owned, rows, norm_sum, squares,
    core_in, own, one_in, two_in, z_in, piece, norm_in, norm_now, square_in,
    square_now, send_sem, recv_sem, l_sem,
):
    x, y, z, core = place_of_device()
    quarter_id = 2 * y + x
    across = device_at(x, y, z, 1 - core)
    by_x = device_at(1 - x, y, z, core)
    by_y = device_at(x, 1 - y, z, core)
    by_both = device_at(1 - x, 1 - y, z, core)
    plus, minus = core, 1 - core
    first_bit = x * minus + y * plus
    second_bit = y * minus + x * plus
    one = device_at(x + minus * (1 - 2 * x), y + plus * (1 - 2 * y), z, core)
    two = device_at(x + plus * (1 - 2 * x), y + minus * (1 - 2 * y), z, core)
    along_z = [device_at(x, y, (z + k) % 4, core) for k in range(1, 4)]
    seats = seat_partners(x, y, z, core)
    seat = 2 * z + core
    quarter_x, quarter_y = 2 * y + (1 - x), 2 * (1 - y) + x
    chunks = own.shape[0]
    number = 0
    copies = []

    def move(source, target, partner):
        nonlocal number
        copy = post(source, target, send_sem, recv_sem, number, partner)
        number += 1
        copies.append(copy)
        return copy

    loads = []
    for i in range(chunks):
        copy = pltpu.make_async_copy(
            held.at[pl.ds(32 * i + 16 * core, 16)], own.at[i], l_sem.at[i]
        )
        copy.start()
        loads.append(copy)
    greet(seats + [by_x, by_y, by_both])
    half = own.shape[2] // 2
    parts = [(i, pl.ds(half * side, half)) for i in range(chunks) for side in range(2)]
    core_moves = [
        move(held.at[pl.ds(32 * i + 16 * (1 - core), 16), rows_], core_in.at[i, :, rows_], across)
        for i, rows_ in parts
    ]
    norm_now[0] = norm_part[...]
    norm_moves = [move(norm_now.at[0], norm_in.at[0], across)]
    for k in range(1, 8):
        move(upper.at[(seat + k) % 8], rows.at[seat], seats[k - 1])
    row_moves = copies[-7:]
    keep_row = pltpu.make_async_copy(upper.at[seat], rows.at[seat], l_sem.at[chunks])
    keep_row.start()

    def add_in(target, first, incoming, count, part):
        @pl.loop(0, count)
        def _(j):
            target[first + j, part, :] = (
                target[first + j, part, :].astype(F32) + incoming[j, part, :].astype(F32)
            ).astype(BF16)

    one_moves, two_moves, z_moves, near_moves, corner_moves, keeps = [], [], [], [], [], []

    def stage_core(n):
        i, part = parts[n]
        if n % 2 == 0:
            loads[i].wait()
        core_moves[n].wait_recv()
        add_in(own.at[i], 0, core_in.at[i], 16, part)
        one_moves.append(
            move(
                own.at[i, pl.ds(8 * (1 - first_bit), 8), part], one_in.at[i, :, part], one
            )
        )

    def stage_one(n):
        i, part = parts[n]
        one_moves[n].wait_recv()
        add_in(own.at[i], 8 * first_bit, one_in.at[i], 8, part)
        two_moves.append(
            move(
                own.at[i, pl.ds(8 * first_bit + 4 * (1 - second_bit), 4), part],
                two_in.at[i, :, part],
                two,
            )
        )

    def stage_two(n):
        i, part = parts[n]
        two_moves[n].wait_recv()
        base = 8 * first_bit + 4 * second_bit
        add_in(own.at[i], base, two_in.at[i], 4, part)
        z_moves.append(
            [
                move(
                    own.at[i, base + (z + k) % 4, part], z_in.at[i, k - 1, part], along_z[k - 1]
                )
                for k in range(1, 4)
            ]
        )

    def stage_z(n):
        i, part = parts[n]
        for copy in z_moves[n]:
            copy.wait_recv()
        total = own[i, 8 * first_bit + 4 * second_bit + z, part, :].astype(F32)
        for k in range(3):
            total = total + z_in[i, k, part, :].astype(F32)
        piece[i, part, :] = total.astype(BF16)
        square_now[0] += jnp.sum((total * total).reshape(-1, 8, total.shape[1]), axis=0)
        here = owned.at[4 * quarter_id + i, part]
        near_moves.append(
            [move(piece.at[i, part], here, partner) for partner in (by_x, by_y)]
        )
        if n >= len(parts) - 2:
            corner_moves.append(move(piece.at[i, part], here, by_both))
        keep = pltpu.make_async_copy(piece.at[i, part], here, l_sem.at[chunks + 1 + n])
        keep.start()
        keeps.append(keep)

    def stage_turn(n):
        i, part = parts[n]
        side = n % 2
        near_moves[n][1 - side].wait_recv()
        far_id = quarter_y if side == 0 else quarter_x
        here = owned.at[4 * far_id + i, part]
        corner_moves.append(move(here, here, by_x if side == 0 else by_y))

    def norm_stage(step, partner):
        norm_moves[step].wait_recv()
        norm_now[step + 1] = norm_now[step] + norm_in[step]
        if partner is not None:
            norm_moves.append(move(norm_now.at[step + 1], norm_in.at[step + 1], partner))

    square_now[...] = jnp.zeros_like(square_now)
    for n in range(8):
        stage_core(n)
        if n == 1:
            norm_stage(0, by_x)
        if n == 3:
            norm_stage(1, by_y)
        if n == 5:
            norm_stage(2, None)
    norm_z = [move(norm_now.at[3], norm_in.at[2 + k], along_z[k - 1]) for k in range(1, 4)]
    for n in range(8 + 5):
        if n < 8:
            stage_one(n)
        if 0 <= n - 1 < 8:
            stage_two(n - 1)
        if 0 <= n - 3 < 8:
            stage_z(n - 3)
        if 0 <= n - 5 < 6:
            stage_turn(n - 5)

    def in_order(own_value, incoming):
        values = [own_value] + [incoming(k) for k in range(1, 4)]
        total = None
        for place in range(4):
            picked = values[0]
            for k in range(1, 4):
                picked = jnp.where((z + 4 - k) % 4 == place, values[k], picked)
            total = picked if total is None else total + picked
        return total

    square_moves = []

    def square_stage(step, partner):
        square_moves.append(move(square_now.at[step], square_in.at[step], partner))
        square_moves[step].wait_recv()
        square_now[step + 1] = square_now[step] + square_in[step]

    square_stage(0, by_x)
    square_stage(1, by_y)
    square_stage(2, across)
    square_z = [
        move(square_now.at[3], square_in.at[2 + k], along_z[k - 1]) for k in range(1, 4)
    ]
    for copy in norm_z:
        copy.wait_recv()
    norm_sum[...] = in_order(norm_now[3], lambda k: norm_in[2 + k])
    for copy in square_z:
        copy.wait_recv()
    squares[...] = in_order(square_now[3], lambda k: square_in[2 + k])
    straight = [near_moves[n][n % 2] for n in range(6)] + near_moves[6] + near_moves[7]
    for copy in row_moves + straight + corner_moves:
        copy.wait_recv()
    for copy in copies:
        copy.wait_send()
    keep_row.wait()
    for keep in keeps:
        keep.wait()


def reduce_end(held, upper, norm_part):
    slots, depth, lanes = held.shape
    chunks = 4
    count = 8 + 1 + 7 + 8 + 8 + 24 + 24 + 2 + 3 + 3 + 3
    return pl.pallas_call(
        reduce_kernel,
        name="reduce_end",
        out_shape=[
            jax.ShapeDtypeStruct((slots // 8, depth, lanes), BF16),
            jax.ShapeDtypeStruct(upper.shape, BF16),
            jax.ShapeDtypeStruct(norm_part.shape, F32),
            jax.ShapeDtypeStruct((8, lanes), F32),
        ],
        in_specs=[any_spec(), any_spec(), vmem_spec()],
        out_specs=[any_spec(), any_spec(), vmem_spec(), vmem_spec()],
        scratch_shapes=[
            pltpu.VMEM((chunks, 16, depth, lanes), BF16),
            pltpu.VMEM((chunks, 16, depth, lanes), BF16),
            pltpu.VMEM((chunks, 8, depth, lanes), BF16),
            pltpu.VMEM((chunks, 4, depth, lanes), BF16),
            pltpu.VMEM((chunks, 3, depth, lanes), BF16),
            pltpu.VMEM((chunks, depth, lanes), BF16),
            pltpu.VMEM((6, *norm_part.shape), F32),
            pltpu.VMEM((4, *norm_part.shape), F32),
            pltpu.VMEM((6, 8, lanes), F32),
            pltpu.VMEM((4, 8, lanes), F32),
            pltpu.SemaphoreType.DMA((count,)),
            pltpu.SemaphoreType.DMA((count,)),
            pltpu.SemaphoreType.DMA((3 * chunks + 1,)),
        ],
        compiler_params=pltpu.CompilerParams(
            collective_id=1, has_side_effects=True, vmem_limit_bytes=40 * 2**20
        ),
        cost_estimate=pl.CostEstimate(
            flops=0, bytes_accessed=300 * 2**20, transcendentals=0
        ),
    )(held, upper, norm_part)


def finish_kernel(
    counts, owned, master, first, second, grad_rows, out_rows, squares, norm_sum, norm_params,
    norm_first, norm_second,
    clip_out, first_out, second_out, master_out, copy_out, grad_rows_out, out_rows_out,
    total_out, norm_clip_out, norm_first_out, norm_second_out, norm_params_out,
    clip, new_first, new_second, new_master, new_copy, wide_grad, wide_out, o_sem,
):
    norms = norm_sum[...]
    total = jnp.sqrt(jnp.sum(squares[...]) + jnp.sum(norms * norms))
    factor = 1.0 / jnp.maximum(total, 1.0)
    correction = 1.0 - 0.5**STEP

    def step(weight, grad, low, high, rate):
        low = 0.5 * low + 0.5 * grad
        high = 0.5 * high + 0.5 * grad * grad
        update = low / correction / (jnp.sqrt(high / correction) + 1e-08)
        return weight - rate * (update + 0.01 * weight), low, high

    outs = (
        (clip, clip_out), (new_first, first_out), (new_second, second_out),
        (new_master, master_out), (new_copy, copy_out),
    )
    capacity = master.shape[0]

    def send(number, place):
        return pltpu.make_async_copy(
            outs[number][0].at[place], outs[number][1].at[place],
            o_sem.at[number * capacity + place],
        )

    count = counts[lax.axis_index("seq")]

    @pl.loop(0, capacity)
    def _(place):
        keep = (lax.broadcast(place, clip.shape[1:])) < count
        grad = jnp.where(keep, owned[place].astype(F32), 0.0) * factor
        weight, low, high = step(master[place], grad, first[place], second[place], 0.05)
        weight = jnp.where(keep, weight, 0.0)
        clip[place] = grad
        new_first[place] = jnp.where(keep, low, 0.0)
        new_second[place] = jnp.where(keep, high, 0.0)
        new_master[place] = weight
        new_copy[place] = weight.astype(BF16)
        for number in range(len(outs)):
            send(number, place).start()

    moves = []
    for number, (low, wide, target) in enumerate(
        ((grad_rows, wide_grad, grad_rows_out), (out_rows, wide_out, out_rows_out))
    ):

        @pl.loop(0, low.shape[0])
        def _(j, low=low, wide=wide):
            wide[j] = low[j].astype(F32)

        moves.append(pltpu.make_async_copy(wide, target, o_sem.at[5 * capacity + number]))
        moves[-1].start()
    clipped = norms * factor
    weight, low, high = step(norm_params[...], clipped, norm_first[...], norm_second[...], 0.25)
    total_out[...] = jnp.broadcast_to(total, total_out.shape)
    norm_clip_out[...] = clipped
    norm_first_out[...] = low
    norm_second_out[...] = high
    norm_params_out[...] = weight

    @pl.loop(0, capacity)
    def _(place):
        for number in range(len(outs)):
            send(number, place).wait()

    for move in moves:
        move.wait()


def finish_step(
    counts, owned, master, first, second, grad_rows, out_rows, squares, norm_sum, norm_params,
    norm_first, norm_second,
):
    tiles = jax.ShapeDtypeStruct(master.shape, F32)
    rows = jax.ShapeDtypeStruct(grad_rows.shape, F32)
    norms = jax.ShapeDtypeStruct(norm_params.shape, F32)
    return pl.pallas_call(
        finish_kernel,
        name="finish_step",
        out_shape=[
            tiles, tiles, tiles, tiles, jax.ShapeDtypeStruct(master.shape, BF16), rows, rows,
            jax.ShapeDtypeStruct((1, 128), F32), norms, norms, norms, norms,
        ],
        in_specs=[smem_spec()] + [vmem_spec()] * 11,
        out_specs=[any_spec()] * 7 + [vmem_spec()] * 5,
        scratch_shapes=[pltpu.VMEM(master.shape, F32)] * 4
        + [pltpu.VMEM(master.shape, BF16)]
        + [pltpu.VMEM(grad_rows.shape, F32)] * 2
        + [pltpu.SemaphoreType.DMA((5 * master.shape[0] + 2,))],
        compiler_params=pltpu.CompilerParams(vmem_limit_bytes=44 * 2**20),
        cost_estimate=pl.CostEstimate(
            flops=0, bytes_accessed=40 * 2**20, transcendentals=0
        ),
    )(
        counts, owned, master, first, second, grad_rows, out_rows, squares, norm_sum, norm_params,
        norm_first, norm_second,
    )


def local_by_rows(
    residual_in,
    cotangent,
    segments,
    owners,
    master_tiles,
    first_tiles,
    second_tiles,
    norm_params,
    norm_first,
    norm_second,
):
    local_rows, positions, model_width = residual_in.shape
    seq_devices = lax.axis_size("seq")
    seq_index = lax.axis_index("seq")
    length = positions * seq_devices
    tile_total = owners.shape[0]
    capacity, _, tile_width = master_tiles.shape
    quarter = capacity // 4
    pairs = model_width // tile_width
    places = jnp.arange(tile_total, dtype=jnp.int32)
    before = (owners[None, :] == owners[:, None]) & (places[None, :] < places[:, None])
    ranks = jnp.sum(before.astype(jnp.int32), axis=1)
    core, depth_z, part_id = owners % 2, owners // 2, ranks // quarter
    major = jnp.where(core == 0, part_id % 2, part_id // 2)
    minor = jnp.where(core == 0, part_id // 2, part_id % 2)
    weight_table = core * 64 + depth_z * 16 + ranks
    grad_table = (ranks % quarter) * 32 + core * 16 + major * 8 + minor * 4 + depth_z
    seats = jnp.arange(seq_devices, dtype=jnp.int32)
    counts = jnp.sum((owners[None, :] == seats[:, None]).astype(jnp.int32), axis=1)
    tiles, hidden = gather_start(master_tiles, residual_in)
    hidden = hidden.reshape(length, model_width)
    later, tiles = lax.optimization_barrier((cotangent, tiles))
    upper = lax.all_to_all(later.astype(BF16), "seq", split_axis=0, concat_axis=0, tiled=True)
    upper = upper.reshape(length, model_width)
    doc_ids = lax.dynamic_slice_in_dim(segments, seq_index, 1, 0)
    doc_row = doc_ids
    begin = jnp.sum((doc_ids < doc_ids[0, ::QUERY, None]).astype(jnp.int32), axis=1) // QUERY
    end = jnp.sum((doc_ids <= doc_ids[0, QUERY - 1 :: QUERY, None]).astype(jnp.int32), axis=1)
    many = (end - begin * QUERY + BLOCK - 1) // BLOCK
    spans = jnp.stack([jnp.minimum(begin, (length - many * BLOCK) // QUERY), many])
    *saved, after = forward_layers(
        weight_table, spans, norm_params, doc_row, hidden, tiles, pairs
    )
    out_rows = lax.all_to_all(
        after.reshape(residual_in.shape), "seq", split_axis=0, concat_axis=0, tiled=True
    )
    lower, held, norm_part = backward_layers(
        weight_table, grad_table, spans, counts, norm_params, doc_row, upper, saved, tiles,
    )
    owned, grad_rows, norm_sum, squares = reduce_end(
        held, lower.reshape(residual_in.shape), norm_part
    )
    (
        clipped, new_first, new_second, new_weight, new_copies, input_grad, residual_out,
        total, norm_clip, new_norm_f, new_norm_s, new_norm,
    ) = finish_step(
        counts, owned, master_tiles, first_tiles, second_tiles, grad_rows, out_rows, squares,
        norm_sum, norm_params, norm_first, norm_second,
    )
    return (
        residual_out,
        input_grad,
        clipped,
        total[0, :1],
        new_first,
        new_second,
        new_weight,
        new_copies,
        norm_clip,
        new_norm_f,
        new_norm_s,
        new_norm,
    )


def local(residual_in, *others):
    whole_rows = residual_in.shape[0] == lax.axis_size("seq")
    step = local_by_rows if whole_rows else local_by_heads
    return step(residual_in, *others)


def solution(mesh):
    by_rows = P("rows", "seq", None)
    by_slots = P("seq", None, None)
    return jax.shard_map(
        local,
        mesh=mesh,
        in_specs=(
            by_rows, by_rows, P("rows", None), P(), by_slots, by_slots, by_slots, P(), P(), P(),
        ),
        out_specs=(
            by_rows, by_rows, by_slots, P(), by_slots, by_slots, by_slots, by_slots,
            P(), P(), P(), P(),
        ),
        check_vma=False,
    )
```

```python
import jax
import jax.numpy as jnp
from jax import lax
from jax.experimental import pallas as pl
from jax.experimental.pallas import tpu as pltpu

from jax.sharding import PartitionSpec as P

HEADS = 8
LAYERS = 2
STEP = 5


def norm_layer(values, gain, offset):
    center = values - jnp.mean(values, axis=-1, keepdims=True)
    spread = jnp.mean(center * center, axis=-1, keepdims=True)
    return center * lax.rsqrt(spread + 1e-05) * gain + offset


def matmul(left, right):
    return jnp.dot(left, right, preferred_element_type=jnp.float32)


def left_product(left, right):
    return lax.dot_general(
        left, right, (((0,), (0,)), ((), ())), preferred_element_type=jnp.float32
    )


def right_product(left, right):
    return lax.dot_general(
        left, right, (((1,), (1,)), ((), ())), preferred_element_type=jnp.float32
    )


def assemble(weight_tiles, layer_number):
    first_tile = 48 * layer_number
    model_width = weight_tiles.shape[1]
    qkv_weight = (
        weight_tiles[first_tile : first_tile + 12].transpose(1, 0, 2).reshape(model_width, -1)
    )
    out_weight = (
        weight_tiles[first_tile + 12 : first_tile + 16].transpose(1, 0, 2).reshape(model_width, -1)
    )
    up_weight = (
        weight_tiles[first_tile + 16 : first_tile + 32].transpose(1, 0, 2).reshape(model_width, -1)
    )
    down_block = weight_tiles[first_tile + 32 : first_tile + 48].reshape(4, 4, model_width, -1)
    down_weight = down_block.transpose(0, 2, 1, 3).reshape(4 * model_width, model_width)
    return (qkv_weight, out_weight, up_weight, down_weight)


def split_tiles(qkv_grad, out_grad, up_grad, down_grad, tile_width):
    model_width = qkv_grad.shape[0]
    pieces = [
        qkv_grad.reshape(model_width, -1, tile_width).transpose(1, 0, 2),
        out_grad.reshape(model_width, -1, tile_width).transpose(1, 0, 2),
        up_grad.reshape(model_width, -1, tile_width).transpose(1, 0, 2),
        down_grad.reshape(4, model_width, 4, tile_width)
        .transpose(0, 2, 1, 3)
        .reshape(16, model_width, tile_width),
    ]
    return jnp.concatenate(pieces, axis=0)


def attend_forward(queries, key_rows, value_rows, doc_ids, block_rows, scale):
    length = queries.shape[0]

    def one_block(number):
        first_row = number * block_rows
        query_block = lax.dynamic_slice_in_dim(queries, first_row, block_rows, 0)
        doc_block = lax.dynamic_slice_in_dim(doc_ids, first_row, block_rows, 0)
        same_doc = doc_block[:, None] == doc_ids[None, :]
        scores = jnp.where(same_doc, right_product(query_block, key_rows) * scale, -1e30)
        largest = jnp.max(scores, axis=-1, keepdims=True)
        row_total = jnp.sum(jnp.exp(scores - largest), axis=-1, keepdims=True)
        logsum = largest + jnp.log(row_total)
        weights = jnp.where(same_doc, jnp.exp(scores - logsum), 0.0).astype(jnp.bfloat16)
        return (matmul(weights, value_rows).astype(jnp.bfloat16), logsum[:, 0])

    outputs, logsums = lax.map(one_block, jnp.arange(length // block_rows))
    return (outputs.reshape(length, -1), logsums.reshape(length))


def attend_backward(queries, key_rows, value_rows, doc_ids, logsums, out_grads, block_rows, scale):
    length, head_dim = queries.shape

    def one_block(carry, number):
        key_grad, value_grad = carry
        first_row = number * block_rows
        query_block = lax.dynamic_slice_in_dim(queries, first_row, block_rows, 0)
        doc_block = lax.dynamic_slice_in_dim(doc_ids, first_row, block_rows, 0)
        logsum_block = lax.dynamic_slice_in_dim(logsums, first_row, block_rows, 0)
        grad_block = lax.dynamic_slice_in_dim(out_grads, first_row, block_rows, 0)
        same_doc = doc_block[:, None] == doc_ids[None, :]
        scores = jnp.where(same_doc, right_product(query_block, key_rows) * scale, -1e30)
        probs = jnp.where(same_doc, jnp.exp(scores - logsum_block[:, None]), 0.0)
        prob_grad = right_product(grad_block, value_rows)
        inner_sum = jnp.sum(probs * prob_grad, axis=-1, keepdims=True)
        score_grad = (probs * (prob_grad - inner_sum)).astype(jnp.bfloat16)
        query_grad = matmul(score_grad, key_rows) * scale
        key_grad = key_grad + left_product(score_grad, query_block) * scale
        value_grad = value_grad + left_product(probs.astype(jnp.bfloat16), grad_block)
        return ((key_grad, value_grad), query_grad)

    zeros_block = jnp.zeros((length, head_dim), jnp.float32)
    (key_grad, value_grad), query_grads = lax.scan(
        one_block, (zeros_block, zeros_block), jnp.arange(length // block_rows)
    )
    stacked = jnp.stack([query_grads.reshape(length, head_dim), key_grad, value_grad], axis=1)
    return stacked.astype(jnp.bfloat16)


def adamw(weight, grad, first, second, learn_rate, correction):
    first = 0.5 * first + 0.5 * grad
    second = 0.5 * second + 0.5 * grad * grad
    update = first / correction / (jnp.sqrt(second / correction) + 1e-08)
    return (weight - learn_rate * (update + 0.01 * weight), first, second)


def local_by_heads(
    residual_in,
    cotangent,
    segments,
    owners,
    master_tiles,
    first_tiles,
    second_tiles,
    norm_params,
    norm_first,
    norm_second,
):
    local_rows, positions, model_width = residual_in.shape
    seq_devices = lax.axis_size("seq")
    seq_index = lax.axis_index("seq")
    head_dim = model_width // HEADS
    group_count = seq_devices // HEADS
    group_rows = local_rows // group_count
    length = positions * seq_devices
    block_rows = min(512, length)
    scale = head_dim ** (-0.5)
    tile_total = owners.shape[0]
    capacity = master_tiles.shape[0]
    tile_width = master_tiles.shape[2]
    places = jnp.arange(tile_total, dtype=jnp.int32)
    before = (owners[None, :] == owners[:, None]) & (places[None, :] < places[:, None])
    ranks = jnp.sum(before.astype(jnp.int32), axis=1)
    slot_ids = owners * capacity + ranks
    local_slots = jnp.arange(capacity, dtype=jnp.int32)
    matches = (owners[:, None] == seq_index) & (ranks[:, None] == local_slots[None, :])
    chosen = jnp.sum(jnp.where(matches, places[:, None], 0), axis=0)
    present = jnp.any(matches, axis=0)
    copies = lax.all_gather(master_tiles.astype(jnp.bfloat16), "seq", axis=0, tiled=True)
    weight_tiles = jnp.take(copies, slot_ids, axis=0)
    my_group = seq_index // HEADS
    doc_rows = lax.dynamic_slice_in_dim(segments, my_group * group_rows, group_rows, 0)
    hidden = residual_in.reshape(-1, model_width)
    saved = []
    for layer_number in range(LAYERS):
        qkv_weight, out_weight, up_weight, down_weight = assemble(weight_tiles, layer_number)
        params = norm_params[4 * layer_number : 4 * layer_number + 4]
        normed, first_pull = jax.vjp(norm_layer, hidden, params[0], params[1])
        normed_low = normed.astype(jnp.bfloat16)
        packed = matmul(normed_low, qkv_weight).astype(jnp.bfloat16)
        outgoing = packed.reshape(group_count, group_rows, positions, 3, HEADS, head_dim)
        outgoing = outgoing.transpose(0, 4, 1, 2, 3, 5).reshape(
            seq_devices, group_rows, positions * 3 * head_dim
        )
        arrived = lax.all_to_all(outgoing, "seq", split_axis=0, concat_axis=2, tiled=True).reshape(
            group_rows, length, 3, head_dim
        )

        def forward_item(items):
            return attend_forward(
                items[0][:, 0], items[0][:, 1], items[0][:, 2], items[1], block_rows, scale
            )

        attended, logsums = lax.map(forward_item, (arrived, doc_rows))
        returning = attended.reshape(1, group_rows, seq_devices, positions * head_dim)
        mixed = lax.all_to_all(returning, "seq", split_axis=2, concat_axis=0, tiled=True)
        mixed = (
            mixed.reshape(group_count, HEADS, group_rows, positions, head_dim)
            .transpose(0, 2, 3, 1, 4)
            .reshape(-1, model_width)
        )
        middle = hidden + matmul(mixed, out_weight)
        normed_two, second_pull = jax.vjp(norm_layer, middle, params[2], params[3])
        normed_two_low = normed_two.astype(jnp.bfloat16)
        inner = matmul(normed_two_low, up_weight)
        active = jax.nn.gelu(inner).astype(jnp.bfloat16)
        hidden = middle + matmul(active, down_weight)
        saved.append(
            (
                first_pull,
                normed_low,
                arrived,
                logsums,
                mixed,
                second_pull,
                normed_two_low,
                inner,
                active,
            )
        )
    grad = cotangent.reshape(-1, model_width)
    tile_parts = [None] * LAYERS
    norm_parts = [None] * LAYERS
    for layer_number in reversed(range(LAYERS)):
        (
            first_pull,
            normed_low,
            arrived,
            logsums,
            mixed,
            second_pull,
            normed_two_low,
            inner,
            active,
        ) = saved[layer_number]
        qkv_weight, out_weight, up_weight, down_weight = assemble(weight_tiles, layer_number)
        grad_low = grad.astype(jnp.bfloat16)
        down_grad = left_product(active, grad_low)
        active_grad = right_product(grad_low, down_weight)
        inner_grad = jax.vjp(jax.nn.gelu, inner)[1](active_grad)[0].astype(jnp.bfloat16)
        up_grad = left_product(normed_two_low, inner_grad)
        middle_part, gain_two, offset_two = second_pull(right_product(inner_grad, up_weight))
        middle_grad = grad + middle_part
        middle_low = middle_grad.astype(jnp.bfloat16)
        out_grad = left_product(mixed, middle_low)
        mixed_grad = right_product(middle_low, out_weight).astype(jnp.bfloat16)
        sending = mixed_grad.reshape(group_count, group_rows, positions, HEADS, head_dim)
        sending = sending.transpose(0, 3, 1, 2, 4).reshape(
            seq_devices, group_rows, positions * head_dim
        )
        head_grads = lax.all_to_all(
            sending, "seq", split_axis=0, concat_axis=2, tiled=True
        ).reshape(group_rows, length, head_dim)

        def backward_item(items):
            arrived_row, doc_row, logsum_row, grad_row = items
            return attend_backward(
                arrived_row[:, 0],
                arrived_row[:, 1],
                arrived_row[:, 2],
                doc_row,
                logsum_row,
                grad_row,
                block_rows,
                scale,
            )

        packed_grads = lax.map(backward_item, (arrived, doc_rows, logsums, head_grads))
        coming = lax.all_to_all(
            packed_grads.reshape(1, group_rows, seq_devices, positions * 3 * head_dim),
            "seq",
            split_axis=2,
            concat_axis=0,
            tiled=True,
        )
        qkv_grad = coming.reshape(group_count, HEADS, group_rows, positions, 3, head_dim)
        qkv_grad = qkv_grad.transpose(0, 2, 3, 4, 1, 5).reshape(-1, 3 * model_width)
        qkv_weight_grad = left_product(normed_low, qkv_grad)
        input_part, gain_one, offset_one = first_pull(right_product(qkv_grad, qkv_weight))
        grad = middle_grad + input_part
        tile_parts[layer_number] = split_tiles(
            qkv_weight_grad, out_grad, up_grad, down_grad, tile_width
        )
        norm_parts[layer_number] = jnp.stack([gain_one, offset_one, gain_two, offset_two])
    dense = jnp.concatenate(tile_parts, axis=0)
    norm_part = jnp.concatenate(norm_parts, axis=0)
    piece = lax.psum_scatter(
        dense.reshape(-1, tile_width), ("rows", "seq"), scatter_dimension=0, tiled=True
    )
    squares, norm_sum = lax.psum((jnp.sum(piece * piece), norm_part), ("rows", "seq"))
    summed = (
        lax.all_gather(piece.astype(jnp.bfloat16), ("rows", "seq"), axis=0, tiled=True)
        .astype(piece.dtype)
        .reshape(dense.shape)
    )
    owned = jnp.take(summed, chosen, axis=0)
    keep = present[:, None, None]
    owned = jnp.where(keep, owned, 0.0)
    total = jnp.sqrt(squares + jnp.sum(norm_sum * norm_sum))
    factor = 1.0 / jnp.maximum(total, 1.0)
    clipped = owned * factor
    norm_clip = norm_sum * factor
    correction = 1.0 - 0.5**STEP
    new_weight, new_first_rows, new_second_rows = adamw(
        master_tiles, clipped, first_tiles, second_tiles, 0.05, correction
    )
    new_weight = jnp.where(keep, new_weight, 0.0)
    new_first_rows = jnp.where(keep, new_first_rows, 0.0)
    new_second_rows = jnp.where(keep, new_second_rows, 0.0)
    new_norm, new_norm_f, new_norm_s = adamw(
        norm_params, norm_clip, norm_first, norm_second, 0.25, correction
    )
    return (
        hidden.reshape(local_rows, positions, model_width),
        grad.reshape(local_rows, positions, model_width),
        clipped,
        total[None],
        new_first_rows,
        new_second_rows,
        new_weight,
        new_weight.astype(jnp.bfloat16),
        norm_clip,
        new_norm_f,
        new_norm_s,
        new_norm,
    )


F32 = jnp.float32
BF16 = jnp.bfloat16
BLOCK = 256
DENSE = 512
DENSE_BACK = 512
QUERY = 128
UNROLL = 4
UNROLL_BACK = 4
VMEM_BYTES = 60 * 1024 * 1024


def dot_nn(left, right):
    return jnp.dot(left, right, preferred_element_type=F32)


def dot_nt(left, right, precision=None):
    return lax.dot_general(
        left, right, (((1,), (1,)), ((), ())), preferred_element_type=F32, precision=precision
    )


def dot_tn(left, right):
    return lax.dot_general(left, right, (((0,), (0,)), ((), ())), preferred_element_type=F32)


def rows_of(number, size=BLOCK):
    return pl.ds(pl.multiple_of(number * size, size), size)


def normalized(values):
    center = values - jnp.mean(values, axis=-1, keepdims=True)
    spread = jnp.mean(center * center, axis=-1, keepdims=True)
    scale = lax.rsqrt(spread + 1e-05)
    return center * scale, scale


GELU_A = 0.7978845608028654
GELU_B = 0.044715


def gelu_value(inner):
    return 0.5 * inner * (1.0 + jnp.tanh(GELU_A * (inner + GELU_B * inner * inner * inner)))


def gelu_both(inner):
    square = inner * inner
    bent = jnp.tanh(inner * (GELU_A + GELU_A * GELU_B * square))
    half = 0.5 + 0.5 * bent
    slope = half + 0.5 * inner * (1.0 - bent * bent) * (GELU_A + 3.0 * GELU_A * GELU_B * square)
    return inner * half, slope


def weight_copy(tiles, table, number, target, column, row, sem):
    depth, width = tiles.shape[1], tiles.shape[2]
    rows = pl.ds(pl.multiple_of(row * depth, depth), depth)
    columns = pl.ds(pl.multiple_of(column * width, width), width)
    return pltpu.make_async_copy(
        tiles.at[table[number]], target.at[rows, columns], sem.at[number]
    )


def weight_group(tiles, table, first, count, per_row, target, sem, act):
    @pl.loop(0, count)
    def _(j):
        copy = weight_copy(
            tiles, table, first + j, target, lax.rem(j, per_row), lax.div(j, per_row), sem
        )
        getattr(copy, act)()


def lane_is_first(shape):
    return lax.broadcasted_iota(jnp.int32, shape, 1) < shape[1] // 2


def stacked(values, lanes_first):
    zero = jnp.zeros_like(values)
    return jnp.concatenate(
        [
            jnp.where(lanes_first, values, zero).astype(BF16),
            jnp.where(lanes_first, zero, values).astype(BF16),
        ],
        axis=0,
    )


def forward_kernel(
    table, spans, norms, doc_row, hidden, tiles,
    below_out, normed_out, packed_out, mixed_out, logsum_out, middle_out, normed_two_out,
    hidden_out,
    w_qkv, w_out, w_up, w_down, flow, normed, packed, mixed, logcol, logsum, middle, normed_two,
    doc_col, w_sem, o_sem,
):
    length, width = hidden.shape
    blocks = length // DENSE
    pairs = mixed.shape[0]
    lanes = mixed.shape[2]
    groups = (
        (0, 12, 12, w_qkv), (12, 4, 4, w_out), (16, 16, 16, w_up), (32, 16, 4, w_down),
    )

    def fetch(layer, group, act):
        first, count, per_row, target = groups[group]
        weight_group(
            tiles, table, 48 * layer + first, count, per_row, target.at[layer], w_sem, act
        )

    for layer in range(LAYERS):
        for group in range(4):
            fetch(layer, group, "start")
    outs = (
        (normed, normed_out), (packed, packed_out), (mixed, mixed_out), (logsum, logsum_out),
        (middle, middle_out), (normed_two, normed_two_out), (flow, below_out),
    )

    def flush(number, layer):
        return pltpu.make_async_copy(outs[number][0], outs[number][1].at[layer], o_sem.at[number])

    def forward_one(layer):
        def again(number):
            pl.when(layer > 0)(lambda: flush(number, layer).wait())

        flush(6, layer).start()
        again(0)
        again(1)
        fetch(layer, 0, "wait")

        @pl.loop(0, blocks)
        def _(number):
            here = rows_of(number, DENSE)
            unit, _ = normalized(flow[here, :])
            low = (unit * norms[pl.ds(4 * layer + 0, 1), :] + norms[pl.ds(4 * layer + 1, 1), :]).astype(BF16)
            normed[here, :] = low
            product = dot_nn(low, w_qkv[layer])
            for j in range(3 * pairs):
                packed[j, here, :] = product[:, j * lanes : (j + 1) * lanes].astype(BF16)

        flush(0, layer).start()
        flush(1, layer).start()
        again(2)
        lane_ids = lax.broadcasted_iota(jnp.int32, (QUERY, lanes), 1)
        first_half = lane_is_first((QUERY, lanes))

        @pl.loop(0, length // QUERY)
        def _(number):
            here = rows_of(number, QUERY)
            low_key = spans[0, number]
            key_count = spans[1, number]
            doc_here = doc_col[here, 0:1]

            def with_keys(many):
                keys_here = pl.ds(pl.multiple_of(low_key * QUERY, QUERY), many * BLOCK)
                same = doc_here == doc_row[0:1, keys_here]
                same = jnp.concatenate([same, same], axis=0)

                def score(pair):
                    heads = stacked(packed[pair, here, :].astype(F32) * 0.125, first_half)
                    return dot_nt(heads, packed[pairs + pair, keys_here, :])

                def settle(scores):
                    scores = jnp.where(same, scores, -1e30)
                    top = jnp.max(scores, axis=-1, keepdims=True)
                    weights = jnp.exp(scores - top)
                    total = jnp.sum(weights, axis=-1, keepdims=True)
                    return weights.astype(BF16), total, top + jnp.log(total)

                def finish(pair, weights, total, logs):
                    result = dot_nn(weights, packed[2 * pairs + pair, keys_here, :]) / total
                    mixed[pair, here, :] = jnp.where(
                        first_half, result[:QUERY], result[QUERY:]
                    ).astype(BF16)
                    old = logcol[here, :]
                    old = jnp.where(lane_ids == 8 * pair, logs[:QUERY], old)
                    logcol[here, :] = jnp.where(lane_ids == 8 * pair + 1, logs[QUERY:], old)

                waiting = None
                ahead = score(0)
                for pair in range(pairs):
                    now = ahead
                    if pair + 1 < pairs:
                        ahead = score(pair + 1)
                    done = settle(now)
                    if waiting is not None:
                        finish(pair - 1, *waiting)
                    waiting = done
                finish(pairs - 1, *waiting)


            for many in range(1, length // BLOCK + 1):
                pl.when(key_count == many)(lambda many=many: with_keys(many))

        flush(2, layer).start()
        turned = logcol[...].T
        again(3)
        for pair in range(pairs):
            logsum[pair, :, :] = turned[8 * pair : 8 * pair + 8, :]
        flush(3, layer).start()
        fetch(layer, 1, "wait")
        fetch(layer, 2, "wait")
        fetch(layer, 3, "wait")
        again(4)
        again(5)
        flush(6, layer).wait()
        chunk = width

        @pl.loop(0, blocks)
        def _(number):
            here = rows_of(number, DENSE)
            side_by_side = jnp.concatenate([mixed[pair, here, :] for pair in range(pairs)], axis=1)
            mid = flow[here, :] + dot_nn(side_by_side, w_out[layer])
            middle[here, :] = mid
            unit, _ = normalized(mid)
            low = (unit * norms[pl.ds(4 * layer + 2, 1), :] + norms[pl.ds(4 * layer + 3, 1), :]).astype(BF16)
            normed_two[here, :] = low
            total = mid
            for c in range(w_up.shape[2] // chunk):
                part = slice(c * chunk, (c + 1) * chunk)
                active = gelu_value(dot_nn(low, w_up[layer, :, part])).astype(BF16)
                total = total + dot_nn(active, w_down[layer, part, :])
            flow[here, :] = total

        flush(4, layer).start()
        flush(5, layer).start()

    flow[...] = hidden[...].astype(F32)
    fill_columns(doc_row, doc_col)

    @pl.loop(0, LAYERS)
    def _(layer):
        forward_one(layer)

    last = pltpu.make_async_copy(normed, hidden_out, o_sem.at[7])
    flush(0, LAYERS - 1).wait()
    normed[...] = flow[...].astype(BF16)
    last.start()
    for number in range(1, 6):
        flush(number, LAYERS - 1).wait()
    last.wait()


def fill_columns(doc_row, doc_col):
    lanes = doc_col.shape[1]

    @pl.loop(0, doc_col.shape[0] // lanes)
    def _(number):
        here = rows_of(number, lanes)
        spread = jnp.broadcast_to(doc_row[0:1, here].astype(F32), (lanes, lanes))
        doc_col[here, :] = spread.T.astype(jnp.int32)


def vmem_spec():
    return pl.BlockSpec(memory_space=pltpu.VMEM)


def any_spec():
    return pl.BlockSpec(memory_space=pl.ANY)


def smem_spec():
    return pl.BlockSpec(memory_space=pltpu.SMEM)


def forward_layers(table, spans, norms, doc_row, hidden, tiles, pairs):
    length, width = hidden.shape
    lanes = tiles.shape[2]
    one = (
        ((length, width), F32),
        ((length, width), BF16),
        ((3 * pairs, length, lanes), BF16),
        ((pairs, length, lanes), BF16),
        ((pairs, 8, length), F32),
        ((length, width), F32),
        ((length, width), BF16),
    )
    shapes = [((LAYERS, *s), d) for s, d in one] + [((length, width), BF16)]
    keep = [pltpu.VMEM(s, d) for s, d in one]
    return pl.pallas_call(
        forward_kernel,
        name="forward_layers",
        out_shape=[jax.ShapeDtypeStruct(s, d) for s, d in shapes],
        in_specs=[smem_spec(), smem_spec()] + [vmem_spec()] * 3 + [any_spec()],
        out_specs=[any_spec()] * len(shapes),
        scratch_shapes=[
            pltpu.VMEM((LAYERS, width, 3 * width), BF16),
            pltpu.VMEM((LAYERS, width, width), BF16),
            pltpu.VMEM((LAYERS, width, 4 * width), BF16),
            pltpu.VMEM((LAYERS, 4 * width, width), BF16),
            *keep[:4],
            pltpu.VMEM((length, lanes), F32),
            *keep[4:],
            pltpu.VMEM((length, lanes), jnp.int32),
            pltpu.SemaphoreType.DMA((48 * LAYERS,)),
            pltpu.SemaphoreType.DMA((8,)),
        ],
        compiler_params=pltpu.CompilerParams(vmem_limit_bytes=VMEM_BYTES),
        cost_estimate=pl.CostEstimate(
            flops=length * width * width * 52, bytes_accessed=40 * 2**20,
            transcendentals=length * length * 8,
        ),
    )(table, spans, norms, doc_row, hidden, tiles)


def backward_kernel(
    table, aims, spans, counts, norms, doc_row, upper_in,
    below_in, normed_in, packed_in, mixed_in, logsum_in, middle_in, normed_two_in, tiles,
    grad_out, tile_grads, norm_grads,
    w_qkv, w_out, w_up, w_down,
    flow, normed, packed, mixed, logsum, middle, normed_two, hidden,
    active, inner_grad, grad_low, mid_grad, mid_low, mixed_grad, delta, packed_grad,
    key_sum, value_sum, staged, blank, doc_col, selector,
    w_sem, i_sem, t_sem, z_sem, o_sem,
):
    length, width = flow.shape
    blocks = length // DENSE_BACK
    pairs, lanes = mixed.shape[0], mixed.shape[2]
    groups = (
        (0, 12, 12, w_qkv), (12, 4, 4, w_out), (16, 16, 16, w_up), (32, 16, 4, w_down),
    )
    ins = (
        (normed_two_in, normed_two), (middle_in, middle), (mixed_in, mixed),
        (packed_in, packed), (logsum_in, logsum), (below_in, hidden), (normed_in, normed),
    )

    def load(number, layer):
        return pltpu.make_async_copy(ins[number][0].at[layer], ins[number][1], i_sem.at[number])

    def fetch(group, layer, act):
        first, count, per_row, target = groups[group]
        weight_group(tiles, table, 48 * layer + first, count, per_row, target, w_sem, act)

    def early(layer):
        load(0, layer).start()
        fetch(2, layer, "start")
        fetch(3, layer, "start")
        load(1, layer).start()
        fetch(1, layer, "start")
        load(2, layer).start()

    def late(layer):
        load(3, layer).start()
        load(4, layer).start()

    take = pltpu.make_async_copy(upper_in, grad_low, o_sem.at[0])
    take.start()
    early(LAYERS - 1)
    late(LAYERS - 1)
    fetch(0, LAYERS - 1, "start")
    load(5, LAYERS - 1).start()
    load(6, LAYERS - 1).start()

    def blank_copies(act):
        capacity = tile_grads.shape[0] // counts.shape[0]
        quarter = capacity // 4

        @pl.loop(0, counts.shape[0])
        def _(owner):
            @pl.loop(counts[owner], capacity)
            def _(place):
                core, depth_z, part = lax.rem(owner, 2), lax.div(owner, 2), lax.div(place, quarter)
                low_bit, high_bit = lax.rem(part, 2), lax.div(part, 2)
                major = low_bit + core * (high_bit - low_bit)
                minor = high_bit + core * (low_bit - high_bit)
                index = lax.rem(place, quarter) * 32 + core * 16 + major * 8 + minor * 4 + depth_z
                getattr(
                    pltpu.make_async_copy(blank, tile_grads.at[index], z_sem.at[index]), act
                )()

    norm_grads[...] = jnp.zeros_like(norm_grads)
    blank[...] = jnp.zeros_like(blank)
    fill_columns(doc_row, doc_col)
    which = lax.broadcasted_iota(jnp.int32, selector.shape, 0)
    lane = lax.broadcasted_iota(jnp.int32, selector.shape, 1)
    head_dim = width // HEADS
    own_head = 2 * lax.div(which, 8) + lax.rem(which, 8)
    fits = (lax.rem(which, 8) < 2) & (lax.div(lane, head_dim) == own_head)
    selector[...] = jnp.where(fits, 1.0, 0.0)
    take.wait()
    flow[...] = grad_low[...].astype(F32)
    chunk = 2 * width
    chunks = w_up.shape[1] // chunk

    def send_tile(place, layer):
        return pltpu.make_async_copy(
            staged.at[place], tile_grads.at[aims[48 * layer + place]], t_sem.at[place]
        )

    def settle_tiles(layer):
        @pl.loop(0, 48)
        def _(place):
            send_tile(place, layer).wait()

    def backward_one(layer):
        def norm_back(values, out_grad, gain, gain_row):
            unit, scale = normalized(values)
            sums = (
                jnp.sum(out_grad * unit, axis=0, keepdims=True),
                jnp.sum(out_grad, axis=0, keepdims=True),
            )
            for which in range(LAYERS):

                @pl.when(layer == which)
                def _(which=which):
                    for side in range(2):
                        row = 4 * which + gain_row + side
                        norm_grads[row : row + 1, :] += sums[side]

            turned = out_grad * gain
            average = jnp.mean(turned, axis=-1, keepdims=True)
            along = jnp.mean(turned * unit, axis=-1, keepdims=True)
            return scale * (turned - average - unit * along)

        load(0, layer).wait()
        fetch(2, layer, "wait")
        fetch(3, layer, "wait")
        load(1, layer).wait()
        fetch(1, layer, "wait")
        load(2, layer).wait()

        @pl.loop(0, blocks)
        def _(number):
            here = rows_of(number, DENSE_BACK)
            upper = flow[here, :]
            low = upper.astype(BF16)
            grad_low[here, :] = low
            normed_here = normed_two[here, :]
            total = jnp.zeros((DENSE_BACK, width), F32)
            for c in range(chunks):
                part = slice(c * chunk, (c + 1) * chunk)
                value, slope = gelu_both(dot_nn(normed_here, w_up[:, part]))
                active[here, part] = value.astype(BF16)
                inner = (slope * dot_nt(low, w_down[part, :])).astype(BF16)
                inner_grad[here, part] = inner
                total = total + dot_nt(inner, w_up[:, part])
            mid = upper + norm_back(middle[here, :], total, norms[pl.ds(4 * layer + 2, 1), :], 2)
            mid_grad[here, :] = mid
            mid_here = mid.astype(BF16)
            mid_low[here, :] = mid_here
            back = dot_nt(mid_here, w_out[...]).astype(BF16)
            for pair in range(pairs):
                mixed_grad[pair, here, :] = back[:, pair * lanes : (pair + 1) * lanes]
            side_by_side = jnp.concatenate([mixed[pair, here, :] for pair in range(pairs)], axis=1)
            both = side_by_side.astype(F32) * back.astype(F32)
            sums = dot_nt(selector[...], both, precision=lax.Precision.HIGHEST)
            for pair in range(pairs):
                delta[pair, :, here] = sums[8 * pair : 8 * pair + 8, :]

        pl.when(layer < LAYERS - 1)(lambda: settle_tiles(layer + 1))

        def emit(block, first):
            for c in range(block.shape[1] // lanes):
                staged[first + c] = block[:, c * lanes : (c + 1) * lanes].astype(BF16)
                send_tile(first + c, layer).start()

        @pl.loop(0, 4)
        def _(c):
            part = rows_of(c, width)
            emit(dot_tn(active[:, part], grad_low[...]), 32 + 4 * c)
            emit(dot_tn(normed_two[...], inner_grad[:, part]), 16 + 4 * c)

        side_by_side = jnp.concatenate([mixed[pair] for pair in range(pairs)], axis=1)
        emit(dot_tn(side_by_side, mid_low[...]), 12)
        pl.when(layer > 0)(lambda: early(layer - 1))
        pl.when(layer == LAYERS - 1)(lambda: blank_copies("start"))
        load(3, layer).wait()
        load(4, layer).wait()
        first_half = lane_is_first((QUERY, lanes))

        key_sum[...] = jnp.zeros_like(key_sum)
        value_sum[...] = jnp.zeros_like(value_sum)

        @pl.loop(0, length // QUERY)
        def _(number):
            here = rows_of(number, QUERY)
            low_key = spans[0, number]
            key_count = spans[1, number]
            doc_here = doc_row[0:1, here]
            doc_here = jnp.concatenate([doc_here, doc_here], axis=1)

            def with_keys(many):
                keys_here = pl.ds(pl.multiple_of(low_key * QUERY, QUERY), many * BLOCK)
                same = doc_col[keys_here, 0:1] == doc_here

                def score(pair):
                    heads = stacked(packed[pair, here, :].astype(F32) * 0.125, first_half)
                    outs = stacked(mixed_grad[pair, here, :].astype(F32), first_half)
                    return (
                        heads,
                        outs,
                        dot_nt(packed[pairs + pair, keys_here, :], heads),
                        dot_nt(packed[2 * pairs + pair, keys_here, :], outs),
                    )

                def settle(pair, heads, outs, scores, from_values):
                    logs = jnp.concatenate([logsum[pair, 0:1, here], logsum[pair, 1:2, here]], axis=1)
                    means = jnp.concatenate([delta[pair, 0:1, here], delta[pair, 1:2, here]], axis=1)
                    weights = jnp.exp(jnp.where(same, scores - logs, -1e30))
                    score_grad = (weights * (from_values - means)).astype(BF16)
                    return heads, outs, weights.astype(BF16), score_grad

                def finish(pair, heads, outs, weights, score_grad):
                    value_sum[pair, keys_here, :] += dot_nn(weights, outs)
                    key_sum[pair, keys_here, :] += dot_nn(score_grad, heads)
                    query_part = dot_tn(score_grad, packed[pairs + pair, keys_here, :]) * 0.125
                    packed_grad[pair, here, :] = jnp.where(
                        first_half, query_part[:QUERY], query_part[QUERY:]
                    ).astype(BF16)

                waiting = None
                ahead = score(0)
                for pair in range(pairs):
                    now = ahead
                    if pair + 1 < pairs:
                        ahead = score(pair + 1)
                    done = settle(pair, *now)
                    if waiting is not None:
                        finish(pair - 1, *waiting)
                    waiting = done
                finish(pairs - 1, *waiting)

            for many in range(1, length // BLOCK + 1):
                pl.when(key_count == many)(lambda many=many: with_keys(many))

        for pair in range(pairs):
            packed_grad[pairs + pair] = key_sum[pair].astype(BF16)
            packed_grad[2 * pairs + pair] = value_sum[pair].astype(BF16)

        pl.when(layer > 0)(lambda: late(layer - 1))
        fetch(0, layer, "wait")
        load(5, layer).wait()
        load(6, layer).wait()

        @pl.loop(0, blocks)
        def _(number):
            here = rows_of(number, DENSE_BACK)
            wide = jnp.concatenate([packed_grad[j, here, :] for j in range(3 * pairs)], axis=1)
            total = dot_nt(wide, w_qkv[...])
            flow[here, :] = mid_grad[here, :] + norm_back(
                hidden[here, :], total, norms[pl.ds(4 * layer + 0, 1), :], 0
            )

        @pl.loop(0, 3)
        def _(c):
            wide = jnp.concatenate([packed_grad[pairs * c + j] for j in range(pairs)], axis=1)
            emit(dot_tn(normed[...], wide), 4 * c)

        @pl.when(layer > 0)
        def _():
            fetch(0, layer - 1, "start")
            load(5, layer - 1).start()
            load(6, layer - 1).start()

    @pl.loop(0, LAYERS)
    def _(step):
        backward_one(LAYERS - 1 - step)

    flush = pltpu.make_async_copy(grad_low, grad_out, o_sem.at[0])
    grad_low[...] = flow[...].astype(BF16)
    flush.start()
    settle_tiles(0)
    flush.wait()
    blank_copies("wait")


def backward_layers(
    table, aims, spans, counts, norms, doc_row, upper, saved, tiles
):
    length, width = upper.shape
    lanes = tiles.shape[2]
    pairs = width // lanes
    slots = tiles.shape[0]
    return pl.pallas_call(
        backward_kernel,
        name="backward_layers",
        out_shape=[
            jax.ShapeDtypeStruct((length, width), BF16),
            jax.ShapeDtypeStruct(tiles.shape, BF16),
            jax.ShapeDtypeStruct(norms.shape, F32),
        ],
        in_specs=[smem_spec()] * 4 + [vmem_spec()] * 2 + [any_spec()] * 9,
        out_specs=[any_spec(), any_spec(), vmem_spec()],
        scratch_shapes=[
            pltpu.VMEM((width, 3 * width), BF16),
            pltpu.VMEM((width, width), BF16),
            pltpu.VMEM((width, 4 * width), BF16),
            pltpu.VMEM((4 * width, width), BF16),
            pltpu.VMEM((length, width), F32),
            pltpu.VMEM((length, width), BF16),
            pltpu.VMEM((3 * pairs, length, lanes), BF16),
            pltpu.VMEM((pairs, length, lanes), BF16),
            pltpu.VMEM((pairs, 8, length), F32),
            pltpu.VMEM((length, width), F32),
            pltpu.VMEM((length, width), BF16),
            pltpu.VMEM((length, width), F32),
            pltpu.VMEM((length, 4 * width), BF16),
            pltpu.VMEM((length, 4 * width), BF16),
            pltpu.VMEM((length, width), BF16),
            pltpu.VMEM((length, width), F32),
            pltpu.VMEM((length, width), BF16),
            pltpu.VMEM((pairs, length, lanes), BF16),
            pltpu.VMEM((pairs, 8, length), F32),
            pltpu.VMEM((3 * pairs, length, lanes), BF16),
            pltpu.VMEM((pairs, length, lanes), F32),
            pltpu.VMEM((pairs, length, lanes), F32),
            pltpu.VMEM((48, width, lanes), BF16),
            pltpu.VMEM((width, lanes), BF16),
            pltpu.VMEM((length, lanes), jnp.int32),
            pltpu.VMEM((8 * pairs, width), F32),
            pltpu.SemaphoreType.DMA((48 * LAYERS,)),
            pltpu.SemaphoreType.DMA((7,)),
            pltpu.SemaphoreType.DMA((48,)),
            pltpu.SemaphoreType.DMA((slots,)),
            pltpu.SemaphoreType.DMA((1,)),
        ],
        compiler_params=pltpu.CompilerParams(vmem_limit_bytes=VMEM_BYTES),
        cost_estimate=pl.CostEstimate(
            flops=length * width * width * 120, bytes_accessed=60 * 2**20,
            transcendentals=length * length * 8,
        ),
    )(
        table, aims, spans, counts, norms, doc_row, upper, *saved, tiles
    )


MESH_IDS = pl.DeviceIdType.MESH


def place_of_device():
    row = lax.axis_index("rows")
    seat = lax.axis_index("seq")
    return row % 2, row // 2, seat // 2, seat % 2


def device_at(x, y, z, core):
    return (2 * y + x, 2 * z + core)


def greet(partners):
    barrier = pltpu.get_barrier_semaphore()
    for partner in partners:
        pl.semaphore_signal(barrier, inc=1, device_id=partner, device_id_type=MESH_IDS)
    pl.semaphore_wait(barrier, len(partners))


def seat_partners(x, y, z, core):
    others = []
    for k in range(1, 8):
        seat = (2 * z + core + k) % 8
        others.append((2 * y + x, seat))
    return others


def post(source, target, send_sem, recv_sem, number, partner):
    copy = pltpu.make_async_remote_copy(
        src_ref=source,
        dst_ref=target,
        send_sem=send_sem.at[number],
        recv_sem=recv_sem.at[number],
        device_id=partner,
        device_id_type=MESH_IDS,
    )
    copy.start()
    return copy


def gather_kernel(master, residual, tiles, rows, wide, low, flat, flat_low, send_sem, recv_sem, l_sem):
    x, y, z, core = place_of_device()
    quarter_id = 2 * y + x
    across = device_at(x, y, z, 1 - core)
    by_x = device_at(1 - x, y, z, core)
    by_y = device_at(x, 1 - y, z, core)
    quarters = (quarter_id, 2 * y + (1 - x), 2 * (1 - y) + x, 3 - quarter_id)
    seats = seat_partners(x, y, z, core)
    seat = 2 * z + core
    load_near = pltpu.make_async_copy(
        master.at[pl.ds(4 * quarter_id, 4)], wide.at[pl.ds(4 * quarter_id, 4)], l_sem.at[0]
    )
    load_near.start()
    far = []
    for k in range(1, 4):
        part = pl.ds(4 * ((quarter_id + k) % 4), 4)
        copy = pltpu.make_async_copy(master.at[part], wide.at[part], l_sem.at[1 + k])
        copy.start()
        far.append(copy)
    load_flat = pltpu.make_async_copy(residual, flat, l_sem.at[1])
    load_flat.start()
    greet(seats + [by_x, by_y])

    def spot(z_from, quarter):
        return core * 64 + z_from * 16 + 4 * quarter

    def convert(first, count):
        @pl.loop(0, count)
        def _(j):
            low[first + j] = wide[first + j].astype(BF16)

    def make(source, target, number, partner):
        return pltpu.make_async_remote_copy(
            src_ref=source, dst_ref=target, send_sem=send_sem.at[number],
            recv_sem=recv_sem.at[number], device_id=partner, device_id_type=MESH_IDS,
        )

    def relay(number, first, count, partner):
        part = pl.ds(first, count)
        return make(tiles.at[part], tiles.at[part], number, partner)

    mine = pl.ds(core * 64 + z * 16, 16)
    own_here = pl.ds(spot(z, quarter_id), 4)

    def hop(way, step):
        toward = device_at(x, y, lax.rem(z + (1 if way == 0 else 3), 4), core)
        number = 3 * way + step - 1
        if step == 1:
            return make(low.at[pl.ds(4 * quarter_id, 4)], tiles.at[own_here], number, toward)
        z_from = lax.rem(z + (5 - step if way == 0 else step - 1), 4)
        return relay(number, spot(z_from, quarter_id), 4, toward)

    def can_send(way, step):
        if way == 0:
            return (z < 3) & (z >= step - 1)
        return (z > 0) & (z <= 4 - step)

    def arrives(way, step):
        return z >= step if way == 0 else z <= 3 - step

    def source(way, step):
        return lax.rem(z + (4 - step if way == 0 else step), 4)

    steps = [(way, step) for step in range(1, 4) for way in range(2)]

    def fan(way, step):
        base = 6 + 9 * (3 * way + step - 1)
        z_from = source(way, step)
        return [
            relay(base, spot(z_from, quarters[0]), 4, by_x),
            relay(base + 1, spot(z_from, quarters[0]), 4, by_y),
            relay(base + 2, spot(z_from, quarters[0]), 4, across),
            relay(base + 3, spot(z_from, quarters[1]), 2, by_y),
            relay(base + 4, spot(z_from, quarters[1]), 4, across),
            relay(base + 5, spot(z_from, quarters[2]) + 2, 2, by_x),
            relay(base + 6, spot(z_from, quarters[2]), 4, across),
            relay(base + 7, spot(z_from, quarters[3]), 2, across),
            relay(base + 8, spot(z_from, quarters[3]) + 2, 2, across),
        ]

    load_near.wait()
    convert(4 * quarter_id, 4)
    for way in range(2):
        pl.when(can_send(way, 1))(lambda way=way: hop(way, 1).start())
    for k in range(1, 4):
        far[k - 1].wait()
        convert(4 * ((quarter_id + k) % 4), 4)
    keep_tiles = pltpu.make_async_copy(low, tiles.at[mine], l_sem.at[6])
    keep_tiles.start()
    own_across = make(low, tiles.at[mine], 60, across)
    own_across.start()
    load_flat.wait()

    @pl.loop(0, flat.shape[0])
    def _(j):
        flat_low[j] = flat[j].astype(BF16)

    keep_row = pltpu.make_async_copy(flat_low.at[seat], rows.at[seat], l_sem.at[5])
    keep_row.start()
    row_moves = [
        make(flat_low.at[(seat + k) % 8], rows.at[seat], 60 + k, seats[k - 1])
        for k in range(1, 8)
    ]

    def take(way, step):
        hop(way, step).wait_recv()
        if step < 3:
            pl.when(can_send(way, step + 1))(lambda: hop(way, step + 1).start())
        for copy in fan(way, step)[:3]:
            copy.start()

    def turn(way, step):
        moves = fan(way, step)
        moves[0].wait_recv()
        moves[3].start()
        moves[4].start()
        moves[1].wait_recv()
        moves[5].start()
        moves[6].start()

    def finish(way, step):
        moves = fan(way, step)
        moves[3].wait_recv()
        moves[7].start()
        moves[5].wait_recv()
        moves[8].start()

    def drain(way, step):
        moves = fan(way, step)
        for number in (2, 4, 6, 7, 8):
            moves[number].wait_recv()
        for copy in moves:
            copy.wait_send()

    def each(act, chosen):
        for way, step in chosen:
            pl.when(arrives(way, step))(lambda way=way, step=step: act(way, step))

    each(take, steps[:2])
    each(take, steps[2:4])
    each(turn, steps[:2])
    each(take, steps[4:])
    for copy in row_moves:
        copy.start()
    each(turn, steps[2:4])
    each(finish, steps[:2])
    each(turn, steps[4:])
    each(finish, steps[2:])
    own_across.wait_recv()
    each(drain, steps)
    for way, step in steps:
        pl.when(can_send(way, step))(lambda way=way, step=step: hop(way, step).wait_send())
    for copy in row_moves:
        copy.wait_recv()
        copy.wait_send()
    own_across.wait_send()
    keep_row.wait()
    keep_tiles.wait()


def gather_start(master_tiles, residual):
    capacity, depth, lanes = master_tiles.shape
    count = 68
    return pl.pallas_call(
        gather_kernel,
        name="gather_start",
        out_shape=[
            jax.ShapeDtypeStruct((8 * capacity, depth, lanes), BF16),
            jax.ShapeDtypeStruct(residual.shape, BF16),
        ],
        in_specs=[any_spec()] * 2,
        out_specs=[any_spec()] * 2,
        scratch_shapes=[
            pltpu.VMEM(master_tiles.shape, F32),
            pltpu.VMEM(master_tiles.shape, BF16),
            pltpu.VMEM(residual.shape, F32),
            pltpu.VMEM(residual.shape, BF16),
            pltpu.SemaphoreType.DMA((count,)),
            pltpu.SemaphoreType.DMA((count,)),
            pltpu.SemaphoreType.DMA((7,)),
        ],
        compiler_params=pltpu.CompilerParams(
            collective_id=0, has_side_effects=True, vmem_limit_bytes=VMEM_BYTES
        ),
        cost_estimate=pl.CostEstimate(
            flops=0, bytes_accessed=200 * 2**20, transcendentals=0
        ),
    )(master_tiles, residual)


def reduce_kernel(
    held, upper, norm_part, owned, rows, norm_sum, squares,
    core_in, own, one_in, two_in, z_in, piece, norm_in, norm_now, square_in,
    square_now, send_sem, recv_sem, l_sem,
):
    x, y, z, core = place_of_device()
    quarter_id = 2 * y + x
    across = device_at(x, y, z, 1 - core)
    by_x = device_at(1 - x, y, z, core)
    by_y = device_at(x, 1 - y, z, core)
    by_both = device_at(1 - x, 1 - y, z, core)
    plus, minus = core, 1 - core
    first_bit = x * minus + y * plus
    second_bit = y * minus + x * plus
    one = device_at(x + minus * (1 - 2 * x), y + plus * (1 - 2 * y), z, core)
    two = device_at(x + plus * (1 - 2 * x), y + minus * (1 - 2 * y), z, core)
    along_z = [device_at(x, y, (z + k) % 4, core) for k in range(1, 4)]
    seats = seat_partners(x, y, z, core)
    seat = 2 * z + core
    quarter_x, quarter_y = 2 * y + (1 - x), 2 * (1 - y) + x
    chunks = own.shape[0]
    number = 0
    copies = []

    def move(source, target, partner):
        nonlocal number
        copy = post(source, target, send_sem, recv_sem, number, partner)
        number += 1
        copies.append(copy)
        return copy

    loads = []
    for i in range(chunks):
        copy = pltpu.make_async_copy(
            held.at[pl.ds(32 * i + 16 * core, 16)], own.at[i], l_sem.at[i]
        )
        copy.start()
        loads.append(copy)
    greet(seats + [by_x, by_y, by_both])
    half = own.shape[2] // 2
    parts = [(i, pl.ds(half * side, half)) for i in range(chunks) for side in range(2)]
    core_moves = [
        move(held.at[pl.ds(32 * i + 16 * (1 - core), 16), rows_], core_in.at[i, :, rows_], across)
        for i, rows_ in parts
    ]
    norm_now[0] = norm_part[...]
    norm_moves = [move(norm_now.at[0], norm_in.at[0], across)]
    for k in range(1, 8):
        move(upper.at[(seat + k) % 8], rows.at[seat], seats[k - 1])
    row_moves = copies[-7:]
    keep_row = pltpu.make_async_copy(upper.at[seat], rows.at[seat], l_sem.at[chunks])
    keep_row.start()

    def add_in(target, first, incoming, count, part):
        @pl.loop(0, count)
        def _(j):
            target[first + j, part, :] = (
                target[first + j, part, :].astype(F32) + incoming[j, part, :].astype(F32)
            ).astype(BF16)

    one_moves, two_moves, z_moves, near_moves, corner_moves, keeps = [], [], [], [], [], []

    def stage_core(n):
        i, part = parts[n]
        if n % 2 == 0:
            loads[i].wait()
        core_moves[n].wait_recv()
        add_in(own.at[i], 0, core_in.at[i], 16, part)
        one_moves.append(
            move(
                own.at[i, pl.ds(8 * (1 - first_bit), 8), part], one_in.at[i, :, part], one
            )
        )

    def stage_one(n):
        i, part = parts[n]
        one_moves[n].wait_recv()
        add_in(own.at[i], 8 * first_bit, one_in.at[i], 8, part)
        two_moves.append(
            move(
                own.at[i, pl.ds(8 * first_bit + 4 * (1 - second_bit), 4), part],
                two_in.at[i, :, part],
                two,
            )
        )

    def stage_two(n):
        i, part = parts[n]
        two_moves[n].wait_recv()
        base = 8 * first_bit + 4 * second_bit
        add_in(own.at[i], base, two_in.at[i], 4, part)
        z_moves.append(
            [
                move(
                    own.at[i, base + (z + k) % 4, part], z_in.at[i, k - 1, part], along_z[k - 1]
                )
                for k in range(1, 4)
            ]
        )

    def stage_z(n):
        i, part = parts[n]
        for copy in z_moves[n]:
            copy.wait_recv()
        total = own[i, 8 * first_bit + 4 * second_bit + z, part, :].astype(F32)
        for k in range(3):
            total = total + z_in[i, k, part, :].astype(F32)
        piece[i, part, :] = total.astype(BF16)
        square_now[0] += jnp.sum((total * total).reshape(-1, 8, total.shape[1]), axis=0)
        here = owned.at[4 * quarter_id + i, part]
        near_moves.append(
            [move(piece.at[i, part], here, partner) for partner in (by_x, by_y)]
        )
        if n >= len(parts) - 2:
            corner_moves.append(move(piece.at[i, part], here, by_both))
        keep = pltpu.make_async_copy(piece.at[i, part], here, l_sem.at[chunks + 1 + n])
        keep.start()
        keeps.append(keep)

    def stage_turn(n):
        i, part = parts[n]
        side = n % 2
        near_moves[n][1 - side].wait_recv()
        far_id = quarter_y if side == 0 else quarter_x
        here = owned.at[4 * far_id + i, part]
        corner_moves.append(move(here, here, by_x if side == 0 else by_y))

    def norm_stage(step, partner):
        norm_moves[step].wait_recv()
        norm_now[step + 1] = norm_now[step] + norm_in[step]
        if partner is not None:
            norm_moves.append(move(norm_now.at[step + 1], norm_in.at[step + 1], partner))

    square_now[...] = jnp.zeros_like(square_now)
    for n in range(8):
        stage_core(n)
        if n == 1:
            norm_stage(0, by_x)
        if n == 3:
            norm_stage(1, by_y)
        if n == 5:
            norm_stage(2, None)
    norm_z = [move(norm_now.at[3], norm_in.at[2 + k], along_z[k - 1]) for k in range(1, 4)]
    for n in range(8 + 5):
        if n < 8:
            stage_one(n)
        if 0 <= n - 1 < 8:
            stage_two(n - 1)
        if 0 <= n - 3 < 8:
            stage_z(n - 3)
        if 0 <= n - 5 < 6:
            stage_turn(n - 5)

    def in_order(own_value, incoming):
        values = [own_value] + [incoming(k) for k in range(1, 4)]
        total = None
        for place in range(4):
            picked = values[0]
            for k in range(1, 4):
                picked = jnp.where((z + 4 - k) % 4 == place, values[k], picked)
            total = picked if total is None else total + picked
        return total

    square_moves = []

    def square_stage(step, partner):
        square_moves.append(move(square_now.at[step], square_in.at[step], partner))
        square_moves[step].wait_recv()
        square_now[step + 1] = square_now[step] + square_in[step]

    square_stage(0, by_x)
    square_stage(1, by_y)
    square_stage(2, across)
    square_z = [
        move(square_now.at[3], square_in.at[2 + k], along_z[k - 1]) for k in range(1, 4)
    ]
    for copy in norm_z:
        copy.wait_recv()
    norm_sum[...] = in_order(norm_now[3], lambda k: norm_in[2 + k])
    for copy in square_z:
        copy.wait_recv()
    squares[...] = in_order(square_now[3], lambda k: square_in[2 + k])
    straight = [near_moves[n][n % 2] for n in range(6)] + near_moves[6] + near_moves[7]
    for copy in row_moves + straight + corner_moves:
        copy.wait_recv()
    for copy in copies:
        copy.wait_send()
    keep_row.wait()
    for keep in keeps:
        keep.wait()


def reduce_end(held, upper, norm_part):
    slots, depth, lanes = held.shape
    chunks = 4
    count = 8 + 1 + 7 + 8 + 8 + 24 + 24 + 2 + 3 + 3 + 3
    return pl.pallas_call(
        reduce_kernel,
        name="reduce_end",
        out_shape=[
            jax.ShapeDtypeStruct((slots // 8, depth, lanes), BF16),
            jax.ShapeDtypeStruct(upper.shape, BF16),
            jax.ShapeDtypeStruct(norm_part.shape, F32),
            jax.ShapeDtypeStruct((8, lanes), F32),
        ],
        in_specs=[any_spec(), any_spec(), vmem_spec()],
        out_specs=[any_spec(), any_spec(), vmem_spec(), vmem_spec()],
        scratch_shapes=[
            pltpu.VMEM((chunks, 16, depth, lanes), BF16),
            pltpu.VMEM((chunks, 16, depth, lanes), BF16),
            pltpu.VMEM((chunks, 8, depth, lanes), BF16),
            pltpu.VMEM((chunks, 4, depth, lanes), BF16),
            pltpu.VMEM((chunks, 3, depth, lanes), BF16),
            pltpu.VMEM((chunks, depth, lanes), BF16),
            pltpu.VMEM((6, *norm_part.shape), F32),
            pltpu.VMEM((4, *norm_part.shape), F32),
            pltpu.VMEM((6, 8, lanes), F32),
            pltpu.VMEM((4, 8, lanes), F32),
            pltpu.SemaphoreType.DMA((count,)),
            pltpu.SemaphoreType.DMA((count,)),
            pltpu.SemaphoreType.DMA((3 * chunks + 1,)),
        ],
        compiler_params=pltpu.CompilerParams(
            collective_id=1, has_side_effects=True, vmem_limit_bytes=40 * 2**20
        ),
        cost_estimate=pl.CostEstimate(
            flops=0, bytes_accessed=300 * 2**20, transcendentals=0
        ),
    )(held, upper, norm_part)


def finish_kernel(
    counts, owned, master, first, second, grad_rows, out_rows, squares, norm_sum, norm_params,
    norm_first, norm_second,
    clip_out, first_out, second_out, master_out, copy_out, grad_rows_out, out_rows_out,
    total_out, norm_clip_out, norm_first_out, norm_second_out, norm_params_out,
    clip, new_first, new_second, new_master, new_copy, wide_grad, wide_out, o_sem,
):
    norms = norm_sum[...]
    total = jnp.sqrt(jnp.sum(squares[...]) + jnp.sum(norms * norms))
    factor = 1.0 / jnp.maximum(total, 1.0)
    correction = 1.0 - 0.5**STEP

    def step(weight, grad, low, high, rate):
        low = 0.5 * low + 0.5 * grad
        high = 0.5 * high + 0.5 * grad * grad
        update = low / correction / (jnp.sqrt(high / correction) + 1e-08)
        return weight - rate * (update + 0.01 * weight), low, high

    outs = (
        (clip, clip_out), (new_first, first_out), (new_second, second_out),
        (new_master, master_out), (new_copy, copy_out),
    )
    capacity = master.shape[0]

    def send(number, place):
        return pltpu.make_async_copy(
            outs[number][0].at[place], outs[number][1].at[place],
            o_sem.at[number * capacity + place],
        )

    count = counts[lax.axis_index("seq")]

    @pl.loop(0, capacity)
    def _(place):
        keep = (lax.broadcast(place, clip.shape[1:])) < count
        grad = jnp.where(keep, owned[place].astype(F32), 0.0) * factor
        weight, low, high = step(master[place], grad, first[place], second[place], 0.05)
        weight = jnp.where(keep, weight, 0.0)
        clip[place] = grad
        new_first[place] = jnp.where(keep, low, 0.0)
        new_second[place] = jnp.where(keep, high, 0.0)
        new_master[place] = weight
        new_copy[place] = weight.astype(BF16)
        for number in range(len(outs)):
            send(number, place).start()

    moves = []
    for number, (low, wide, target) in enumerate(
        ((grad_rows, wide_grad, grad_rows_out), (out_rows, wide_out, out_rows_out))
    ):

        @pl.loop(0, low.shape[0])
        def _(j, low=low, wide=wide):
            wide[j] = low[j].astype(F32)

        moves.append(pltpu.make_async_copy(wide, target, o_sem.at[5 * capacity + number]))
        moves[-1].start()
    clipped = norms * factor
    weight, low, high = step(norm_params[...], clipped, norm_first[...], norm_second[...], 0.25)
    total_out[...] = jnp.broadcast_to(total, total_out.shape)
    norm_clip_out[...] = clipped
    norm_first_out[...] = low
    norm_second_out[...] = high
    norm_params_out[...] = weight

    @pl.loop(0, capacity)
    def _(place):
        for number in range(len(outs)):
            send(number, place).wait()

    for move in moves:
        move.wait()


def finish_step(
    counts, owned, master, first, second, grad_rows, out_rows, squares, norm_sum, norm_params,
    norm_first, norm_second,
):
    tiles = jax.ShapeDtypeStruct(master.shape, F32)
    rows = jax.ShapeDtypeStruct(grad_rows.shape, F32)
    norms = jax.ShapeDtypeStruct(norm_params.shape, F32)
    return pl.pallas_call(
        finish_kernel,
        name="finish_step",
        out_shape=[
            tiles, tiles, tiles, tiles, jax.ShapeDtypeStruct(master.shape, BF16), rows, rows,
            jax.ShapeDtypeStruct((1, 128), F32), norms, norms, norms, norms,
        ],
        in_specs=[smem_spec()] + [vmem_spec()] * 11,
        out_specs=[any_spec()] * 7 + [vmem_spec()] * 5,
        scratch_shapes=[pltpu.VMEM(master.shape, F32)] * 4
        + [pltpu.VMEM(master.shape, BF16)]
        + [pltpu.VMEM(grad_rows.shape, F32)] * 2
        + [pltpu.SemaphoreType.DMA((5 * master.shape[0] + 2,))],
        compiler_params=pltpu.CompilerParams(vmem_limit_bytes=44 * 2**20),
        cost_estimate=pl.CostEstimate(
            flops=0, bytes_accessed=40 * 2**20, transcendentals=0
        ),
    )(
        counts, owned, master, first, second, grad_rows, out_rows, squares, norm_sum, norm_params,
        norm_first, norm_second,
    )


def local_by_rows(
    residual_in,
    cotangent,
    segments,
    owners,
    master_tiles,
    first_tiles,
    second_tiles,
    norm_params,
    norm_first,
    norm_second,
):
    local_rows, positions, model_width = residual_in.shape
    seq_devices = lax.axis_size("seq")
    seq_index = lax.axis_index("seq")
    length = positions * seq_devices
    tile_total = owners.shape[0]
    capacity, _, tile_width = master_tiles.shape
    quarter = capacity // 4
    pairs = model_width // tile_width
    places = jnp.arange(tile_total, dtype=jnp.int32)
    before = (owners[None, :] == owners[:, None]) & (places[None, :] < places[:, None])
    ranks = jnp.sum(before.astype(jnp.int32), axis=1)
    core, depth_z, part_id = owners % 2, owners // 2, ranks // quarter
    major = jnp.where(core == 0, part_id % 2, part_id // 2)
    minor = jnp.where(core == 0, part_id // 2, part_id % 2)
    weight_table = core * 64 + depth_z * 16 + ranks
    grad_table = (ranks % quarter) * 32 + core * 16 + major * 8 + minor * 4 + depth_z
    seats = jnp.arange(seq_devices, dtype=jnp.int32)
    counts = jnp.sum((owners[None, :] == seats[:, None]).astype(jnp.int32), axis=1)
    tiles, hidden = gather_start(master_tiles, residual_in)
    hidden = hidden.reshape(length, model_width)
    later, tiles = lax.optimization_barrier((cotangent, tiles))
    upper = lax.all_to_all(later.astype(BF16), "seq", split_axis=0, concat_axis=0, tiled=True)
    upper = upper.reshape(length, model_width)
    doc_ids = lax.dynamic_slice_in_dim(segments, seq_index, 1, 0)
    doc_row = doc_ids
    begin = jnp.sum((doc_ids < doc_ids[0, ::QUERY, None]).astype(jnp.int32), axis=1) // QUERY
    end = jnp.sum((doc_ids <= doc_ids[0, QUERY - 1 :: QUERY, None]).astype(jnp.int32), axis=1)
    many = (end - begin * QUERY + BLOCK - 1) // BLOCK
    spans = jnp.stack([jnp.minimum(begin, (length - many * BLOCK) // QUERY), many])
    *saved, after = forward_layers(
        weight_table, spans, norm_params, doc_row, hidden, tiles, pairs
    )
    out_rows = lax.all_to_all(
        after.reshape(residual_in.shape), "seq", split_axis=0, concat_axis=0, tiled=True
    )
    lower, held, norm_part = backward_layers(
        weight_table, grad_table, spans, counts, norm_params, doc_row, upper, saved, tiles,
    )
    owned, grad_rows, norm_sum, squares = reduce_end(
        held, lower.reshape(residual_in.shape), norm_part
    )
    (
        clipped, new_first, new_second, new_weight, new_copies, input_grad, residual_out,
        total, norm_clip, new_norm_f, new_norm_s, new_norm,
    ) = finish_step(
        counts, owned, master_tiles, first_tiles, second_tiles, grad_rows, out_rows, squares,
        norm_sum, norm_params, norm_first, norm_second,
    )
    return (
        residual_out,
        input_grad,
        clipped,
        total[0, :1],
        new_first,
        new_second,
        new_weight,
        new_copies,
        norm_clip,
        new_norm_f,
        new_norm_s,
        new_norm,
    )


def local(residual_in, *others):
    whole_rows = residual_in.shape[0] == lax.axis_size("seq")
    step = local_by_rows if whole_rows else local_by_heads
    return step(residual_in, *others)


def solution(mesh):
    by_rows = P("rows", "seq", None)
    by_slots = P("seq", None, None)
    return jax.shard_map(
        local,
        mesh=mesh,
        in_specs=(
            by_rows, by_rows, P("rows", None), P(), by_slots, by_slots, by_slots, P(), P(), P(),
        ),
        out_specs=(
            by_rows, by_rows, by_slots, P(), by_slots, by_slots, by_slots, by_slots,
            P(), P(), P(), P(),
        ),
        check_vma=False,
    )
```

```python
import jax
import jax.numpy as jnp
from jax import lax
from jax.experimental import pallas as pl
from jax.experimental.pallas import tpu as pltpu

from jax.sharding import PartitionSpec as P

HEADS = 8
LAYERS = 2
STEP = 5


def norm_layer(values, gain, offset):
    center = values - jnp.mean(values, axis=-1, keepdims=True)
    spread = jnp.mean(center * center, axis=-1, keepdims=True)
    return center * lax.rsqrt(spread + 1e-05) * gain + offset


def matmul(left, right):
    return jnp.dot(left, right, preferred_element_type=jnp.float32)


def left_product(left, right):
    return lax.dot_general(
        left, right, (((0,), (0,)), ((), ())), preferred_element_type=jnp.float32
    )


def right_product(left, right):
    return lax.dot_general(
        left, right, (((1,), (1,)), ((), ())), preferred_element_type=jnp.float32
    )


def assemble(weight_tiles, layer_number):
    first_tile = 48 * layer_number
    model_width = weight_tiles.shape[1]
    qkv_weight = (
        weight_tiles[first_tile : first_tile + 12].transpose(1, 0, 2).reshape(model_width, -1)
    )
    out_weight = (
        weight_tiles[first_tile + 12 : first_tile + 16].transpose(1, 0, 2).reshape(model_width, -1)
    )
    up_weight = (
        weight_tiles[first_tile + 16 : first_tile + 32].transpose(1, 0, 2).reshape(model_width, -1)
    )
    down_block = weight_tiles[first_tile + 32 : first_tile + 48].reshape(4, 4, model_width, -1)
    down_weight = down_block.transpose(0, 2, 1, 3).reshape(4 * model_width, model_width)
    return (qkv_weight, out_weight, up_weight, down_weight)


def split_tiles(qkv_grad, out_grad, up_grad, down_grad, tile_width):
    model_width = qkv_grad.shape[0]
    pieces = [
        qkv_grad.reshape(model_width, -1, tile_width).transpose(1, 0, 2),
        out_grad.reshape(model_width, -1, tile_width).transpose(1, 0, 2),
        up_grad.reshape(model_width, -1, tile_width).transpose(1, 0, 2),
        down_grad.reshape(4, model_width, 4, tile_width)
        .transpose(0, 2, 1, 3)
        .reshape(16, model_width, tile_width),
    ]
    return jnp.concatenate(pieces, axis=0)


def attend_forward(queries, key_rows, value_rows, doc_ids, block_rows, scale):
    length = queries.shape[0]

    def one_block(number):
        first_row = number * block_rows
        query_block = lax.dynamic_slice_in_dim(queries, first_row, block_rows, 0)
        doc_block = lax.dynamic_slice_in_dim(doc_ids, first_row, block_rows, 0)
        same_doc = doc_block[:, None] == doc_ids[None, :]
        scores = jnp.where(same_doc, right_product(query_block, key_rows) * scale, -1e30)
        largest = jnp.max(scores, axis=-1, keepdims=True)
        row_total = jnp.sum(jnp.exp(scores - largest), axis=-1, keepdims=True)
        logsum = largest + jnp.log(row_total)
        weights = jnp.where(same_doc, jnp.exp(scores - logsum), 0.0).astype(jnp.bfloat16)
        return (matmul(weights, value_rows).astype(jnp.bfloat16), logsum[:, 0])

    outputs, logsums = lax.map(one_block, jnp.arange(length // block_rows))
    return (outputs.reshape(length, -1), logsums.reshape(length))


def attend_backward(queries, key_rows, value_rows, doc_ids, logsums, out_grads, block_rows, scale):
    length, head_dim = queries.shape

    def one_block(carry, number):
        key_grad, value_grad = carry
        first_row = number * block_rows
        query_block = lax.dynamic_slice_in_dim(queries, first_row, block_rows, 0)
        doc_block = lax.dynamic_slice_in_dim(doc_ids, first_row, block_rows, 0)
        logsum_block = lax.dynamic_slice_in_dim(logsums, first_row, block_rows, 0)
        grad_block = lax.dynamic_slice_in_dim(out_grads, first_row, block_rows, 0)
        same_doc = doc_block[:, None] == doc_ids[None, :]
        scores = jnp.where(same_doc, right_product(query_block, key_rows) * scale, -1e30)
        probs = jnp.where(same_doc, jnp.exp(scores - logsum_block[:, None]), 0.0)
        prob_grad = right_product(grad_block, value_rows)
        inner_sum = jnp.sum(probs * prob_grad, axis=-1, keepdims=True)
        score_grad = (probs * (prob_grad - inner_sum)).astype(jnp.bfloat16)
        query_grad = matmul(score_grad, key_rows) * scale
        key_grad = key_grad + left_product(score_grad, query_block) * scale
        value_grad = value_grad + left_product(probs.astype(jnp.bfloat16), grad_block)
        return ((key_grad, value_grad), query_grad)

    zeros_block = jnp.zeros((length, head_dim), jnp.float32)
    (key_grad, value_grad), query_grads = lax.scan(
        one_block, (zeros_block, zeros_block), jnp.arange(length // block_rows)
    )
    stacked = jnp.stack([query_grads.reshape(length, head_dim), key_grad, value_grad], axis=1)
    return stacked.astype(jnp.bfloat16)


def adamw(weight, grad, first, second, learn_rate, correction):
    first = 0.5 * first + 0.5 * grad
    second = 0.5 * second + 0.5 * grad * grad
    update = first / correction / (jnp.sqrt(second / correction) + 1e-08)
    return (weight - learn_rate * (update + 0.01 * weight), first, second)


def local_by_heads(
    residual_in,
    cotangent,
    segments,
    owners,
    master_tiles,
    first_tiles,
    second_tiles,
    norm_params,
    norm_first,
    norm_second,
):
    local_rows, positions, model_width = residual_in.shape
    seq_devices = lax.axis_size("seq")
    seq_index = lax.axis_index("seq")
    head_dim = model_width // HEADS
    group_count = seq_devices // HEADS
    group_rows = local_rows // group_count
    length = positions * seq_devices
    block_rows = min(512, length)
    scale = head_dim ** (-0.5)
    tile_total = owners.shape[0]
    capacity = master_tiles.shape[0]
    tile_width = master_tiles.shape[2]
    places = jnp.arange(tile_total, dtype=jnp.int32)
    before = (owners[None, :] == owners[:, None]) & (places[None, :] < places[:, None])
    ranks = jnp.sum(before.astype(jnp.int32), axis=1)
    slot_ids = owners * capacity + ranks
    local_slots = jnp.arange(capacity, dtype=jnp.int32)
    matches = (owners[:, None] == seq_index) & (ranks[:, None] == local_slots[None, :])
    chosen = jnp.sum(jnp.where(matches, places[:, None], 0), axis=0)
    present = jnp.any(matches, axis=0)
    copies = lax.all_gather(master_tiles.astype(jnp.bfloat16), "seq", axis=0, tiled=True)
    weight_tiles = jnp.take(copies, slot_ids, axis=0)
    my_group = seq_index // HEADS
    doc_rows = lax.dynamic_slice_in_dim(segments, my_group * group_rows, group_rows, 0)
    hidden = residual_in.reshape(-1, model_width)
    saved = []
    for layer_number in range(LAYERS):
        qkv_weight, out_weight, up_weight, down_weight = assemble(weight_tiles, layer_number)
        params = norm_params[4 * layer_number : 4 * layer_number + 4]
        normed, first_pull = jax.vjp(norm_layer, hidden, params[0], params[1])
        normed_low = normed.astype(jnp.bfloat16)
        packed = matmul(normed_low, qkv_weight).astype(jnp.bfloat16)
        outgoing = packed.reshape(group_count, group_rows, positions, 3, HEADS, head_dim)
        outgoing = outgoing.transpose(0, 4, 1, 2, 3, 5).reshape(
            seq_devices, group_rows, positions * 3 * head_dim
        )
        arrived = lax.all_to_all(outgoing, "seq", split_axis=0, concat_axis=2, tiled=True).reshape(
            group_rows, length, 3, head_dim
        )

        def forward_item(items):
            return attend_forward(
                items[0][:, 0], items[0][:, 1], items[0][:, 2], items[1], block_rows, scale
            )

        attended, logsums = lax.map(forward_item, (arrived, doc_rows))
        returning = attended.reshape(1, group_rows, seq_devices, positions * head_dim)
        mixed = lax.all_to_all(returning, "seq", split_axis=2, concat_axis=0, tiled=True)
        mixed = (
            mixed.reshape(group_count, HEADS, group_rows, positions, head_dim)
            .transpose(0, 2, 3, 1, 4)
            .reshape(-1, model_width)
        )
        middle = hidden + matmul(mixed, out_weight)
        normed_two, second_pull = jax.vjp(norm_layer, middle, params[2], params[3])
        normed_two_low = normed_two.astype(jnp.bfloat16)
        inner = matmul(normed_two_low, up_weight)
        active = jax.nn.gelu(inner).astype(jnp.bfloat16)
        hidden = middle + matmul(active, down_weight)
        saved.append(
            (
                first_pull,
                normed_low,
                arrived,
                logsums,
                mixed,
                second_pull,
                normed_two_low,
                inner,
                active,
            )
        )
    grad = cotangent.reshape(-1, model_width)
    tile_parts = [None] * LAYERS
    norm_parts = [None] * LAYERS
    for layer_number in reversed(range(LAYERS)):
        (
            first_pull,
            normed_low,
            arrived,
            logsums,
            mixed,
            second_pull,
            normed_two_low,
            inner,
            active,
        ) = saved[layer_number]
        qkv_weight, out_weight, up_weight, down_weight = assemble(weight_tiles, layer_number)
        grad_low = grad.astype(jnp.bfloat16)
        down_grad = left_product(active, grad_low)
        active_grad = right_product(grad_low, down_weight)
        inner_grad = jax.vjp(jax.nn.gelu, inner)[1](active_grad)[0].astype(jnp.bfloat16)
        up_grad = left_product(normed_two_low, inner_grad)
        middle_part, gain_two, offset_two = second_pull(right_product(inner_grad, up_weight))
        middle_grad = grad + middle_part
        middle_low = middle_grad.astype(jnp.bfloat16)
        out_grad = left_product(mixed, middle_low)
        mixed_grad = right_product(middle_low, out_weight).astype(jnp.bfloat16)
        sending = mixed_grad.reshape(group_count, group_rows, positions, HEADS, head_dim)
        sending = sending.transpose(0, 3, 1, 2, 4).reshape(
            seq_devices, group_rows, positions * head_dim
        )
        head_grads = lax.all_to_all(
            sending, "seq", split_axis=0, concat_axis=2, tiled=True
        ).reshape(group_rows, length, head_dim)

        def backward_item(items):
            arrived_row, doc_row, logsum_row, grad_row = items
            return attend_backward(
                arrived_row[:, 0],
                arrived_row[:, 1],
                arrived_row[:, 2],
                doc_row,
                logsum_row,
                grad_row,
                block_rows,
                scale,
            )

        packed_grads = lax.map(backward_item, (arrived, doc_rows, logsums, head_grads))
        coming = lax.all_to_all(
            packed_grads.reshape(1, group_rows, seq_devices, positions * 3 * head_dim),
            "seq",
            split_axis=2,
            concat_axis=0,
            tiled=True,
        )
        qkv_grad = coming.reshape(group_count, HEADS, group_rows, positions, 3, head_dim)
        qkv_grad = qkv_grad.transpose(0, 2, 3, 4, 1, 5).reshape(-1, 3 * model_width)
        qkv_weight_grad = left_product(normed_low, qkv_grad)
        input_part, gain_one, offset_one = first_pull(right_product(qkv_grad, qkv_weight))
        grad = middle_grad + input_part
        tile_parts[layer_number] = split_tiles(
            qkv_weight_grad, out_grad, up_grad, down_grad, tile_width
        )
        norm_parts[layer_number] = jnp.stack([gain_one, offset_one, gain_two, offset_two])
    dense = jnp.concatenate(tile_parts, axis=0)
    norm_part = jnp.concatenate(norm_parts, axis=0)
    piece = lax.psum_scatter(
        dense.reshape(-1, tile_width), ("rows", "seq"), scatter_dimension=0, tiled=True
    )
    squares, norm_sum = lax.psum((jnp.sum(piece * piece), norm_part), ("rows", "seq"))
    summed = (
        lax.all_gather(piece.astype(jnp.bfloat16), ("rows", "seq"), axis=0, tiled=True)
        .astype(piece.dtype)
        .reshape(dense.shape)
    )
    owned = jnp.take(summed, chosen, axis=0)
    keep = present[:, None, None]
    owned = jnp.where(keep, owned, 0.0)
    total = jnp.sqrt(squares + jnp.sum(norm_sum * norm_sum))
    factor = 1.0 / jnp.maximum(total, 1.0)
    clipped = owned * factor
    norm_clip = norm_sum * factor
    correction = 1.0 - 0.5**STEP
    new_weight, new_first_rows, new_second_rows = adamw(
        master_tiles, clipped, first_tiles, second_tiles, 0.05, correction
    )
    new_weight = jnp.where(keep, new_weight, 0.0)
    new_first_rows = jnp.where(keep, new_first_rows, 0.0)
    new_second_rows = jnp.where(keep, new_second_rows, 0.0)
    new_norm, new_norm_f, new_norm_s = adamw(
        norm_params, norm_clip, norm_first, norm_second, 0.25, correction
    )
    return (
        hidden.reshape(local_rows, positions, model_width),
        grad.reshape(local_rows, positions, model_width),
        clipped,
        total[None],
        new_first_rows,
        new_second_rows,
        new_weight,
        new_weight.astype(jnp.bfloat16),
        norm_clip,
        new_norm_f,
        new_norm_s,
        new_norm,
    )


F32 = jnp.float32
BF16 = jnp.bfloat16
BLOCK = 256
DENSE = 512
DENSE_BACK = 512
QUERY = 128
UNROLL = 4
UNROLL_BACK = 4
VMEM_BYTES = 60 * 1024 * 1024


def dot_nn(left, right):
    return jnp.dot(left, right, preferred_element_type=F32)


def dot_nt(left, right, precision=None):
    return lax.dot_general(
        left, right, (((1,), (1,)), ((), ())), preferred_element_type=F32, precision=precision
    )


def dot_tn(left, right):
    return lax.dot_general(left, right, (((0,), (0,)), ((), ())), preferred_element_type=F32)


def rows_of(number, size=BLOCK):
    return pl.ds(pl.multiple_of(number * size, size), size)


def normalized(values):
    center = values - jnp.mean(values, axis=-1, keepdims=True)
    spread = jnp.mean(center * center, axis=-1, keepdims=True)
    scale = lax.rsqrt(spread + 1e-05)
    return center * scale, scale


GELU_A = 0.7978845608028654
GELU_B = 0.044715


def gelu_value(inner):
    return 0.5 * inner * (1.0 + jnp.tanh(GELU_A * (inner + GELU_B * inner * inner * inner)))


def gelu_both(inner):
    square = inner * inner
    bent = jnp.tanh(inner * (GELU_A + GELU_A * GELU_B * square))
    half = 0.5 + 0.5 * bent
    slope = half + 0.5 * inner * (1.0 - bent * bent) * (GELU_A + 3.0 * GELU_A * GELU_B * square)
    return inner * half, slope


def weight_copy(tiles, table, number, target, column, row, sem):
    depth, width = tiles.shape[1], tiles.shape[2]
    rows = pl.ds(pl.multiple_of(row * depth, depth), depth)
    columns = pl.ds(pl.multiple_of(column * width, width), width)
    return pltpu.make_async_copy(
        tiles.at[table[number]], target.at[rows, columns], sem.at[number]
    )


def weight_group(tiles, table, first, count, per_row, target, sem, act):
    @pl.loop(0, count)
    def _(j):
        copy = weight_copy(
            tiles, table, first + j, target, lax.rem(j, per_row), lax.div(j, per_row), sem
        )
        getattr(copy, act)()


def lane_is_first(shape):
    return lax.broadcasted_iota(jnp.int32, shape, 1) < shape[1] // 2


def stacked(values, lanes_first):
    zero = jnp.zeros_like(values)
    return jnp.concatenate(
        [
            jnp.where(lanes_first, values, zero).astype(BF16),
            jnp.where(lanes_first, zero, values).astype(BF16),
        ],
        axis=0,
    )


def forward_kernel(
    table, spans, norms, doc_row, hidden, tiles,
    below_out, normed_out, packed_out, mixed_out, logsum_out, middle_out, normed_two_out,
    hidden_out,
    w_qkv, w_out, w_up, w_down, flow, normed, packed, mixed, logcol, logsum, middle, normed_two,
    doc_col, w_sem, o_sem,
):
    length, width = hidden.shape
    blocks = length // DENSE
    pairs = mixed.shape[0]
    lanes = mixed.shape[2]
    groups = (
        (0, 12, 12, w_qkv), (12, 4, 4, w_out), (16, 16, 16, w_up), (32, 16, 4, w_down),
    )

    def fetch(layer, group, act):
        first, count, per_row, target = groups[group]
        weight_group(
            tiles, table, 48 * layer + first, count, per_row, target.at[layer], w_sem, act
        )

    for layer in range(LAYERS):
        for group in range(4):
            fetch(layer, group, "start")
    outs = (
        (normed, normed_out), (packed, packed_out), (mixed, mixed_out), (logsum, logsum_out),
        (middle, middle_out), (normed_two, normed_two_out), (flow, below_out),
    )

    def flush(number, layer):
        return pltpu.make_async_copy(outs[number][0], outs[number][1].at[layer], o_sem.at[number])

    def forward_one(layer):
        def again(number):
            pl.when(layer > 0)(lambda: flush(number, layer).wait())

        flush(6, layer).start()
        again(0)
        again(1)
        fetch(layer, 0, "wait")

        @pl.loop(0, length // 512)
        def _(number):
            here = rows_of(number, 512)
            unit, _ = normalized(flow[here, :])
            low = (unit * norms[pl.ds(4 * layer + 0, 1), :] + norms[pl.ds(4 * layer + 1, 1), :]).astype(BF16)
            normed[here, :] = low
            product = dot_nn(low, w_qkv[layer])
            for j in range(3 * pairs):
                packed[j, here, :] = product[:, j * lanes : (j + 1) * lanes].astype(BF16)

        flush(0, layer).start()
        flush(1, layer).start()
        again(2)
        lane_ids = lax.broadcasted_iota(jnp.int32, (QUERY, lanes), 1)
        first_half = lane_is_first((QUERY, lanes))

        @pl.loop(0, length // QUERY)
        def _(number):
            here = rows_of(number, QUERY)
            low_key = spans[0, number]
            key_count = spans[1, number]
            doc_here = doc_col[here, 0:1]

            def with_keys(many):
                keys_here = pl.ds(pl.multiple_of(low_key * QUERY, QUERY), many * BLOCK)
                same = doc_here == doc_row[0:1, keys_here]
                same = jnp.concatenate([same, same], axis=0)

                def score(pair):
                    heads = stacked(packed[pair, here, :].astype(F32) * 0.125, first_half)
                    return dot_nt(heads, packed[pairs + pair, keys_here, :])

                def settle(scores):
                    scores = jnp.where(same, scores, -1e30)
                    top = jnp.max(scores, axis=-1, keepdims=True)
                    weights = jnp.exp(scores - top)
                    total = jnp.sum(weights, axis=-1, keepdims=True)
                    return weights.astype(BF16), total, top + jnp.log(total)

                def finish(pair, weights, total, logs):
                    result = dot_nn(weights, packed[2 * pairs + pair, keys_here, :]) / total
                    mixed[pair, here, :] = jnp.where(
                        first_half, result[:QUERY], result[QUERY:]
                    ).astype(BF16)
                    old = logcol[here, :]
                    old = jnp.where(lane_ids == 8 * pair, logs[:QUERY], old)
                    logcol[here, :] = jnp.where(lane_ids == 8 * pair + 1, logs[QUERY:], old)

                waiting = None
                ahead = score(0)
                for pair in range(pairs):
                    now = ahead
                    if pair + 1 < pairs:
                        ahead = score(pair + 1)
                    done = settle(now)
                    if waiting is not None:
                        finish(pair - 1, *waiting)
                    waiting = done
                finish(pairs - 1, *waiting)


            for many in range(1, length // BLOCK + 1):
                pl.when(key_count == many)(lambda many=many: with_keys(many))

        flush(2, layer).start()
        turned = logcol[...].T
        again(3)
        for pair in range(pairs):
            logsum[pair, :, :] = turned[8 * pair : 8 * pair + 8, :]
        flush(3, layer).start()
        fetch(layer, 1, "wait")
        fetch(layer, 2, "wait")
        fetch(layer, 3, "wait")
        again(4)
        again(5)
        flush(6, layer).wait()
        chunk = width

        @pl.loop(0, length // 1024)
        def _(number):
            here = rows_of(number, 1024)
            side_by_side = jnp.concatenate([mixed[pair, here, :] for pair in range(pairs)], axis=1)
            mid = flow[here, :] + dot_nn(side_by_side, w_out[layer])
            middle[here, :] = mid
            unit, _ = normalized(mid)
            low = (unit * norms[pl.ds(4 * layer + 2, 1), :] + norms[pl.ds(4 * layer + 3, 1), :]).astype(BF16)
            normed_two[here, :] = low
            total = mid
            for c in range(w_up.shape[2] // chunk):
                part = slice(c * chunk, (c + 1) * chunk)
                active = gelu_value(dot_nn(low, w_up[layer, :, part])).astype(BF16)
                total = total + dot_nn(active, w_down[layer, part, :])
            flow[here, :] = total

        flush(4, layer).start()
        flush(5, layer).start()

    flow[...] = hidden[...].astype(F32)
    fill_columns(doc_row, doc_col)

    @pl.loop(0, LAYERS)
    def _(layer):
        forward_one(layer)

    last = pltpu.make_async_copy(normed, hidden_out, o_sem.at[7])
    flush(0, LAYERS - 1).wait()
    normed[...] = flow[...].astype(BF16)
    last.start()
    for number in range(1, 6):
        flush(number, LAYERS - 1).wait()
    last.wait()


def fill_columns(doc_row, doc_col):
    lanes = doc_col.shape[1]

    @pl.loop(0, doc_col.shape[0] // lanes)
    def _(number):
        here = rows_of(number, lanes)
        spread = jnp.broadcast_to(doc_row[0:1, here].astype(F32), (lanes, lanes))
        doc_col[here, :] = spread.T.astype(jnp.int32)


def vmem_spec():
    return pl.BlockSpec(memory_space=pltpu.VMEM)


def any_spec():
    return pl.BlockSpec(memory_space=pl.ANY)


def smem_spec():
    return pl.BlockSpec(memory_space=pltpu.SMEM)


def forward_layers(table, spans, norms, doc_row, hidden, tiles, pairs):
    length, width = hidden.shape
    lanes = tiles.shape[2]
    one = (
        ((length, width), F32),
        ((length, width), BF16),
        ((3 * pairs, length, lanes), BF16),
        ((pairs, length, lanes), BF16),
        ((pairs, 8, length), F32),
        ((length, width), F32),
        ((length, width), BF16),
    )
    shapes = [((LAYERS, *s), d) for s, d in one] + [((length, width), BF16)]
    keep = [pltpu.VMEM(s, d) for s, d in one]
    return pl.pallas_call(
        forward_kernel,
        name="forward_layers",
        out_shape=[jax.ShapeDtypeStruct(s, d) for s, d in shapes],
        in_specs=[smem_spec(), smem_spec()] + [vmem_spec()] * 3 + [any_spec()],
        out_specs=[any_spec()] * len(shapes),
        scratch_shapes=[
            pltpu.VMEM((LAYERS, width, 3 * width), BF16),
            pltpu.VMEM((LAYERS, width, width), BF16),
            pltpu.VMEM((LAYERS, width, 4 * width), BF16),
            pltpu.VMEM((LAYERS, 4 * width, width), BF16),
            *keep[:4],
            pltpu.VMEM((length, lanes), F32),
            *keep[4:],
            pltpu.VMEM((length, lanes), jnp.int32),
            pltpu.SemaphoreType.DMA((48 * LAYERS,)),
            pltpu.SemaphoreType.DMA((8,)),
        ],
        compiler_params=pltpu.CompilerParams(vmem_limit_bytes=VMEM_BYTES),
        cost_estimate=pl.CostEstimate(
            flops=length * width * width * 52, bytes_accessed=40 * 2**20,
            transcendentals=length * length * 8,
        ),
    )(table, spans, norms, doc_row, hidden, tiles)


def backward_kernel(
    table, aims, spans, counts, norms, doc_row, upper_in,
    below_in, normed_in, packed_in, mixed_in, logsum_in, middle_in, normed_two_in, tiles,
    grad_out, tile_grads, norm_grads,
    w_qkv, w_out, w_up, w_down,
    flow, normed, packed, mixed, logsum, middle, normed_two, hidden,
    active, inner_grad, grad_low, mid_grad, mid_low, mixed_grad, delta, packed_grad,
    key_sum, value_sum, staged, blank, doc_col, selector,
    w_sem, i_sem, t_sem, z_sem, o_sem,
):
    length, width = flow.shape
    blocks = length // DENSE_BACK
    pairs, lanes = mixed.shape[0], mixed.shape[2]
    groups = (
        (0, 12, 12, w_qkv), (12, 4, 4, w_out), (16, 16, 16, w_up), (32, 16, 4, w_down),
    )
    ins = (
        (normed_two_in, normed_two), (middle_in, middle), (mixed_in, mixed),
        (packed_in, packed), (logsum_in, logsum), (below_in, hidden), (normed_in, normed),
    )

    def load(number, layer):
        return pltpu.make_async_copy(ins[number][0].at[layer], ins[number][1], i_sem.at[number])

    def fetch(group, layer, act):
        first, count, per_row, target = groups[group]
        weight_group(tiles, table, 48 * layer + first, count, per_row, target, w_sem, act)

    def early(layer):
        load(0, layer).start()
        fetch(2, layer, "start")
        fetch(3, layer, "start")
        load(1, layer).start()
        fetch(1, layer, "start")
        load(2, layer).start()

    def late(layer):
        load(3, layer).start()
        load(4, layer).start()

    take = pltpu.make_async_copy(upper_in, grad_low, o_sem.at[0])
    take.start()
    early(LAYERS - 1)
    late(LAYERS - 1)
    fetch(0, LAYERS - 1, "start")
    load(5, LAYERS - 1).start()
    load(6, LAYERS - 1).start()

    def blank_copies(act):
        capacity = tile_grads.shape[0] // counts.shape[0]
        quarter = capacity // 4

        @pl.loop(0, counts.shape[0])
        def _(owner):
            @pl.loop(counts[owner], capacity)
            def _(place):
                core, depth_z, part = lax.rem(owner, 2), lax.div(owner, 2), lax.div(place, quarter)
                low_bit, high_bit = lax.rem(part, 2), lax.div(part, 2)
                major = low_bit + core * (high_bit - low_bit)
                minor = high_bit + core * (low_bit - high_bit)
                index = lax.rem(place, quarter) * 32 + core * 16 + major * 8 + minor * 4 + depth_z
                getattr(
                    pltpu.make_async_copy(blank, tile_grads.at[index], z_sem.at[index]), act
                )()

    norm_grads[...] = jnp.zeros_like(norm_grads)
    blank[...] = jnp.zeros_like(blank)
    fill_columns(doc_row, doc_col)
    which = lax.broadcasted_iota(jnp.int32, selector.shape, 0)
    lane = lax.broadcasted_iota(jnp.int32, selector.shape, 1)
    head_dim = width // HEADS
    own_head = 2 * lax.div(which, 8) + lax.rem(which, 8)
    fits = (lax.rem(which, 8) < 2) & (lax.div(lane, head_dim) == own_head)
    selector[...] = jnp.where(fits, 1.0, 0.0).astype(BF16)
    take.wait()
    flow[...] = grad_low[...].astype(F32)
    chunk = 2 * width
    chunks = w_up.shape[1] // chunk

    def send_tile(place, layer):
        return pltpu.make_async_copy(
            staged.at[place], tile_grads.at[aims[48 * layer + place]], t_sem.at[place]
        )

    def settle_tiles(layer):
        @pl.loop(0, 48)
        def _(place):
            send_tile(place, layer).wait()

    def backward_one(layer):
        def norm_back(values, out_grad, gain, gain_row):
            unit, scale = normalized(values)
            sums = (
                jnp.sum(out_grad * unit, axis=0, keepdims=True),
                jnp.sum(out_grad, axis=0, keepdims=True),
            )
            for which in range(LAYERS):

                @pl.when(layer == which)
                def _(which=which):
                    for side in range(2):
                        row = 4 * which + gain_row + side
                        norm_grads[row : row + 1, :] += sums[side]

            turned = out_grad * gain
            average = jnp.mean(turned, axis=-1, keepdims=True)
            along = jnp.mean(turned * unit, axis=-1, keepdims=True)
            return scale * (turned - average - unit * along)

        load(0, layer).wait()
        fetch(2, layer, "wait")
        fetch(3, layer, "wait")
        load(1, layer).wait()
        fetch(1, layer, "wait")
        load(2, layer).wait()

        @pl.loop(0, blocks)
        def _(number):
            here = rows_of(number, DENSE_BACK)
            upper = flow[here, :]
            low = upper.astype(BF16)
            grad_low[here, :] = low
            normed_here = normed_two[here, :]
            total = jnp.zeros((DENSE_BACK, width), F32)
            for c in range(chunks):
                part = slice(c * chunk, (c + 1) * chunk)
                value, slope = gelu_both(dot_nn(normed_here, w_up[:, part]))
                active[here, part] = value.astype(BF16)
                inner = (slope * dot_nt(low, w_down[part, :])).astype(BF16)
                inner_grad[here, part] = inner
                total = total + dot_nt(inner, w_up[:, part])
            mid = upper + norm_back(middle[here, :], total, norms[pl.ds(4 * layer + 2, 1), :], 2)
            mid_grad[here, :] = mid
            mid_here = mid.astype(BF16)
            mid_low[here, :] = mid_here
            back = dot_nt(mid_here, w_out[...]).astype(BF16)
            for pair in range(pairs):
                mixed_grad[pair, here, :] = back[:, pair * lanes : (pair + 1) * lanes]
            side_by_side = jnp.concatenate([mixed[pair, here, :] for pair in range(pairs)], axis=1)
            both = side_by_side.astype(F32) * back.astype(F32)
            high = both.astype(BF16)
            rest = (both - high.astype(F32)).astype(BF16)
            sums = dot_nt(selector[...], high) + dot_nt(selector[...], rest)
            for pair in range(pairs):
                delta[pair, :, here] = sums[8 * pair : 8 * pair + 8, :]

        pl.when(layer < LAYERS - 1)(lambda: settle_tiles(layer + 1))

        def emit(block, first):
            for c in range(block.shape[1] // lanes):
                staged[first + c] = block[:, c * lanes : (c + 1) * lanes].astype(BF16)
                send_tile(first + c, layer).start()

        @pl.loop(0, 4)
        def _(c):
            part = rows_of(c, width)
            emit(dot_tn(active[:, part], grad_low[...]), 32 + 4 * c)
            emit(dot_tn(normed_two[...], inner_grad[:, part]), 16 + 4 * c)

        side_by_side = jnp.concatenate([mixed[pair] for pair in range(pairs)], axis=1)
        emit(dot_tn(side_by_side, mid_low[...]), 12)
        pl.when(layer > 0)(lambda: early(layer - 1))
        pl.when(layer == LAYERS - 1)(lambda: blank_copies("start"))
        load(3, layer).wait()
        load(4, layer).wait()
        first_half = lane_is_first((QUERY, lanes))

        key_sum[...] = jnp.zeros_like(key_sum)
        value_sum[...] = jnp.zeros_like(value_sum)

        @pl.loop(0, length // QUERY)
        def _(number):
            here = rows_of(number, QUERY)
            low_key = spans[0, number]
            key_count = spans[1, number]
            doc_here = doc_row[0:1, here]
            doc_here = jnp.concatenate([doc_here, doc_here], axis=1)

            def with_keys(many):
                keys_here = pl.ds(pl.multiple_of(low_key * QUERY, QUERY), many * BLOCK)
                same = doc_col[keys_here, 0:1] == doc_here

                def score(pair):
                    heads = stacked(packed[pair, here, :].astype(F32) * 0.125, first_half)
                    outs = stacked(mixed_grad[pair, here, :].astype(F32), first_half)
                    return (
                        heads,
                        outs,
                        dot_nt(packed[pairs + pair, keys_here, :], heads),
                        dot_nt(packed[2 * pairs + pair, keys_here, :], outs),
                    )

                def settle(pair, heads, outs, scores, from_values):
                    logs = jnp.concatenate([logsum[pair, 0:1, here], logsum[pair, 1:2, here]], axis=1)
                    means = jnp.concatenate([delta[pair, 0:1, here], delta[pair, 1:2, here]], axis=1)
                    weights = jnp.exp(jnp.where(same, scores - logs, -1e30))
                    score_grad = (weights * (from_values - means)).astype(BF16)
                    return heads, outs, weights.astype(BF16), score_grad

                def finish(pair, heads, outs, weights, score_grad):
                    value_sum[pair, keys_here, :] += dot_nn(weights, outs)
                    key_sum[pair, keys_here, :] += dot_nn(score_grad, heads)
                    query_part = dot_tn(score_grad, packed[pairs + pair, keys_here, :]) * 0.125
                    packed_grad[pair, here, :] = jnp.where(
                        first_half, query_part[:QUERY], query_part[QUERY:]
                    ).astype(BF16)

                waiting = None
                ahead = score(0)
                for pair in range(pairs):
                    now = ahead
                    if pair + 1 < pairs:
                        ahead = score(pair + 1)
                    done = settle(pair, *now)
                    if waiting is not None:
                        finish(pair - 1, *waiting)
                    waiting = done
                finish(pairs - 1, *waiting)

            for many in range(1, length // BLOCK + 1):
                pl.when(key_count == many)(lambda many=many: with_keys(many))

        for pair in range(pairs):
            packed_grad[pairs + pair] = key_sum[pair].astype(BF16)
            packed_grad[2 * pairs + pair] = value_sum[pair].astype(BF16)

        pl.when(layer > 0)(lambda: late(layer - 1))
        fetch(0, layer, "wait")
        load(5, layer).wait()
        load(6, layer).wait()

        @pl.loop(0, blocks)
        def _(number):
            here = rows_of(number, DENSE_BACK)
            wide = jnp.concatenate([packed_grad[j, here, :] for j in range(3 * pairs)], axis=1)
            total = dot_nt(wide, w_qkv[...])
            flow[here, :] = mid_grad[here, :] + norm_back(
                hidden[here, :], total, norms[pl.ds(4 * layer + 0, 1), :], 0
            )

        @pl.loop(0, 3)
        def _(c):
            wide = jnp.concatenate([packed_grad[pairs * c + j] for j in range(pairs)], axis=1)
            emit(dot_tn(normed[...], wide), 4 * c)

        @pl.when(layer > 0)
        def _():
            fetch(0, layer - 1, "start")
            load(5, layer - 1).start()
            load(6, layer - 1).start()

    @pl.loop(0, LAYERS)
    def _(step):
        backward_one(LAYERS - 1 - step)

    flush = pltpu.make_async_copy(grad_low, grad_out, o_sem.at[0])
    grad_low[...] = flow[...].astype(BF16)
    flush.start()
    settle_tiles(0)
    flush.wait()
    blank_copies("wait")


def backward_layers(
    table, aims, spans, counts, norms, doc_row, upper, saved, tiles
):
    length, width = upper.shape
    lanes = tiles.shape[2]
    pairs = width // lanes
    slots = tiles.shape[0]
    return pl.pallas_call(
        backward_kernel,
        name="backward_layers",
        out_shape=[
            jax.ShapeDtypeStruct((length, width), BF16),
            jax.ShapeDtypeStruct(tiles.shape, BF16),
            jax.ShapeDtypeStruct(norms.shape, F32),
        ],
        in_specs=[smem_spec()] * 4 + [vmem_spec()] * 2 + [any_spec()] * 9,
        out_specs=[any_spec(), any_spec(), vmem_spec()],
        scratch_shapes=[
            pltpu.VMEM((width, 3 * width), BF16),
            pltpu.VMEM((width, width), BF16),
            pltpu.VMEM((width, 4 * width), BF16),
            pltpu.VMEM((4 * width, width), BF16),
            pltpu.VMEM((length, width), F32),
            pltpu.VMEM((length, width), BF16),
            pltpu.VMEM((3 * pairs, length, lanes), BF16),
            pltpu.VMEM((pairs, length, lanes), BF16),
            pltpu.VMEM((pairs, 8, length), F32),
            pltpu.VMEM((length, width), F32),
            pltpu.VMEM((length, width), BF16),
            pltpu.VMEM((length, width), F32),
            pltpu.VMEM((length, 4 * width), BF16),
            pltpu.VMEM((length, 4 * width), BF16),
            pltpu.VMEM((length, width), BF16),
            pltpu.VMEM((length, width), F32),
            pltpu.VMEM((length, width), BF16),
            pltpu.VMEM((pairs, length, lanes), BF16),
            pltpu.VMEM((pairs, 8, length), F32),
            pltpu.VMEM((3 * pairs, length, lanes), BF16),
            pltpu.VMEM((pairs, length, lanes), F32),
            pltpu.VMEM((pairs, length, lanes), F32),
            pltpu.VMEM((48, width, lanes), BF16),
            pltpu.VMEM((width, lanes), BF16),
            pltpu.VMEM((length, lanes), jnp.int32),
            pltpu.VMEM((8 * pairs, width), BF16),
            pltpu.SemaphoreType.DMA((48 * LAYERS,)),
            pltpu.SemaphoreType.DMA((7,)),
            pltpu.SemaphoreType.DMA((48,)),
            pltpu.SemaphoreType.DMA((slots,)),
            pltpu.SemaphoreType.DMA((1,)),
        ],
        compiler_params=pltpu.CompilerParams(vmem_limit_bytes=VMEM_BYTES),
        cost_estimate=pl.CostEstimate(
            flops=length * width * width * 120, bytes_accessed=60 * 2**20,
            transcendentals=length * length * 8,
        ),
    )(
        table, aims, spans, counts, norms, doc_row, upper, *saved, tiles
    )


MESH_IDS = pl.DeviceIdType.MESH


def place_of_device():
    row = lax.axis_index("rows")
    seat = lax.axis_index("seq")
    return row % 2, row // 2, seat // 2, seat % 2


def device_at(x, y, z, core):
    return (2 * y + x, 2 * z + core)


def greet(partners):
    barrier = pltpu.get_barrier_semaphore()
    for partner in partners:
        pl.semaphore_signal(barrier, inc=1, device_id=partner, device_id_type=MESH_IDS)
    pl.semaphore_wait(barrier, len(partners))


def seat_partners(x, y, z, core):
    others = []
    for k in range(1, 8):
        seat = (2 * z + core + k) % 8
        others.append((2 * y + x, seat))
    return others


def post(source, target, send_sem, recv_sem, number, partner):
    copy = pltpu.make_async_remote_copy(
        src_ref=source,
        dst_ref=target,
        send_sem=send_sem.at[number],
        recv_sem=recv_sem.at[number],
        device_id=partner,
        device_id_type=MESH_IDS,
    )
    copy.start()
    return copy


def gather_kernel(master, residual, tiles, rows, wide, low, flat, flat_low, send_sem, recv_sem, l_sem):
    x, y, z, core = place_of_device()
    quarter_id = 2 * y + x
    across = device_at(x, y, z, 1 - core)
    by_x = device_at(1 - x, y, z, core)
    by_y = device_at(x, 1 - y, z, core)
    quarters = (quarter_id, 2 * y + (1 - x), 2 * (1 - y) + x, 3 - quarter_id)
    seats = seat_partners(x, y, z, core)
    seat = 2 * z + core
    load_near = pltpu.make_async_copy(
        master.at[pl.ds(4 * quarter_id, 4)], wide.at[pl.ds(4 * quarter_id, 4)], l_sem.at[0]
    )
    load_near.start()
    far = []
    for k in range(1, 4):
        part = pl.ds(4 * ((quarter_id + k) % 4), 4)
        copy = pltpu.make_async_copy(master.at[part], wide.at[part], l_sem.at[1 + k])
        copy.start()
        far.append(copy)
    load_flat = pltpu.make_async_copy(residual, flat, l_sem.at[1])
    load_flat.start()
    greet(seats + [by_x, by_y])

    def spot(z_from, quarter):
        return core * 64 + z_from * 16 + 4 * quarter

    def convert(first, count):
        @pl.loop(0, count)
        def _(j):
            low[first + j] = wide[first + j].astype(BF16)

    def make(source, target, number, partner):
        return pltpu.make_async_remote_copy(
            src_ref=source, dst_ref=target, send_sem=send_sem.at[number],
            recv_sem=recv_sem.at[number], device_id=partner, device_id_type=MESH_IDS,
        )

    def relay(number, first, count, partner):
        part = pl.ds(first, count)
        return make(tiles.at[part], tiles.at[part], number, partner)

    mine = pl.ds(core * 64 + z * 16, 16)

    def hop(way, step, half):
        toward = device_at(x, y, lax.rem(z + (1 if way == 0 else 3), 4), core)
        number = 6 * way + 2 * (step - 1) + half
        if step == 1:
            near = pl.ds(spot(z, quarter_id) + 2 * half, 2)
            return make(low.at[pl.ds(4 * quarter_id + 2 * half, 2)], tiles.at[near], number, toward)
        z_from = lax.rem(z + (5 - step if way == 0 else step - 1), 4)
        return relay(number, spot(z_from, quarter_id) + 2 * half, 2, toward)

    def can_send(way, step):
        if way == 0:
            return (z < 3) & (z >= step - 1)
        return (z > 0) & (z <= 4 - step)

    def arrives(way, step):
        return z >= step if way == 0 else z <= 3 - step

    def source(way, step):
        return lax.rem(z + (4 - step if way == 0 else step), 4)

    rounds = [
        [(way, step, half) for half in range(2) for way in range(2)] for step in range(1, 4)
    ]
    steps = rounds[0] + rounds[1] + rounds[2]

    def fan(way, step, half):
        base = 12 + 7 * (6 * way + 2 * (step - 1) + half)
        z_from = source(way, step)
        spots = [spot(z_from, quarter) + 2 * half for quarter in quarters]
        return [
            relay(base, spots[0], 2, by_x),
            relay(base + 1, spots[0], 2, by_y),
            relay(base + 2, spots[0], 2, across),
            relay(base + 3, spots[1 + half], 2, by_x if half else by_y),
            relay(base + 4, spots[1], 2, across),
            relay(base + 5, spots[2], 2, across),
            relay(base + 6, spots[3], 2, across),
        ]

    load_near.wait()
    convert(4 * quarter_id, 4)
    for way, step, half in rounds[0]:
        pl.when(can_send(way, 1))(lambda way=way, half=half: hop(way, 1, half).start())
    for k in range(1, 4):
        far[k - 1].wait()
        convert(4 * ((quarter_id + k) % 4), 4)
    keep_tiles = pltpu.make_async_copy(low, tiles.at[mine], l_sem.at[6])
    keep_tiles.start()
    own_across = make(low, tiles.at[mine], 96, across)
    own_across.start()
    load_flat.wait()

    @pl.loop(0, flat.shape[0])
    def _(j):
        flat_low[j] = flat[j].astype(BF16)

    keep_row = pltpu.make_async_copy(flat_low.at[seat], rows.at[seat], l_sem.at[5])
    keep_row.start()
    row_moves = [
        make(flat_low.at[(seat + k) % 8], rows.at[seat], 96 + k, seats[k - 1])
        for k in range(1, 8)
    ]

    def take(way, step, half):
        hop(way, step, half).wait_recv()
        if step < 3:
            pl.when(can_send(way, step + 1))(lambda: hop(way, step + 1, half).start())
        for copy in fan(way, step, half)[:3]:
            copy.start()

    def turn(way, step, half):
        moves = fan(way, step, half)
        for side in (half, 1 - half):
            moves[side].wait_recv()
            if side == half:
                moves[3].start()
            moves[4 + side].start()

    def finish(way, step, half):
        moves = fan(way, step, half)
        moves[3].wait_recv()
        moves[6].start()

    def drain(way, step, half):
        moves = fan(way, step, half)
        for number in (2, 4, 5, 6):
            moves[number].wait_recv()
        for copy in moves:
            copy.wait_send()

    def each(act, chosen):
        for key in chosen:
            pl.when(arrives(key[0], key[1]))(lambda key=key: act(*key))

    each(take, rounds[0])
    each(take, rounds[1][:2])
    each(turn, rounds[0][:2])
    each(take, rounds[1][2:])
    each(turn, rounds[0][2:])
    each(take, rounds[2])
    for copy in row_moves:
        copy.start()
    each(turn, rounds[1])
    each(finish, rounds[0])
    each(turn, rounds[2])
    each(finish, rounds[1] + rounds[2])
    own_across.wait_recv()
    each(drain, steps)
    for way, step, half in steps:
        pl.when(can_send(way, step))(
            lambda way=way, step=step, half=half: hop(way, step, half).wait_send()
        )
    for copy in row_moves:
        copy.wait_recv()
        copy.wait_send()
    own_across.wait_send()
    keep_row.wait()
    keep_tiles.wait()


def gather_start(master_tiles, residual):
    capacity, depth, lanes = master_tiles.shape
    count = 104
    return pl.pallas_call(
        gather_kernel,
        name="gather_start",
        out_shape=[
            jax.ShapeDtypeStruct((8 * capacity, depth, lanes), BF16),
            jax.ShapeDtypeStruct(residual.shape, BF16),
        ],
        in_specs=[any_spec()] * 2,
        out_specs=[any_spec()] * 2,
        scratch_shapes=[
            pltpu.VMEM(master_tiles.shape, F32),
            pltpu.VMEM(master_tiles.shape, BF16),
            pltpu.VMEM(residual.shape, F32),
            pltpu.VMEM(residual.shape, BF16),
            pltpu.SemaphoreType.DMA((count,)),
            pltpu.SemaphoreType.DMA((count,)),
            pltpu.SemaphoreType.DMA((7,)),
        ],
        compiler_params=pltpu.CompilerParams(
            collective_id=0, has_side_effects=True, vmem_limit_bytes=VMEM_BYTES
        ),
        cost_estimate=pl.CostEstimate(
            flops=0, bytes_accessed=200 * 2**20, transcendentals=0
        ),
    )(master_tiles, residual)


def reduce_kernel(
    held, upper, norm_part, owned, rows, norm_sum, squares,
    core_in, own, one_in, two_in, z_in, piece, norm_in, norm_now, square_in,
    square_now, send_sem, recv_sem, l_sem,
):
    x, y, z, core = place_of_device()
    quarter_id = 2 * y + x
    across = device_at(x, y, z, 1 - core)
    by_x = device_at(1 - x, y, z, core)
    by_y = device_at(x, 1 - y, z, core)
    by_both = device_at(1 - x, 1 - y, z, core)
    plus, minus = core, 1 - core
    first_bit = x * minus + y * plus
    second_bit = y * minus + x * plus
    one = device_at(x + minus * (1 - 2 * x), y + plus * (1 - 2 * y), z, core)
    two = device_at(x + plus * (1 - 2 * x), y + minus * (1 - 2 * y), z, core)
    along_z = [device_at(x, y, (z + k) % 4, core) for k in range(1, 4)]
    seats = seat_partners(x, y, z, core)
    seat = 2 * z + core
    quarter_x, quarter_y = 2 * y + (1 - x), 2 * (1 - y) + x
    chunks = own.shape[0]
    number = 0
    copies = []

    def move(source, target, partner):
        nonlocal number
        copy = post(source, target, send_sem, recv_sem, number, partner)
        number += 1
        copies.append(copy)
        return copy

    loads = []
    for i in range(chunks):
        copy = pltpu.make_async_copy(
            held.at[pl.ds(32 * i + 16 * core, 16)], own.at[i], l_sem.at[i]
        )
        copy.start()
        loads.append(copy)
    greet(seats + [by_x, by_y, by_both])
    half = own.shape[2] // 2
    parts = [(i, pl.ds(half * side, half)) for i in range(chunks) for side in range(2)]
    core_moves = [
        move(held.at[pl.ds(32 * i + 16 * (1 - core), 16), rows_], core_in.at[i, :, rows_], across)
        for i, rows_ in parts
    ]
    norm_now[0] = norm_part[...]
    norm_moves = [move(norm_now.at[0], norm_in.at[0], across)]
    for k in range(1, 8):
        move(upper.at[(seat + k) % 8], rows.at[seat], seats[k - 1])
    row_moves = copies[-7:]
    keep_row = pltpu.make_async_copy(upper.at[seat], rows.at[seat], l_sem.at[chunks])
    keep_row.start()

    def add_in(target, first, incoming, count, part):
        @pl.loop(0, count)
        def _(j):
            target[first + j, part, :] = (
                target[first + j, part, :].astype(F32) + incoming[j, part, :].astype(F32)
            ).astype(BF16)

    one_moves, two_moves, z_moves, near_moves, corner_moves, keeps = [], [], [], [], [], []

    def stage_core(n):
        i, part = parts[n]
        if n % 2 == 0:
            loads[i].wait()
        core_moves[n].wait_recv()
        add_in(own.at[i], 0, core_in.at[i], 16, part)
        one_moves.append(
            move(
                own.at[i, pl.ds(8 * (1 - first_bit), 8), part], one_in.at[i, :, part], one
            )
        )

    def stage_one(n):
        i, part = parts[n]
        one_moves[n].wait_recv()
        add_in(own.at[i], 8 * first_bit, one_in.at[i], 8, part)
        two_moves.append(
            move(
                own.at[i, pl.ds(8 * first_bit + 4 * (1 - second_bit), 4), part],
                two_in.at[i, :, part],
                two,
            )
        )

    def stage_two(n):
        i, part = parts[n]
        two_moves[n].wait_recv()
        base = 8 * first_bit + 4 * second_bit
        add_in(own.at[i], base, two_in.at[i], 4, part)
        z_moves.append(
            [
                move(
                    own.at[i, base + (z + k) % 4, part], z_in.at[i, k - 1, part], along_z[k - 1]
                )
                for k in range(1, 4)
            ]
        )

    def stage_z(n):
        i, part = parts[n]
        for copy in z_moves[n]:
            copy.wait_recv()
        total = own[i, 8 * first_bit + 4 * second_bit + z, part, :].astype(F32)
        for k in range(3):
            total = total + z_in[i, k, part, :].astype(F32)
        piece[i, part, :] = total.astype(BF16)
        square_now[0] += jnp.sum((total * total).reshape(-1, 8, total.shape[1]), axis=0)
        here = owned.at[4 * quarter_id + i, part]
        near_moves.append(
            [move(piece.at[i, part], here, partner) for partner in (by_x, by_y)]
        )
        if n >= len(parts) - 2:
            corner_moves.append(move(piece.at[i, part], here, by_both))
        keep = pltpu.make_async_copy(piece.at[i, part], here, l_sem.at[chunks + 1 + n])
        keep.start()
        keeps.append(keep)

    def stage_turn(n):
        i, part = parts[n]
        side = n % 2
        near_moves[n][1 - side].wait_recv()
        far_id = quarter_y if side == 0 else quarter_x
        here = owned.at[4 * far_id + i, part]
        corner_moves.append(move(here, here, by_x if side == 0 else by_y))

    def norm_stage(step, partner):
        norm_moves[step].wait_recv()
        norm_now[step + 1] = norm_now[step] + norm_in[step]
        if partner is not None:
            norm_moves.append(move(norm_now.at[step + 1], norm_in.at[step + 1], partner))

    square_now[...] = jnp.zeros_like(square_now)
    for n in range(8):
        stage_core(n)
        if n == 1:
            norm_stage(0, by_x)
        if n == 3:
            norm_stage(1, by_y)
        if n == 5:
            norm_stage(2, None)
    norm_z = [move(norm_now.at[3], norm_in.at[2 + k], along_z[k - 1]) for k in range(1, 4)]
    for n in range(8 + 5):
        if n < 8:
            stage_one(n)
        if 0 <= n - 1 < 8:
            stage_two(n - 1)
        if 0 <= n - 3 < 8:
            stage_z(n - 3)
        if 0 <= n - 5 < 6:
            stage_turn(n - 5)

    def in_order(own_value, incoming):
        values = [own_value] + [incoming(k) for k in range(1, 4)]
        total = None
        for place in range(4):
            picked = values[0]
            for k in range(1, 4):
                picked = jnp.where((z + 4 - k) % 4 == place, values[k], picked)
            total = picked if total is None else total + picked
        return total

    square_moves = []

    def square_stage(step, partner):
        square_moves.append(move(square_now.at[step], square_in.at[step], partner))
        square_moves[step].wait_recv()
        square_now[step + 1] = square_now[step] + square_in[step]

    square_stage(0, by_x)
    square_stage(1, by_y)
    square_stage(2, across)
    square_z = [
        move(square_now.at[3], square_in.at[2 + k], along_z[k - 1]) for k in range(1, 4)
    ]
    for copy in norm_z:
        copy.wait_recv()
    norm_sum[...] = in_order(norm_now[3], lambda k: norm_in[2 + k])
    for copy in square_z:
        copy.wait_recv()
    squares[...] = in_order(square_now[3], lambda k: square_in[2 + k])
    straight = [near_moves[n][n % 2] for n in range(6)] + near_moves[6] + near_moves[7]
    for copy in row_moves + straight + corner_moves:
        copy.wait_recv()
    for copy in copies:
        copy.wait_send()
    keep_row.wait()
    for keep in keeps:
        keep.wait()


def reduce_end(held, upper, norm_part):
    slots, depth, lanes = held.shape
    chunks = 4
    count = 8 + 1 + 7 + 8 + 8 + 24 + 24 + 2 + 3 + 3 + 3
    return pl.pallas_call(
        reduce_kernel,
        name="reduce_end",
        out_shape=[
            jax.ShapeDtypeStruct((slots // 8, depth, lanes), BF16),
            jax.ShapeDtypeStruct(upper.shape, BF16),
            jax.ShapeDtypeStruct(norm_part.shape, F32),
            jax.ShapeDtypeStruct((8, lanes), F32),
        ],
        in_specs=[any_spec(), any_spec(), vmem_spec()],
        out_specs=[any_spec(), any_spec(), vmem_spec(), vmem_spec()],
        scratch_shapes=[
            pltpu.VMEM((chunks, 16, depth, lanes), BF16),
            pltpu.VMEM((chunks, 16, depth, lanes), BF16),
            pltpu.VMEM((chunks, 8, depth, lanes), BF16),
            pltpu.VMEM((chunks, 4, depth, lanes), BF16),
            pltpu.VMEM((chunks, 3, depth, lanes), BF16),
            pltpu.VMEM((chunks, depth, lanes), BF16),
            pltpu.VMEM((6, *norm_part.shape), F32),
            pltpu.VMEM((4, *norm_part.shape), F32),
            pltpu.VMEM((6, 8, lanes), F32),
            pltpu.VMEM((4, 8, lanes), F32),
            pltpu.SemaphoreType.DMA((count,)),
            pltpu.SemaphoreType.DMA((count,)),
            pltpu.SemaphoreType.DMA((3 * chunks + 1,)),
        ],
        compiler_params=pltpu.CompilerParams(
            collective_id=1, has_side_effects=True, vmem_limit_bytes=VMEM_BYTES
        ),
        cost_estimate=pl.CostEstimate(
            flops=0, bytes_accessed=300 * 2**20, transcendentals=0
        ),
    )(held, upper, norm_part)


def finish_kernel(
    counts, owned_in, master_in, first_in, second_in, grad_rows_in, out_rows_in, squares, norm_sum,
    norm_params, norm_first, norm_second,
    clip_out, first_out, second_out, master_out, copy_out, grad_rows_out, out_rows_out,
    total_out, norm_clip_out, norm_first_out, norm_second_out, norm_params_out,
    owned, master, first, second, grad_rows, out_rows,
    clip, new_first, new_second, new_master, new_copy, wide_grad, wide_out, i_sem, o_sem,
):
    ins = ((owned_in, owned), (master_in, master), (first_in, first), (second_in, second))
    capacity = master.shape[0]

    def bring(number, place):
        return pltpu.make_async_copy(
            ins[number][0].at[place], ins[number][1].at[place],
            i_sem.at[number * capacity + place],
        )

    @pl.loop(0, capacity)
    def _(place):
        for number in range(len(ins)):
            bring(number, place).start()

    bring_rows = [
        pltpu.make_async_copy(source, target, i_sem.at[4 * capacity + number])
        for number, (source, target) in enumerate(
            ((grad_rows_in, grad_rows), (out_rows_in, out_rows))
        )
    ]
    for copy in bring_rows:
        copy.start()
    norms = norm_sum[...]
    total = jnp.sqrt(jnp.sum(squares[...]) + jnp.sum(norms * norms))
    factor = 1.0 / jnp.maximum(total, 1.0)
    correction = 1.0 - 0.5**STEP

    def step(weight, grad, low, high, rate):
        low = 0.5 * low + 0.5 * grad
        high = 0.5 * high + 0.5 * grad * grad
        update = low / correction / (jnp.sqrt(high / correction) + 1e-08)
        return weight - rate * (update + 0.01 * weight), low, high

    outs = (
        (clip, clip_out), (new_first, first_out), (new_second, second_out),
        (new_master, master_out), (new_copy, copy_out),
    )

    def send(number, place):
        return pltpu.make_async_copy(
            outs[number][0].at[place], outs[number][1].at[place],
            o_sem.at[number * capacity + place],
        )

    count = counts[lax.axis_index("seq")]

    @pl.loop(0, capacity)
    def _(place):
        for number in range(len(ins)):
            bring(number, place).wait()
        keep = (lax.broadcast(place, clip.shape[1:])) < count
        grad = jnp.where(keep, owned[place].astype(F32), 0.0) * factor
        weight, low, high = step(master[place], grad, first[place], second[place], 0.05)
        weight = jnp.where(keep, weight, 0.0)
        clip[place] = grad
        new_first[place] = jnp.where(keep, low, 0.0)
        new_second[place] = jnp.where(keep, high, 0.0)
        new_master[place] = weight
        new_copy[place] = weight.astype(BF16)
        for number in range(len(outs)):
            send(number, place).start()

    moves = []
    for number, (low, wide, target) in enumerate(
        ((grad_rows, wide_grad, grad_rows_out), (out_rows, wide_out, out_rows_out))
    ):

        bring_rows[number].wait()

        @pl.loop(0, low.shape[0])
        def _(j, low=low, wide=wide):
            wide[j] = low[j].astype(F32)

        moves.append(pltpu.make_async_copy(wide, target, o_sem.at[5 * capacity + number]))
        moves[-1].start()
    clipped = norms * factor
    weight, low, high = step(norm_params[...], clipped, norm_first[...], norm_second[...], 0.25)
    total_out[...] = jnp.broadcast_to(total, total_out.shape)
    norm_clip_out[...] = clipped
    norm_first_out[...] = low
    norm_second_out[...] = high
    norm_params_out[...] = weight

    @pl.loop(0, capacity)
    def _(place):
        for number in range(len(outs)):
            send(number, place).wait()

    for move in moves:
        move.wait()


def finish_step(
    counts, owned, master, first, second, grad_rows, out_rows, squares, norm_sum, norm_params,
    norm_first, norm_second,
):
    tiles = jax.ShapeDtypeStruct(master.shape, F32)
    rows = jax.ShapeDtypeStruct(grad_rows.shape, F32)
    norms = jax.ShapeDtypeStruct(norm_params.shape, F32)
    return pl.pallas_call(
        finish_kernel,
        name="finish_step",
        out_shape=[
            tiles, tiles, tiles, tiles, jax.ShapeDtypeStruct(master.shape, BF16), rows, rows,
            jax.ShapeDtypeStruct((1, 128), F32), norms, norms, norms, norms,
        ],
        in_specs=[smem_spec()] + [any_spec()] * 6 + [vmem_spec()] * 5,
        out_specs=[any_spec()] * 7 + [vmem_spec()] * 5,
        scratch_shapes=[pltpu.VMEM(owned.shape, BF16)]
        + [pltpu.VMEM(master.shape, F32)] * 3
        + [pltpu.VMEM(grad_rows.shape, BF16)] * 2
        + [pltpu.VMEM(master.shape, F32)] * 4
        + [pltpu.VMEM(master.shape, BF16)]
        + [pltpu.VMEM(grad_rows.shape, F32)] * 2
        + [pltpu.SemaphoreType.DMA((4 * master.shape[0] + 2,))]
        + [pltpu.SemaphoreType.DMA((5 * master.shape[0] + 2,))],
        compiler_params=pltpu.CompilerParams(vmem_limit_bytes=VMEM_BYTES),
        cost_estimate=pl.CostEstimate(
            flops=0, bytes_accessed=40 * 2**20, transcendentals=0
        ),
    )(
        counts, owned, master, first, second, grad_rows, out_rows, squares, norm_sum, norm_params,
        norm_first, norm_second,
    )


def local_by_rows(
    residual_in,
    cotangent,
    segments,
    owners,
    master_tiles,
    first_tiles,
    second_tiles,
    norm_params,
    norm_first,
    norm_second,
):
    local_rows, positions, model_width = residual_in.shape
    seq_devices = lax.axis_size("seq")
    seq_index = lax.axis_index("seq")
    length = positions * seq_devices
    tile_total = owners.shape[0]
    capacity, _, tile_width = master_tiles.shape
    quarter = capacity // 4
    pairs = model_width // tile_width
    places = jnp.arange(tile_total, dtype=jnp.int32)
    before = (owners[None, :] == owners[:, None]) & (places[None, :] < places[:, None])
    ranks = jnp.sum(before.astype(jnp.int32), axis=1)
    core, depth_z, part_id = owners % 2, owners // 2, ranks // quarter
    major = jnp.where(core == 0, part_id % 2, part_id // 2)
    minor = jnp.where(core == 0, part_id // 2, part_id % 2)
    weight_table = core * 64 + depth_z * 16 + ranks
    grad_table = (ranks % quarter) * 32 + core * 16 + major * 8 + minor * 4 + depth_z
    seats = jnp.arange(seq_devices, dtype=jnp.int32)
    counts = jnp.sum((owners[None, :] == seats[:, None]).astype(jnp.int32), axis=1)
    tiles, hidden = gather_start(master_tiles, residual_in)
    hidden = hidden.reshape(length, model_width)
    later, tiles = lax.optimization_barrier((cotangent, tiles))
    upper = lax.all_to_all(later.astype(BF16), "seq", split_axis=0, concat_axis=0, tiled=True)
    upper = upper.reshape(length, model_width)
    doc_ids = lax.dynamic_slice_in_dim(segments, seq_index, 1, 0)
    doc_row = doc_ids
    begin = jnp.sum((doc_ids < doc_ids[0, ::QUERY, None]).astype(jnp.int32), axis=1) // QUERY
    end = jnp.sum((doc_ids <= doc_ids[0, QUERY - 1 :: QUERY, None]).astype(jnp.int32), axis=1)
    many = (end - begin * QUERY + BLOCK - 1) // BLOCK
    spans = jnp.stack([jnp.minimum(begin, (length - many * BLOCK) // QUERY), many])
    *saved, after = forward_layers(
        weight_table, spans, norm_params, doc_row, hidden, tiles, pairs
    )
    out_rows = lax.all_to_all(
        after.reshape(residual_in.shape), "seq", split_axis=0, concat_axis=0, tiled=True
    )
    lower, held, norm_part = backward_layers(
        weight_table, grad_table, spans, counts, norm_params, doc_row, upper, saved, tiles,
    )
    owned, grad_rows, norm_sum, squares = reduce_end(
        held, lower.reshape(residual_in.shape), norm_part
    )
    (
        clipped, new_first, new_second, new_weight, new_copies, input_grad, residual_out,
        total, norm_clip, new_norm_f, new_norm_s, new_norm,
    ) = finish_step(
        counts, owned, master_tiles, first_tiles, second_tiles, grad_rows, out_rows, squares,
        norm_sum, norm_params, norm_first, norm_second,
    )
    return (
        residual_out,
        input_grad,
        clipped,
        total[0, :1],
        new_first,
        new_second,
        new_weight,
        new_copies,
        norm_clip,
        new_norm_f,
        new_norm_s,
        new_norm,
    )


def local(residual_in, *others):
    whole_rows = residual_in.shape[0] == lax.axis_size("seq")
    step = local_by_rows if whole_rows else local_by_heads
    return step(residual_in, *others)


def solution(mesh):
    by_rows = P("rows", "seq", None)
    by_slots = P("seq", None, None)
    return jax.shard_map(
        local,
        mesh=mesh,
        in_specs=(
            by_rows, by_rows, P("rows", None), P(), by_slots, by_slots, by_slots, P(), P(), P(),
        ),
        out_specs=(
            by_rows, by_rows, by_slots, P(), by_slots, by_slots, by_slots, by_slots,
            P(), P(), P(), P(),
        ),
        check_vma=False,
    )
```

```python
import jax
import jax.numpy as jnp
from jax import lax
from jax.experimental import pallas as pl
from jax.experimental.pallas import tpu as pltpu

from jax.sharding import PartitionSpec as P

HEADS = 8
LAYERS = 2
STEP = 5


def norm_layer(values, gain, offset):
    center = values - jnp.mean(values, axis=-1, keepdims=True)
    spread = jnp.mean(center * center, axis=-1, keepdims=True)
    return center * lax.rsqrt(spread + 1e-05) * gain + offset


def matmul(left, right):
    return jnp.dot(left, right, preferred_element_type=jnp.float32)


def left_product(left, right):
    return lax.dot_general(
        left, right, (((0,), (0,)), ((), ())), preferred_element_type=jnp.float32
    )


def right_product(left, right):
    return lax.dot_general(
        left, right, (((1,), (1,)), ((), ())), preferred_element_type=jnp.float32
    )


def assemble(weight_tiles, layer_number):
    first_tile = 48 * layer_number
    model_width = weight_tiles.shape[1]
    qkv_weight = (
        weight_tiles[first_tile : first_tile + 12].transpose(1, 0, 2).reshape(model_width, -1)
    )
    out_weight = (
        weight_tiles[first_tile + 12 : first_tile + 16].transpose(1, 0, 2).reshape(model_width, -1)
    )
    up_weight = (
        weight_tiles[first_tile + 16 : first_tile + 32].transpose(1, 0, 2).reshape(model_width, -1)
    )
    down_block = weight_tiles[first_tile + 32 : first_tile + 48].reshape(4, 4, model_width, -1)
    down_weight = down_block.transpose(0, 2, 1, 3).reshape(4 * model_width, model_width)
    return (qkv_weight, out_weight, up_weight, down_weight)


def split_tiles(qkv_grad, out_grad, up_grad, down_grad, tile_width):
    model_width = qkv_grad.shape[0]
    pieces = [
        qkv_grad.reshape(model_width, -1, tile_width).transpose(1, 0, 2),
        out_grad.reshape(model_width, -1, tile_width).transpose(1, 0, 2),
        up_grad.reshape(model_width, -1, tile_width).transpose(1, 0, 2),
        down_grad.reshape(4, model_width, 4, tile_width)
        .transpose(0, 2, 1, 3)
        .reshape(16, model_width, tile_width),
    ]
    return jnp.concatenate(pieces, axis=0)


def attend_forward(queries, key_rows, value_rows, doc_ids, block_rows, scale):
    length = queries.shape[0]

    def one_block(number):
        first_row = number * block_rows
        query_block = lax.dynamic_slice_in_dim(queries, first_row, block_rows, 0)
        doc_block = lax.dynamic_slice_in_dim(doc_ids, first_row, block_rows, 0)
        same_doc = doc_block[:, None] == doc_ids[None, :]
        scores = jnp.where(same_doc, right_product(query_block, key_rows) * scale, -1e30)
        largest = jnp.max(scores, axis=-1, keepdims=True)
        row_total = jnp.sum(jnp.exp(scores - largest), axis=-1, keepdims=True)
        logsum = largest + jnp.log(row_total)
        weights = jnp.where(same_doc, jnp.exp(scores - logsum), 0.0).astype(jnp.bfloat16)
        return (matmul(weights, value_rows).astype(jnp.bfloat16), logsum[:, 0])

    outputs, logsums = lax.map(one_block, jnp.arange(length // block_rows))
    return (outputs.reshape(length, -1), logsums.reshape(length))


def attend_backward(queries, key_rows, value_rows, doc_ids, logsums, out_grads, block_rows, scale):
    length, head_dim = queries.shape

    def one_block(carry, number):
        key_grad, value_grad = carry
        first_row = number * block_rows
        query_block = lax.dynamic_slice_in_dim(queries, first_row, block_rows, 0)
        doc_block = lax.dynamic_slice_in_dim(doc_ids, first_row, block_rows, 0)
        logsum_block = lax.dynamic_slice_in_dim(logsums, first_row, block_rows, 0)
        grad_block = lax.dynamic_slice_in_dim(out_grads, first_row, block_rows, 0)
        same_doc = doc_block[:, None] == doc_ids[None, :]
        scores = jnp.where(same_doc, right_product(query_block, key_rows) * scale, -1e30)
        probs = jnp.where(same_doc, jnp.exp(scores - logsum_block[:, None]), 0.0)
        prob_grad = right_product(grad_block, value_rows)
        inner_sum = jnp.sum(probs * prob_grad, axis=-1, keepdims=True)
        score_grad = (probs * (prob_grad - inner_sum)).astype(jnp.bfloat16)
        query_grad = matmul(score_grad, key_rows) * scale
        key_grad = key_grad + left_product(score_grad, query_block) * scale
        value_grad = value_grad + left_product(probs.astype(jnp.bfloat16), grad_block)
        return ((key_grad, value_grad), query_grad)

    zeros_block = jnp.zeros((length, head_dim), jnp.float32)
    (key_grad, value_grad), query_grads = lax.scan(
        one_block, (zeros_block, zeros_block), jnp.arange(length // block_rows)
    )
    stacked = jnp.stack([query_grads.reshape(length, head_dim), key_grad, value_grad], axis=1)
    return stacked.astype(jnp.bfloat16)


def adamw(weight, grad, first, second, learn_rate, correction):
    first = 0.5 * first + 0.5 * grad
    second = 0.5 * second + 0.5 * grad * grad
    update = first / correction / (jnp.sqrt(second / correction) + 1e-08)
    return (weight - learn_rate * (update + 0.01 * weight), first, second)


def local_by_heads(
    residual_in,
    cotangent,
    segments,
    owners,
    master_tiles,
    first_tiles,
    second_tiles,
    norm_params,
    norm_first,
    norm_second,
):
    local_rows, positions, model_width = residual_in.shape
    seq_devices = lax.axis_size("seq")
    seq_index = lax.axis_index("seq")
    head_dim = model_width // HEADS
    group_count = seq_devices // HEADS
    group_rows = local_rows // group_count
    length = positions * seq_devices
    block_rows = min(512, length)
    scale = head_dim ** (-0.5)
    tile_total = owners.shape[0]
    capacity = master_tiles.shape[0]
    tile_width = master_tiles.shape[2]
    places = jnp.arange(tile_total, dtype=jnp.int32)
    before = (owners[None, :] == owners[:, None]) & (places[None, :] < places[:, None])
    ranks = jnp.sum(before.astype(jnp.int32), axis=1)
    slot_ids = owners * capacity + ranks
    local_slots = jnp.arange(capacity, dtype=jnp.int32)
    matches = (owners[:, None] == seq_index) & (ranks[:, None] == local_slots[None, :])
    chosen = jnp.sum(jnp.where(matches, places[:, None], 0), axis=0)
    present = jnp.any(matches, axis=0)
    copies = lax.all_gather(master_tiles.astype(jnp.bfloat16), "seq", axis=0, tiled=True)
    weight_tiles = jnp.take(copies, slot_ids, axis=0)
    my_group = seq_index // HEADS
    doc_rows = lax.dynamic_slice_in_dim(segments, my_group * group_rows, group_rows, 0)
    hidden = residual_in.reshape(-1, model_width)
    saved = []
    for layer_number in range(LAYERS):
        qkv_weight, out_weight, up_weight, down_weight = assemble(weight_tiles, layer_number)
        params = norm_params[4 * layer_number : 4 * layer_number + 4]
        normed, first_pull = jax.vjp(norm_layer, hidden, params[0], params[1])
        normed_low = normed.astype(jnp.bfloat16)
        packed = matmul(normed_low, qkv_weight).astype(jnp.bfloat16)
        outgoing = packed.reshape(group_count, group_rows, positions, 3, HEADS, head_dim)
        outgoing = outgoing.transpose(0, 4, 1, 2, 3, 5).reshape(
            seq_devices, group_rows, positions * 3 * head_dim
        )
        arrived = lax.all_to_all(outgoing, "seq", split_axis=0, concat_axis=2, tiled=True).reshape(
            group_rows, length, 3, head_dim
        )

        def forward_item(items):
            return attend_forward(
                items[0][:, 0], items[0][:, 1], items[0][:, 2], items[1], block_rows, scale
            )

        attended, logsums = lax.map(forward_item, (arrived, doc_rows))
        returning = attended.reshape(1, group_rows, seq_devices, positions * head_dim)
        mixed = lax.all_to_all(returning, "seq", split_axis=2, concat_axis=0, tiled=True)
        mixed = (
            mixed.reshape(group_count, HEADS, group_rows, positions, head_dim)
            .transpose(0, 2, 3, 1, 4)
            .reshape(-1, model_width)
        )
        middle = hidden + matmul(mixed, out_weight)
        normed_two, second_pull = jax.vjp(norm_layer, middle, params[2], params[3])
        normed_two_low = normed_two.astype(jnp.bfloat16)
        inner = matmul(normed_two_low, up_weight)
        active = jax.nn.gelu(inner).astype(jnp.bfloat16)
        hidden = middle + matmul(active, down_weight)
        saved.append(
            (
                first_pull,
                normed_low,
                arrived,
                logsums,
                mixed,
                second_pull,
                normed_two_low,
                inner,
                active,
            )
        )
    grad = cotangent.reshape(-1, model_width)
    tile_parts = [None] * LAYERS
    norm_parts = [None] * LAYERS
    for layer_number in reversed(range(LAYERS)):
        (
            first_pull,
            normed_low,
            arrived,
            logsums,
            mixed,
            second_pull,
            normed_two_low,
            inner,
            active,
        ) = saved[layer_number]
        qkv_weight, out_weight, up_weight, down_weight = assemble(weight_tiles, layer_number)
        grad_low = grad.astype(jnp.bfloat16)
        down_grad = left_product(active, grad_low)
        active_grad = right_product(grad_low, down_weight)
        inner_grad = jax.vjp(jax.nn.gelu, inner)[1](active_grad)[0].astype(jnp.bfloat16)
        up_grad = left_product(normed_two_low, inner_grad)
        middle_part, gain_two, offset_two = second_pull(right_product(inner_grad, up_weight))
        middle_grad = grad + middle_part
        middle_low = middle_grad.astype(jnp.bfloat16)
        out_grad = left_product(mixed, middle_low)
        mixed_grad = right_product(middle_low, out_weight).astype(jnp.bfloat16)
        sending = mixed_grad.reshape(group_count, group_rows, positions, HEADS, head_dim)
        sending = sending.transpose(0, 3, 1, 2, 4).reshape(
            seq_devices, group_rows, positions * head_dim
        )
        head_grads = lax.all_to_all(
            sending, "seq", split_axis=0, concat_axis=2, tiled=True
        ).reshape(group_rows, length, head_dim)

        def backward_item(items):
            arrived_row, doc_row, logsum_row, grad_row = items
            return attend_backward(
                arrived_row[:, 0],
                arrived_row[:, 1],
                arrived_row[:, 2],
                doc_row,
                logsum_row,
                grad_row,
                block_rows,
                scale,
            )

        packed_grads = lax.map(backward_item, (arrived, doc_rows, logsums, head_grads))
        coming = lax.all_to_all(
            packed_grads.reshape(1, group_rows, seq_devices, positions * 3 * head_dim),
            "seq",
            split_axis=2,
            concat_axis=0,
            tiled=True,
        )
        qkv_grad = coming.reshape(group_count, HEADS, group_rows, positions, 3, head_dim)
        qkv_grad = qkv_grad.transpose(0, 2, 3, 4, 1, 5).reshape(-1, 3 * model_width)
        qkv_weight_grad = left_product(normed_low, qkv_grad)
        input_part, gain_one, offset_one = first_pull(right_product(qkv_grad, qkv_weight))
        grad = middle_grad + input_part
        tile_parts[layer_number] = split_tiles(
            qkv_weight_grad, out_grad, up_grad, down_grad, tile_width
        )
        norm_parts[layer_number] = jnp.stack([gain_one, offset_one, gain_two, offset_two])
    dense = jnp.concatenate(tile_parts, axis=0)
    norm_part = jnp.concatenate(norm_parts, axis=0)
    piece = lax.psum_scatter(
        dense.reshape(-1, tile_width), ("rows", "seq"), scatter_dimension=0, tiled=True
    )
    squares, norm_sum = lax.psum((jnp.sum(piece * piece), norm_part), ("rows", "seq"))
    summed = (
        lax.all_gather(piece.astype(jnp.bfloat16), ("rows", "seq"), axis=0, tiled=True)
        .astype(piece.dtype)
        .reshape(dense.shape)
    )
    owned = jnp.take(summed, chosen, axis=0)
    keep = present[:, None, None]
    owned = jnp.where(keep, owned, 0.0)
    total = jnp.sqrt(squares + jnp.sum(norm_sum * norm_sum))
    factor = 1.0 / jnp.maximum(total, 1.0)
    clipped = owned * factor
    norm_clip = norm_sum * factor
    correction = 1.0 - 0.5**STEP
    new_weight, new_first_rows, new_second_rows = adamw(
        master_tiles, clipped, first_tiles, second_tiles, 0.05, correction
    )
    new_weight = jnp.where(keep, new_weight, 0.0)
    new_first_rows = jnp.where(keep, new_first_rows, 0.0)
    new_second_rows = jnp.where(keep, new_second_rows, 0.0)
    new_norm, new_norm_f, new_norm_s = adamw(
        norm_params, norm_clip, norm_first, norm_second, 0.25, correction
    )
    return (
        hidden.reshape(local_rows, positions, model_width),
        grad.reshape(local_rows, positions, model_width),
        clipped,
        total[None],
        new_first_rows,
        new_second_rows,
        new_weight,
        new_weight.astype(jnp.bfloat16),
        norm_clip,
        new_norm_f,
        new_norm_s,
        new_norm,
    )


F32 = jnp.float32
BF16 = jnp.bfloat16
BLOCK = 256
DENSE = 512
DENSE_BACK = 512
QUERY = 128
UNROLL = 4
UNROLL_BACK = 4
VMEM_BYTES = 60 * 1024 * 1024


def dot_nn(left, right):
    return jnp.dot(left, right, preferred_element_type=F32)


def dot_nt(left, right, precision=None):
    return lax.dot_general(
        left, right, (((1,), (1,)), ((), ())), preferred_element_type=F32, precision=precision
    )


def dot_tn(left, right):
    return lax.dot_general(left, right, (((0,), (0,)), ((), ())), preferred_element_type=F32)


def rows_of(number, size=BLOCK):
    return pl.ds(pl.multiple_of(number * size, size), size)


def normalized(values):
    center = values - jnp.mean(values, axis=-1, keepdims=True)
    spread = jnp.mean(center * center, axis=-1, keepdims=True)
    scale = lax.rsqrt(spread + 1e-05)
    return center * scale, scale


GELU_A = 0.7978845608028654
GELU_B = 0.044715


def gelu_value(inner):
    return 0.5 * inner * (1.0 + jnp.tanh(GELU_A * (inner + GELU_B * inner * inner * inner)))


def gelu_both(inner):
    square = inner * inner
    bent = jnp.tanh(inner * (GELU_A + GELU_A * GELU_B * square))
    half = 0.5 + 0.5 * bent
    slope = half + 0.5 * inner * (1.0 - bent * bent) * (GELU_A + 3.0 * GELU_A * GELU_B * square)
    return inner * half, slope


def weight_copy(tiles, table, number, target, column, row, sem):
    depth, width = tiles.shape[1], tiles.shape[2]
    rows = pl.ds(pl.multiple_of(row * depth, depth), depth)
    columns = pl.ds(pl.multiple_of(column * width, width), width)
    return pltpu.make_async_copy(
        tiles.at[table[number]], target.at[rows, columns], sem.at[number]
    )


def weight_group(tiles, table, first, count, per_row, target, sem, act):
    @pl.loop(0, count)
    def _(j):
        copy = weight_copy(
            tiles, table, first + j, target, lax.rem(j, per_row), lax.div(j, per_row), sem
        )
        getattr(copy, act)()


def lane_is_first(shape):
    return lax.broadcasted_iota(jnp.int32, shape, 1) < shape[1] // 2


def stacked(values, lanes_first):
    zero = jnp.zeros_like(values)
    return jnp.concatenate(
        [
            jnp.where(lanes_first, values, zero).astype(BF16),
            jnp.where(lanes_first, zero, values).astype(BF16),
        ],
        axis=0,
    )


def forward_kernel(
    table, spans, norms, doc_row, hidden, tiles,
    below_out, normed_out, packed_out, mixed_out, logsum_out, middle_out, normed_two_out,
    hidden_out,
    w_qkv, w_out, w_up, w_down, flow, normed, packed, mixed, logcol, logsum, middle, normed_two,
    doc_col, w_sem, o_sem,
):
    length, width = hidden.shape
    blocks = length // DENSE
    pairs = mixed.shape[0]
    lanes = mixed.shape[2]
    groups = (
        (0, 12, 12, w_qkv), (12, 4, 4, w_out), (16, 16, 16, w_up), (32, 16, 4, w_down),
    )

    def fetch(layer, group, act):
        first, count, per_row, target = groups[group]
        weight_group(
            tiles, table, 48 * layer + first, count, per_row, target.at[layer], w_sem, act
        )

    for layer in range(LAYERS):
        for group in range(4):
            fetch(layer, group, "start")
    outs = (
        (normed, normed_out), (packed, packed_out), (mixed, mixed_out), (logsum, logsum_out),
        (middle, middle_out), (normed_two, normed_two_out), (flow, below_out),
    )

    def flush(number, layer):
        return pltpu.make_async_copy(outs[number][0], outs[number][1].at[layer], o_sem.at[number])

    def forward_one(layer):
        def again(number):
            pl.when(layer > 0)(lambda: flush(number, layer).wait())

        flush(6, layer).start()
        again(0)
        again(1)
        fetch(layer, 0, "wait")

        @pl.loop(0, length // 512)
        def _(number):
            here = rows_of(number, 512)
            unit, _ = normalized(flow[here, :])
            low = (unit * norms[pl.ds(4 * layer + 0, 1), :] + norms[pl.ds(4 * layer + 1, 1), :]).astype(BF16)
            normed[here, :] = low
            product = dot_nn(low, w_qkv[layer])
            for j in range(3 * pairs):
                packed[j, here, :] = product[:, j * lanes : (j + 1) * lanes].astype(BF16)

        flush(0, layer).start()
        flush(1, layer).start()
        again(2)
        lane_ids = lax.broadcasted_iota(jnp.int32, (QUERY, lanes), 1)
        first_half = lane_is_first((QUERY, lanes))

        @pl.loop(0, length // QUERY)
        def _(number):
            here = rows_of(number, QUERY)
            low_key = spans[0, number]
            key_count = spans[1, number]
            doc_here = doc_col[here, 0:1]

            def with_keys(many):
                keys_here = pl.ds(pl.multiple_of(low_key * QUERY, QUERY), many * BLOCK)
                same = doc_here == doc_row[0:1, keys_here]
                same = jnp.concatenate([same, same], axis=0)

                def score(pair):
                    heads = stacked(packed[pair, here, :].astype(F32) * 0.125, first_half)
                    return dot_nt(heads, packed[pairs + pair, keys_here, :])

                def settle(scores):
                    scores = jnp.where(same, scores, -1e30)
                    top = jnp.max(scores, axis=-1, keepdims=True)
                    weights = jnp.exp(scores - top)
                    total = jnp.sum(weights, axis=-1, keepdims=True)
                    return weights.astype(BF16), total, top + jnp.log(total)

                def finish(pair, weights, total, logs):
                    result = dot_nn(weights, packed[2 * pairs + pair, keys_here, :]) / total
                    mixed[pair, here, :] = jnp.where(
                        first_half, result[:QUERY], result[QUERY:]
                    ).astype(BF16)
                    old = logcol[here, :]
                    old = jnp.where(lane_ids == 8 * pair, logs[:QUERY], old)
                    logcol[here, :] = jnp.where(lane_ids == 8 * pair + 1, logs[QUERY:], old)

                waiting = None
                ahead = score(0)
                for pair in range(pairs):
                    now = ahead
                    if pair + 1 < pairs:
                        ahead = score(pair + 1)
                    done = settle(now)
                    if waiting is not None:
                        finish(pair - 1, *waiting)
                    waiting = done
                finish(pairs - 1, *waiting)


            for many in range(1, length // BLOCK + 1):
                pl.when(key_count == many)(lambda many=many: with_keys(many))

        flush(2, layer).start()
        turned = logcol[...].T
        again(3)
        for pair in range(pairs):
            logsum[pair, :, :] = turned[8 * pair : 8 * pair + 8, :]
        flush(3, layer).start()
        fetch(layer, 1, "wait")
        fetch(layer, 2, "wait")
        fetch(layer, 3, "wait")
        again(4)
        again(5)
        flush(6, layer).wait()
        chunk = width

        @pl.loop(0, length // 1024)
        def _(number):
            here = rows_of(number, 1024)
            side_by_side = jnp.concatenate([mixed[pair, here, :] for pair in range(pairs)], axis=1)
            mid = flow[here, :] + dot_nn(side_by_side, w_out[layer])
            middle[here, :] = mid
            unit, _ = normalized(mid)
            low = (unit * norms[pl.ds(4 * layer + 2, 1), :] + norms[pl.ds(4 * layer + 3, 1), :]).astype(BF16)
            normed_two[here, :] = low
            total = mid
            for c in range(w_up.shape[2] // chunk):
                part = slice(c * chunk, (c + 1) * chunk)
                active = gelu_value(dot_nn(low, w_up[layer, :, part])).astype(BF16)
                total = total + dot_nn(active, w_down[layer, part, :])
            flow[here, :] = total

        flush(4, layer).start()
        flush(5, layer).start()

    flow[...] = hidden[...].astype(F32)
    fill_columns(doc_row, doc_col)

    @pl.loop(0, LAYERS)
    def _(layer):
        forward_one(layer)

    last = pltpu.make_async_copy(normed, hidden_out, o_sem.at[7])
    flush(0, LAYERS - 1).wait()
    normed[...] = flow[...].astype(BF16)
    last.start()
    for number in range(1, 6):
        flush(number, LAYERS - 1).wait()
    last.wait()


def fill_columns(doc_row, doc_col):
    lanes = doc_col.shape[1]

    @pl.loop(0, doc_col.shape[0] // lanes)
    def _(number):
        here = rows_of(number, lanes)
        spread = jnp.broadcast_to(doc_row[0:1, here].astype(F32), (lanes, lanes))
        doc_col[here, :] = spread.T.astype(jnp.int32)


def vmem_spec():
    return pl.BlockSpec(memory_space=pltpu.VMEM)


def any_spec():
    return pl.BlockSpec(memory_space=pl.ANY)


def smem_spec():
    return pl.BlockSpec(memory_space=pltpu.SMEM)


def forward_layers(table, spans, norms, doc_row, hidden, tiles, pairs):
    length, width = hidden.shape
    lanes = tiles.shape[2]
    one = (
        ((length, width), F32),
        ((length, width), BF16),
        ((3 * pairs, length, lanes), BF16),
        ((pairs, length, lanes), BF16),
        ((pairs, 8, length), F32),
        ((length, width), F32),
        ((length, width), BF16),
    )
    shapes = [((LAYERS, *s), d) for s, d in one] + [((length, width), BF16)]
    keep = [pltpu.VMEM(s, d) for s, d in one]
    return pl.pallas_call(
        forward_kernel,
        name="forward_layers",
        out_shape=[jax.ShapeDtypeStruct(s, d) for s, d in shapes],
        in_specs=[smem_spec(), smem_spec()] + [vmem_spec()] * 3 + [any_spec()],
        out_specs=[any_spec()] * len(shapes),
        scratch_shapes=[
            pltpu.VMEM((LAYERS, width, 3 * width), BF16),
            pltpu.VMEM((LAYERS, width, width), BF16),
            pltpu.VMEM((LAYERS, width, 4 * width), BF16),
            pltpu.VMEM((LAYERS, 4 * width, width), BF16),
            *keep[:4],
            pltpu.VMEM((length, lanes), F32),
            *keep[4:],
            pltpu.VMEM((length, lanes), jnp.int32),
            pltpu.SemaphoreType.DMA((48 * LAYERS,)),
            pltpu.SemaphoreType.DMA((8,)),
        ],
        compiler_params=pltpu.CompilerParams(vmem_limit_bytes=VMEM_BYTES),
        cost_estimate=pl.CostEstimate(
            flops=length * width * width * 52, bytes_accessed=40 * 2**20,
            transcendentals=length * length * 8,
        ),
    )(table, spans, norms, doc_row, hidden, tiles)


def backward_kernel(
    table, aims, spans, counts, norms, doc_row, upper_in,
    below_in, normed_in, packed_in, mixed_in, logsum_in, middle_in, normed_two_in, tiles,
    grad_out, tile_grads, norm_grads,
    w_qkv, w_out, w_up, w_down,
    flow, normed, packed, mixed, logsum, middle, normed_two, hidden,
    active, inner_grad, grad_low, mid_grad, mid_low, mixed_grad, delta, packed_grad,
    key_sum, value_sum, staged, blank, doc_col, selector,
    w_sem, i_sem, t_sem, z_sem, o_sem,
):
    length, width = flow.shape
    blocks = length // DENSE_BACK
    pairs, lanes = mixed.shape[0], mixed.shape[2]
    groups = (
        (0, 12, 12, w_qkv), (12, 4, 4, w_out), (16, 16, 16, w_up), (32, 16, 4, w_down),
    )
    ins = (
        (normed_two_in, normed_two), (middle_in, middle), (mixed_in, mixed),
        (packed_in, packed), (logsum_in, logsum), (below_in, hidden), (normed_in, normed),
    )

    def load(number, layer):
        return pltpu.make_async_copy(ins[number][0].at[layer], ins[number][1], i_sem.at[number])

    def fetch(group, layer, act):
        first, count, per_row, target = groups[group]
        weight_group(tiles, table, 48 * layer + first, count, per_row, target, w_sem, act)

    def early(layer):
        load(0, layer).start()
        fetch(2, layer, "start")
        fetch(3, layer, "start")
        load(1, layer).start()
        fetch(1, layer, "start")
        load(2, layer).start()

    def late(layer):
        load(3, layer).start()
        load(4, layer).start()

    take = pltpu.make_async_copy(upper_in, grad_low, o_sem.at[0])
    take.start()
    early(LAYERS - 1)
    late(LAYERS - 1)
    fetch(0, LAYERS - 1, "start")
    load(5, LAYERS - 1).start()
    load(6, LAYERS - 1).start()

    def blank_copies(act):
        capacity = tile_grads.shape[0] // counts.shape[0]
        quarter = capacity // 4

        @pl.loop(0, counts.shape[0])
        def _(owner):
            @pl.loop(counts[owner], capacity)
            def _(place):
                core, depth_z, part = lax.rem(owner, 2), lax.div(owner, 2), lax.div(place, quarter)
                low_bit, high_bit = lax.rem(part, 2), lax.div(part, 2)
                major = low_bit + core * (high_bit - low_bit)
                minor = high_bit + core * (low_bit - high_bit)
                index = lax.rem(place, quarter) * 32 + core * 16 + major * 8 + minor * 4 + depth_z
                getattr(
                    pltpu.make_async_copy(blank, tile_grads.at[index], z_sem.at[index]), act
                )()

    norm_grads[...] = jnp.zeros_like(norm_grads)
    blank[...] = jnp.zeros_like(blank)
    fill_columns(doc_row, doc_col)
    which = lax.broadcasted_iota(jnp.int32, selector.shape, 0)
    lane = lax.broadcasted_iota(jnp.int32, selector.shape, 1)
    head_dim = width // HEADS
    own_head = 2 * lax.div(which, 8) + lax.rem(which, 8)
    fits = (lax.rem(which, 8) < 2) & (lax.div(lane, head_dim) == own_head)
    selector[...] = jnp.where(fits, 1.0, 0.0).astype(BF16)
    take.wait()
    flow[...] = grad_low[...].astype(F32)
    chunk = 2 * width
    chunks = w_up.shape[1] // chunk

    def send_tile(place, layer):
        return pltpu.make_async_copy(
            staged.at[place], tile_grads.at[aims[48 * layer + place]], t_sem.at[place]
        )

    def settle_tiles(layer):
        @pl.loop(0, 48)
        def _(place):
            send_tile(place, layer).wait()

    def backward_one(layer):
        def norm_back(values, out_grad, gain, gain_row):
            unit, scale = normalized(values)
            sums = (
                jnp.sum(out_grad * unit, axis=0, keepdims=True),
                jnp.sum(out_grad, axis=0, keepdims=True),
            )
            for which in range(LAYERS):

                @pl.when(layer == which)
                def _(which=which):
                    for side in range(2):
                        row = 4 * which + gain_row + side
                        norm_grads[row : row + 1, :] += sums[side]

            turned = out_grad * gain
            average = jnp.mean(turned, axis=-1, keepdims=True)
            along = jnp.mean(turned * unit, axis=-1, keepdims=True)
            return scale * (turned - average - unit * along)

        load(0, layer).wait()
        fetch(2, layer, "wait")
        fetch(3, layer, "wait")
        load(1, layer).wait()
        fetch(1, layer, "wait")
        load(2, layer).wait()

        @pl.loop(0, blocks)
        def _(number):
            here = rows_of(number, DENSE_BACK)
            upper = flow[here, :]
            low = upper.astype(BF16)
            grad_low[here, :] = low
            normed_here = normed_two[here, :]
            total = jnp.zeros((DENSE_BACK, width), F32)
            for c in range(chunks):
                part = slice(c * chunk, (c + 1) * chunk)
                value, slope = gelu_both(dot_nn(normed_here, w_up[:, part]))
                active[here, part] = value.astype(BF16)
                inner = (slope * dot_nt(low, w_down[part, :])).astype(BF16)
                inner_grad[here, part] = inner
                total = total + dot_nt(inner, w_up[:, part])
            mid = upper + norm_back(middle[here, :], total, norms[pl.ds(4 * layer + 2, 1), :], 2)
            mid_grad[here, :] = mid
            mid_here = mid.astype(BF16)
            mid_low[here, :] = mid_here
            back = dot_nt(mid_here, w_out[...]).astype(BF16)
            for pair in range(pairs):
                mixed_grad[pair, here, :] = back[:, pair * lanes : (pair + 1) * lanes]
            side_by_side = jnp.concatenate([mixed[pair, here, :] for pair in range(pairs)], axis=1)
            both = side_by_side.astype(F32) * back.astype(F32)
            high = both.astype(BF16)
            rest = (both - high.astype(F32)).astype(BF16)
            sums = dot_nt(selector[...], high) + dot_nt(selector[...], rest)
            for pair in range(pairs):
                delta[pair, :, here] = sums[8 * pair : 8 * pair + 8, :]

        pl.when(layer < LAYERS - 1)(lambda: settle_tiles(layer + 1))

        def emit(block, first):
            for c in range(block.shape[1] // lanes):
                staged[first + c] = block[:, c * lanes : (c + 1) * lanes].astype(BF16)
                send_tile(first + c, layer).start()

        @pl.loop(0, 4)
        def _(c):
            part = rows_of(c, width)
            emit(dot_tn(active[:, part], grad_low[...]), 32 + 4 * c)
            emit(dot_tn(normed_two[...], inner_grad[:, part]), 16 + 4 * c)

        side_by_side = jnp.concatenate([mixed[pair] for pair in range(pairs)], axis=1)
        emit(dot_tn(side_by_side, mid_low[...]), 12)
        pl.when(layer > 0)(lambda: early(layer - 1))
        pl.when(layer == LAYERS - 1)(lambda: blank_copies("start"))
        load(3, layer).wait()
        load(4, layer).wait()
        first_half = lane_is_first((QUERY, lanes))

        key_sum[...] = jnp.zeros_like(key_sum)
        value_sum[...] = jnp.zeros_like(value_sum)

        @pl.loop(0, length // QUERY)
        def _(number):
            here = rows_of(number, QUERY)
            low_key = spans[0, number]
            key_count = spans[1, number]
            doc_here = doc_row[0:1, here]
            doc_here = jnp.concatenate([doc_here, doc_here], axis=1)

            def with_keys(many):
                keys_here = pl.ds(pl.multiple_of(low_key * QUERY, QUERY), many * BLOCK)
                same = doc_col[keys_here, 0:1] == doc_here

                def score(pair):
                    heads = stacked(packed[pair, here, :].astype(F32) * 0.125, first_half)
                    outs = stacked(mixed_grad[pair, here, :].astype(F32), first_half)
                    return (
                        heads,
                        outs,
                        dot_nt(packed[pairs + pair, keys_here, :], heads),
                        dot_nt(packed[2 * pairs + pair, keys_here, :], outs),
                    )

                def settle(pair, heads, outs, scores, from_values):
                    logs = jnp.concatenate([logsum[pair, 0:1, here], logsum[pair, 1:2, here]], axis=1)
                    means = jnp.concatenate([delta[pair, 0:1, here], delta[pair, 1:2, here]], axis=1)
                    weights = jnp.exp(jnp.where(same, scores - logs, -1e30))
                    score_grad = (weights * (from_values - means)).astype(BF16)
                    return heads, outs, weights.astype(BF16), score_grad

                def finish(pair, heads, outs, weights, score_grad):
                    value_sum[pair, keys_here, :] += dot_nn(weights, outs)
                    key_sum[pair, keys_here, :] += dot_nn(score_grad, heads)
                    query_part = dot_tn(score_grad, packed[pairs + pair, keys_here, :]) * 0.125
                    packed_grad[pair, here, :] = jnp.where(
                        first_half, query_part[:QUERY], query_part[QUERY:]
                    ).astype(BF16)

                waiting = None
                ahead = score(0)
                for pair in range(pairs):
                    now = ahead
                    if pair + 1 < pairs:
                        ahead = score(pair + 1)
                    done = settle(pair, *now)
                    if waiting is not None:
                        finish(pair - 1, *waiting)
                    waiting = done
                finish(pairs - 1, *waiting)

            for many in range(1, length // BLOCK + 1):
                pl.when(key_count == many)(lambda many=many: with_keys(many))

        for pair in range(pairs):
            packed_grad[pairs + pair] = key_sum[pair].astype(BF16)
            packed_grad[2 * pairs + pair] = value_sum[pair].astype(BF16)

        pl.when(layer > 0)(lambda: late(layer - 1))
        fetch(0, layer, "wait")
        load(5, layer).wait()
        load(6, layer).wait()

        @pl.loop(0, blocks)
        def _(number):
            here = rows_of(number, DENSE_BACK)
            wide = jnp.concatenate([packed_grad[j, here, :] for j in range(3 * pairs)], axis=1)
            total = dot_nt(wide, w_qkv[...])
            flow[here, :] = mid_grad[here, :] + norm_back(
                hidden[here, :], total, norms[pl.ds(4 * layer + 0, 1), :], 0
            )

        @pl.loop(0, 3)
        def _(c):
            wide = jnp.concatenate([packed_grad[pairs * c + j] for j in range(pairs)], axis=1)
            emit(dot_tn(normed[...], wide), 4 * c)

        @pl.when(layer > 0)
        def _():
            fetch(0, layer - 1, "start")
            load(5, layer - 1).start()
            load(6, layer - 1).start()

    @pl.loop(0, LAYERS)
    def _(step):
        backward_one(LAYERS - 1 - step)

    flush = pltpu.make_async_copy(grad_low, grad_out, o_sem.at[0])
    grad_low[...] = flow[...].astype(BF16)
    flush.start()
    settle_tiles(0)
    flush.wait()
    blank_copies("wait")


def backward_layers(
    table, aims, spans, counts, norms, doc_row, upper, saved, tiles
):
    length, width = upper.shape
    lanes = tiles.shape[2]
    pairs = width // lanes
    slots = tiles.shape[0]
    return pl.pallas_call(
        backward_kernel,
        name="backward_layers",
        out_shape=[
            jax.ShapeDtypeStruct((length, width), BF16),
            jax.ShapeDtypeStruct(tiles.shape, BF16),
            jax.ShapeDtypeStruct(norms.shape, F32),
        ],
        in_specs=[smem_spec()] * 4 + [vmem_spec()] * 2 + [any_spec()] * 9,
        out_specs=[any_spec(), any_spec(), vmem_spec()],
        scratch_shapes=[
            pltpu.VMEM((width, 3 * width), BF16),
            pltpu.VMEM((width, width), BF16),
            pltpu.VMEM((width, 4 * width), BF16),
            pltpu.VMEM((4 * width, width), BF16),
            pltpu.VMEM((length, width), F32),
            pltpu.VMEM((length, width), BF16),
            pltpu.VMEM((3 * pairs, length, lanes), BF16),
            pltpu.VMEM((pairs, length, lanes), BF16),
            pltpu.VMEM((pairs, 8, length), F32),
            pltpu.VMEM((length, width), F32),
            pltpu.VMEM((length, width), BF16),
            pltpu.VMEM((length, width), F32),
            pltpu.VMEM((length, 4 * width), BF16),
            pltpu.VMEM((length, 4 * width), BF16),
            pltpu.VMEM((length, width), BF16),
            pltpu.VMEM((length, width), F32),
            pltpu.VMEM((length, width), BF16),
            pltpu.VMEM((pairs, length, lanes), BF16),
            pltpu.VMEM((pairs, 8, length), F32),
            pltpu.VMEM((3 * pairs, length, lanes), BF16),
            pltpu.VMEM((pairs, length, lanes), F32),
            pltpu.VMEM((pairs, length, lanes), F32),
            pltpu.VMEM((48, width, lanes), BF16),
            pltpu.VMEM((width, lanes), BF16),
            pltpu.VMEM((length, lanes), jnp.int32),
            pltpu.VMEM((8 * pairs, width), BF16),
            pltpu.SemaphoreType.DMA((48 * LAYERS,)),
            pltpu.SemaphoreType.DMA((7,)),
            pltpu.SemaphoreType.DMA((48,)),
            pltpu.SemaphoreType.DMA((slots,)),
            pltpu.SemaphoreType.DMA((1,)),
        ],
        compiler_params=pltpu.CompilerParams(vmem_limit_bytes=VMEM_BYTES),
        cost_estimate=pl.CostEstimate(
            flops=length * width * width * 120, bytes_accessed=60 * 2**20,
            transcendentals=length * length * 8,
        ),
    )(
        table, aims, spans, counts, norms, doc_row, upper, *saved, tiles
    )


MESH_IDS = pl.DeviceIdType.MESH


def place_of_device():
    row = lax.axis_index("rows")
    seat = lax.axis_index("seq")
    return row % 2, row // 2, seat // 2, seat % 2


def device_at(x, y, z, core):
    return (2 * y + x, 2 * z + core)


def greet(partners):
    barrier = pltpu.get_barrier_semaphore()
    for partner in partners:
        pl.semaphore_signal(barrier, inc=1, device_id=partner, device_id_type=MESH_IDS)
    pl.semaphore_wait(barrier, len(partners))


def seat_partners(x, y, z, core):
    mirrored = (3 - z, (z + 2) % 4, z + 1 - 2 * (z % 2))
    others = [2 * far + side for far in mirrored for side in (core, 1 - core)]
    others.append(2 * z + 1 - core)
    return others, [(2 * y + x, other) for other in others]


def post(source, target, send_sem, recv_sem, number, partner):
    copy = pltpu.make_async_remote_copy(
        src_ref=source,
        dst_ref=target,
        send_sem=send_sem.at[number],
        recv_sem=recv_sem.at[number],
        device_id=partner,
        device_id_type=MESH_IDS,
    )
    copy.start()
    return copy


def gather_kernel(master, residual, tiles, rows, wide, low, flat, flat_low, send_sem, recv_sem, l_sem):
    x, y, z, core = place_of_device()
    quarter_id = 2 * y + x
    across = device_at(x, y, z, 1 - core)
    by_x = device_at(1 - x, y, z, core)
    by_y = device_at(x, 1 - y, z, core)
    quarters = (quarter_id, 2 * y + (1 - x), 2 * (1 - y) + x, 3 - quarter_id)
    others, seats = seat_partners(x, y, z, core)
    seat = 2 * z + core
    load_near = pltpu.make_async_copy(
        master.at[pl.ds(4 * quarter_id, 4)], wide.at[pl.ds(4 * quarter_id, 4)], l_sem.at[0]
    )
    load_near.start()
    far = []
    for k in range(1, 4):
        part = pl.ds(4 * ((quarter_id + k) % 4), 4)
        copy = pltpu.make_async_copy(master.at[part], wide.at[part], l_sem.at[1 + k])
        copy.start()
        far.append(copy)
    load_flat = pltpu.make_async_copy(residual, flat, l_sem.at[1])
    load_flat.start()
    greet(seats + [by_x, by_y])

    def spot(z_from, quarter):
        return core * 64 + z_from * 16 + 4 * quarter

    def convert(first, count):
        @pl.loop(0, count)
        def _(j):
            low[first + j] = wide[first + j].astype(BF16)

    def make(source, target, number, partner):
        return pltpu.make_async_remote_copy(
            src_ref=source, dst_ref=target, send_sem=send_sem.at[number],
            recv_sem=recv_sem.at[number], device_id=partner, device_id_type=MESH_IDS,
        )

    def relay(number, first, count, partner):
        part = pl.ds(first, count)
        return make(tiles.at[part], tiles.at[part], number, partner)

    mine = pl.ds(core * 64 + z * 16, 16)

    def hop(way, step, half):
        toward = device_at(x, y, lax.rem(z + (1 if way == 0 else 3), 4), core)
        number = 6 * way + 2 * (step - 1) + half
        if step == 1:
            near = pl.ds(spot(z, quarter_id) + 2 * half, 2)
            return make(low.at[pl.ds(4 * quarter_id + 2 * half, 2)], tiles.at[near], number, toward)
        z_from = lax.rem(z + (5 - step if way == 0 else step - 1), 4)
        return relay(number, spot(z_from, quarter_id) + 2 * half, 2, toward)

    def can_send(way, step):
        if way == 0:
            return (z < 3) & (z >= step - 1)
        return (z > 0) & (z <= 4 - step)

    def arrives(way, step):
        return z >= step if way == 0 else z <= 3 - step

    def source(way, step):
        return lax.rem(z + (4 - step if way == 0 else step), 4)

    rounds = [
        [(way, step, half) for half in range(2) for way in range(2)] for step in range(1, 4)
    ]
    steps = rounds[0] + rounds[1] + rounds[2]

    def fan(way, step, half):
        base = 12 + 7 * (6 * way + 2 * (step - 1) + half)
        z_from = source(way, step)
        spots = [spot(z_from, quarter) + 2 * half for quarter in quarters]
        return [
            relay(base, spots[0], 2, by_x),
            relay(base + 1, spots[0], 2, by_y),
            relay(base + 2, spots[0], 2, across),
            relay(base + 3, spots[1 + half], 2, by_x if half else by_y),
            relay(base + 4, spots[1], 2, across),
            relay(base + 5, spots[2], 2, across),
            relay(base + 6, spots[3], 2, across),
        ]

    load_near.wait()
    convert(4 * quarter_id, 4)
    for way, step, half in rounds[0]:
        pl.when(can_send(way, 1))(lambda way=way, half=half: hop(way, 1, half).start())
    for k in range(1, 4):
        far[k - 1].wait()
        convert(4 * ((quarter_id + k) % 4), 4)
    keep_tiles = pltpu.make_async_copy(low, tiles.at[mine], l_sem.at[6])
    keep_tiles.start()
    own_across = make(low, tiles.at[mine], 96, across)
    own_across.start()
    load_flat.wait()

    @pl.loop(0, flat.shape[0])
    def _(j):
        flat_low[j] = flat[j].astype(BF16)

    keep_row = pltpu.make_async_copy(flat_low.at[seat], rows.at[seat], l_sem.at[5])
    keep_row.start()
    row_moves = [
        make(flat_low.at[others[k - 1]], rows.at[seat], 96 + k, seats[k - 1])
        for k in range(1, 8)
    ]

    def take(way, step, half):
        hop(way, step, half).wait_recv()
        if step < 3:
            pl.when(can_send(way, step + 1))(lambda: hop(way, step + 1, half).start())
        for copy in fan(way, step, half)[:3]:
            copy.start()

    def turn(way, step, half):
        moves = fan(way, step, half)
        for side in (half, 1 - half):
            moves[side].wait_recv()
            if side == half:
                moves[3].start()
            moves[4 + side].start()

    def finish(way, step, half):
        moves = fan(way, step, half)
        moves[3].wait_recv()
        moves[6].start()

    def drain(way, step, half):
        moves = fan(way, step, half)
        for number in (2, 4, 5, 6):
            moves[number].wait_recv()
        for copy in moves:
            copy.wait_send()

    def each(act, chosen):
        for key in chosen:
            pl.when(arrives(key[0], key[1]))(lambda key=key: act(*key))

    each(take, rounds[0])
    each(take, rounds[1][:2])
    each(turn, rounds[0][:2])
    each(take, rounds[1][2:])
    each(turn, rounds[0][2:])
    each(take, rounds[2])
    for copy in row_moves:
        copy.start()
    each(turn, rounds[1])
    each(finish, rounds[0])
    each(turn, rounds[2])
    each(finish, rounds[1] + rounds[2])
    own_across.wait_recv()
    each(drain, steps)
    for way, step, half in steps:
        pl.when(can_send(way, step))(
            lambda way=way, step=step, half=half: hop(way, step, half).wait_send()
        )
    for copy in row_moves:
        copy.wait_recv()
        copy.wait_send()
    own_across.wait_send()
    keep_row.wait()
    keep_tiles.wait()


def gather_start(master_tiles, residual):
    capacity, depth, lanes = master_tiles.shape
    count = 104
    return pl.pallas_call(
        gather_kernel,
        name="gather_start",
        out_shape=[
            jax.ShapeDtypeStruct((8 * capacity, depth, lanes), BF16),
            jax.ShapeDtypeStruct(residual.shape, BF16),
        ],
        in_specs=[any_spec()] * 2,
        out_specs=[any_spec()] * 2,
        scratch_shapes=[
            pltpu.VMEM(master_tiles.shape, F32),
            pltpu.VMEM(master_tiles.shape, BF16),
            pltpu.VMEM(residual.shape, F32),
            pltpu.VMEM(residual.shape, BF16),
            pltpu.SemaphoreType.DMA((count,)),
            pltpu.SemaphoreType.DMA((count,)),
            pltpu.SemaphoreType.DMA((7,)),
        ],
        compiler_params=pltpu.CompilerParams(
            collective_id=0, has_side_effects=True, vmem_limit_bytes=VMEM_BYTES
        ),
        cost_estimate=pl.CostEstimate(
            flops=0, bytes_accessed=200 * 2**20, transcendentals=0
        ),
    )(master_tiles, residual)


def reduce_kernel(
    held, upper, norm_part, owned, rows, norm_sum, squares,
    core_in, own, one_in, two_in, z_in, piece, norm_in, norm_now, square_in,
    square_now, send_sem, recv_sem, l_sem,
):
    x, y, z, core = place_of_device()
    quarter_id = 2 * y + x
    across = device_at(x, y, z, 1 - core)
    by_x = device_at(1 - x, y, z, core)
    by_y = device_at(x, 1 - y, z, core)
    by_both = device_at(1 - x, 1 - y, z, core)
    plus, minus = core, 1 - core
    first_bit = x * minus + y * plus
    second_bit = y * minus + x * plus
    one = device_at(x + minus * (1 - 2 * x), y + plus * (1 - 2 * y), z, core)
    two = device_at(x + plus * (1 - 2 * x), y + minus * (1 - 2 * y), z, core)
    along_z = [device_at(x, y, (z + k) % 4, core) for k in range(1, 4)]
    others, seats = seat_partners(x, y, z, core)
    seat = 2 * z + core
    quarter_x, quarter_y = 2 * y + (1 - x), 2 * (1 - y) + x
    chunks = own.shape[0]
    number = 0
    copies = []

    def move(source, target, partner):
        nonlocal number
        copy = post(source, target, send_sem, recv_sem, number, partner)
        number += 1
        copies.append(copy)
        return copy

    loads = []
    for i in range(chunks):
        copy = pltpu.make_async_copy(
            held.at[pl.ds(32 * i + 16 * core, 16)], own.at[i], l_sem.at[i]
        )
        copy.start()
        loads.append(copy)
    greet(seats + [by_x, by_y, by_both])
    half = own.shape[2] // 2
    parts = [(i, pl.ds(half * side, half)) for i in range(chunks) for side in range(2)]
    core_moves = [
        move(held.at[pl.ds(32 * i + 16 * (1 - core), 16), rows_], core_in.at[i, :, rows_], across)
        for i, rows_ in parts
    ]
    norm_now[0] = norm_part[...]
    norm_moves = [move(norm_now.at[0], norm_in.at[0], across)]
    for k in range(1, 8):
        move(upper.at[others[k - 1]], rows.at[seat], seats[k - 1])
    row_moves = copies[-7:]
    keep_row = pltpu.make_async_copy(upper.at[seat], rows.at[seat], l_sem.at[chunks])
    keep_row.start()

    def add_in(target, first, incoming, count, part):
        @pl.loop(0, count)
        def _(j):
            target[first + j, part, :] = (
                target[first + j, part, :].astype(F32) + incoming[j, part, :].astype(F32)
            ).astype(BF16)

    one_moves, two_moves, z_moves, near_moves, corner_moves, keeps = [], [], [], [], [], []

    def stage_core(n):
        i, part = parts[n]
        if n % 2 == 0:
            loads[i].wait()
        core_moves[n].wait_recv()
        add_in(own.at[i], 0, core_in.at[i], 16, part)
        one_moves.append(
            move(
                own.at[i, pl.ds(8 * (1 - first_bit), 8), part], one_in.at[i, :, part], one
            )
        )

    def stage_one(n):
        i, part = parts[n]
        one_moves[n].wait_recv()
        add_in(own.at[i], 8 * first_bit, one_in.at[i], 8, part)
        two_moves.append(
            move(
                own.at[i, pl.ds(8 * first_bit + 4 * (1 - second_bit), 4), part],
                two_in.at[i, :, part],
                two,
            )
        )

    def stage_two(n):
        i, part = parts[n]
        two_moves[n].wait_recv()
        base = 8 * first_bit + 4 * second_bit
        add_in(own.at[i], base, two_in.at[i], 4, part)
        z_moves.append(
            [
                move(
                    own.at[i, base + (z + k) % 4, part], z_in.at[i, k - 1, part], along_z[k - 1]
                )
                for k in range(1, 4)
            ]
        )

    def stage_z(n):
        i, part = parts[n]
        for copy in z_moves[n]:
            copy.wait_recv()
        total = own[i, 8 * first_bit + 4 * second_bit + z, part, :].astype(F32)
        for k in range(3):
            total = total + z_in[i, k, part, :].astype(F32)
        piece[i, part, :] = total.astype(BF16)
        square_now[0] += jnp.sum((total * total).reshape(-1, 8, total.shape[1]), axis=0)
        here = owned.at[4 * quarter_id + i, part]
        near_moves.append(
            [move(piece.at[i, part], here, partner) for partner in (by_x, by_y)]
        )
        if n >= len(parts) - 2:
            corner_moves.append(move(piece.at[i, part], here, by_both))
        keep = pltpu.make_async_copy(piece.at[i, part], here, l_sem.at[chunks + 1 + n])
        keep.start()
        keeps.append(keep)

    def stage_turn(n):
        i, part = parts[n]
        side = n % 2
        near_moves[n][1 - side].wait_recv()
        far_id = quarter_y if side == 0 else quarter_x
        here = owned.at[4 * far_id + i, part]
        corner_moves.append(move(here, here, by_x if side == 0 else by_y))

    def norm_stage(step, partner):
        norm_moves[step].wait_recv()
        norm_now[step + 1] = norm_now[step] + norm_in[step]
        if partner is not None:
            norm_moves.append(move(norm_now.at[step + 1], norm_in.at[step + 1], partner))

    square_now[...] = jnp.zeros_like(square_now)
    for n in range(8):
        stage_core(n)
        if n == 1:
            norm_stage(0, by_x)
        if n == 3:
            norm_stage(1, by_y)
        if n == 5:
            norm_stage(2, None)
    norm_z = [move(norm_now.at[3], norm_in.at[2 + k], along_z[k - 1]) for k in range(1, 4)]
    for n in range(8 + 5):
        if n < 8:
            stage_one(n)
        if 0 <= n - 1 < 8:
            stage_two(n - 1)
        if 0 <= n - 3 < 8:
            stage_z(n - 3)
        if 0 <= n - 5 < 6:
            stage_turn(n - 5)

    def in_order(own_value, incoming):
        values = [own_value] + [incoming(k) for k in range(1, 4)]
        total = None
        for place in range(4):
            picked = values[0]
            for k in range(1, 4):
                picked = jnp.where((z + 4 - k) % 4 == place, values[k], picked)
            total = picked if total is None else total + picked
        return total

    square_moves = []

    def square_stage(step, partner):
        square_moves.append(move(square_now.at[step], square_in.at[step], partner))
        square_moves[step].wait_recv()
        square_now[step + 1] = square_now[step] + square_in[step]

    square_stage(0, by_x)
    square_stage(1, by_y)
    square_stage(2, across)
    square_z = [
        move(square_now.at[3], square_in.at[2 + k], along_z[k - 1]) for k in range(1, 4)
    ]
    for copy in norm_z:
        copy.wait_recv()
    norm_sum[...] = in_order(norm_now[3], lambda k: norm_in[2 + k])
    for copy in square_z:
        copy.wait_recv()
    squares[...] = in_order(square_now[3], lambda k: square_in[2 + k])
    straight = [near_moves[n][n % 2] for n in range(6)] + near_moves[6] + near_moves[7]
    for copy in row_moves + straight + corner_moves:
        copy.wait_recv()
    for copy in copies:
        copy.wait_send()
    keep_row.wait()
    for keep in keeps:
        keep.wait()


def reduce_end(held, upper, norm_part):
    slots, depth, lanes = held.shape
    chunks = 4
    count = 8 + 1 + 7 + 8 + 8 + 24 + 24 + 2 + 3 + 3 + 3
    return pl.pallas_call(
        reduce_kernel,
        name="reduce_end",
        out_shape=[
            jax.ShapeDtypeStruct((slots // 8, depth, lanes), BF16),
            jax.ShapeDtypeStruct(upper.shape, BF16),
            jax.ShapeDtypeStruct(norm_part.shape, F32),
            jax.ShapeDtypeStruct((8, lanes), F32),
        ],
        in_specs=[any_spec(), any_spec(), vmem_spec()],
        out_specs=[any_spec(), any_spec(), vmem_spec(), vmem_spec()],
        scratch_shapes=[
            pltpu.VMEM((chunks, 16, depth, lanes), BF16),
            pltpu.VMEM((chunks, 16, depth, lanes), BF16),
            pltpu.VMEM((chunks, 8, depth, lanes), BF16),
            pltpu.VMEM((chunks, 4, depth, lanes), BF16),
            pltpu.VMEM((chunks, 3, depth, lanes), BF16),
            pltpu.VMEM((chunks, depth, lanes), BF16),
            pltpu.VMEM((6, *norm_part.shape), F32),
            pltpu.VMEM((4, *norm_part.shape), F32),
            pltpu.VMEM((6, 8, lanes), F32),
            pltpu.VMEM((4, 8, lanes), F32),
            pltpu.SemaphoreType.DMA((count,)),
            pltpu.SemaphoreType.DMA((count,)),
            pltpu.SemaphoreType.DMA((3 * chunks + 1,)),
        ],
        compiler_params=pltpu.CompilerParams(
            collective_id=1, has_side_effects=True, vmem_limit_bytes=VMEM_BYTES
        ),
        cost_estimate=pl.CostEstimate(
            flops=0, bytes_accessed=300 * 2**20, transcendentals=0
        ),
    )(held, upper, norm_part)


def finish_kernel(
    counts, owned_in, master_in, first_in, second_in, grad_rows_in, out_rows_in, squares, norm_sum,
    norm_params, norm_first, norm_second,
    clip_out, first_out, second_out, master_out, copy_out, grad_rows_out, out_rows_out,
    total_out, norm_clip_out, norm_first_out, norm_second_out, norm_params_out,
    owned, master, first, second, grad_rows, out_rows,
    clip, new_first, new_second, new_master, new_copy, wide_grad, wide_out, i_sem, o_sem,
):
    ins = ((owned_in, owned), (master_in, master), (first_in, first), (second_in, second))
    capacity = master.shape[0]

    def bring(number, place):
        return pltpu.make_async_copy(
            ins[number][0].at[place], ins[number][1].at[place],
            i_sem.at[number * capacity + place],
        )

    @pl.loop(0, capacity)
    def _(place):
        for number in range(len(ins)):
            bring(number, place).start()

    bring_rows = [
        pltpu.make_async_copy(source, target, i_sem.at[4 * capacity + number])
        for number, (source, target) in enumerate(
            ((grad_rows_in, grad_rows), (out_rows_in, out_rows))
        )
    ]
    for copy in bring_rows:
        copy.start()
    norms = norm_sum[...]
    total = jnp.sqrt(jnp.sum(squares[...]) + jnp.sum(norms * norms))
    factor = 1.0 / jnp.maximum(total, 1.0)
    correction = 1.0 - 0.5**STEP

    def step(weight, grad, low, high, rate):
        low = 0.5 * low + 0.5 * grad
        high = 0.5 * high + 0.5 * grad * grad
        update = low / correction / (jnp.sqrt(high / correction) + 1e-08)
        return weight - rate * (update + 0.01 * weight), low, high

    outs = (
        (clip, clip_out), (new_first, first_out), (new_second, second_out),
        (new_master, master_out), (new_copy, copy_out),
    )

    def send(number, place):
        return pltpu.make_async_copy(
            outs[number][0].at[place], outs[number][1].at[place],
            o_sem.at[number * capacity + place],
        )

    count = counts[lax.axis_index("seq")]

    @pl.loop(0, capacity)
    def _(place):
        for number in range(len(ins)):
            bring(number, place).wait()
        keep = (lax.broadcast(place, clip.shape[1:])) < count
        grad = jnp.where(keep, owned[place].astype(F32), 0.0) * factor
        weight, low, high = step(master[place], grad, first[place], second[place], 0.05)
        weight = jnp.where(keep, weight, 0.0)
        clip[place] = grad
        new_first[place] = jnp.where(keep, low, 0.0)
        new_second[place] = jnp.where(keep, high, 0.0)
        new_master[place] = weight
        new_copy[place] = weight.astype(BF16)
        for number in range(len(outs)):
            send(number, place).start()

    moves = []
    for number, (low, wide, target) in enumerate(
        ((grad_rows, wide_grad, grad_rows_out), (out_rows, wide_out, out_rows_out))
    ):

        bring_rows[number].wait()

        @pl.loop(0, low.shape[0])
        def _(j, low=low, wide=wide):
            wide[j] = low[j].astype(F32)

        moves.append(pltpu.make_async_copy(wide, target, o_sem.at[5 * capacity + number]))
        moves[-1].start()
    clipped = norms * factor
    weight, low, high = step(norm_params[...], clipped, norm_first[...], norm_second[...], 0.25)
    total_out[...] = jnp.broadcast_to(total, total_out.shape)
    norm_clip_out[...] = clipped
    norm_first_out[...] = low
    norm_second_out[...] = high
    norm_params_out[...] = weight

    @pl.loop(0, capacity)
    def _(place):
        for number in range(len(outs)):
            send(number, place).wait()

    for move in moves:
        move.wait()


def finish_step(
    counts, owned, master, first, second, grad_rows, out_rows, squares, norm_sum, norm_params,
    norm_first, norm_second,
):
    tiles = jax.ShapeDtypeStruct(master.shape, F32)
    rows = jax.ShapeDtypeStruct(grad_rows.shape, F32)
    norms = jax.ShapeDtypeStruct(norm_params.shape, F32)
    return pl.pallas_call(
        finish_kernel,
        name="finish_step",
        out_shape=[
            tiles, tiles, tiles, tiles, jax.ShapeDtypeStruct(master.shape, BF16), rows, rows,
            jax.ShapeDtypeStruct((1, 128), F32), norms, norms, norms, norms,
        ],
        in_specs=[smem_spec()] + [any_spec()] * 6 + [vmem_spec()] * 5,
        out_specs=[any_spec()] * 7 + [vmem_spec()] * 5,
        scratch_shapes=[pltpu.VMEM(owned.shape, BF16)]
        + [pltpu.VMEM(master.shape, F32)] * 3
        + [pltpu.VMEM(grad_rows.shape, BF16)] * 2
        + [pltpu.VMEM(master.shape, F32)] * 4
        + [pltpu.VMEM(master.shape, BF16)]
        + [pltpu.VMEM(grad_rows.shape, F32)] * 2
        + [pltpu.SemaphoreType.DMA((4 * master.shape[0] + 2,))]
        + [pltpu.SemaphoreType.DMA((5 * master.shape[0] + 2,))],
        compiler_params=pltpu.CompilerParams(vmem_limit_bytes=VMEM_BYTES),
        cost_estimate=pl.CostEstimate(
            flops=0, bytes_accessed=40 * 2**20, transcendentals=0
        ),
    )(
        counts, owned, master, first, second, grad_rows, out_rows, squares, norm_sum, norm_params,
        norm_first, norm_second,
    )


def local_by_rows(
    residual_in,
    cotangent,
    segments,
    owners,
    master_tiles,
    first_tiles,
    second_tiles,
    norm_params,
    norm_first,
    norm_second,
):
    local_rows, positions, model_width = residual_in.shape
    seq_devices = lax.axis_size("seq")
    seq_index = lax.axis_index("seq")
    length = positions * seq_devices
    tile_total = owners.shape[0]
    capacity, _, tile_width = master_tiles.shape
    quarter = capacity // 4
    pairs = model_width // tile_width
    places = jnp.arange(tile_total, dtype=jnp.int32)
    before = (owners[None, :] == owners[:, None]) & (places[None, :] < places[:, None])
    ranks = jnp.sum(before.astype(jnp.int32), axis=1)
    core, depth_z, part_id = owners % 2, owners // 2, ranks // quarter
    major = jnp.where(core == 0, part_id % 2, part_id // 2)
    minor = jnp.where(core == 0, part_id // 2, part_id % 2)
    weight_table = core * 64 + depth_z * 16 + ranks
    grad_table = (ranks % quarter) * 32 + core * 16 + major * 8 + minor * 4 + depth_z
    seats = jnp.arange(seq_devices, dtype=jnp.int32)
    counts = jnp.sum((owners[None, :] == seats[:, None]).astype(jnp.int32), axis=1)
    tiles, hidden = gather_start(master_tiles, residual_in)
    hidden = hidden.reshape(length, model_width)
    later, tiles = lax.optimization_barrier((cotangent, tiles))
    upper = lax.all_to_all(later.astype(BF16), "seq", split_axis=0, concat_axis=0, tiled=True)
    upper = upper.reshape(length, model_width)
    doc_ids = lax.dynamic_slice_in_dim(segments, seq_index, 1, 0)
    doc_row = doc_ids
    begin = jnp.sum((doc_ids < doc_ids[0, ::QUERY, None]).astype(jnp.int32), axis=1) // QUERY
    end = jnp.sum((doc_ids <= doc_ids[0, QUERY - 1 :: QUERY, None]).astype(jnp.int32), axis=1)
    many = (end - begin * QUERY + BLOCK - 1) // BLOCK
    spans = jnp.stack([jnp.minimum(begin, (length - many * BLOCK) // QUERY), many])
    *saved, after = forward_layers(
        weight_table, spans, norm_params, doc_row, hidden, tiles, pairs
    )
    out_rows = lax.all_to_all(
        after.reshape(residual_in.shape), "seq", split_axis=0, concat_axis=0, tiled=True
    )
    lower, held, norm_part = backward_layers(
        weight_table, grad_table, spans, counts, norm_params, doc_row, upper, saved, tiles,
    )
    owned, grad_rows, norm_sum, squares = reduce_end(
        held, lower.reshape(residual_in.shape), norm_part
    )
    (
        clipped, new_first, new_second, new_weight, new_copies, input_grad, residual_out,
        total, norm_clip, new_norm_f, new_norm_s, new_norm,
    ) = finish_step(
        counts, owned, master_tiles, first_tiles, second_tiles, grad_rows, out_rows, squares,
        norm_sum, norm_params, norm_first, norm_second,
    )
    return (
        residual_out,
        input_grad,
        clipped,
        total[0, :1],
        new_first,
        new_second,
        new_weight,
        new_copies,
        norm_clip,
        new_norm_f,
        new_norm_s,
        new_norm,
    )


def local(residual_in, *others):
    whole_rows = residual_in.shape[0] == lax.axis_size("seq")
    step = local_by_rows if whole_rows else local_by_heads
    return step(residual_in, *others)


def solution(mesh):
    by_rows = P("rows", "seq", None)
    by_slots = P("seq", None, None)
    return jax.shard_map(
        local,
        mesh=mesh,
        in_specs=(
            by_rows, by_rows, P("rows", None), P(), by_slots, by_slots, by_slots, P(), P(), P(),
        ),
        out_specs=(
            by_rows, by_rows, by_slots, P(), by_slots, by_slots, by_slots, by_slots,
            P(), P(), P(), P(),
        ),
        check_vma=False,
    )
```
